32 devices in a mesh: heads: 4 (over z), rows: 8 (over y, x, core).
Axes of the slice: x: 2, y: 2, z: 4, core: 2. Of those that a mesh axis runs over, the one named last changes fastest.
Arguments:
- tokens: bfloat16 [4, 2048, 1024], P(None, 'rows'), may hold values from -6 to 6
- cam_index: int32 [4, 2048], P(None, 'rows'), may hold values from 0 to 31
- patches: bfloat16 [4, 2048, 768], P(None, 'rows'), may hold values from -6 to 6
- patch_len: int32 [4], replicated, may hold values from 512 to 2048, as said below
- camera_table: bfloat16 [32, 2, 1024], replicated, may hold values from -3 to 3
- self_weights: bfloat16 [3, 1024, 1024], P(None, None, 'heads'), may hold values from -0.1875 to 0.1875
- self_output: bfloat16 [1024, 1024], P('heads'), may hold values from -4 to 4
- cross_gain: bfloat16 [1024], replicated, may hold values from 0.5 to 1.5
- cross_query: bfloat16 [1024, 1024], P(None, 'heads'), may hold values from -0.1875 to 0.1875
- cross_pair: bfloat16 [2, 1024, 1024], P(None, None, 'heads'), may hold values from -0.1875 to 0.1875
- cross_output: bfloat16 [1024, 1024], P('heads'), may hold values from -4 to 4
- patch_weights: bfloat16 [768, 1024], replicated, may hold values from -0.21875 to 0.21875
- hidden_gain: bfloat16 [1024], replicated, may hold values from 0.5 to 1.5
- widen_weights: bfloat16 [1024, 4096], P(None, 'heads'), may hold values from -0.1875 to 0.1875
- narrow_weights: bfloat16 [4096, 1024], P('heads'), may hold values from -0.09375 to 0.09375
- cotangent: bfloat16 [4, 2048, 1024], P(None, 'rows'), may hold values from -6 to 6
Outputs:
- tokens_out: bfloat16 [4, 2048, 1024], P(None, 'rows')
- input_grad: float32 [4, 2048, 1024], P(None, 'rows')
- patch_grad: float32 [4, 2048, 768], P(None, 'rows')
- grad_camera_table: float32 [32, 2, 1024], P(None, None, 'heads')
- grad_self_weights: float32 [3, 1024, 1024], P(None, None, 'heads')
- grad_self_output: float32 [1024, 1024], P('heads')
- grad_cross_gain: float32 [1024], P('heads')
- grad_cross_query: float32 [1024, 1024], P(None, 'heads')
- grad_cross_pair: float32 [2, 1024, 1024], P(None, None, 'heads')
- grad_cross_output: float32 [1024, 1024], P('heads')
- grad_patch_weights: float32 [768, 1024], P(None, 'heads')
- grad_hidden_gain: float32 [1024], P('heads')
- grad_widen_weights: float32 [1024, 4096], P(None, 'heads')
- grad_narrow_weights: float32 [4096, 1024], P('heads')
The draws below stay inside these ranges and needn't reach their ends.
Inputs may be any that keep to these rules, and one draw needn't show every extreme that they name: `patch_len`: each entry is 2048 or a quarter of 2048; both values occur in every draw. Live patch tokens are the first ones of the object.
All inputs are finite; a program needn't handle non-finite values.
Results may differ from the reference program's by a relative error of at most 0.028.
The reference program's roundings to bfloat16 on the way count: a program that leaves them out, or rounds other values in their place, can miss the bound.
Values may be sent and summed in bfloat16 or wider, within the bound.
No kernel may reach another device: no remote copies, remote signals or barrier semaphores. Data moves between devices by JAX's collectives and lax.ppermute only.
A program may use at most 448 MiB of HBM per device.

```python
import jax
import jax.numpy as jnp
from jax import lax

D = 1024
HEAD_DIM = 64
FF = 4096
PD = 768
CAMS = 32
MICRO = 4
TOK_DEV = 256
TOKENS = 2048
PATCHES = 2048


def draw_patch_len(key, part):
    order = jax.random.permutation(key, MICRO)
    return jnp.where(order % 2 == 0, PATCHES, PATCHES // 4).astype(jnp.int32)


def place_ends(values, key, smallest, top_value):
    longest = values.shape.index(max(values.shape))
    spots = []
    for shift in (0, 1):
        where = [jax.random.randint(jax.random.fold_in(key, axis), (), 0, length) for axis, length in enumerate(values.shape)]
        where[longest] = (where[longest] + shift) % values.shape[longest]
        spots.append(tuple(where))
    return values.at[spots[0]].set(smallest).at[spots[1]].set(top_value)


def block_scale(stream_key, dims, split, smallest, high):
    gain = 1.0
    for axis_at, blocks in split:
        steps = jax.random.uniform(jax.random.fold_in(jax.random.fold_in(stream_key, 6), axis_at), (blocks,), jnp.float32, smallest / len(split), high / len(split))
        gain = gain * jnp.repeat(jnp.exp(steps), dims[axis_at] // blocks).reshape((-1,) + (1,) * (len(dims) - 1 - axis_at))
    return gain


def gaussian(stream_key, dims, spread, limit, shards=(), held_as=jnp.bfloat16):
    values = jax.random.normal(stream_key, dims, jnp.float32) * spread
    if len(shards) > 0:
        values = block_scale(stream_key, dims, shards, -0.22, 0.18) * values
    return jnp.clip(values, min=-limit, max=limit).astype(held_as)


def setup_inputs(seed: int = 0) -> dict:
    keys = jax.random.split(jax.random.key(seed), 17)
    return {
        "tokens": gaussian(keys[0], (MICRO, TOKENS, D), 1.0, 6.0, ((1, 8),)),
        "cam_index": place_ends(jax.random.randint(keys[1], (MICRO, TOKENS), 0, CAMS), jax.random.fold_in(keys[1], 1), 0, CAMS - 1).astype(jnp.int32),
        "patches": gaussian(keys[2], (MICRO, PATCHES, PD), 1.0, 6.0, ((1, 8),)),
        "patch_len": draw_patch_len(jax.random.fold_in(keys[16], 71), 0),
        "camera_table": gaussian(keys[4], (CAMS, 2, D), 0.5, 3.0),
        "self_weights": gaussian(keys[5], (3, D, D), D ** -0.5, 0.1875, ((2, 4),)),
        "self_output": gaussian(keys[6], (D, D), 2 ** -0.5, 4.0, ((0, 4),)),
        "cross_gain": jnp.clip(1.0 + 0.1 * jax.random.normal(keys[7], (D,), jnp.float32), 0.5, 1.5).astype(jnp.bfloat16),
        "cross_query": gaussian(keys[8], (D, D), D ** -0.5, 0.1875, ((1, 4),)),
        "cross_pair": gaussian(keys[9], (2, D, D), D ** -0.5, 0.1875, ((2, 4),)),
        "cross_output": gaussian(keys[10], (D, D), 2 ** -0.5, 4.0, ((0, 4),)),
        "patch_weights": gaussian(keys[11], (PD, D), PD ** -0.5, 0.21875),
        "hidden_gain": jnp.clip(1.0 + 0.1 * jax.random.normal(keys[12], (D,), jnp.float32), 0.5, 1.5).astype(jnp.bfloat16),
        "widen_weights": gaussian(keys[13], (D, FF), D ** -0.5, 0.1875, ((1, 4),)),
        "narrow_weights": gaussian(keys[14], (FF, D), FF ** -0.5, 0.09375, ((0, 4),)),
        "cotangent": gaussian(keys[15], (MICRO, TOKENS, D), 1.0, 6.0, ((1, 8),)),
    }


@jax.custom_vjp
def low(v):
    return lax.optimization_barrier(v.astype(jnp.bfloat16)).astype(jnp.float32)

@jax.custom_vjp
def low_back(v):
    return v

def low_keep(v):
    return (low(v), None)

def low_pass(kept, grad):
    return (grad,)

def back_keep(v):
    return (v, None)

def back_low(kept, grad):
    return (low(grad),)
low.defvjp(low_keep, low_pass)
low_back.defvjp(back_keep, back_low)
EPSILON = 1e-05
HIGHEST = lax.Precision.HIGHEST

def product(former, latter):
    return jnp.dot(former, latter, precision=HIGHEST)

def layer_norm(inputs):
    centred = inputs - lax.optimization_barrier(jnp.mean(inputs, axis=-1, keepdims=True))
    return centred * lax.rsqrt(lax.optimization_barrier(jnp.mean(centred * centred, axis=-1, keepdims=True)) + EPSILON)

def by_heads(matrix):
    return matrix.reshape(matrix.shape[0], -1, HEAD_DIM)

def attend(queries, key_rows, value_rows, mask_add):
    score_scale = HEAD_DIM ** (-0.5)
    blocks = queries.reshape(-1, TOK_DEV, queries.shape[1], queries.shape[2])

    def query_block(block_rows):
        scores = low_back(jnp.einsum('qhe,khe->hqk', block_rows, key_rows, precision=HIGHEST) * score_scale) + mask_add
        attn_probs = low(jax.nn.softmax(scores, axis=-1))
        mixed_out = jnp.einsum('hqk,khe->qhe', attn_probs, value_rows, precision=HIGHEST)
        return low(low_back(mixed_out))
    return lax.map(jax.checkpoint(query_block), blocks).reshape(queries.shape[0], -1)

def block_forward(inputs, patch_rows, camera_table, self_weights, self_output, cross_gain, cross_query, cross_pair, cross_output, patch_weights, hidden_gain, widen_weights, narrow_weights, onehot, mask_add):
    shift_scale = product(onehot, camera_table.reshape(CAMS, -1)).reshape(-1, 2, D)
    normed_one = low(layer_norm(inputs) * (1.0 + shift_scale[:, 0]) + shift_scale[:, 1])
    queries = low(low_back(product(normed_one, self_weights[0])))
    key_rows = low(low_back(product(normed_one, self_weights[1])))
    value_rows = low(low_back(product(normed_one, self_weights[2])))
    self_mixed = attend(by_heads(queries), by_heads(key_rows), by_heads(value_rows), 0.0)
    after_self = inputs + low_back(product(self_mixed, self_output))
    normed_two = low(layer_norm(after_self) * cross_gain)
    cross_q = low(low_back(product(normed_two, cross_query)))
    patch_mid = low(low_back(product(patch_rows, patch_weights)))
    cross_k = low(low_back(product(patch_mid, cross_pair[0])))
    cross_v = low(low_back(product(patch_mid, cross_pair[1])))
    cross_mixed = attend(by_heads(cross_q), by_heads(cross_k), by_heads(cross_v), mask_add)
    after_cross = after_self + low_back(product(cross_mixed, cross_output))
    normed_three = low(layer_norm(after_cross) * hidden_gain)
    activated = low(jax.nn.gelu(low_back(product(normed_three, widen_weights)), approximate=True))
    return after_cross + low_back(product(activated, narrow_weights))

def reference(tokens, cam_index, patches, patch_len, camera_table, self_weights, self_output, cross_gain, cross_query, cross_pair, cross_output, patch_weights, hidden_gain, widen_weights, narrow_weights, cotangent):
    weights = tuple((matrix.astype(jnp.float32) for matrix in (camera_table, self_weights, self_output, cross_gain, cross_query, cross_pair, cross_output, patch_weights, hidden_gain, widen_weights, narrow_weights)))

    def one_batch(running, slices):
        token_rows, cam_rows, patch_rows, length, grad_rows = slices
        onehot = (cam_rows[:, None] == jnp.arange(CAMS)[None, :]).astype(jnp.float32)
        mask_add = jnp.where(jnp.arange(PATCHES) < length, 0.0, -1e+30).astype(jnp.float32)

        def forward(inputs, patch_inputs, *params):
            return block_forward(inputs, patch_inputs, *params, onehot, mask_add)
        result, pullback = jax.vjp(forward, token_rows.astype(jnp.float32), patch_rows.astype(jnp.float32), *weights)
        gradients = pullback(grad_rows.astype(jnp.float32))
        updated = tuple((former + latter for former, latter in zip(running, gradients[2:])))
        return (updated, (result.astype(jnp.bfloat16), gradients[0], gradients[1]))
    starting = tuple((jnp.zeros(matrix.shape, jnp.float32) for matrix in weights))
    totals, (outputs, input_grads, patch_grads) = lax.scan(one_batch, starting, (tokens, cam_index, patches, patch_len, cotangent))
    return (outputs, input_grads, patch_grads) + totals
```

```python
import jax
import jax.numpy as jnp
from jax import lax
from jax.experimental import pallas as pl
from jax.experimental.pallas import tpu as pltpu
from jax.sharding import PartitionSpec as P

HEAD_DIM = 64
EPSILON = 1e-05
SCALE = HEAD_DIM ** (-0.5)
LOW = jnp.bfloat16
WIDE = jnp.float32

NN = (((1,), (0,)), ((), ()))
NT = (((1,), (1,)), ((), ()))
TN = (((0,), (0,)), ((), ()))


def mul(left, right, dims=NN):
    return lax.dot_general(left, right, dims, preferred_element_type=WIDE)


def attend_block(scaled_q, keys, values_t, live):
    peak = None
    for c in range(live):
        top = jnp.max(mul(keys(c), scaled_q), axis=0, keepdims=True)
        peak = top if peak is None else jnp.maximum(peak, top)
    total = 0.0
    mixed = 0.0
    for c in range(live):
        raised = jnp.exp(mul(keys(c), scaled_q) - peak)
        total = total + jnp.sum(raised, axis=0, keepdims=True)
        mixed = mixed + mul(values_t(c), raised.astype(LOW))
    return mixed / total, peak + jnp.log(total)


def attend_block_back(scaled_q, queries, grad_t, grad, keys, keys_t, values, log_total, spread):
    probs = jnp.exp(mul(keys, scaled_q) - log_total)
    grad_scores = (probs * (mul(values, grad_t) - spread)).astype(LOW)
    return (mul(keys_t, grad_scores), mul(grad_scores, queries), mul(probs.astype(LOW), grad))


def estimate(rows, cols, passes):
    return pl.CostEstimate(
        flops=int(rows * cols * 1200 * passes), transcendentals=int(rows * cols), bytes_accessed=int(rows * 2048)
    )


VMEM_LIMIT = 48 << 20


def self_forward(qkv):
    blocks, pairs, _, width, rows = qkv.shape

    def kernel(q_ref, k_ref, v_ref, mixed_ref, wide_ref, log_ref, keys):
        @pl.when(pl.program_id(1) == 0)
        def _():
            for c in range(blocks):
                keys[c] = k_ref[c].T

        mixed, log_total = attend_block(
            q_ref[...] * LOW(SCALE), lambda c: keys[c], lambda c: v_ref[c], blocks
        )
        mixed_ref[...] = mixed.astype(LOW)
        wide_ref[...] = mixed
        log_ref[...] = log_total

    block = pl.BlockSpec((None, None, width, rows), lambda p, i: (i, p, 0, 0))
    return pl.pallas_call(
        kernel,
        grid=(pairs, blocks),
        in_specs=[
            pl.BlockSpec((None, None, None, width, rows), lambda p, i: (i, p, 0, 0, 0)),
            pl.BlockSpec((blocks, None, None, width, rows), lambda p, i: (0, p, 1, 0, 0)),
            pl.BlockSpec((blocks, None, None, width, rows), lambda p, i: (0, p, 2, 0, 0)),
        ],
        out_specs=[block, block, pl.BlockSpec((None, None, 1, rows), lambda p, i: (i, p, 0, 0))],
        out_shape=[
            jax.ShapeDtypeStruct((blocks, pairs, width, rows), LOW),
            jax.ShapeDtypeStruct((blocks, pairs, width, rows), WIDE),
            jax.ShapeDtypeStruct((blocks, pairs, 1, rows), WIDE),
        ],
        scratch_shapes=[pltpu.VMEM((blocks, rows, width), LOW)],
        name="self_forward",
        cost_estimate=estimate(blocks * rows, blocks * rows * pairs, 2),
        compiler_params=pltpu.CompilerParams(vmem_limit_bytes=VMEM_LIMIT),
    )(qkv, qkv, qkv)


def self_backward(qkv, grad_mixed, wide, log_total):
    blocks, pairs, _, width, rows = qkv.shape

    def kernel(q_ref, k_ref, v_ref, g_ref, wide_ref, log_ref, out_ref, keys, values, grad_k, grad_v):
        i = pl.program_id(1)

        @pl.when(i == 0)
        def _():
            for c in range(blocks):
                keys[c] = k_ref[c].T
                values[c] = v_ref[c].T
            grad_k[...] = jnp.zeros_like(grad_k)
            grad_v[...] = jnp.zeros_like(grad_v)

        scaled_q = q_ref[...] * LOW(SCALE)
        grad_t = g_ref[...]
        spread = jnp.sum(grad_t.astype(WIDE) * wide_ref[...], axis=0, keepdims=True)
        logs = log_ref[...]
        queries, grad = scaled_q.T, grad_t.T
        grad_q = jnp.zeros((width, rows), WIDE)
        for c in range(blocks):
            term_q, term_k, term_v = attend_block_back(
                scaled_q, queries, grad_t, grad, keys[c], k_ref[c], values[c], logs, spread
            )
            grad_q += term_q
            grad_k[c] += term_k
            grad_v[c] += term_v
        out_ref[i, 0] = (grad_q * SCALE).astype(LOW)

        @pl.when(i == blocks - 1)
        def _():
            for c in range(blocks):
                out_ref[c, 1] = grad_k[c].T.astype(LOW)
                out_ref[c, 2] = grad_v[c].T.astype(LOW)

    block = pl.BlockSpec((None, None, width, rows), lambda p, i: (i, p, 0, 0))
    return pl.pallas_call(
        kernel,
        grid=(pairs, blocks),
        in_specs=[
            pl.BlockSpec((None, None, None, width, rows), lambda p, i: (i, p, 0, 0, 0)),
            pl.BlockSpec((blocks, None, None, width, rows), lambda p, i: (0, p, 1, 0, 0)),
            pl.BlockSpec((blocks, None, None, width, rows), lambda p, i: (0, p, 2, 0, 0)),
            block,
            block,
            pl.BlockSpec((None, None, 1, rows), lambda p, i: (i, p, 0, 0)),
        ],
        out_specs=pl.BlockSpec((blocks, None, 3, width, rows), lambda p, i: (0, p, 0, 0, 0)),
        out_shape=jax.ShapeDtypeStruct((blocks, pairs, 3, width, rows), LOW),
        scratch_shapes=[pltpu.VMEM((blocks, rows, width), LOW)] * 2
        + [pltpu.VMEM((blocks, rows, width), WIDE)] * 2,
        name="self_backward",
        cost_estimate=estimate(blocks * rows, blocks * rows * pairs, 4),
        compiler_params=pltpu.CompilerParams(vmem_limit_bytes=VMEM_LIMIT),
    )(qkv, qkv, qkv, grad_mixed, wide, log_total)


def by_length(length, full, blocks, run):
    @pl.when(length * 4 > full)
    def _():
        run(blocks)

    @pl.when(length * 4 <= full)
    def _():
        run(blocks // 4)


def cross_forward(queries_t, pair_t, lengths):
    blocks, _, cols, all_patches = pair_t.shape
    objects = lengths.shape[0]
    heads = cols // HEAD_DIM
    rows, patch_rows = queries_t.shape[1] // objects, all_patches // objects

    def kernel(len_ref, q_ref, pair_ref, mixed_ref, wide_ref, log_ref, keys):
        scaled_q = q_ref[...] * LOW(SCALE)

        def run(live):
            for c in range(live):
                keys[c] = pair_ref[c, 0].T
            mixed, log_total = attend_block(
                scaled_q, lambda c: keys[c], lambda c: pair_ref[c, 1], live
            )
            mixed_ref[...] = mixed.astype(LOW)
            wide_ref[...] = mixed
            log_ref[...] = log_total

        by_length(len_ref[pl.program_id(0)], blocks * patch_rows, blocks, run)

    block = pl.BlockSpec((HEAD_DIM, rows), lambda b, j, lens: (j, b))
    return pl.pallas_call(
        kernel,
        grid_spec=pltpu.PrefetchScalarGridSpec(
            num_scalar_prefetch=1,
            grid=(objects, heads),
            in_specs=[
                block,
                pl.BlockSpec((blocks, 2, HEAD_DIM, patch_rows), lambda b, j, lens: (0, 0, j, b)),
            ],
            out_specs=[block, block, pl.BlockSpec((None, 1, rows), lambda b, j, lens: (j, 0, b))],
            scratch_shapes=[pltpu.VMEM((blocks, patch_rows, HEAD_DIM), LOW)],
        ),
        out_shape=[
            jax.ShapeDtypeStruct(queries_t.shape, LOW),
            jax.ShapeDtypeStruct(queries_t.shape, WIDE),
            jax.ShapeDtypeStruct((heads, 1, queries_t.shape[1]), WIDE),
        ],
        name="cross_forward",
        cost_estimate=estimate(objects * rows, blocks * patch_rows * heads, 1.4),
        compiler_params=pltpu.CompilerParams(vmem_limit_bytes=VMEM_LIMIT),
    )(lengths, queries_t, pair_t)


def cross_backward(queries_t, pair_t, lengths, grad_t_all, wide, log_total):
    blocks, _, cols, all_patches = pair_t.shape
    objects = lengths.shape[0]
    heads = cols // HEAD_DIM
    rows, patch_rows = queries_t.shape[1] // objects, all_patches // objects

    def kernel(len_ref, q_ref, pair_ref, g_ref, wide_ref, log_ref, out_q, out_pair):
        scaled_q = q_ref[...] * LOW(SCALE)
        grad_t = g_ref[...]
        spread = jnp.sum(grad_t.astype(WIDE) * wide_ref[...], axis=0, keepdims=True)
        logs = log_ref[...]
        queries, grad = scaled_q.T, grad_t.T

        def run(live):
            grad_q = jnp.zeros((HEAD_DIM, rows), WIDE)
            for c in range(live):
                keys_t = pair_ref[c, 0]
                term_q, term_k, term_v = attend_block_back(
                    scaled_q, queries, grad_t, grad, keys_t.T, keys_t, pair_ref[c, 1].T, logs, spread
                )
                grad_q += term_q
                out_pair[c, 0] = term_k.T.astype(LOW)
                out_pair[c, 1] = term_v.T.astype(LOW)
            for c in range(live, blocks):
                out_pair[c] = jnp.zeros_like(out_pair[c])
            out_q[...] = (grad_q * SCALE).astype(LOW)

        by_length(len_ref[pl.program_id(0)], blocks * patch_rows, blocks, run)

    block = pl.BlockSpec((HEAD_DIM, rows), lambda b, j, lens: (j, b))
    pair_block = pl.BlockSpec((blocks, 2, HEAD_DIM, patch_rows), lambda b, j, lens: (0, 0, j, b))
    return pl.pallas_call(
        kernel,
        grid_spec=pltpu.PrefetchScalarGridSpec(
            num_scalar_prefetch=1,
            grid=(objects, heads),
            in_specs=[
                block,
                pair_block,
                block,
                block,
                pl.BlockSpec((None, 1, rows), lambda b, j, lens: (j, 0, b)),
            ],
            out_specs=[block, pair_block],
        ),
        out_shape=[
            jax.ShapeDtypeStruct(queries_t.shape, LOW),
            jax.ShapeDtypeStruct(pair_t.shape, LOW),
        ],
        name="cross_backward",
        cost_estimate=estimate(objects * rows, blocks * patch_rows * heads, 2.5),
        compiler_params=pltpu.CompilerParams(vmem_limit_bytes=VMEM_LIMIT),
    )(lengths, queries_t, pair_t, grad_t_all, wide, log_total)


def shift(value, step, pairs=None):
    size = lax.axis_size("heads")
    return lax.ppermute(value, "heads", [((i + step) % size, i) for i in range(size)])


def gather_heads(value):
    size = lax.axis_size("heads")
    if size != 4:
        return [value] + [shift(value, step) for step in range(1, size)]
    after, before = shift(value, 1), shift(value, -1)
    inner = lax.ppermute(after, "heads", [(1, 0), (2, 1)]) + lax.ppermute(before, "heads", [(1, 2), (2, 3)])
    return [value, after, inner, before]


def scatter_heads(partial):
    size, me = lax.axis_size("heads"), lax.axis_index("heads")

    def part(step):
        return lax.dynamic_index_in_dim(partial, (me + step) % size, 0, keepdims=False)

    if size != 4:
        total = part(0)
        for step in range(1, size):
            total = total + shift(part(step).astype(LOW), -step).astype(WIDE)
        return total
    far = part(2).astype(LOW)
    up = lax.ppermute(far, "heads", [(0, 1), (1, 2)]).astype(WIDE)
    down = lax.ppermute(far, "heads", [(2, 1), (3, 2)]).astype(WIDE)
    from_below = shift((part(1) + up).astype(LOW), -1)
    from_above = shift((part(3) + down).astype(LOW), 1)
    return part(0) + from_below.astype(WIDE) + from_above.astype(WIDE)


def in_order(parts):
    size, me = lax.axis_size("heads"), lax.axis_index("heads")
    out = jnp.zeros((size,) + parts[0].shape, parts[0].dtype)
    for step, value in enumerate(parts):
        out = lax.dynamic_update_index_in_dim(out, value, (me + step) % size, 0)
    return out.reshape((-1,) + parts[0].shape[1:])


def sum_heads(partial):
    size = lax.axis_size("heads")
    split = partial.reshape((size, -1) + partial.shape[1:])
    return in_order(gather_heads(scatter_heads(split).astype(LOW)))


def exchange_rows(value):
    return lax.all_to_all(value, "rows", 0, 0, tiled=True)


def normed(value):
    centred = value - jnp.mean(value, axis=-1, keepdims=True)
    rate = lax.rsqrt(jnp.mean(centred * centred, axis=-1, keepdims=True) + EPSILON)
    return centred * rate, rate


def normed_back(grad, unit, rate):
    return rate * (
        grad
        - jnp.mean(grad, axis=-1, keepdims=True)
        - unit * jnp.mean(grad * unit, axis=-1, keepdims=True)
    )


def gelu_tanh(pre_act):
    return jax.nn.gelu(pre_act, approximate=True)


def add_trees(former, latter):
    return jax.tree.map(jnp.add, former, latter)


def per_device(
    tokens,
    cam_index,
    patches,
    patch_len,
    camera_table,
    self_weights,
    self_output,
    cross_gain,
    cross_query,
    cross_pair,
    cross_output,
    patch_weights,
    hidden_gain,
    widen_weights,
    narrow_weights,
    cotangent,
):
    batches, rows, width = tokens.shape
    cols = self_weights.shape[2]
    heads = cols // HEAD_DIM
    codes = camera_table.shape[0]
    patch_rows, patch_width = patches.shape[1:]
    n_rows, n_heads = lax.axis_size("rows"), lax.axis_size("heads")
    row_rank, head_rank = lax.axis_index("rows"), lax.axis_index("heads")
    groups = 2 if batches % 2 == 0 and heads * (batches // 2) % n_rows == 0 else 1
    objects = batches // groups
    pairs, left_over = divmod(heads * objects, n_rows)
    whole_pairs = left_over == 0
    full_lengths = jnp.full((objects,), n_rows * rows, jnp.int32)
    count = objects * rows

    def own_columns(value):
        return lax.dynamic_slice_in_dim(value, head_rank * cols, cols, value.ndim - 1)

    table_flat = camera_table.reshape(codes, -1)
    cross_gain_f = cross_gain.astype(WIDE)
    hidden_gain_f = hidden_gain.astype(WIDE)

    qkv_rows = (
        self_weights.reshape(3, width, heads, HEAD_DIM).transpose(2, 0, 3, 1).reshape(3 * cols, width)
    )
    pair_rows = cross_pair.transpose(0, 2, 1).reshape(2 * cols, width)
    query_rows = cross_query.T

    local = jnp.stack([self_output, cross_output, query_rows])
    piece = cols // n_rows
    local = lax.dynamic_slice_in_dim(local, row_rank * piece, piece, 1)
    whole = lax.all_gather(lax.all_gather(local, "heads", axis=0), "rows", axis=0)
    whole = whole.transpose(2, 1, 0, 3, 4).reshape(3, n_heads, cols, width)
    whole = lax.dynamic_slice_in_dim(
        jnp.concatenate([whole, whole], axis=1), head_rank, n_heads, 1
    ).reshape(3, n_heads * cols, width)
    self_whole, cross_whole, query_whole = whole[0], whole[1], whole[2]

    def over_all_columns(value_t, weight):
        return mul(jnp.concatenate(gather_heads(value_t), axis=0), weight, TN)

    def to_pairs(value_t, depth):
        value = value_t.reshape(heads, depth, objects, rows).transpose(2, 0, 1, 3)
        return value.reshape(n_rows, pairs, depth, rows)

    def from_pairs(value, depth):
        value = value.reshape(objects, heads, depth, rows).transpose(1, 2, 0, 3)
        return value.reshape(heads * depth, objects * rows)

    def one_group(group):
        part = slice(group * objects, (group + 1) * objects)
        inputs = tokens[part].reshape(count, width).astype(WIDE)
        patch_in = patches[part].reshape(objects * patch_rows, patch_width)
        lengths = patch_len[part]
        grad_low = cotangent[part].reshape(count, width)
        onehot = (cam_index[part].reshape(count)[:, None] == jnp.arange(codes)[None, :]).astype(LOW)
        shift_scale = mul(onehot, table_flat)
        gain_one = 1.0 + shift_scale[:, :width]
        unit_one, rate_one = normed(inputs)
        normed_one = (unit_one * gain_one + shift_scale[:, width:]).astype(LOW)
        qkv_t = mul(qkv_rows, normed_one, NT).astype(LOW)
        if whole_pairs:
            qkv = exchange_rows(to_pairs(qkv_t, 3 * HEAD_DIM))
            qkv = qkv.reshape(n_rows, pairs, 3, HEAD_DIM, rows)
        else:
            by_kind = qkv_t.reshape(heads, 3, HEAD_DIM, count).transpose(1, 0, 2, 3)
            by_kind = by_kind.reshape(3, cols, count)
            self_pair = lax.all_gather(by_kind[1:], "rows", axis=0)
        patch_mid = mul(patch_in, patch_weights).astype(LOW)
        own_pair = mul(pair_rows, patch_mid, NT).astype(LOW).reshape(2, cols, -1)
        pair_t = lax.all_gather(own_pair, "rows", axis=0)
        yield
        if whole_pairs:
            mixed, self_wide, self_log = self_forward(qkv)
            self_mixed_t = from_pairs(exchange_rows(mixed), HEAD_DIM)
        else:
            self_mixed_t, self_wide, self_log = cross_forward(by_kind[0], self_pair, full_lengths)
        after_self = inputs + over_all_columns(self_mixed_t, self_whole)
        yield
        unit_two, rate_two = normed(after_self)
        normed_two = (unit_two * cross_gain_f).astype(LOW)
        cross_q_t = mul(query_rows, normed_two, NT).astype(LOW)
        cross_mixed_t, cross_wide, cross_log = cross_forward(cross_q_t, pair_t, lengths)
        after_cross = after_self + over_all_columns(cross_mixed_t, cross_whole)
        yield
        unit_three, rate_three = normed(after_cross)
        normed_three = (unit_three * hidden_gain_f).astype(LOW)
        pre_act = mul(normed_three, widen_weights)
        activated, act_back = jax.vjp(gelu_tanh, pre_act)
        activated = activated.astype(LOW)
        grad_pre = act_back(mul(grad_low, narrow_weights, NT))[0].astype(LOW)
        grad_three = sum_heads(mul(grad_pre, widen_weights, NT)).astype(WIDE)
        hidden_sum = sum_heads(mul(activated, narrow_weights)).astype(WIDE)
        result = (after_cross + hidden_sum).astype(LOW)
        narrow_term = mul(activated, grad_low, TN)
        widen_term = mul(normed_three, grad_pre, TN)
        yield
        hidden_gain_term = jnp.sum(own_columns(grad_three * unit_three), axis=0)
        grad_cross = grad_low.astype(WIDE) + normed_back(
            grad_three * hidden_gain_f, unit_three, rate_three
        )
        grad_cross_low = grad_cross.astype(LOW)
        cross_output_term = mul(cross_mixed_t, grad_cross_low)
        grad_mixed_t = mul(cross_output, grad_cross_low, NT).astype(LOW)
        grad_cq_t, grad_pair_t = cross_backward(
            cross_q_t, pair_t, lengths, grad_mixed_t, cross_wide, cross_log
        )
        grad_two = over_all_columns(grad_cq_t, query_whole)
        grad_pair_t = lax.psum_scatter(grad_pair_t, "rows", scatter_dimension=0, tiled=False)
        grad_pair_t = grad_pair_t.reshape(2 * cols, -1)
        query_term = mul(normed_two, grad_cq_t, (((0,), (1,)), ((), ())))
        yield
        cross_gain_term = jnp.sum(own_columns(grad_two * unit_two), axis=0)
        grad_self = grad_cross + normed_back(grad_two * cross_gain_f, unit_two, rate_two)
        grad_self_low = grad_self.astype(LOW)
        self_output_term = mul(self_mixed_t, grad_self_low)
        grad_self_mixed_t = mul(self_output, grad_self_low, NT).astype(LOW)
        if whole_pairs:
            grad_mixed = exchange_rows(to_pairs(grad_self_mixed_t, HEAD_DIM))
            grad_qkv = self_backward(qkv, grad_mixed, self_wide, self_log)
            grad_qkv = exchange_rows(grad_qkv.reshape(n_rows, pairs, 3 * HEAD_DIM, rows))
            grad_qkv_t = from_pairs(grad_qkv, 3 * HEAD_DIM)
        else:
            grad_q_t, grad_kv_t = cross_backward(
                by_kind[0], self_pair, full_lengths, grad_self_mixed_t, self_wide, self_log
            )
            grad_kv_t = lax.psum_scatter(grad_kv_t, "rows", scatter_dimension=0, tiled=False)
            grad_qkv_t = jnp.concatenate([grad_q_t[None], grad_kv_t]).reshape(3, heads, HEAD_DIM, count)
            grad_qkv_t = grad_qkv_t.transpose(1, 0, 2, 3).reshape(3 * cols, count)
        yield
        pair_term = mul(patch_mid, grad_pair_t, (((0,), (1,)), ((), ())))
        grad_mid = sum_heads(mul(grad_pair_t, pair_rows, TN))
        patch_term = mul(patch_in, own_columns(grad_mid), TN)
        patch_grad = mul(grad_mid, patch_weights, NT)
        yield
        grad_one = sum_heads(mul(grad_qkv_t, qkv_rows, TN)).astype(WIDE)
        self_term = mul(normed_one, grad_qkv_t, (((0,), (1,)), ((), ())))
        input_grad = grad_self + normed_back(grad_one * gain_one, unit_one, rate_one)
        own_grad = own_columns(grad_one)
        table_term = jnp.stack(
            [
                lax.dot_general(onehot.astype(WIDE), v, TN, precision=lax.Precision.HIGHEST)
                for v in (own_grad * own_columns(unit_one), own_grad)
            ],
            axis=1,
        )
        yield (
            result.reshape(objects, rows, width),
            input_grad.reshape(objects, rows, width),
            patch_grad.reshape(objects, patch_rows, patch_width),
            (narrow_term, widen_term),
            (
                table_term,
                self_term,
                self_output_term,
                cross_gain_term,
                query_term,
                pair_term,
                cross_output_term,
                patch_term,
                hidden_gain_term,
            ),
        )

    steps = [one_group(group) for group in range(groups)]
    done = [None] * groups
    while done[-1] is None:
        for index, step in enumerate(steps):
            done[index] = next(step)
    outputs, input_grads, patch_grads = (
        jnp.concatenate([values[i] for values in done], axis=0) for i in range(3)
    )
    hidden = done[0][3]
    rest = done[0][4]
    for values in done[1:]:
        hidden, rest = add_trees(hidden, values[3]), add_trees(rest, values[4])

    def reduce_rows(value):
        return lax.psum(value.astype(LOW), "rows")

    narrow_total, widen_total = (reduce_rows(value) for value in hidden)
    (narrow_total, widen_total), rest = lax.optimization_barrier(((narrow_total, widen_total), rest))
    rest = list(rest)
    rest[1] = (
        rest[1].reshape(width, heads, 3, HEAD_DIM).transpose(2, 0, 1, 3).reshape(3, width, cols)
    )
    rest[5] = rest[5].reshape(width, 2, cols).transpose(1, 0, 2)
    totals = [reduce_rows(value) for value in rest]
    totals = [value.astype(WIDE) for value in totals + [widen_total, narrow_total]]
    return (outputs, input_grads, patch_grads) + tuple(totals)


def solution(mesh):
    in_specs = (
        P(None, "rows", None),
        P(None, "rows"),
        P(None, "rows", None),
        P(),
        P(),
        P(None, None, "heads"),
        P("heads", None),
        P(),
        P(None, "heads"),
        P(None, None, "heads"),
        P("heads", None),
        P(),
        P(),
        P(None, "heads"),
        P("heads", None),
        P(None, "rows", None),
    )
    out_specs = (
        P(None, "rows", None),
        P(None, "rows", None),
        P(None, "rows", None),
        P(None, None, "heads"),
        P(None, None, "heads"),
        P("heads", None),
        P("heads"),
        P(None, "heads"),
        P(None, None, "heads"),
        P("heads", None),
        P(None, "heads"),
        P("heads"),
        P(None, "heads"),
        P("heads", None),
    )
    return jax.shard_map(
        per_device, mesh=mesh, in_specs=in_specs, out_specs=out_specs, check_vma=False
    )
```

```python
import jax
import jax.numpy as jnp
from jax import lax
from jax.experimental import pallas as pl
from jax.experimental.pallas import tpu as pltpu
from jax.sharding import PartitionSpec as P

HEAD_DIM = 64
EPSILON = 1e-05
SCALE = HEAD_DIM ** (-0.5)
LOW = jnp.bfloat16
WIDE = jnp.float32

NN = (((1,), (0,)), ((), ()))
NT = (((1,), (1,)), ((), ()))
TN = (((0,), (0,)), ((), ()))
T_LAST = (((0,), (1,)), ((), ()))


def mul(left, right, dims=NN):
    return lax.dot_general(left, right, dims, preferred_element_type=WIDE)


def load_values(values, block, values_t):
    rows = values_t.shape[1]
    at = slice(block * rows, (block + 1) * rows)
    values[at, :HEAD_DIM] = values_t.T
    values[at, HEAD_DIM:] = jnp.ones((rows, HEAD_DIM), values.dtype)


def attend_block(queries, keys_t, values):
    scores = mul(queries, keys_t)
    peak = jnp.max(scores, axis=1, keepdims=True)
    both = mul(jnp.exp(scores - peak).astype(LOW), values).T
    total = both[HEAD_DIM : HEAD_DIM + 1]
    return both[:HEAD_DIM] / total, peak.T + jnp.log(total)


def attend_block_back(scaled_q, grad_t, keys, keys_t, values, log_total, spread):
    probs = jnp.exp(mul(keys, scaled_q) - log_total)
    grad_scores = (probs * (mul(values, grad_t) - spread)).astype(LOW)
    return (
        (mul(keys_t, grad_scores) * SCALE).astype(LOW),
        mul(grad_scores, scaled_q.T),
        mul(probs.astype(LOW), grad_t.T),
    )


def estimate(rows, cols, passes):
    return pl.CostEstimate(
        flops=int(rows * cols * 1200 * passes), transcendentals=int(rows * cols), bytes_accessed=int(rows * 2048)
    )


VMEM_LIMIT = 48 << 20


def by_length(length, full, blocks, run):
    @pl.when(length * 4 > full)
    def _():
        run(blocks)

    @pl.when(length * 4 <= full)
    def _():
        run(blocks // 4)


def cross_forward(queries_t, pair_t, lengths):
    blocks, _, cols, all_patches = pair_t.shape
    objects = lengths.shape[0]
    heads = cols // HEAD_DIM
    rows, patch_rows = queries_t.shape[1] // objects, all_patches // objects

    def kernel(len_ref, q_ref, pair_ref, mixed_ref, wide_ref, log_ref, keys_t, values):
        queries = (q_ref[...] * LOW(SCALE)).T

        def run(live):
            for c in range(live):
                keys_t[:, c * patch_rows : (c + 1) * patch_rows] = pair_ref[c, 0]
                load_values(values, c, pair_ref[c, 1])
            size = live * patch_rows
            mixed, log_total = attend_block(queries, keys_t[:, :size], values[:size])
            mixed_ref[...] = mixed.astype(LOW)
            wide_ref[...] = mixed
            log_ref[...] = log_total

        by_length(len_ref[pl.program_id(0)], blocks * patch_rows, blocks, run)

    block = pl.BlockSpec((HEAD_DIM, rows), lambda b, j, lens: (j, b))
    return pl.pallas_call(
        kernel,
        grid_spec=pltpu.PrefetchScalarGridSpec(
            num_scalar_prefetch=1,
            grid=(objects, heads),
            in_specs=[
                block,
                pl.BlockSpec((blocks, 2, HEAD_DIM, patch_rows), lambda b, j, lens: (0, 0, j, b)),
            ],
            out_specs=[block, block, pl.BlockSpec((None, 1, rows), lambda b, j, lens: (j, 0, b))],
            scratch_shapes=[
                pltpu.VMEM((HEAD_DIM, blocks * patch_rows), LOW),
                pltpu.VMEM((blocks * patch_rows, 2 * HEAD_DIM), LOW),
            ],
        ),
        out_shape=[
            jax.ShapeDtypeStruct(queries_t.shape, LOW),
            jax.ShapeDtypeStruct(queries_t.shape, WIDE),
            jax.ShapeDtypeStruct((heads, 1, queries_t.shape[1]), WIDE),
        ],
        name="cross_forward",
        cost_estimate=estimate(objects * rows, blocks * patch_rows * heads, 1.4),
        compiler_params=pltpu.CompilerParams(vmem_limit_bytes=VMEM_LIMIT),
    )(lengths, queries_t, pair_t)


def cross_backward(queries_t, pair_t, lengths, grad_t_all, wide, log_total):
    blocks, _, cols, all_patches = pair_t.shape
    objects = lengths.shape[0]
    heads = cols // HEAD_DIM
    rows, patch_rows = queries_t.shape[1] // objects, all_patches // objects

    def kernel(len_ref, q_ref, pair_ref, g_ref, wide_ref, log_ref, out_q, out_pair, keys, keys_t, values):
        grad_t = g_ref[...]
        spread = jnp.sum(grad_t.astype(WIDE) * wide_ref[...], axis=0, keepdims=True)

        def run(live):
            for c in range(live):
                at = slice(c * patch_rows, (c + 1) * patch_rows)
                keys[at] = pair_ref[c, 0].T
                keys_t[:, at] = pair_ref[c, 0]
                values[at] = pair_ref[c, 1].T
            size = live * patch_rows
            out_q[...], grad_k, grad_v = attend_block_back(
                q_ref[...] * LOW(SCALE),
                grad_t,
                keys[:size],
                keys_t[:, :size],
                values[:size],
                log_ref[...],
                spread,
            )
            for c in range(live):
                at = slice(c * patch_rows, (c + 1) * patch_rows)
                out_pair[c, 0] = grad_k[at].T.astype(LOW)
                out_pair[c, 1] = grad_v[at].T.astype(LOW)
            for c in range(live, blocks):
                out_pair[c] = jnp.zeros_like(out_pair[c])

        by_length(len_ref[pl.program_id(0)], blocks * patch_rows, blocks, run)

    block = pl.BlockSpec((HEAD_DIM, rows), lambda b, j, lens: (j, b))
    pair_block = pl.BlockSpec((blocks, 2, HEAD_DIM, patch_rows), lambda b, j, lens: (0, 0, j, b))
    return pl.pallas_call(
        kernel,
        grid_spec=pltpu.PrefetchScalarGridSpec(
            num_scalar_prefetch=1,
            grid=(objects, heads),
            in_specs=[
                block,
                pair_block,
                block,
                block,
                pl.BlockSpec((None, 1, rows), lambda b, j, lens: (j, 0, b)),
            ],
            out_specs=[block, pair_block],
            scratch_shapes=[
                pltpu.VMEM((blocks * patch_rows, HEAD_DIM), LOW),
                pltpu.VMEM((HEAD_DIM, blocks * patch_rows), LOW),
                pltpu.VMEM((blocks * patch_rows, HEAD_DIM), LOW),
            ],
        ),
        out_shape=[
            jax.ShapeDtypeStruct(queries_t.shape, LOW),
            jax.ShapeDtypeStruct(pair_t.shape, LOW),
        ],
        name="cross_backward",
        cost_estimate=estimate(objects * rows, blocks * patch_rows * heads, 2.5),
        compiler_params=pltpu.CompilerParams(vmem_limit_bytes=VMEM_LIMIT),
    )(lengths, queries_t, pair_t, grad_t_all, wide, log_total)


def shift(value, step):
    size = lax.axis_size("heads")
    return lax.ppermute(value, "heads", [((i + step) % size, i) for i in range(size)])


def gather_heads(value):
    size = lax.axis_size("heads")
    if size != 4:
        return [value] + [shift(value, step) for step in range(1, size)]
    after, before = shift(value, 1), shift(value, -1)
    inner = lax.ppermute(after, "heads", [(1, 0), (2, 1)]) + lax.ppermute(before, "heads", [(1, 2), (2, 3)])
    return [value, after, inner, before]


def scatter_heads(partial):
    size, me = lax.axis_size("heads"), lax.axis_index("heads")

    def part(step):
        return lax.dynamic_index_in_dim(partial, (me + step) % size, 0, keepdims=False)

    if size != 4:
        total = part(0)
        for step in range(1, size):
            total = total + shift(part(step).astype(LOW), -step).astype(WIDE)
        return total
    far = part(2).astype(LOW)
    up = lax.ppermute(far, "heads", [(0, 1), (1, 2)]).astype(WIDE)
    down = lax.ppermute(far, "heads", [(2, 1), (3, 2)]).astype(WIDE)
    from_below = shift((part(1) + up).astype(LOW), -1)
    from_above = shift((part(3) + down).astype(LOW), 1)
    return part(0) + from_below.astype(WIDE) + from_above.astype(WIDE)


def in_order(parts):
    size, me = lax.axis_size("heads"), lax.axis_index("heads")
    out = jnp.zeros((size,) + parts[0].shape, parts[0].dtype)
    for step, value in enumerate(parts):
        out = lax.dynamic_update_index_in_dim(out, value, (me + step) % size, 0)
    return out.reshape((-1,) + parts[0].shape[1:])


def sum_heads(partial):
    size = lax.axis_size("heads")
    split = partial.reshape((size, -1) + partial.shape[1:])
    return in_order(gather_heads(scatter_heads(split).astype(LOW)))


def exchange_rows(value):
    return lax.all_to_all(value, "rows", 0, 0, tiled=True)


def normed(value):
    centred = value - jnp.mean(value, axis=-1, keepdims=True)
    rate = lax.rsqrt(jnp.mean(centred * centred, axis=-1, keepdims=True) + EPSILON)
    return centred * rate, rate


def normed_back(grad, unit, rate):
    return rate * (
        grad
        - jnp.mean(grad, axis=-1, keepdims=True)
        - unit * jnp.mean(grad * unit, axis=-1, keepdims=True)
    )


def gelu_tanh(pre_act):
    return jax.nn.gelu(pre_act, approximate=True)


def add_trees(former, latter):
    return jax.tree.map(jnp.add, former, latter)


def pair_forward(queries, pair, key_at, length=None):
    blocks, _, width, rows = queries.shape
    pair_rows = pair.shape[3]
    lengths = jnp.full((1,), blocks * pair_rows, jnp.int32) if length is None else length

    def kernel(len_ref, q_ref, k_ref, v_ref, mixed_ref, wide_ref, log_ref, keys_t, values):
        def run(live):
            @pl.when(pl.program_id(0) == 0)
            def _():
                for c in range(live):
                    keys_t[:, c * pair_rows : (c + 1) * pair_rows] = k_ref[c]
                    load_values(values, c, v_ref[c])

            size = live * pair_rows
            mixed, log_total = attend_block(
                (q_ref[...] * LOW(SCALE)).T, keys_t[:, :size], values[:size]
            )
            mixed_ref[...] = mixed.astype(LOW)
            wide_ref[...] = mixed
            log_ref[...] = log_total

        if length is None:
            run(blocks)
        else:
            by_length(len_ref[0], blocks * pair_rows, blocks, run)

    block = pl.BlockSpec((None, width, rows), lambda i, lens: (i, 0, 0))
    return pl.pallas_call(
        kernel,
        grid_spec=pltpu.PrefetchScalarGridSpec(
            num_scalar_prefetch=1,
            grid=(blocks,),
            in_specs=[
                pl.BlockSpec((None, None, width, rows), lambda i, lens: (i, 0, 0, 0)),
                pl.BlockSpec((blocks, None, width, pair_rows), lambda i, lens: (0, key_at, 0, 0)),
                pl.BlockSpec((blocks, None, width, pair_rows), lambda i, lens: (0, key_at + 1, 0, 0)),
            ],
            out_specs=[block, block, pl.BlockSpec((None, 1, rows), lambda i, lens: (i, 0, 0))],
            scratch_shapes=[
                pltpu.VMEM((width, blocks * pair_rows), LOW),
                pltpu.VMEM((blocks * pair_rows, 2 * width), LOW),
            ],
        ),
        out_shape=[
            jax.ShapeDtypeStruct((blocks, width, rows), LOW),
            jax.ShapeDtypeStruct((blocks, width, rows), WIDE),
            jax.ShapeDtypeStruct((blocks, 1, rows), WIDE),
        ],
        name="pair_forward",
        cost_estimate=estimate(blocks * rows, blocks * pair_rows, 2 if length is None else 1.4),
        compiler_params=pltpu.CompilerParams(vmem_limit_bytes=VMEM_LIMIT),
    )(lengths, queries, pair, pair)


def pair_backward(queries, pair, key_at, length, grad_mixed, wide, log_total):
    blocks, _, width, rows = queries.shape
    lengths = jnp.full((1,), blocks * rows, jnp.int32) if length is None else length

    def kernel(len_ref, q_ref, k_ref, v_ref, g_ref, wide_ref, log_ref, out_ref, keys, keys_t, values, grad_k, grad_v):
        i = pl.program_id(0)

        def run(live):
            size = live * rows

            @pl.when(i == 0)
            def _():
                for c in range(live):
                    at = slice(c * rows, (c + 1) * rows)
                    keys[at] = k_ref[c].T
                    keys_t[:, at] = k_ref[c]
                    values[at] = v_ref[c].T

            grad_t = g_ref[...]
            spread = jnp.sum(grad_t.astype(WIDE) * wide_ref[...], axis=0, keepdims=True)
            out_ref[i, 0], term_k, term_v = attend_block_back(
                q_ref[...] * LOW(SCALE),
                grad_t,
                keys[:size],
                keys_t[:, :size],
                values[:size],
                log_ref[...],
                spread,
            )

            @pl.when(i == 0)
            def _():
                grad_k[:size] = term_k
                grad_v[:size] = term_v

            @pl.when(i > 0)
            def _():
                grad_k[:size] += term_k
                grad_v[:size] += term_v

            @pl.when(i == blocks - 1)
            def _():
                for c in range(live):
                    at = slice(c * rows, (c + 1) * rows)
                    out_ref[c, 1] = grad_k[at].T.astype(LOW)
                    out_ref[c, 2] = grad_v[at].T.astype(LOW)
                for c in range(live, blocks):
                    out_ref[c, 1:] = jnp.zeros_like(out_ref[c, 1:])

        if length is None:
            run(blocks)
        else:
            by_length(len_ref[0], blocks * rows, blocks, run)

    block = pl.BlockSpec((None, width, rows), lambda i, lens: (i, 0, 0))
    return pl.pallas_call(
        kernel,
        grid_spec=pltpu.PrefetchScalarGridSpec(
            num_scalar_prefetch=1,
            grid=(blocks,),
            in_specs=[
                pl.BlockSpec((None, None, width, rows), lambda i, lens: (i, 0, 0, 0)),
                pl.BlockSpec((blocks, None, width, rows), lambda i, lens: (0, key_at, 0, 0)),
                pl.BlockSpec((blocks, None, width, rows), lambda i, lens: (0, key_at + 1, 0, 0)),
                block,
                block,
                pl.BlockSpec((None, 1, rows), lambda i, lens: (i, 0, 0)),
            ],
            out_specs=pl.BlockSpec((blocks, 3, width, rows), lambda i, lens: (0, 0, 0, 0)),
            scratch_shapes=[
                pltpu.VMEM((blocks * rows, width), LOW),
                pltpu.VMEM((width, blocks * rows), LOW),
                pltpu.VMEM((blocks * rows, width), LOW),
                pltpu.VMEM((blocks * rows, width), WIDE),
                pltpu.VMEM((blocks * rows, width), WIDE),
            ],
        ),
        out_shape=jax.ShapeDtypeStruct((blocks, 3, width, rows), LOW),
        name="pair_backward",
        cost_estimate=estimate(blocks * rows, blocks * rows, 3 if length is None else 2),
        compiler_params=pltpu.CompilerParams(vmem_limit_bytes=VMEM_LIMIT),
    )(lengths, queries, pair, pair, grad_mixed, wide, log_total)


def swap(value, axis):
    return lax.ppermute(value, axis, [(0, 1), (1, 0)])


def sum_near(partial):
    low = partial.astype(LOW)
    return low.astype(WIDE) + swap(low, "near").astype(WIDE)


def halves(value):
    size = value.shape[0] // 2
    near = lax.axis_index("near")
    return (
        lax.dynamic_slice_in_dim(value, near * size, size, 0),
        lax.dynamic_slice_in_dim(value, (1 - near) * size, size, 0),
    )


def half_sum_near(partial):
    mine, other = halves(partial)
    return mine + swap(other.astype(LOW), "near").astype(WIDE)


def over_heads(value):
    far, near = lax.axis_index("far"), lax.axis_index("near")
    value = jnp.stack([value, swap(value, "far")])
    value = jnp.stack([value, swap(value, "near")])
    value = jnp.where(far == 0, value, jnp.flip(value, 1))
    value = jnp.where(near == 0, value, jnp.flip(value, 0))
    value = value.transpose(1, 2, 0, 3, 4)
    return value.reshape(2 * value.shape[1], 2 * value.shape[3], -1)


def paired_device(
    tokens,
    cam_index,
    patches,
    patch_len,
    camera_table,
    self_weights,
    self_output,
    cross_gain,
    cross_query,
    cross_pair,
    cross_output,
    patch_weights,
    hidden_gain,
    widen_weights,
    narrow_weights,
    cotangent,
):
    _, rows, width = tokens.shape
    cols = self_weights.shape[2]
    hidden = widen_weights.shape[1]
    heads = cols // HEAD_DIM
    codes = camera_table.shape[0]
    patch_width = patches.shape[2]
    n_rows = lax.axis_size("rows")
    row_rank = lax.axis_index("rows")
    far, near = lax.axis_index("far"), lax.axis_index("near")
    own = 2 * far + near
    other = 2 * (1 - far) + near
    groups = tokens.shape[0] // 2

    def piece(value):
        size = value.shape[0] // n_rows
        return lax.dynamic_slice_in_dim(value, row_rank * size, size, 0)

    def shard_columns(value):
        return [
            lax.dynamic_slice_in_dim(value, index * cols, cols, value.ndim - 1)
            for index in (own, other)
        ]

    qkv_rows = self_weights.reshape(3, width, heads, HEAD_DIM).transpose(2, 0, 3, 1)
    qkv_rows = qkv_rows.reshape(3 * cols, width)
    pair_rows = cross_pair.reshape(2, width, heads, HEAD_DIM).transpose(2, 0, 3, 1)
    pair_rows = pair_rows.reshape(2 * cols, width)
    query_rows = cross_query.T

    first = swap(piece(qkv_rows), "far")
    qkv_other = lax.all_gather(first, "rows", axis=0, tiled=True)
    mine = [piece(v) for v in (self_output, query_rows, cross_output, pair_rows, widen_weights, narrow_weights)]
    across = swap(jnp.concatenate(mine, axis=0), "far")
    sizes = [v.shape[0] for v in mine]
    starts = [sum(sizes[:i]) for i in range(len(sizes) + 1)]
    across = [across[a:b] for a, b in zip(starts[:-1], starts[1:])]
    two = jnp.stack([jnp.stack(mine[:3]), jnp.stack(across[:3])])
    four = jnp.concatenate([two, swap(two, "near")])

    def put_together(value):
        whole = lax.all_gather(value, "rows", axis=1)
        return whole.reshape(value.shape[0] * cols, width)

    self_whole = put_together(four[:, 0])
    query_whole = put_together(four[:, 1])
    cross_whole = put_together(four[:, 2])
    pair_other = lax.all_gather(across[3], "rows", axis=0, tiled=True)
    widen_other = lax.all_gather(across[4], "rows", axis=0, tiled=True)
    narrow_other = lax.all_gather(across[5], "rows", axis=0, tiled=True)

    table_flat = camera_table.reshape(codes, -1)
    cross_gain_f = cross_gain.astype(WIDE)
    hidden_gain_f = hidden_gain.astype(WIDE)

    def two_rows(weight, weight_other, value):
        return jnp.concatenate(
            [mul(weight, value, NT).astype(LOW), mul(weight_other, value, NT).astype(LOW)]
        )

    def over_all_columns(value_t, weight):
        return mul(jnp.concatenate([value_t, swap(value_t, "near")]), weight, TN)

    def one_group(group):
        def object_of(value):
            return lax.dynamic_index_in_dim(value, groups * far + group, 0, keepdims=False)

        inputs = object_of(tokens).astype(WIDE)
        patch_in = object_of(patches)
        length = object_of(patch_len)[None]
        grad_low = object_of(cotangent)
        onehot = (object_of(cam_index)[:, None] == jnp.arange(codes)[None, :]).astype(LOW)
        shift_scale = mul(onehot, table_flat)
        gain_one = 1.0 + shift_scale[:, :width]
        unit_one, rate_one = normed(inputs)
        normed_one = (unit_one * gain_one + shift_scale[:, width:]).astype(LOW)
        qkv_t = two_rows(qkv_rows, qkv_other, normed_one)
        qkv = exchange_rows(qkv_t.reshape(n_rows, 3, HEAD_DIM, rows))
        patch_mid = mul(patch_in, patch_weights).astype(LOW)
        pair_t = two_rows(pair_rows, pair_other, patch_mid)
        pair = exchange_rows(pair_t.reshape(n_rows, 2, HEAD_DIM, rows))
        mixed, self_wide, self_log = pair_forward(qkv, qkv, 1)
        self_mixed_t = exchange_rows(mixed).reshape(2 * cols, rows)
        after_self = inputs + over_all_columns(self_mixed_t, self_whole)
        unit_two, rate_two = normed(after_self)
        normed_two = (unit_two * cross_gain_f).astype(LOW)
        cross_q = mul(query_whole[: 2 * cols], normed_two, NT).astype(LOW)
        cross_q = exchange_rows(cross_q.reshape(n_rows, 1, HEAD_DIM, rows))
        mixed, cross_wide, cross_log = pair_forward(cross_q, pair, 0, length)
        cross_mixed_t = exchange_rows(mixed).reshape(2 * cols, rows)
        after_cross = after_self + over_all_columns(cross_mixed_t, cross_whole)
        unit_three, rate_three = normed(after_cross)
        normed_three = (unit_three * hidden_gain_f).astype(LOW)
        activated, grad_pre = [], []
        for widen, narrow in ((widen_weights, narrow_weights), (widen_other, narrow_other)):
            result, act_back = jax.vjp(gelu_tanh, mul(normed_three, widen))
            activated.append(result.astype(LOW))
            grad_pre.append(act_back(mul(grad_low, narrow, NT))[0].astype(LOW))
        grad_three = sum_near(
            mul(grad_pre[0], widen_weights, NT) + mul(grad_pre[1], widen_other, NT)
        )
        hidden_half = half_sum_near(
            mul(activated[0], narrow_weights) + mul(activated[1], narrow_other)
        )
        result = (halves(after_cross)[0] + hidden_half).astype(LOW)
        yield (
            "hidden",
            {
                "widen": [(normed_three, value, TN) for value in grad_pre],
                "narrow": [(value, grad_low, TN) for value in activated],
            },
        )
        hidden_gain_term = jnp.sum(grad_three * unit_three, axis=0)
        grad_cross = grad_low.astype(WIDE) + normed_back(
            grad_three * hidden_gain_f, unit_three, rate_three
        )
        grad_cross_low = grad_cross.astype(LOW)
        grad_mixed = mul(cross_whole[: 2 * cols], grad_cross_low, NT).astype(LOW)
        grad_mixed = exchange_rows(grad_mixed.reshape(n_rows, HEAD_DIM, rows))
        grads = pair_backward(cross_q, pair, 0, length, grad_mixed, cross_wide, cross_log)
        grads = exchange_rows(grads)
        grad_cq_t = grads[:, 0].reshape(2 * cols, rows)
        grad_pair = grads[:, 1:].reshape(2, heads, 2, HEAD_DIM, rows)
        grad_two = over_all_columns(grad_cq_t, query_whole)
        cross_gain_term = jnp.sum(grad_two * unit_two, axis=0)
        grad_self = grad_cross + normed_back(grad_two * cross_gain_f, unit_two, rate_two)
        grad_self_low = grad_self.astype(LOW)
        grad_mixed = mul(self_whole[: 2 * cols], grad_self_low, NT).astype(LOW)
        grad_mixed = exchange_rows(grad_mixed.reshape(n_rows, HEAD_DIM, rows))
        grads = pair_backward(qkv, qkv, 1, None, grad_mixed, self_wide, self_log)
        grads = exchange_rows(grads)
        grad_pair_t = grad_pair.reshape(2, 2 * cols, rows)
        grad_mid = sum_near(
            mul(grad_pair_t[0], pair_rows, TN) + mul(grad_pair_t[1], pair_other, TN)
        ).astype(LOW)
        patch_half = mul(halves(grad_mid)[0], patch_weights, NT).astype(LOW)
        by_kind = grad_pair.transpose(0, 2, 1, 3, 4).reshape(2, 2, cols, rows)
        yield (
            "middle",
            {
                "query": [(normed_two, grad_cq_t[i : i + cols], T_LAST) for i in (0, cols)],
                "pair": [[(patch_mid, by_kind[s, k], T_LAST) for k in range(2)] for s in range(2)],
                "patch": [(patch_in, value, TN) for value in shard_columns(grad_mid)],
                "cross_output": [
                    (cross_mixed_t[i : i + cols], grad_cross_low, NN) for i in (0, cols)
                ],
                "self_output": [(self_mixed_t[i : i + cols], grad_self_low, NN) for i in (0, cols)],
            },
        )
        grad_qkv_t = grads.reshape(2, 3 * cols, rows)
        grad_one = half_sum_near(
            mul(grad_qkv_t[0], qkv_rows, TN) + mul(grad_qkv_t[1], qkv_other, TN)
        )
        by_kind = grads.reshape(2, heads, 3, HEAD_DIM, rows).transpose(0, 2, 1, 3, 4)
        by_kind = by_kind.reshape(2, 3, cols, rows)
        gain_half, unit_half, rate_half, self_half = (
            halves(value)[0] for value in (gain_one, unit_one, rate_one, grad_self)
        )
        input_half = self_half + normed_back(grad_one * gain_half, unit_half, rate_half)
        onehot_half = halves(onehot)[0].astype(WIDE)
        table_term = jnp.concatenate(
            [
                lax.dot_general(onehot_half, value, TN, precision=lax.Precision.HIGHEST)
                for value in (grad_one * unit_half, grad_one)
            ],
            axis=0,
        )
        yield (
            "last",
            {
                "self": [[(normed_one, by_kind[s, k], T_LAST) for k in range(3)] for s in range(2)],
            },
        )
        yield "done", (result, input_half.astype(LOW), patch_half, table_term, hidden_gain_term, cross_gain_term)

    def product(*terms):
        dims = terms[0][2]
        left = jnp.concatenate([term[0] for term in terms], axis=dims[0][0][0])
        right = jnp.concatenate([term[1] for term in terms], axis=dims[0][1][0])
        return mul(left, right, dims).astype(LOW)

    def is_term(value):
        return isinstance(value, tuple)

    def sum_rows(both):
        part = lax.psum_scatter(both, "rows", scatter_dimension=1, tiled=True)
        total = part[0].astype(WIDE) + swap(part[1], "far").astype(WIDE)
        return lax.all_gather(total.astype(LOW), "rows", axis=0, tiled=True)

    steps = [one_group(group) for group in range(groups)]
    asked = [next(step) for step in steps]
    terms = {}
    while asked[0][0] != "done":
        gathered = [value for _, value in asked]
        terms.update(jax.tree.map(product, *gathered, is_leaf=is_term))
        if asked[0][0] == "hidden":
            hidden_total = sum_rows(
                jnp.stack([jnp.concatenate([terms["widen"][s], terms["narrow"][s]]) for s in range(2)])
            )
        elif asked[0][0] == "middle":
            output_total = sum_rows(
                jnp.stack(
                    [jnp.concatenate([terms["cross_output"][s], terms["self_output"][s]]) for s in range(2)]
                )
            )
            cross_total = sum_rows(
                jnp.stack(
                    [jnp.concatenate([terms["query"][s], *terms["pair"][s], terms["patch"][s]]) for s in range(2)]
                )
            )
        asked = [next(step) for step in steps]
    results, input_halves, patch_halves, tables, *gains = zip(*[value for _, value in asked])
    table = sum_near(sum(tables[1:], tables[0]))
    gain_terms = [sum(values[1:], values[0])[None] for values in gains]
    small = jnp.concatenate([table] + gain_terms + [jnp.zeros((62, width), WIDE)], axis=0).astype(LOW)
    last_total = sum_rows(
        jnp.stack(
            [jnp.concatenate([*terms["self"][s], value]) for s, value in enumerate(shard_columns(small))]
        )
    )
    outputs = over_heads(jnp.stack(results))
    input_grads = over_heads(jnp.stack(input_halves))
    patch_grads = over_heads(jnp.stack(patch_halves))
    kinds = last_total[: 3 * width].reshape(3, width, cols)
    table_total = last_total[3 * width : 3 * width + 2 * codes].reshape(2, codes, cols)
    gain_total = last_total[3 * width + 2 * codes :]
    gradients = (
        table_total.transpose(1, 0, 2),
        kinds,
        output_total[cols:],
        gain_total[1],
        cross_total[:width],
        cross_total[width : 3 * width].reshape(2, width, cols),
        output_total[:cols],
        cross_total[3 * width :],
        gain_total[0],
        hidden_total[:width],
        hidden_total[width:],
    )
    return (outputs, input_grads.astype(WIDE), patch_grads.astype(WIDE)) + tuple(
        value.astype(WIDE) for value in gradients
    )


def per_device(
    tokens,
    cam_index,
    patches,
    patch_len,
    camera_table,
    self_weights,
    self_output,
    cross_gain,
    cross_query,
    cross_pair,
    cross_output,
    patch_weights,
    hidden_gain,
    widen_weights,
    narrow_weights,
    cotangent,
):
    batches, rows, width = tokens.shape
    cols = self_weights.shape[2]
    heads = cols // HEAD_DIM
    codes = camera_table.shape[0]
    patch_rows, patch_width = patches.shape[1:]
    n_rows, n_heads = lax.axis_size("rows"), lax.axis_size("heads")
    row_rank, head_rank = lax.axis_index("rows"), lax.axis_index("heads")
    groups = 1
    objects = batches // groups
    full_lengths = jnp.full((objects,), n_rows * rows, jnp.int32)
    count = objects * rows

    def own_columns(value):
        return lax.dynamic_slice_in_dim(value, head_rank * cols, cols, value.ndim - 1)

    table_flat = camera_table.reshape(codes, -1)
    cross_gain_f = cross_gain.astype(WIDE)
    hidden_gain_f = hidden_gain.astype(WIDE)

    qkv_rows = (
        self_weights.reshape(3, width, heads, HEAD_DIM).transpose(2, 0, 3, 1).reshape(3 * cols, width)
    )
    qkv_rows_back = self_weights.transpose(0, 2, 1).reshape(3 * cols, width)
    pair_rows = cross_pair.transpose(0, 2, 1).reshape(2 * cols, width)
    query_rows = cross_query.T

    local = jnp.stack([self_output, cross_output, query_rows])
    piece = cols // n_rows
    local = lax.dynamic_slice_in_dim(local, row_rank * piece, piece, 1)
    whole = lax.all_gather(jnp.stack(gather_heads(local)), "rows", axis=0)
    whole = whole.transpose(2, 1, 0, 3, 4).reshape(3, n_heads * cols, width)
    self_whole, cross_whole, query_whole = whole[0], whole[1], whole[2]

    def over_all_columns(value_t, weight):
        return mul(jnp.concatenate(gather_heads(value_t), axis=0), weight, TN)

    def by_object(weight, value):
        return jnp.stack(
            [mul(weight, value[i * rows : (i + 1) * rows], NT).astype(LOW) for i in range(objects)]
        )

    def column_terms(value, grads_t):
        return [
            mul(value, grads_t[i : i + cols], (((0,), (1,)), ((), ())))
            for i in range(0, grads_t.shape[0], cols)
        ]

    def one_group(group):
        part = slice(group * objects, (group + 1) * objects)
        inputs = tokens[part].reshape(count, width).astype(WIDE)
        patch_in = patches[part].reshape(objects * patch_rows, patch_width)
        lengths = patch_len[part]
        grad_low = cotangent[part].reshape(count, width)
        onehot = (cam_index[part].reshape(count)[:, None] == jnp.arange(codes)[None, :]).astype(LOW)
        shift_scale = mul(onehot, table_flat)
        gain_one = 1.0 + shift_scale[:, :width]
        unit_one, rate_one = normed(inputs)
        normed_one = (unit_one * gain_one + shift_scale[:, width:]).astype(LOW)
        qkv_t = by_object(qkv_rows, normed_one)
        by_kind = qkv_t.reshape(objects, heads, 3, HEAD_DIM, rows).transpose(2, 1, 3, 0, 4)
        by_kind = by_kind.reshape(3, cols, count)
        self_pair = lax.all_gather(by_kind[1:], "rows", axis=0)
        patch_mid = mul(patch_in, patch_weights).astype(LOW)
        own_pair = mul(pair_rows, patch_mid, NT).astype(LOW).reshape(2, cols, -1)
        pair_t = lax.all_gather(own_pair, "rows", axis=0)
        self_mixed_t, self_wide, self_log = cross_forward(by_kind[0], self_pair, full_lengths)
        after_self = inputs + over_all_columns(self_mixed_t, self_whole)
        unit_two, rate_two = normed(after_self)
        normed_two = (unit_two * cross_gain_f).astype(LOW)
        cross_q_t = mul(query_rows, normed_two, NT).astype(LOW)
        cross_mixed_t, cross_wide, cross_log = cross_forward(cross_q_t, pair_t, lengths)
        after_cross = after_self + over_all_columns(cross_mixed_t, cross_whole)
        unit_three, rate_three = normed(after_cross)
        normed_three = (unit_three * hidden_gain_f).astype(LOW)
        pre_act = mul(normed_three, widen_weights)
        activated, act_back = jax.vjp(gelu_tanh, pre_act)
        activated = activated.astype(LOW)
        grad_pre = act_back(mul(grad_low, narrow_weights, NT))[0].astype(LOW)
        grad_three = sum_heads(mul(grad_pre, widen_weights, NT)).astype(WIDE)
        yield "heads", {"hidden": mul(activated, narrow_weights)}
        yield "rows", {
            "narrow": mul(activated, grad_low, TN),
            "widen": mul(normed_three, grad_pre, TN),
        }
        hidden_gain_term = jnp.sum(own_columns(grad_three * unit_three), axis=0)
        grad_cross = grad_low.astype(WIDE) + normed_back(
            grad_three * hidden_gain_f, unit_three, rate_three
        )
        grad_cross_low = grad_cross.astype(LOW)
        cross_output_term = mul(cross_mixed_t, grad_cross_low)
        grad_mixed_t = mul(cross_output, grad_cross_low, NT).astype(LOW)
        grad_cq_t, grad_pair_t = cross_backward(
            cross_q_t, pair_t, lengths, grad_mixed_t, cross_wide, cross_log
        )
        grad_two = over_all_columns(grad_cq_t, query_whole)
        grad_pair_t = lax.psum_scatter(grad_pair_t, "rows", scatter_dimension=0, tiled=False)
        grad_pair_t = grad_pair_t.reshape(2 * cols, -1)
        query_term = mul(normed_two, grad_cq_t, (((0,), (1,)), ((), ())))
        cross_gain_term = jnp.sum(own_columns(grad_two * unit_two), axis=0)
        grad_self = grad_cross + normed_back(grad_two * cross_gain_f, unit_two, rate_two)
        grad_self_low = grad_self.astype(LOW)
        self_output_term = mul(self_mixed_t, grad_self_low)
        yield "heads", {"patch": mul(grad_pair_t, pair_rows, TN)}
        yield "rows", {
            "query": query_term,
            "pair": column_terms(patch_mid, grad_pair_t),
            "cross_output": cross_output_term,
            "self_output": self_output_term,
        }
        grad_self_mixed_t = mul(self_output, grad_self_low, NT).astype(LOW)
        grad_q_t, grad_kv_t = cross_backward(
            by_kind[0], self_pair, full_lengths, grad_self_mixed_t, self_wide, self_log
        )
        grad_kv_t = lax.psum_scatter(grad_kv_t, "rows", scatter_dimension=0, tiled=False)
        grad_qkv_t = jnp.concatenate([grad_q_t[None], grad_kv_t]).reshape(3 * cols, count)
        grad_qkv_t = yield "after", (grad_qkv_t, ["patch", "narrow", "widen"])
        grad_mid = yield "take", "patch"
        patch_term = mul(patch_in, own_columns(grad_mid), TN)
        patch_grad = mul(grad_mid, patch_weights, NT)
        grad_one = sum_heads(mul(grad_qkv_t, qkv_rows_back, TN))
        grad_one = yield "after", (grad_one, ["query", "pair", "cross_output", "self_output"])
        grad_one = grad_one.astype(WIDE)
        input_grad = grad_self + normed_back(grad_one * gain_one, unit_one, rate_one)
        own_grad = own_columns(grad_one)
        table_term = jnp.stack(
            [
                lax.dot_general(onehot.astype(WIDE), v, TN, precision=lax.Precision.HIGHEST)
                for v in (own_grad * own_columns(unit_one), own_grad)
            ],
            axis=1,
        )
        small = [patch_term, table_term.reshape(2 * codes, cols)]
        small += [hidden_gain_term[None], cross_gain_term[None], jnp.zeros((14, cols), WIDE)]
        yield "rows", {
            "self": column_terms(normed_one, grad_qkv_t),
            "small": jnp.concatenate(small, axis=0),
        }
        hidden_sum = yield "take", "hidden"
        result = (after_cross + hidden_sum.astype(WIDE)).astype(LOW)
        yield (
            "done",
            (
                result.reshape(objects, rows, width),
                input_grad.reshape(objects, rows, width),
                patch_grad.reshape(objects, patch_rows, patch_width),
            ),
        )

    steps = [one_group(group) for group in range(groups)]
    asked = [next(step) for step in steps]
    totals, ahead = {}, []
    while asked[0][0] != "done":
        kind, what = asked[0]
        answers = [None] * groups
        if kind == "take":
            answers = jnp.split(totals[what], groups)
        elif kind == "after":
            early = {name: totals[name] for name in what[1]}
            answers = [value for _, (value, _) in asked]
            answers[-1], early = lax.optimization_barrier((answers[-1], early))
            totals.update(early)
        else:
            terms = [value for _, value in asked]
            if kind == "heads":
                terms = jax.tree.map(lambda *parts: jnp.concatenate(parts, axis=0), *terms)
            else:
                for value in terms[1:]:
                    terms[0] = add_trees(terms[0], value)
                terms = terms[0]
            if kind == "rows":
                terms = jax.tree.map(lambda value: value.astype(LOW), terms)
            if kind == "heads":
                totals.update({name: sum_heads(value) for name, value in terms.items()})
            else:
                before = {name: totals[name] for name in ahead}
                terms, before = lax.optimization_barrier((terms, before))
                totals.update(before)
                totals.update(lax.psum(terms, kind))
                ahead = list(terms)
        asked = [step.send(value) for step, value in zip(steps, answers)]
    outputs, input_grads, patch_grads = (
        jnp.concatenate([value[i] for _, value in asked], axis=0) for i in range(3)
    )
    patch_total, table_total, gains = jnp.split(
        totals["small"], [patch_width, patch_width + 2 * codes]
    )
    gradients = (
        table_total.reshape(codes, 2, cols),
        jnp.stack(totals["self"]),
        totals["self_output"],
        gains[1],
        totals["query"],
        jnp.stack(totals["pair"]),
        totals["cross_output"],
        patch_total,
        gains[0],
        totals["widen"],
        totals["narrow"],
    )
    return (outputs, input_grads, patch_grads) + tuple(value.astype(WIDE) for value in gradients)


def solution(mesh):
    sizes = mesh.shape
    paired = sizes["heads"] == 4 and sizes["rows"] == 8
    heads = ("far", "near") if paired else "heads"
    if paired:
        names = (*heads, "rows")
        mesh = jax.sharding.Mesh(mesh.devices.reshape(2, 2, sizes["rows"]), names)
    in_specs = (
        P(None, "rows", None),
        P(None, "rows"),
        P(None, "rows", None),
        P(),
        P(),
        P(None, None, heads),
        P(heads, None),
        P(),
        P(None, heads),
        P(None, None, heads),
        P(heads, None),
        P(),
        P(),
        P(None, heads),
        P(heads, None),
        P(None, "rows", None),
    )
    out_specs = (
        P(None, "rows", None),
        P(None, "rows", None),
        P(None, "rows", None),
        P(None, None, heads),
        P(None, None, heads),
        P(heads, None),
        P(heads),
        P(None, heads),
        P(None, None, heads),
        P(heads, None),
        P(None, heads),
        P(heads),
        P(None, heads),
        P(heads, None),
    )
    return jax.shard_map(
        paired_device if paired else per_device,
        mesh=mesh,
        in_specs=in_specs,
        out_specs=out_specs,
        check_vma=False,
    )
```

```python
import jax
import jax.numpy as jnp
from jax import lax
from jax.experimental import pallas as pl
from jax.experimental.pallas import tpu as pltpu
from jax.sharding import PartitionSpec as P

HEAD_DIM = 64
EPSILON = 1e-05
SCALE = HEAD_DIM ** (-0.5)
LOW = jnp.bfloat16
WIDE = jnp.float32

NN = (((1,), (0,)), ((), ()))
NT = (((1,), (1,)), ((), ()))
TN = (((0,), (0,)), ((), ()))
T_LAST = (((0,), (1,)), ((), ()))


def mul(left, right, dims=NN):
    return lax.dot_general(left, right, dims, preferred_element_type=WIDE)


def load_values(values, block, values_t):
    rows = values_t.shape[1]
    at = slice(block * rows, (block + 1) * rows)
    values[at, :HEAD_DIM] = values_t.T
    values[at, HEAD_DIM:] = jnp.ones((rows, HEAD_DIM), values.dtype)


def attend_block(queries, keys_t, values):
    scores = mul(queries, keys_t)
    peak = jnp.max(scores, axis=1, keepdims=True)
    both = mul(jnp.exp(scores - peak).astype(LOW), values).T
    total = both[HEAD_DIM : HEAD_DIM + 1]
    return both[:HEAD_DIM] / total, peak.T + jnp.log(total)


def attend_block_back(scaled_q, grad_t, keys, keys_t, values, log_total, spread):
    probs = jnp.exp(mul(keys, scaled_q) - log_total)
    grad_scores = (probs * (mul(values, grad_t) - spread)).astype(LOW)
    return (
        (mul(keys_t, grad_scores) * SCALE).astype(LOW),
        mul(grad_scores, scaled_q.T),
        mul(probs.astype(LOW), grad_t.T),
    )


def estimate(rows, cols, passes):
    return pl.CostEstimate(
        flops=int(rows * cols * 1200 * passes), transcendentals=int(rows * cols), bytes_accessed=int(rows * 2048)
    )


VMEM_LIMIT = 48 << 20


def by_length(length, full, blocks, run):
    @pl.when(length * 4 > full)
    def _():
        run(blocks)

    @pl.when(length * 4 <= full)
    def _():
        run(blocks // 4)


def cross_forward(queries_t, pair_t, lengths):
    blocks, _, cols, all_patches = pair_t.shape
    objects = lengths.shape[0]
    heads = cols // HEAD_DIM
    rows, patch_rows = queries_t.shape[1] // objects, all_patches // objects

    def kernel(len_ref, q_ref, pair_ref, mixed_ref, wide_ref, log_ref, keys_t, values):
        queries = (q_ref[...] * LOW(SCALE)).T

        def run(live):
            for c in range(live):
                keys_t[:, c * patch_rows : (c + 1) * patch_rows] = pair_ref[c, 0]
                load_values(values, c, pair_ref[c, 1])
            size = live * patch_rows
            mixed, log_total = attend_block(queries, keys_t[:, :size], values[:size])
            mixed_ref[...] = mixed.astype(LOW)
            wide_ref[...] = mixed
            log_ref[...] = log_total

        by_length(len_ref[pl.program_id(0)], blocks * patch_rows, blocks, run)

    block = pl.BlockSpec((HEAD_DIM, rows), lambda b, j, lens: (j, b))
    return pl.pallas_call(
        kernel,
        grid_spec=pltpu.PrefetchScalarGridSpec(
            num_scalar_prefetch=1,
            grid=(objects, heads),
            in_specs=[
                block,
                pl.BlockSpec((blocks, 2, HEAD_DIM, patch_rows), lambda b, j, lens: (0, 0, j, b)),
            ],
            out_specs=[block, block, pl.BlockSpec((None, 1, rows), lambda b, j, lens: (j, 0, b))],
            scratch_shapes=[
                pltpu.VMEM((HEAD_DIM, blocks * patch_rows), LOW),
                pltpu.VMEM((blocks * patch_rows, 2 * HEAD_DIM), LOW),
            ],
        ),
        out_shape=[
            jax.ShapeDtypeStruct(queries_t.shape, LOW),
            jax.ShapeDtypeStruct(queries_t.shape, WIDE),
            jax.ShapeDtypeStruct((heads, 1, queries_t.shape[1]), WIDE),
        ],
        name="cross_forward",
        cost_estimate=estimate(objects * rows, blocks * patch_rows * heads, 1.4),
        compiler_params=pltpu.CompilerParams(vmem_limit_bytes=VMEM_LIMIT),
    )(lengths, queries_t, pair_t)


def cross_backward(queries_t, pair_t, lengths, grad_t_all, wide, log_total):
    blocks, _, cols, all_patches = pair_t.shape
    objects = lengths.shape[0]
    heads = cols // HEAD_DIM
    rows, patch_rows = queries_t.shape[1] // objects, all_patches // objects

    def kernel(len_ref, q_ref, pair_ref, g_ref, wide_ref, log_ref, out_q, out_pair, keys, keys_t, values):
        grad_t = g_ref[...]
        spread = jnp.sum(grad_t.astype(WIDE) * wide_ref[...], axis=0, keepdims=True)

        def run(live):
            for c in range(live):
                at = slice(c * patch_rows, (c + 1) * patch_rows)
                keys[at] = pair_ref[c, 0].T
                keys_t[:, at] = pair_ref[c, 0]
                values[at] = pair_ref[c, 1].T
            size = live * patch_rows
            out_q[...], grad_k, grad_v = attend_block_back(
                q_ref[...] * LOW(SCALE),
                grad_t,
                keys[:size],
                keys_t[:, :size],
                values[:size],
                log_ref[...],
                spread,
            )
            for c in range(live):
                at = slice(c * patch_rows, (c + 1) * patch_rows)
                out_pair[c, 0] = grad_k[at].T.astype(LOW)
                out_pair[c, 1] = grad_v[at].T.astype(LOW)
            for c in range(live, blocks):
                out_pair[c] = jnp.zeros_like(out_pair[c])

        by_length(len_ref[pl.program_id(0)], blocks * patch_rows, blocks, run)

    block = pl.BlockSpec((HEAD_DIM, rows), lambda b, j, lens: (j, b))
    pair_block = pl.BlockSpec((blocks, 2, HEAD_DIM, patch_rows), lambda b, j, lens: (0, 0, j, b))
    return pl.pallas_call(
        kernel,
        grid_spec=pltpu.PrefetchScalarGridSpec(
            num_scalar_prefetch=1,
            grid=(objects, heads),
            in_specs=[
                block,
                pair_block,
                block,
                block,
                pl.BlockSpec((None, 1, rows), lambda b, j, lens: (j, 0, b)),
            ],
            out_specs=[block, pair_block],
            scratch_shapes=[
                pltpu.VMEM((blocks * patch_rows, HEAD_DIM), LOW),
                pltpu.VMEM((HEAD_DIM, blocks * patch_rows), LOW),
                pltpu.VMEM((blocks * patch_rows, HEAD_DIM), LOW),
            ],
        ),
        out_shape=[
            jax.ShapeDtypeStruct(queries_t.shape, LOW),
            jax.ShapeDtypeStruct(pair_t.shape, LOW),
        ],
        name="cross_backward",
        cost_estimate=estimate(objects * rows, blocks * patch_rows * heads, 2.5),
        compiler_params=pltpu.CompilerParams(vmem_limit_bytes=VMEM_LIMIT),
    )(lengths, queries_t, pair_t, grad_t_all, wide, log_total)


def shift(value, step):
    size = lax.axis_size("heads")
    return lax.ppermute(value, "heads", [((i + step) % size, i) for i in range(size)])


def gather_heads(value):
    size = lax.axis_size("heads")
    if size != 4:
        return [value] + [shift(value, step) for step in range(1, size)]
    after, before = shift(value, 1), shift(value, -1)
    inner = lax.ppermute(after, "heads", [(1, 0), (2, 1)]) + lax.ppermute(before, "heads", [(1, 2), (2, 3)])
    return [value, after, inner, before]


def scatter_heads(partial):
    size, me = lax.axis_size("heads"), lax.axis_index("heads")

    def part(step):
        return lax.dynamic_index_in_dim(partial, (me + step) % size, 0, keepdims=False)

    if size != 4:
        total = part(0)
        for step in range(1, size):
            total = total + shift(part(step).astype(LOW), -step).astype(WIDE)
        return total
    far = part(2).astype(LOW)
    up = lax.ppermute(far, "heads", [(0, 1), (1, 2)]).astype(WIDE)
    down = lax.ppermute(far, "heads", [(2, 1), (3, 2)]).astype(WIDE)
    from_below = shift((part(1) + up).astype(LOW), -1)
    from_above = shift((part(3) + down).astype(LOW), 1)
    return part(0) + from_below.astype(WIDE) + from_above.astype(WIDE)


def in_order(parts):
    size, me = lax.axis_size("heads"), lax.axis_index("heads")
    out = jnp.zeros((size,) + parts[0].shape, parts[0].dtype)
    for step, value in enumerate(parts):
        out = lax.dynamic_update_index_in_dim(out, value, (me + step) % size, 0)
    return out.reshape((-1,) + parts[0].shape[1:])


def sum_heads(partial):
    size = lax.axis_size("heads")
    split = partial.reshape((size, -1) + partial.shape[1:])
    return in_order(gather_heads(scatter_heads(split).astype(LOW)))


def exchange_rows(value):
    return lax.all_to_all(value, "rows", 0, 0, tiled=True)


def normed(value):
    centred = value - jnp.mean(value, axis=-1, keepdims=True)
    rate = lax.rsqrt(jnp.mean(centred * centred, axis=-1, keepdims=True) + EPSILON)
    return centred * rate, rate


def normed_back(grad, unit, rate):
    return rate * (
        grad
        - jnp.mean(grad, axis=-1, keepdims=True)
        - unit * jnp.mean(grad * unit, axis=-1, keepdims=True)
    )


def gelu_tanh(pre_act):
    return jax.nn.gelu(pre_act, approximate=True)


def add_trees(former, latter):
    return jax.tree.map(jnp.add, former, latter)


def pair_forward(queries, pair, key_at, length=None):
    blocks, objects, _, width, rows = queries.shape
    pair_rows = pair.shape[4]
    lengths = jnp.full((objects,), blocks * pair_rows, jnp.int32) if length is None else length

    def kernel(len_ref, q_ref, k_ref, v_ref, mixed_ref, wide_ref, log_ref, keys_t, values):
        def run(live):
            @pl.when(pl.program_id(1) == 0)
            def _():
                for c in range(live):
                    keys_t[:, c * pair_rows : (c + 1) * pair_rows] = k_ref[c]
                    load_values(values, c, v_ref[c])

            size = live * pair_rows
            mixed, log_total = attend_block(
                (q_ref[...] * LOW(SCALE)).T, keys_t[:, :size], values[:size]
            )
            mixed_ref[...] = mixed.astype(LOW)
            wide_ref[...] = mixed
            log_ref[...] = log_total

        if length is None:
            run(blocks)
        else:
            by_length(len_ref[pl.program_id(0)], blocks * pair_rows, blocks, run)

    block = pl.BlockSpec((None, None, width, rows), lambda o, i, lens: (i, o, 0, 0))
    return pl.pallas_call(
        kernel,
        grid_spec=pltpu.PrefetchScalarGridSpec(
            num_scalar_prefetch=1,
            grid=(objects, blocks),
            in_specs=[
                pl.BlockSpec((None, None, None, width, rows), lambda o, i, lens: (i, o, 0, 0, 0)),
                pl.BlockSpec((blocks, None, None, width, pair_rows), lambda o, i, lens: (0, o, key_at, 0, 0)),
                pl.BlockSpec((blocks, None, None, width, pair_rows), lambda o, i, lens: (0, o, key_at + 1, 0, 0)),
            ],
            out_specs=[block, block, pl.BlockSpec((None, None, 1, rows), lambda o, i, lens: (i, o, 0, 0))],
            scratch_shapes=[
                pltpu.VMEM((width, blocks * pair_rows), LOW),
                pltpu.VMEM((blocks * pair_rows, 2 * width), LOW),
            ],
        ),
        out_shape=[
            jax.ShapeDtypeStruct((blocks, objects, width, rows), LOW),
            jax.ShapeDtypeStruct((blocks, objects, width, rows), WIDE),
            jax.ShapeDtypeStruct((blocks, objects, 1, rows), WIDE),
        ],
        name="pair_forward",
        cost_estimate=estimate(objects * blocks * rows, blocks * pair_rows, 2 if length is None else 1.4),
        compiler_params=pltpu.CompilerParams(vmem_limit_bytes=VMEM_LIMIT),
    )(lengths, queries, pair, pair)


def pair_backward(queries, pair, key_at, length, grad_mixed, wide, log_total):
    blocks, objects, _, width, rows = queries.shape
    lengths = jnp.full((objects,), blocks * rows, jnp.int32) if length is None else length

    def kernel(len_ref, q_ref, k_ref, v_ref, g_ref, wide_ref, log_ref, out_ref, keys, keys_t, values, grad_k, grad_v):
        i = pl.program_id(1)

        def run(live):
            size = live * rows

            @pl.when(i == 0)
            def _():
                for c in range(live):
                    at = slice(c * rows, (c + 1) * rows)
                    keys[at] = k_ref[c].T
                    keys_t[:, at] = k_ref[c]
                    values[at] = v_ref[c].T

            grad_t = g_ref[...]
            spread = jnp.sum(grad_t.astype(WIDE) * wide_ref[...], axis=0, keepdims=True)
            out_ref[i, 0], term_k, term_v = attend_block_back(
                q_ref[...] * LOW(SCALE),
                grad_t,
                keys[:size],
                keys_t[:, :size],
                values[:size],
                log_ref[...],
                spread,
            )

            @pl.when(i == 0)
            def _():
                grad_k[:size] = term_k
                grad_v[:size] = term_v

            @pl.when(i > 0)
            def _():
                grad_k[:size] += term_k
                grad_v[:size] += term_v

            @pl.when(i == blocks - 1)
            def _():
                for c in range(live):
                    at = slice(c * rows, (c + 1) * rows)
                    out_ref[c, 1] = grad_k[at].T.astype(LOW)
                    out_ref[c, 2] = grad_v[at].T.astype(LOW)
                for c in range(live, blocks):
                    out_ref[c, 1:] = jnp.zeros_like(out_ref[c, 1:])

        if length is None:
            run(blocks)
        else:
            by_length(len_ref[pl.program_id(0)], blocks * rows, blocks, run)

    block = pl.BlockSpec((None, None, width, rows), lambda o, i, lens: (i, o, 0, 0))
    return pl.pallas_call(
        kernel,
        grid_spec=pltpu.PrefetchScalarGridSpec(
            num_scalar_prefetch=1,
            grid=(objects, blocks),
            in_specs=[
                pl.BlockSpec((None, None, None, width, rows), lambda o, i, lens: (i, o, 0, 0, 0)),
                pl.BlockSpec((blocks, None, None, width, rows), lambda o, i, lens: (0, o, key_at, 0, 0)),
                pl.BlockSpec((blocks, None, None, width, rows), lambda o, i, lens: (0, o, key_at + 1, 0, 0)),
                block,
                block,
                pl.BlockSpec((None, None, 1, rows), lambda o, i, lens: (i, o, 0, 0)),
            ],
            out_specs=pl.BlockSpec((blocks, None, 3, width, rows), lambda o, i, lens: (0, o, 0, 0, 0)),
            scratch_shapes=[
                pltpu.VMEM((blocks * rows, width), LOW),
                pltpu.VMEM((width, blocks * rows), LOW),
                pltpu.VMEM((blocks * rows, width), LOW),
                pltpu.VMEM((blocks * rows, width), WIDE),
                pltpu.VMEM((blocks * rows, width), WIDE),
            ],
        ),
        out_shape=jax.ShapeDtypeStruct((blocks, objects, 3, width, rows), LOW),
        name="pair_backward",
        cost_estimate=estimate(objects * blocks * rows, blocks * rows, 3 if length is None else 2),
        compiler_params=pltpu.CompilerParams(vmem_limit_bytes=VMEM_LIMIT),
    )(lengths, queries, pair, pair, grad_mixed, wide, log_total)


def swap(value, axis):
    return lax.ppermute(value, axis, [(0, 1), (1, 0)])


def sum_near(partial):
    low = partial.astype(LOW)
    return low.astype(WIDE) + swap(low, "near").astype(WIDE)


def tie(value, *others):
    return lax.optimization_barrier((value, *others))


def paired_device(
    tokens,
    cam_index,
    patches,
    patch_len,
    camera_table,
    self_weights,
    self_output,
    cross_gain,
    cross_query,
    cross_pair,
    cross_output,
    patch_weights,
    hidden_gain,
    widen_weights,
    narrow_weights,
    cotangent,
):
    objects = tokens.shape[0] // 2
    _, rows, width = tokens.shape
    cols = self_weights.shape[2]
    hidden = widen_weights.shape[1]
    heads = cols // HEAD_DIM
    codes = camera_table.shape[0]
    patch_width = patches.shape[2]
    count = objects * rows
    n_rows = lax.axis_size("rows")
    row_rank = lax.axis_index("rows")
    far, near = lax.axis_index("far"), lax.axis_index("near")
    own = 2 * far + near
    other = 2 * (1 - far) + near

    def objects_of(value):
        return lax.dynamic_slice_in_dim(value, objects * far, objects, 0)

    def piece(value):
        size = value.shape[0] // n_rows
        return lax.dynamic_slice_in_dim(value, row_rank * size, size, 0)

    def join_rows(value):
        return lax.all_gather(value, "rows", axis=0, tiled=True)

    def put_together(value):
        whole = lax.all_gather(value, "rows", axis=1)
        return whole.reshape(value.shape[0] * cols, width)

    def both_columns(value):
        return [
            lax.dynamic_slice_in_dim(value, index * cols, cols, value.ndim - 1)
            for index in (own, other)
        ]

    def halves(value):
        value = value.reshape(objects, 2, rows // 2, -1)
        return [
            lax.dynamic_index_in_dim(value, index, 1, keepdims=False).reshape(count // 2, -1)
            for index in (near, 1 - near)
        ]

    def half_sum_near(partial):
        mine, away = halves(partial)
        return mine + swap(away.astype(LOW), "near").astype(WIDE)

    def over_heads(value):
        value = value.reshape(objects, rows // 2, -1)
        value = jnp.stack([value, swap(value, "far")])
        value = jnp.stack([value, swap(value, "near")])
        value = jnp.where(far == 0, value, jnp.flip(value, 1))
        value = jnp.where(near == 0, value, jnp.flip(value, 0))
        return value.transpose(1, 2, 0, 3, 4).reshape(2 * objects, rows, -1)

    def to_pairs(weights, value, slots):
        parts = [
            jnp.concatenate(
                [mul(weight, value[i * rows : (i + 1) * rows], NT).astype(LOW) for weight in weights]
            ).reshape(n_rows, slots, HEAD_DIM, rows)
            for i in range(objects)
        ]
        return exchange_rows(jnp.stack(parts, axis=1))

    def from_pairs(value):
        return value.transpose(0, 2, 3, 1, 4).reshape(-1, count)

    def over_all_columns(value_t, weight):
        return mul(jnp.concatenate([value_t, swap(value_t, "near")]), weight, TN)

    qkv_rows = self_weights.reshape(3, width, heads, HEAD_DIM).transpose(2, 0, 3, 1)
    qkv_rows = qkv_rows.reshape(3 * cols, width)
    pair_rows = cross_pair.reshape(2, width, heads, HEAD_DIM).transpose(2, 0, 3, 1)
    pair_rows = pair_rows.reshape(2 * cols, width)
    query_rows = cross_query.T

    qkv_other = join_rows(swap(piece(qkv_rows), "far"))

    table_flat = camera_table.reshape(codes, -1)
    cross_gain_f = cross_gain.astype(WIDE)
    hidden_gain_f = hidden_gain.astype(WIDE)

    inputs = objects_of(tokens).reshape(count, width).astype(WIDE)
    patch_in = objects_of(patches).reshape(count, patch_width)
    length = objects_of(patch_len)
    grad_low = objects_of(cotangent).reshape(count, width)
    codes_of = objects_of(cam_index).reshape(count)
    onehot = (codes_of[:, None] == jnp.arange(codes)[None, :]).astype(LOW)
    shift_scale = mul(onehot, table_flat)
    gain_one = 1.0 + shift_scale[:, :width]
    unit_one, rate_one = normed(inputs)
    normed_one = (unit_one * gain_one + shift_scale[:, width:]).astype(LOW)

    mine = [piece(v) for v in (self_output, query_rows, cross_output, pair_rows)]
    normed_one, *mine = tie(normed_one, *mine)
    across = swap(jnp.concatenate(mine, axis=0), "far")
    size = cols // n_rows
    two = jnp.stack([jnp.concatenate(mine[:3]), across[: 3 * size]])
    four = jnp.concatenate([two, swap(two, "near")])
    pair_other = join_rows(across[3 * size :])
    self_whole, query_whole, cross_whole = (
        put_together(four[:, i * size : (i + 1) * size]) for i in range(3)
    )

    qkv = to_pairs((qkv_rows, qkv_other), normed_one, 3)
    patch_mid = mul(patch_in, patch_weights).astype(LOW)
    pair = to_pairs((pair_rows, pair_other), patch_mid, 2)

    mine = [piece(widen_weights), piece(narrow_weights)]
    qkv, *mine = tie(qkv, *mine)
    across = swap(jnp.concatenate(mine, axis=0), "far")
    size = width // n_rows
    widen = jnp.concatenate([widen_weights, join_rows(across[:size])], axis=1)
    narrow = jnp.concatenate([narrow_weights, join_rows(across[size:])], axis=0)

    mixed, self_wide, self_log = pair_forward(qkv, qkv, 1)
    self_mixed_t = from_pairs(exchange_rows(mixed)[:, :, None])
    after_self = inputs + over_all_columns(self_mixed_t, self_whole)
    unit_two, rate_two = normed(after_self)
    normed_two = (unit_two * cross_gain_f).astype(LOW)
    cross_q = to_pairs((query_whole[: 2 * cols],), normed_two, 1)
    mixed, cross_wide, cross_log = pair_forward(cross_q, pair, 0, length)
    cross_mixed_t = from_pairs(exchange_rows(mixed)[:, :, None])
    after_cross = after_self + over_all_columns(cross_mixed_t, cross_whole)
    unit_three, rate_three = normed(after_cross)
    normed_three = (unit_three * hidden_gain_f).astype(LOW)
    activated, act_back = jax.vjp(gelu_tanh, mul(normed_three, widen))
    activated = activated.astype(LOW)
    grad_pre = act_back(mul(grad_low, narrow, NT))[0].astype(LOW)
    grad_three = sum_near(mul(grad_pre, widen, NT))
    hidden_half = half_sum_near(mul(activated, narrow))
    result = (halves(after_cross)[0] + hidden_half).astype(LOW)

    def part_rows(both):
        return lax.psum_scatter(both, "rows", scatter_dimension=1, tiled=True)

    def total_rows(part):
        return join_rows((part[0].astype(WIDE) + swap(part[1], "far").astype(WIDE)).astype(LOW))

    def by_shard(left, right):
        return mul(left, right, NN).astype(LOW).reshape(2, -1, right.shape[1])

    hidden_part = part_rows(
        jnp.concatenate(
            [
                mul(value, against, TN).astype(LOW).reshape(2, hidden, width)
                for value, against in ((activated, grad_low), (grad_pre, normed_three))
            ],
            axis=1,
        )
    )

    hidden_gain_term = jnp.sum(grad_three * unit_three, axis=0)
    grad_cross = grad_low.astype(WIDE) + normed_back(
        grad_three * hidden_gain_f, unit_three, rate_three
    )
    grad_cross_low = grad_cross.astype(LOW)
    grad_mixed = to_pairs((cross_whole[: 2 * cols],), grad_cross_low, 1)[:, :, 0]
    grads = pair_backward(cross_q, pair, 0, length, grad_mixed, cross_wide, cross_log)
    grads = exchange_rows(grads)
    grads, hidden_part = tie(grads, hidden_part)
    hidden_total = total_rows(hidden_part)
    outputs = over_heads(result)
    grad_cq_t = from_pairs(grads[:, :, :1])
    grad_pair_t = from_pairs(grads[:, :, 1:])
    grad_two = over_all_columns(grad_cq_t, query_whole)
    cross_gain_term = jnp.sum(grad_two * unit_two, axis=0)
    grad_self = grad_cross + normed_back(grad_two * cross_gain_f, unit_two, rate_two)
    grad_self_low = grad_self.astype(LOW)
    grad_mid = sum_near(
        mul(grad_pair_t, jnp.concatenate([pair_rows, pair_other]), TN)
    ).astype(LOW)
    patch_half = mul(halves(grad_mid)[0], patch_weights, NT).astype(LOW)
    patch_terms = jnp.stack([mul(value, patch_in, TN).astype(LOW) for value in both_columns(grad_mid)])
    patch_terms = jnp.pad(patch_terms, ((0, 0), (0, 0), (0, width - patch_width)))
    middle_part = part_rows(
        jnp.concatenate(
            [
                by_shard(cross_mixed_t, grad_cross_low),
                by_shard(self_mixed_t, grad_self_low),
                by_shard(grad_cq_t, normed_two),
                by_shard(grad_pair_t, patch_mid),
                patch_terms,
            ],
            axis=1,
        )
    )
    grad_mixed = to_pairs((self_whole[: 2 * cols],), grad_self_low, 1)[:, :, 0]
    grad_mixed, hidden_total, outputs = tie(grad_mixed, hidden_total, outputs)
    grads = exchange_rows(pair_backward(qkv, qkv, 1, None, grad_mixed, self_wide, self_log))
    patch_grads = over_heads(patch_half)
    grads, middle_part, patch_grads = tie(grads, middle_part, patch_grads)
    middle_total = total_rows(middle_part)
    grad_qkv_t = from_pairs(grads)
    last_part = part_rows(by_shard(grad_qkv_t, normed_one))
    grad_one = half_sum_near(mul(grad_qkv_t, jnp.concatenate([qkv_rows, qkv_other]), TN))
    gain_half, unit_half, rate_half, self_half = (
        halves(value)[0] for value in (gain_one, unit_one, rate_one, grad_self)
    )
    input_half = self_half + normed_back(grad_one * gain_half, unit_half, rate_half)
    input_half = input_half.astype(LOW)
    onehot_half = halves(onehot)[0].astype(WIDE)
    table_term = jnp.concatenate(
        [
            lax.dot_general(onehot_half, value, TN, precision=lax.Precision.HIGHEST)
            for value in (grad_one * unit_half, grad_one)
        ],
        axis=0,
    )
    small = [sum_near(table_term), hidden_gain_term[None], cross_gain_term[None], jnp.zeros((14, width), WIDE)]
    small = jnp.stack(both_columns(jnp.concatenate(small, axis=0).astype(LOW)))
    small = jnp.sum(lax.all_gather(small, "rows", axis=0).astype(WIDE), axis=0)
    small = small[0] + swap(small[1].astype(LOW), "far").astype(WIDE)
    input_half, middle_total = tie(input_half, middle_total)
    input_grads = over_heads(input_half)
    last_total = total_rows(last_part)

    output_total = middle_total[: 2 * cols]
    query_total = middle_total[2 * cols : 3 * cols]
    pair_total = middle_total[3 * cols : 5 * cols].reshape(heads, 2, HEAD_DIM, width)
    patch_total = middle_total[5 * cols :, :patch_width]
    self_total = last_total.reshape(heads, 3, HEAD_DIM, width)
    gradients = (
        small[: 2 * codes].reshape(2, codes, cols).transpose(1, 0, 2),
        self_total.transpose(1, 3, 0, 2).reshape(3, width, cols),
        output_total[cols:],
        small[2 * codes + 1],
        query_total.T,
        pair_total.transpose(1, 3, 0, 2).reshape(2, width, cols),
        output_total[:cols],
        patch_total.T,
        small[2 * codes],
        hidden_total[hidden:].T,
        hidden_total[:hidden],
    )
    return (outputs, input_grads.astype(WIDE), patch_grads.astype(WIDE)) + tuple(
        value.astype(WIDE) for value in gradients
    )


def per_device(
    tokens,
    cam_index,
    patches,
    patch_len,
    camera_table,
    self_weights,
    self_output,
    cross_gain,
    cross_query,
    cross_pair,
    cross_output,
    patch_weights,
    hidden_gain,
    widen_weights,
    narrow_weights,
    cotangent,
):
    batches, rows, width = tokens.shape
    cols = self_weights.shape[2]
    heads = cols // HEAD_DIM
    codes = camera_table.shape[0]
    patch_rows, patch_width = patches.shape[1:]
    n_rows, n_heads = lax.axis_size("rows"), lax.axis_size("heads")
    row_rank, head_rank = lax.axis_index("rows"), lax.axis_index("heads")
    groups = 1
    objects = batches // groups
    full_lengths = jnp.full((objects,), n_rows * rows, jnp.int32)
    count = objects * rows

    def own_columns(value):
        return lax.dynamic_slice_in_dim(value, head_rank * cols, cols, value.ndim - 1)

    table_flat = camera_table.reshape(codes, -1)
    cross_gain_f = cross_gain.astype(WIDE)
    hidden_gain_f = hidden_gain.astype(WIDE)

    qkv_rows = (
        self_weights.reshape(3, width, heads, HEAD_DIM).transpose(2, 0, 3, 1).reshape(3 * cols, width)
    )
    qkv_rows_back = self_weights.transpose(0, 2, 1).reshape(3 * cols, width)
    pair_rows = cross_pair.transpose(0, 2, 1).reshape(2 * cols, width)
    query_rows = cross_query.T

    local = jnp.stack([self_output, cross_output, query_rows])
    piece = cols // n_rows
    local = lax.dynamic_slice_in_dim(local, row_rank * piece, piece, 1)
    whole = lax.all_gather(jnp.stack(gather_heads(local)), "rows", axis=0)
    whole = whole.transpose(2, 1, 0, 3, 4).reshape(3, n_heads * cols, width)
    self_whole, cross_whole, query_whole = whole[0], whole[1], whole[2]

    def over_all_columns(value_t, weight):
        return mul(jnp.concatenate(gather_heads(value_t), axis=0), weight, TN)

    def by_object(weight, value):
        return jnp.stack(
            [mul(weight, value[i * rows : (i + 1) * rows], NT).astype(LOW) for i in range(objects)]
        )

    def column_terms(value, grads_t):
        return [
            mul(value, grads_t[i : i + cols], (((0,), (1,)), ((), ())))
            for i in range(0, grads_t.shape[0], cols)
        ]

    def one_group(group):
        part = slice(group * objects, (group + 1) * objects)
        inputs = tokens[part].reshape(count, width).astype(WIDE)
        patch_in = patches[part].reshape(objects * patch_rows, patch_width)
        lengths = patch_len[part]
        grad_low = cotangent[part].reshape(count, width)
        onehot = (cam_index[part].reshape(count)[:, None] == jnp.arange(codes)[None, :]).astype(LOW)
        shift_scale = mul(onehot, table_flat)
        gain_one = 1.0 + shift_scale[:, :width]
        unit_one, rate_one = normed(inputs)
        normed_one = (unit_one * gain_one + shift_scale[:, width:]).astype(LOW)
        qkv_t = by_object(qkv_rows, normed_one)
        by_kind = qkv_t.reshape(objects, heads, 3, HEAD_DIM, rows).transpose(2, 1, 3, 0, 4)
        by_kind = by_kind.reshape(3, cols, count)
        self_pair = lax.all_gather(by_kind[1:], "rows", axis=0)
        patch_mid = mul(patch_in, patch_weights).astype(LOW)
        own_pair = mul(pair_rows, patch_mid, NT).astype(LOW).reshape(2, cols, -1)
        pair_t = lax.all_gather(own_pair, "rows", axis=0)
        self_mixed_t, self_wide, self_log = cross_forward(by_kind[0], self_pair, full_lengths)
        after_self = inputs + over_all_columns(self_mixed_t, self_whole)
        unit_two, rate_two = normed(after_self)
        normed_two = (unit_two * cross_gain_f).astype(LOW)
        cross_q_t = mul(query_rows, normed_two, NT).astype(LOW)
        cross_mixed_t, cross_wide, cross_log = cross_forward(cross_q_t, pair_t, lengths)
        after_cross = after_self + over_all_columns(cross_mixed_t, cross_whole)
        unit_three, rate_three = normed(after_cross)
        normed_three = (unit_three * hidden_gain_f).astype(LOW)
        pre_act = mul(normed_three, widen_weights)
        activated, act_back = jax.vjp(gelu_tanh, pre_act)
        activated = activated.astype(LOW)
        grad_pre = act_back(mul(grad_low, narrow_weights, NT))[0].astype(LOW)
        grad_three = sum_heads(mul(grad_pre, widen_weights, NT)).astype(WIDE)
        yield "heads", {"hidden": mul(activated, narrow_weights)}
        yield "rows", {
            "narrow": mul(activated, grad_low, TN),
            "widen": mul(normed_three, grad_pre, TN),
        }
        hidden_gain_term = jnp.sum(own_columns(grad_three * unit_three), axis=0)
        grad_cross = grad_low.astype(WIDE) + normed_back(
            grad_three * hidden_gain_f, unit_three, rate_three
        )
        grad_cross_low = grad_cross.astype(LOW)
        cross_output_term = mul(cross_mixed_t, grad_cross_low)
        grad_mixed_t = mul(cross_output, grad_cross_low, NT).astype(LOW)
        grad_cq_t, grad_pair_t = cross_backward(
            cross_q_t, pair_t, lengths, grad_mixed_t, cross_wide, cross_log
        )
        grad_two = over_all_columns(grad_cq_t, query_whole)
        grad_pair_t = lax.psum_scatter(grad_pair_t, "rows", scatter_dimension=0, tiled=False)
        grad_pair_t = grad_pair_t.reshape(2 * cols, -1)
        query_term = mul(normed_two, grad_cq_t, (((0,), (1,)), ((), ())))
        cross_gain_term = jnp.sum(own_columns(grad_two * unit_two), axis=0)
        grad_self = grad_cross + normed_back(grad_two * cross_gain_f, unit_two, rate_two)
        grad_self_low = grad_self.astype(LOW)
        self_output_term = mul(self_mixed_t, grad_self_low)
        yield "heads", {"patch": mul(grad_pair_t, pair_rows, TN)}
        yield "rows", {
            "query": query_term,
            "pair": column_terms(patch_mid, grad_pair_t),
            "cross_output": cross_output_term,
            "self_output": self_output_term,
        }
        grad_self_mixed_t = mul(self_output, grad_self_low, NT).astype(LOW)
        grad_q_t, grad_kv_t = cross_backward(
            by_kind[0], self_pair, full_lengths, grad_self_mixed_t, self_wide, self_log
        )
        grad_kv_t = lax.psum_scatter(grad_kv_t, "rows", scatter_dimension=0, tiled=False)
        grad_qkv_t = jnp.concatenate([grad_q_t[None], grad_kv_t]).reshape(3 * cols, count)
        grad_qkv_t = yield "after", (grad_qkv_t, ["patch", "narrow", "widen"])
        grad_mid = yield "take", "patch"
        patch_term = mul(patch_in, own_columns(grad_mid), TN)
        patch_grad = mul(grad_mid, patch_weights, NT)
        grad_one = sum_heads(mul(grad_qkv_t, qkv_rows_back, TN))
        grad_one = yield "after", (grad_one, ["query", "pair", "cross_output", "self_output"])
        grad_one = grad_one.astype(WIDE)
        input_grad = grad_self + normed_back(grad_one * gain_one, unit_one, rate_one)
        own_grad = own_columns(grad_one)
        table_term = jnp.stack(
            [
                lax.dot_general(onehot.astype(WIDE), v, TN, precision=lax.Precision.HIGHEST)
                for v in (own_grad * own_columns(unit_one), own_grad)
            ],
            axis=1,
        )
        small = [patch_term, table_term.reshape(2 * codes, cols)]
        small += [hidden_gain_term[None], cross_gain_term[None], jnp.zeros((14, cols), WIDE)]
        yield "rows", {
            "self": column_terms(normed_one, grad_qkv_t),
            "small": jnp.concatenate(small, axis=0),
        }
        hidden_sum = yield "take", "hidden"
        result = (after_cross + hidden_sum.astype(WIDE)).astype(LOW)
        yield (
            "done",
            (
                result.reshape(objects, rows, width),
                input_grad.reshape(objects, rows, width),
                patch_grad.reshape(objects, patch_rows, patch_width),
            ),
        )

    steps = [one_group(group) for group in range(groups)]
    asked = [next(step) for step in steps]
    totals, ahead = {}, []
    while asked[0][0] != "done":
        kind, what = asked[0]
        answers = [None] * groups
        if kind == "take":
            answers = jnp.split(totals[what], groups)
        elif kind == "after":
            early = {name: totals[name] for name in what[1]}
            answers = [value for _, (value, _) in asked]
            answers[-1], early = lax.optimization_barrier((answers[-1], early))
            totals.update(early)
        else:
            terms = [value for _, value in asked]
            if kind == "heads":
                terms = jax.tree.map(lambda *parts: jnp.concatenate(parts, axis=0), *terms)
            else:
                for value in terms[1:]:
                    terms[0] = add_trees(terms[0], value)
                terms = terms[0]
            if kind == "rows":
                terms = jax.tree.map(lambda value: value.astype(LOW), terms)
            if kind == "heads":
                totals.update({name: sum_heads(value) for name, value in terms.items()})
            else:
                before = {name: totals[name] for name in ahead}
                terms, before = lax.optimization_barrier((terms, before))
                totals.update(before)
                totals.update(lax.psum(terms, kind))
                ahead = list(terms)
        asked = [step.send(value) for step, value in zip(steps, answers)]
    outputs, input_grads, patch_grads = (
        jnp.concatenate([value[i] for _, value in asked], axis=0) for i in range(3)
    )
    patch_total, table_total, gains = jnp.split(
        totals["small"], [patch_width, patch_width + 2 * codes]
    )
    gradients = (
        table_total.reshape(codes, 2, cols),
        jnp.stack(totals["self"]),
        totals["self_output"],
        gains[1],
        totals["query"],
        jnp.stack(totals["pair"]),
        totals["cross_output"],
        patch_total,
        gains[0],
        totals["widen"],
        totals["narrow"],
    )
    return (outputs, input_grads, patch_grads) + tuple(value.astype(WIDE) for value in gradients)


def solution(mesh):
    sizes = mesh.shape
    paired = sizes["heads"] == 4 and sizes["rows"] == 8
    heads = ("far", "near") if paired else "heads"
    if paired:
        names = (*heads, "rows")
        mesh = jax.sharding.Mesh(mesh.devices.reshape(2, 2, sizes["rows"]), names)
    in_specs = (
        P(None, "rows", None),
        P(None, "rows"),
        P(None, "rows", None),
        P(),
        P(),
        P(None, None, heads),
        P(heads, None),
        P(),
        P(None, heads),
        P(None, None, heads),
        P(heads, None),
        P(),
        P(),
        P(None, heads),
        P(heads, None),
        P(None, "rows", None),
    )
    out_specs = (
        P(None, "rows", None),
        P(None, "rows", None),
        P(None, "rows", None),
        P(None, None, heads),
        P(None, None, heads),
        P(heads, None),
        P(heads),
        P(None, heads),
        P(None, None, heads),
        P(heads, None),
        P(None, heads),
        P(heads),
        P(None, heads),
        P(heads, None),
    )
    return jax.shard_map(
        paired_device if paired else per_device,
        mesh=mesh,
        in_specs=in_specs,
        out_specs=out_specs,
        check_vma=False,
    )
```

```python
import jax
import jax.numpy as jnp
from jax import lax
from jax.experimental import pallas as pl
from jax.experimental.pallas import tpu as pltpu
from jax.sharding import PartitionSpec as P

HEAD_DIM = 64
EPSILON = 1e-05
SCALE = HEAD_DIM ** (-0.5)
LOW = jnp.bfloat16
WIDE = jnp.float32

NN = (((1,), (0,)), ((), ()))
NT = (((1,), (1,)), ((), ()))
TN = (((0,), (0,)), ((), ()))
T_LAST = (((0,), (1,)), ((), ()))


def mul(left, right, dims=NN):
    return lax.dot_general(left, right, dims, preferred_element_type=WIDE)


def load_values(values, block, values_t):
    rows = values_t.shape[1]
    at = slice(block * rows, (block + 1) * rows)
    values[at, :HEAD_DIM] = values_t.T
    values[at, HEAD_DIM:] = jnp.ones((rows, HEAD_DIM), values.dtype)


def attend_block(queries, keys_t, values):
    scores = mul(queries, keys_t)
    peak = jnp.max(scores, axis=1, keepdims=True)
    both = mul(jnp.exp(scores - peak).astype(LOW), values).T
    total = both[HEAD_DIM : HEAD_DIM + 1]
    return both[:HEAD_DIM] / total, peak.T + jnp.log(total)


def attend_block_back(scaled_q, grad_t, keys, keys_t, values, log_total, spread):
    probs = jnp.exp(mul(keys, scaled_q) - log_total)
    grad_scores = (probs * (mul(values, grad_t) - spread)).astype(LOW)
    return (
        (mul(keys_t, grad_scores) * SCALE).astype(LOW),
        mul(grad_scores, scaled_q.T),
        mul(probs.astype(LOW), grad_t.T),
    )


def estimate(rows, cols, passes):
    return pl.CostEstimate(
        flops=int(rows * cols * 1200 * passes), transcendentals=int(rows * cols), bytes_accessed=int(rows * 2048)
    )


VMEM_LIMIT = 48 << 20


def by_length(length, full, blocks, run):
    @pl.when(length * 4 > full)
    def _():
        run(blocks)

    @pl.when(length * 4 <= full)
    def _():
        run(blocks // 4)


def cross_forward(queries_t, pair_t, lengths):
    blocks, _, cols, all_patches = pair_t.shape
    objects = lengths.shape[0]
    heads = cols // HEAD_DIM
    rows, patch_rows = queries_t.shape[1] // objects, all_patches // objects

    def kernel(len_ref, q_ref, pair_ref, mixed_ref, wide_ref, log_ref, keys_t, values):
        queries = (q_ref[...] * LOW(SCALE)).T

        def run(live):
            for c in range(live):
                keys_t[:, c * patch_rows : (c + 1) * patch_rows] = pair_ref[c, 0]
                load_values(values, c, pair_ref[c, 1])
            size = live * patch_rows
            mixed, log_total = attend_block(queries, keys_t[:, :size], values[:size])
            mixed_ref[...] = mixed.astype(LOW)
            wide_ref[...] = mixed
            log_ref[...] = log_total

        by_length(len_ref[pl.program_id(0)], blocks * patch_rows, blocks, run)

    block = pl.BlockSpec((HEAD_DIM, rows), lambda b, j, lens: (j, b))
    return pl.pallas_call(
        kernel,
        grid_spec=pltpu.PrefetchScalarGridSpec(
            num_scalar_prefetch=1,
            grid=(objects, heads),
            in_specs=[
                block,
                pl.BlockSpec((blocks, 2, HEAD_DIM, patch_rows), lambda b, j, lens: (0, 0, j, b)),
            ],
            out_specs=[block, block, pl.BlockSpec((None, 1, rows), lambda b, j, lens: (j, 0, b))],
            scratch_shapes=[
                pltpu.VMEM((HEAD_DIM, blocks * patch_rows), LOW),
                pltpu.VMEM((blocks * patch_rows, 2 * HEAD_DIM), LOW),
            ],
        ),
        out_shape=[
            jax.ShapeDtypeStruct(queries_t.shape, LOW),
            jax.ShapeDtypeStruct(queries_t.shape, WIDE),
            jax.ShapeDtypeStruct((heads, 1, queries_t.shape[1]), WIDE),
        ],
        name="cross_forward",
        cost_estimate=estimate(objects * rows, blocks * patch_rows * heads, 1.4),
        compiler_params=pltpu.CompilerParams(vmem_limit_bytes=VMEM_LIMIT),
    )(lengths, queries_t, pair_t)


def cross_backward(queries_t, pair_t, lengths, grad_t_all, wide, log_total):
    blocks, _, cols, all_patches = pair_t.shape
    objects = lengths.shape[0]
    heads = cols // HEAD_DIM
    rows, patch_rows = queries_t.shape[1] // objects, all_patches // objects

    def kernel(len_ref, q_ref, pair_ref, g_ref, wide_ref, log_ref, out_q, out_pair, keys, keys_t, values):
        grad_t = g_ref[...]
        spread = jnp.sum(grad_t.astype(WIDE) * wide_ref[...], axis=0, keepdims=True)

        def run(live):
            for c in range(live):
                at = slice(c * patch_rows, (c + 1) * patch_rows)
                keys[at] = pair_ref[c, 0].T
                keys_t[:, at] = pair_ref[c, 0]
                values[at] = pair_ref[c, 1].T
            size = live * patch_rows
            out_q[...], grad_k, grad_v = attend_block_back(
                q_ref[...] * LOW(SCALE),
                grad_t,
                keys[:size],
                keys_t[:, :size],
                values[:size],
                log_ref[...],
                spread,
            )
            for c in range(live):
                at = slice(c * patch_rows, (c + 1) * patch_rows)
                out_pair[c, 0] = grad_k[at].T.astype(LOW)
                out_pair[c, 1] = grad_v[at].T.astype(LOW)
            for c in range(live, blocks):
                out_pair[c] = jnp.zeros_like(out_pair[c])

        by_length(len_ref[pl.program_id(0)], blocks * patch_rows, blocks, run)

    block = pl.BlockSpec((HEAD_DIM, rows), lambda b, j, lens: (j, b))
    pair_block = pl.BlockSpec((blocks, 2, HEAD_DIM, patch_rows), lambda b, j, lens: (0, 0, j, b))
    return pl.pallas_call(
        kernel,
        grid_spec=pltpu.PrefetchScalarGridSpec(
            num_scalar_prefetch=1,
            grid=(objects, heads),
            in_specs=[
                block,
                pair_block,
                block,
                block,
                pl.BlockSpec((None, 1, rows), lambda b, j, lens: (j, 0, b)),
            ],
            out_specs=[block, pair_block],
            scratch_shapes=[
                pltpu.VMEM((blocks * patch_rows, HEAD_DIM), LOW),
                pltpu.VMEM((HEAD_DIM, blocks * patch_rows), LOW),
                pltpu.VMEM((blocks * patch_rows, HEAD_DIM), LOW),
            ],
        ),
        out_shape=[
            jax.ShapeDtypeStruct(queries_t.shape, LOW),
            jax.ShapeDtypeStruct(pair_t.shape, LOW),
        ],
        name="cross_backward",
        cost_estimate=estimate(objects * rows, blocks * patch_rows * heads, 2.5),
        compiler_params=pltpu.CompilerParams(vmem_limit_bytes=VMEM_LIMIT),
    )(lengths, queries_t, pair_t, grad_t_all, wide, log_total)


def shift(value, step):
    size = lax.axis_size("heads")
    return lax.ppermute(value, "heads", [((i + step) % size, i) for i in range(size)])


def gather_heads(value):
    size = lax.axis_size("heads")
    if size != 4:
        return [value] + [shift(value, step) for step in range(1, size)]
    after, before = shift(value, 1), shift(value, -1)
    inner = lax.ppermute(after, "heads", [(1, 0), (2, 1)]) + lax.ppermute(before, "heads", [(1, 2), (2, 3)])
    return [value, after, inner, before]


def scatter_heads(partial):
    size, me = lax.axis_size("heads"), lax.axis_index("heads")

    def part(step):
        return lax.dynamic_index_in_dim(partial, (me + step) % size, 0, keepdims=False)

    if size != 4:
        total = part(0)
        for step in range(1, size):
            total = total + shift(part(step).astype(LOW), -step).astype(WIDE)
        return total
    far = part(2).astype(LOW)
    up = lax.ppermute(far, "heads", [(0, 1), (1, 2)]).astype(WIDE)
    down = lax.ppermute(far, "heads", [(2, 1), (3, 2)]).astype(WIDE)
    from_below = shift((part(1) + up).astype(LOW), -1)
    from_above = shift((part(3) + down).astype(LOW), 1)
    return part(0) + from_below.astype(WIDE) + from_above.astype(WIDE)


def in_order(parts):
    size, me = lax.axis_size("heads"), lax.axis_index("heads")
    out = jnp.zeros((size,) + parts[0].shape, parts[0].dtype)
    for step, value in enumerate(parts):
        out = lax.dynamic_update_index_in_dim(out, value, (me + step) % size, 0)
    return out.reshape((-1,) + parts[0].shape[1:])


def sum_heads(partial):
    size = lax.axis_size("heads")
    split = partial.reshape((size, -1) + partial.shape[1:])
    return in_order(gather_heads(scatter_heads(split).astype(LOW)))


def exchange_rows(value):
    return lax.all_to_all(value, "rows", 0, 0, tiled=True)


def normed(value):
    centred = value - jnp.mean(value, axis=-1, keepdims=True)
    rate = lax.rsqrt(jnp.mean(centred * centred, axis=-1, keepdims=True) + EPSILON)
    return centred * rate, rate


def normed_back(grad, unit, rate):
    return rate * (
        grad
        - jnp.mean(grad, axis=-1, keepdims=True)
        - unit * jnp.mean(grad * unit, axis=-1, keepdims=True)
    )


def gelu_tanh(pre_act):
    return jax.nn.gelu(pre_act, approximate=True)


def add_trees(former, latter):
    return jax.tree.map(jnp.add, former, latter)


def pair_forward(queries, pair, key_at, length=None):
    blocks, objects, _, width, rows = queries.shape
    pair_rows = pair.shape[4]
    lengths = jnp.full((objects,), blocks * pair_rows, jnp.int32) if length is None else length

    def kernel(len_ref, q_ref, k_ref, v_ref, mixed_ref, wide_ref, log_ref, keys_t, values):
        def run(live):
            @pl.when(pl.program_id(1) == 0)
            def _():
                for c in range(live):
                    keys_t[:, c * pair_rows : (c + 1) * pair_rows] = k_ref[c]
                    load_values(values, c, v_ref[c])

            size = live * pair_rows
            mixed, log_total = attend_block(
                (q_ref[...] * LOW(SCALE)).T, keys_t[:, :size], values[:size]
            )
            mixed_ref[...] = mixed.astype(LOW)
            wide_ref[...] = mixed
            log_ref[...] = log_total

        if length is None:
            run(blocks)
        else:
            by_length(len_ref[pl.program_id(0)], blocks * pair_rows, blocks, run)

    block = pl.BlockSpec((None, None, width, rows), lambda o, i, lens: (i, o, 0, 0))
    return pl.pallas_call(
        kernel,
        grid_spec=pltpu.PrefetchScalarGridSpec(
            num_scalar_prefetch=1,
            grid=(objects, blocks),
            in_specs=[
                pl.BlockSpec((None, None, None, width, rows), lambda o, i, lens: (i, o, 0, 0, 0)),
                pl.BlockSpec((blocks, None, None, width, pair_rows), lambda o, i, lens: (0, o, key_at, 0, 0)),
                pl.BlockSpec((blocks, None, None, width, pair_rows), lambda o, i, lens: (0, o, key_at + 1, 0, 0)),
            ],
            out_specs=[block, block, pl.BlockSpec((None, None, 1, rows), lambda o, i, lens: (i, o, 0, 0))],
            scratch_shapes=[
                pltpu.VMEM((width, blocks * pair_rows), LOW),
                pltpu.VMEM((blocks * pair_rows, 2 * width), LOW),
            ],
        ),
        out_shape=[
            jax.ShapeDtypeStruct((blocks, objects, width, rows), LOW),
            jax.ShapeDtypeStruct((blocks, objects, width, rows), WIDE),
            jax.ShapeDtypeStruct((blocks, objects, 1, rows), WIDE),
        ],
        name="pair_forward",
        cost_estimate=estimate(objects * blocks * rows, blocks * pair_rows, 2 if length is None else 1.4),
        compiler_params=pltpu.CompilerParams(vmem_limit_bytes=VMEM_LIMIT),
    )(lengths, queries, pair, pair)


def pair_backward(queries, pair, key_at, length, grad_mixed, wide, log_total):
    blocks, objects, _, width, rows = queries.shape
    lengths = jnp.full((objects,), blocks * rows, jnp.int32) if length is None else length

    def kernel(len_ref, q_ref, k_ref, v_ref, g_ref, wide_ref, log_ref, out_ref, keys, keys_t, values, grad_k, grad_v):
        i = pl.program_id(1)

        def run(live):
            size = live * rows

            @pl.when(i == 0)
            def _():
                for c in range(live):
                    at = slice(c * rows, (c + 1) * rows)
                    keys[at] = k_ref[c].T
                    keys_t[:, at] = k_ref[c]
                    values[at] = v_ref[c].T

            grad_t = g_ref[...]
            spread = jnp.sum(grad_t.astype(WIDE) * wide_ref[...], axis=0, keepdims=True)
            out_ref[i, 0], term_k, term_v = attend_block_back(
                q_ref[...] * LOW(SCALE),
                grad_t,
                keys[:size],
                keys_t[:, :size],
                values[:size],
                log_ref[...],
                spread,
            )

            @pl.when(i == 0)
            def _():
                grad_k[:size] = term_k
                grad_v[:size] = term_v

            @pl.when(i > 0)
            def _():
                grad_k[:size] += term_k
                grad_v[:size] += term_v

            @pl.when(i == blocks - 1)
            def _():
                for c in range(live):
                    at = slice(c * rows, (c + 1) * rows)
                    out_ref[c, 1] = grad_k[at].T.astype(LOW)
                    out_ref[c, 2] = grad_v[at].T.astype(LOW)
                for c in range(live, blocks):
                    out_ref[c, 1:] = jnp.zeros_like(out_ref[c, 1:])

        if length is None:
            run(blocks)
        else:
            by_length(len_ref[pl.program_id(0)], blocks * rows, blocks, run)

    block = pl.BlockSpec((None, None, width, rows), lambda o, i, lens: (i, o, 0, 0))
    return pl.pallas_call(
        kernel,
        grid_spec=pltpu.PrefetchScalarGridSpec(
            num_scalar_prefetch=1,
            grid=(objects, blocks),
            in_specs=[
                pl.BlockSpec((None, None, None, width, rows), lambda o, i, lens: (i, o, 0, 0, 0)),
                pl.BlockSpec((blocks, None, None, width, rows), lambda o, i, lens: (0, o, key_at, 0, 0)),
                pl.BlockSpec((blocks, None, None, width, rows), lambda o, i, lens: (0, o, key_at + 1, 0, 0)),
                block,
                block,
                pl.BlockSpec((None, None, 1, rows), lambda o, i, lens: (i, o, 0, 0)),
            ],
            out_specs=pl.BlockSpec((blocks, None, 3, width, rows), lambda o, i, lens: (0, o, 0, 0, 0)),
            scratch_shapes=[
                pltpu.VMEM((blocks * rows, width), LOW),
                pltpu.VMEM((width, blocks * rows), LOW),
                pltpu.VMEM((blocks * rows, width), LOW),
                pltpu.VMEM((blocks * rows, width), WIDE),
                pltpu.VMEM((blocks * rows, width), WIDE),
            ],
        ),
        out_shape=jax.ShapeDtypeStruct((blocks, objects, 3, width, rows), LOW),
        name="pair_backward",
        cost_estimate=estimate(objects * blocks * rows, blocks * rows, 3 if length is None else 2),
        compiler_params=pltpu.CompilerParams(vmem_limit_bytes=VMEM_LIMIT),
    )(lengths, queries, pair, pair, grad_mixed, wide, log_total)


def swap(value, axis):
    return lax.ppermute(value, axis, [(0, 1), (1, 0)])


def sum_near(partial):
    low = partial.astype(LOW)
    return low.astype(WIDE) + swap(low, "near").astype(WIDE)


def tie(value, *others):
    return lax.optimization_barrier((value, *others))


def paired_device(
    tokens,
    cam_index,
    patches,
    patch_len,
    camera_table,
    self_weights,
    self_output,
    cross_gain,
    cross_query,
    cross_pair,
    cross_output,
    patch_weights,
    hidden_gain,
    widen_weights,
    narrow_weights,
    cotangent,
):
    objects = tokens.shape[0] // 2
    _, rows, width = tokens.shape
    cols = self_weights.shape[2]
    hidden = widen_weights.shape[1]
    heads = cols // HEAD_DIM
    codes = camera_table.shape[0]
    patch_width = patches.shape[2]
    count = objects * rows
    n_rows = lax.axis_size("rows")
    row_rank = lax.axis_index("rows")
    far, near = lax.axis_index("far"), lax.axis_index("near")

    def objects_of(value):
        return lax.dynamic_slice_in_dim(value, objects * far, objects, 0)

    def piece(value):
        size = value.shape[0] // n_rows
        return lax.dynamic_slice_in_dim(value, row_rank * size, size, 0)

    def join_rows(value):
        return lax.all_gather(value, "rows", axis=0, tiled=True)

    def both_columns(value):
        return [
            lax.dynamic_slice_in_dim(value, (2 * index + near) * cols, cols, value.ndim - 1)
            for index in range(2)
        ]

    def in_order(mine, away, axis=0):
        size = mine.shape[axis]
        shape = list(mine.shape)
        shape[axis] *= 2
        out = lax.dynamic_update_slice_in_dim(jnp.zeros(shape, mine.dtype), mine, far * size, axis)
        return lax.dynamic_update_slice_in_dim(out, away, (1 - far) * size, axis)

    def halves(value):
        value = value.reshape(objects, 2, rows // 2, -1)
        return [
            lax.dynamic_index_in_dim(value, index, 1, keepdims=False).reshape(count // 2, -1)
            for index in (near, 1 - near)
        ]

    def half_sum_near(partial):
        mine, away = halves(partial)
        return mine + swap(away.astype(LOW), "near").astype(WIDE)

    def swap_over_heads(value):
        value = value.reshape(objects, rows // 2, -1)
        value = jnp.stack([value, swap(value, "far")])
        value = jnp.stack([value, swap(value, "near")])
        value = jnp.where(far == 0, value, jnp.flip(value, 1))
        value = jnp.where(near == 0, value, jnp.flip(value, 0))
        return value.transpose(1, 2, 0, 3, 4).reshape(2 * objects, rows, -1)

    def over_heads(value):
        value = lax.all_gather(value.reshape(objects, rows // 2, -1), ("far", "near"), axis=0)
        value = value.reshape(2, 2, objects, rows // 2, -1).transpose(0, 2, 1, 3, 4)
        return value.reshape(2 * objects, rows, -1)

    def to_pairs(weights, value, slots):
        parts = [
            mul(weights, value[i * rows : (i + 1) * rows], NT)
            .astype(LOW)
            .reshape(n_rows, slots, HEAD_DIM, rows)
            for i in range(objects)
        ]
        return exchange_rows(jnp.stack(parts, axis=1))

    def from_pairs(value):
        return value.transpose(0, 2, 3, 1, 4).reshape(-1, count)

    def over_all_columns(value_t, weight):
        return mul(jnp.concatenate([value_t, swap(value_t, "near")]), weight, TN)

    qkv_rows = self_weights.reshape(3, width, heads, HEAD_DIM).transpose(2, 0, 3, 1)
    qkv_rows = qkv_rows.reshape(3 * cols, width)
    pair_rows = cross_pair.reshape(2, width, heads, HEAD_DIM).transpose(2, 0, 3, 1)
    pair_rows = pair_rows.reshape(2 * cols, width)
    query_rows = cross_query.T

    qkv_away = join_rows(swap(piece(qkv_rows), "far"))

    table_flat = camera_table.reshape(codes, -1)
    cross_gain_f = cross_gain.astype(WIDE)
    hidden_gain_f = hidden_gain.astype(WIDE)

    inputs = objects_of(tokens).reshape(count, width).astype(WIDE)
    patch_in = objects_of(patches).reshape(count, patch_width)
    length = objects_of(patch_len)
    grad_low = objects_of(cotangent).reshape(count, width)
    codes_of = objects_of(cam_index).reshape(count)
    onehot = (codes_of[:, None] == jnp.arange(codes)[None, :]).astype(LOW)
    shift_scale = mul(onehot, table_flat)
    gain_one = 1.0 + shift_scale[:, :width]
    unit_one, rate_one = normed(inputs)
    normed_one = (unit_one * gain_one + shift_scale[:, width:]).astype(LOW)

    mine = [piece(v) for v in (self_output, query_rows, cross_output, pair_rows)]
    normed_one, *mine = tie(normed_one, *mine)
    mine = jnp.concatenate(mine, axis=0)
    across = swap(mine, "far")
    size = cols // n_rows
    two = in_order(mine[None, : 3 * size], across[None, : 3 * size])
    four = jnp.concatenate([two, swap(two, "near")])
    sent = jnp.concatenate([four.reshape(-1, width), across[3 * size :]])
    sent = lax.all_gather(sent, "rows", axis=0)
    pair_away = sent[:, 12 * size :].reshape(2 * cols, width)
    whole = sent[:, : 12 * size].reshape(n_rows, 4, 3, size, width).transpose(2, 1, 0, 3, 4)
    self_whole, query_whole, cross_whole = whole.reshape(3, 4 * cols, width)

    qkv_both = in_order(qkv_rows, qkv_away)
    qkv = to_pairs(qkv_both, normed_one, 3)
    patch_mid = mul(patch_in, patch_weights).astype(LOW)
    pair_both = in_order(pair_rows, pair_away)
    pair = to_pairs(pair_both, patch_mid, 2)

    mine = [piece(widen_weights), piece(narrow_weights)]
    qkv, *mine = tie(qkv, *mine)
    across = swap(jnp.concatenate(mine, axis=0), "far")
    sent = lax.all_gather(across, "rows", axis=0)
    size = width // n_rows
    widen = in_order(widen_weights, sent[:, :size].reshape(width, hidden), axis=1)
    narrow = in_order(narrow_weights, sent[:, size:].reshape(hidden, width))

    mixed, self_wide, self_log = pair_forward(qkv, qkv, 1)
    self_mixed_t = from_pairs(exchange_rows(mixed)[:, :, None])
    after_self = inputs + over_all_columns(self_mixed_t, self_whole)
    unit_two, rate_two = normed(after_self)
    normed_two = (unit_two * cross_gain_f).astype(LOW)
    cross_q = to_pairs(query_whole[: 2 * cols], normed_two, 1)
    mixed, cross_wide, cross_log = pair_forward(cross_q, pair, 0, length)
    cross_mixed_t = from_pairs(exchange_rows(mixed)[:, :, None])
    after_cross = after_self + over_all_columns(cross_mixed_t, cross_whole)
    unit_three, rate_three = normed(after_cross)
    normed_three = (unit_three * hidden_gain_f).astype(LOW)
    activated, act_back = jax.vjp(gelu_tanh, mul(normed_three, widen))
    activated = activated.astype(LOW)
    grad_pre = act_back(mul(grad_low, narrow, NT))[0].astype(LOW)
    grad_three = sum_near(mul(grad_pre, widen, NT))
    hidden_half = half_sum_near(mul(activated, narrow))
    result = (halves(after_cross)[0] + hidden_half).astype(LOW)

    def part_rows(both):
        both = both.reshape(-1, both.shape[-1])
        return lax.psum_scatter(both, ("far", "rows"), scatter_dimension=0, tiled=True)

    def by_shard(left, right):
        return mul(left, right, NN).astype(LOW).reshape(2, -1, right.shape[1])

    hidden_part = part_rows(
        jnp.concatenate(
            [
                mul(value, against, TN).astype(LOW).reshape(2, hidden, width)
                for value, against in ((activated, grad_low), (grad_pre, normed_three))
            ],
            axis=1,
        )
    )

    hidden_gain_term = jnp.sum(grad_three * unit_three, axis=0)
    grad_cross = grad_low.astype(WIDE) + normed_back(
        grad_three * hidden_gain_f, unit_three, rate_three
    )
    grad_cross_low = grad_cross.astype(LOW)
    grad_mixed = to_pairs(cross_whole[: 2 * cols], grad_cross_low, 1)[:, :, 0]
    grads = pair_backward(cross_q, pair, 0, length, grad_mixed, cross_wide, cross_log)
    grads = exchange_rows(grads)
    hidden_total = join_rows(hidden_part)
    outputs = over_heads(result)
    grad_cq_t = from_pairs(grads[:, :, :1])
    grad_pair_t = from_pairs(grads[:, :, 1:])
    grad_two = over_all_columns(grad_cq_t, query_whole)
    cross_gain_term = jnp.sum(grad_two * unit_two, axis=0)
    grad_self = grad_cross + normed_back(grad_two * cross_gain_f, unit_two, rate_two)
    grad_self_low = grad_self.astype(LOW)
    grad_mid = sum_near(
        mul(grad_pair_t, pair_both, TN)
    ).astype(LOW)
    patch_half = mul(halves(grad_mid)[0], patch_weights, NT).astype(LOW)
    patch_terms = jnp.stack([mul(value, patch_in, TN).astype(LOW) for value in both_columns(grad_mid)])
    patch_terms = jnp.pad(patch_terms, ((0, 0), (0, 0), (0, width - patch_width)))
    middle_part = part_rows(
        jnp.concatenate(
            [
                by_shard(cross_mixed_t, grad_cross_low),
                by_shard(self_mixed_t, grad_self_low),
                by_shard(grad_cq_t, normed_two),
                by_shard(grad_pair_t, patch_mid),
                patch_terms,
            ],
            axis=1,
        )
    )
    grad_mixed = to_pairs(self_whole[: 2 * cols], grad_self_low, 1)[:, :, 0]
    grad_mixed, hidden_total, outputs = tie(grad_mixed, hidden_total, outputs)
    grads = exchange_rows(pair_backward(qkv, qkv, 1, None, grad_mixed, self_wide, self_log))
    patch_grads = over_heads(patch_half)
    grads, middle_part, patch_grads = tie(grads, middle_part, patch_grads)
    middle_total = join_rows(middle_part)
    grad_qkv_t = from_pairs(grads)
    last_part = part_rows(by_shard(grad_qkv_t, normed_one))
    grad_one = half_sum_near(mul(grad_qkv_t, qkv_both, TN))
    gain_half, unit_half, rate_half, self_half = (
        halves(value)[0] for value in (gain_one, unit_one, rate_one, grad_self)
    )
    input_half = self_half + normed_back(grad_one * gain_half, unit_half, rate_half)
    input_half = input_half.astype(LOW)
    onehot_half = halves(onehot)[0].astype(WIDE)
    table_term = jnp.concatenate(
        [
            lax.dot_general(onehot_half, value, TN, precision=lax.Precision.HIGHEST)
            for value in (grad_one * unit_half, grad_one)
        ],
        axis=0,
    )
    small = [sum_near(table_term), hidden_gain_term[None], cross_gain_term[None], jnp.zeros((14, width), WIDE)]
    small = jnp.stack(both_columns(jnp.concatenate(small, axis=0).astype(LOW)))
    small = jnp.sum(lax.all_gather(small, "rows", axis=0).astype(WIDE), axis=0).astype(LOW)
    small_own, small_away = (
        lax.dynamic_index_in_dim(small, index, 0, keepdims=False) for index in (far, 1 - far)
    )
    small = small_own.astype(WIDE) + swap(small_away, "far").astype(WIDE)
    input_half, middle_total = tie(input_half, middle_total)
    input_grads = swap_over_heads(input_half)
    last_total = join_rows(last_part)

    output_total = middle_total[: 2 * cols]
    query_total = middle_total[2 * cols : 3 * cols]
    pair_total = middle_total[3 * cols : 5 * cols].reshape(heads, 2, HEAD_DIM, width)
    patch_total = middle_total[5 * cols :, :patch_width]
    self_total = last_total.reshape(heads, 3, HEAD_DIM, width)
    gradients = (
        small[: 2 * codes].reshape(2, codes, cols).transpose(1, 0, 2),
        self_total.transpose(1, 3, 0, 2).reshape(3, width, cols),
        output_total[cols:],
        small[2 * codes + 1],
        query_total.T,
        pair_total.transpose(1, 3, 0, 2).reshape(2, width, cols),
        output_total[:cols],
        patch_total.T,
        small[2 * codes],
        hidden_total[hidden:].T,
        hidden_total[:hidden],
    )
    return (outputs, input_grads.astype(WIDE), patch_grads.astype(WIDE)) + tuple(
        value.astype(WIDE) for value in gradients
    )


def per_device(
    tokens,
    cam_index,
    patches,
    patch_len,
    camera_table,
    self_weights,
    self_output,
    cross_gain,
    cross_query,
    cross_pair,
    cross_output,
    patch_weights,
    hidden_gain,
    widen_weights,
    narrow_weights,
    cotangent,
):
    batches, rows, width = tokens.shape
    cols = self_weights.shape[2]
    heads = cols // HEAD_DIM
    codes = camera_table.shape[0]
    patch_rows, patch_width = patches.shape[1:]
    n_rows, n_heads = lax.axis_size("rows"), lax.axis_size("heads")
    row_rank, head_rank = lax.axis_index("rows"), lax.axis_index("heads")
    groups = 1
    objects = batches // groups
    full_lengths = jnp.full((objects,), n_rows * rows, jnp.int32)
    count = objects * rows

    def own_columns(value):
        return lax.dynamic_slice_in_dim(value, head_rank * cols, cols, value.ndim - 1)

    table_flat = camera_table.reshape(codes, -1)
    cross_gain_f = cross_gain.astype(WIDE)
    hidden_gain_f = hidden_gain.astype(WIDE)

    qkv_rows = (
        self_weights.reshape(3, width, heads, HEAD_DIM).transpose(2, 0, 3, 1).reshape(3 * cols, width)
    )
    qkv_rows_back = self_weights.transpose(0, 2, 1).reshape(3 * cols, width)
    pair_rows = cross_pair.transpose(0, 2, 1).reshape(2 * cols, width)
    query_rows = cross_query.T

    local = jnp.stack([self_output, cross_output, query_rows])
    piece = cols // n_rows
    local = lax.dynamic_slice_in_dim(local, row_rank * piece, piece, 1)
    whole = lax.all_gather(jnp.stack(gather_heads(local)), "rows", axis=0)
    whole = whole.transpose(2, 1, 0, 3, 4).reshape(3, n_heads * cols, width)
    self_whole, cross_whole, query_whole = whole[0], whole[1], whole[2]

    def over_all_columns(value_t, weight):
        return mul(jnp.concatenate(gather_heads(value_t), axis=0), weight, TN)

    def by_object(weight, value):
        return jnp.stack(
            [mul(weight, value[i * rows : (i + 1) * rows], NT).astype(LOW) for i in range(objects)]
        )

    def column_terms(value, grads_t):
        return [
            mul(value, grads_t[i : i + cols], (((0,), (1,)), ((), ())))
            for i in range(0, grads_t.shape[0], cols)
        ]

    def one_group(group):
        part = slice(group * objects, (group + 1) * objects)
        inputs = tokens[part].reshape(count, width).astype(WIDE)
        patch_in = patches[part].reshape(objects * patch_rows, patch_width)
        lengths = patch_len[part]
        grad_low = cotangent[part].reshape(count, width)
        onehot = (cam_index[part].reshape(count)[:, None] == jnp.arange(codes)[None, :]).astype(LOW)
        shift_scale = mul(onehot, table_flat)
        gain_one = 1.0 + shift_scale[:, :width]
        unit_one, rate_one = normed(inputs)
        normed_one = (unit_one * gain_one + shift_scale[:, width:]).astype(LOW)
        qkv_t = by_object(qkv_rows, normed_one)
        by_kind = qkv_t.reshape(objects, heads, 3, HEAD_DIM, rows).transpose(2, 1, 3, 0, 4)
        by_kind = by_kind.reshape(3, cols, count)
        self_pair = lax.all_gather(by_kind[1:], "rows", axis=0)
        patch_mid = mul(patch_in, patch_weights).astype(LOW)
        own_pair = mul(pair_rows, patch_mid, NT).astype(LOW).reshape(2, cols, -1)
        pair_t = lax.all_gather(own_pair, "rows", axis=0)
        self_mixed_t, self_wide, self_log = cross_forward(by_kind[0], self_pair, full_lengths)
        after_self = inputs + over_all_columns(self_mixed_t, self_whole)
        unit_two, rate_two = normed(after_self)
        normed_two = (unit_two * cross_gain_f).astype(LOW)
        cross_q_t = mul(query_rows, normed_two, NT).astype(LOW)
        cross_mixed_t, cross_wide, cross_log = cross_forward(cross_q_t, pair_t, lengths)
        after_cross = after_self + over_all_columns(cross_mixed_t, cross_whole)
        unit_three, rate_three = normed(after_cross)
        normed_three = (unit_three * hidden_gain_f).astype(LOW)
        pre_act = mul(normed_three, widen_weights)
        activated, act_back = jax.vjp(gelu_tanh, pre_act)
        activated = activated.astype(LOW)
        grad_pre = act_back(mul(grad_low, narrow_weights, NT))[0].astype(LOW)
        grad_three = sum_heads(mul(grad_pre, widen_weights, NT)).astype(WIDE)
        yield "heads", {"hidden": mul(activated, narrow_weights)}
        yield "rows", {
            "narrow": mul(activated, grad_low, TN),
            "widen": mul(normed_three, grad_pre, TN),
        }
        hidden_gain_term = jnp.sum(own_columns(grad_three * unit_three), axis=0)
        grad_cross = grad_low.astype(WIDE) + normed_back(
            grad_three * hidden_gain_f, unit_three, rate_three
        )
        grad_cross_low = grad_cross.astype(LOW)
        cross_output_term = mul(cross_mixed_t, grad_cross_low)
        grad_mixed_t = mul(cross_output, grad_cross_low, NT).astype(LOW)
        grad_cq_t, grad_pair_t = cross_backward(
            cross_q_t, pair_t, lengths, grad_mixed_t, cross_wide, cross_log
        )
        grad_two = over_all_columns(grad_cq_t, query_whole)
        grad_pair_t = lax.psum_scatter(grad_pair_t, "rows", scatter_dimension=0, tiled=False)
        grad_pair_t = grad_pair_t.reshape(2 * cols, -1)
        query_term = mul(normed_two, grad_cq_t, (((0,), (1,)), ((), ())))
        cross_gain_term = jnp.sum(own_columns(grad_two * unit_two), axis=0)
        grad_self = grad_cross + normed_back(grad_two * cross_gain_f, unit_two, rate_two)
        grad_self_low = grad_self.astype(LOW)
        self_output_term = mul(self_mixed_t, grad_self_low)
        yield "heads", {"patch": mul(grad_pair_t, pair_rows, TN)}
        yield "rows", {
            "query": query_term,
            "pair": column_terms(patch_mid, grad_pair_t),
            "cross_output": cross_output_term,
            "self_output": self_output_term,
        }
        grad_self_mixed_t = mul(self_output, grad_self_low, NT).astype(LOW)
        grad_q_t, grad_kv_t = cross_backward(
            by_kind[0], self_pair, full_lengths, grad_self_mixed_t, self_wide, self_log
        )
        grad_kv_t = lax.psum_scatter(grad_kv_t, "rows", scatter_dimension=0, tiled=False)
        grad_qkv_t = jnp.concatenate([grad_q_t[None], grad_kv_t]).reshape(3 * cols, count)
        grad_qkv_t = yield "after", (grad_qkv_t, ["patch", "narrow", "widen"])
        grad_mid = yield "take", "patch"
        patch_term = mul(patch_in, own_columns(grad_mid), TN)
        patch_grad = mul(grad_mid, patch_weights, NT)
        grad_one = sum_heads(mul(grad_qkv_t, qkv_rows_back, TN))
        grad_one = yield "after", (grad_one, ["query", "pair", "cross_output", "self_output"])
        grad_one = grad_one.astype(WIDE)
        input_grad = grad_self + normed_back(grad_one * gain_one, unit_one, rate_one)
        own_grad = own_columns(grad_one)
        table_term = jnp.stack(
            [
                lax.dot_general(onehot.astype(WIDE), v, TN, precision=lax.Precision.HIGHEST)
                for v in (own_grad * own_columns(unit_one), own_grad)
            ],
            axis=1,
        )
        small = [patch_term, table_term.reshape(2 * codes, cols)]
        small += [hidden_gain_term[None], cross_gain_term[None], jnp.zeros((14, cols), WIDE)]
        yield "rows", {
            "self": column_terms(normed_one, grad_qkv_t),
            "small": jnp.concatenate(small, axis=0),
        }
        hidden_sum = yield "take", "hidden"
        result = (after_cross + hidden_sum.astype(WIDE)).astype(LOW)
        yield (
            "done",
            (
                result.reshape(objects, rows, width),
                input_grad.reshape(objects, rows, width),
                patch_grad.reshape(objects, patch_rows, patch_width),
            ),
        )

    steps = [one_group(group) for group in range(groups)]
    asked = [next(step) for step in steps]
    totals, ahead = {}, []
    while asked[0][0] != "done":
        kind, what = asked[0]
        answers = [None] * groups
        if kind == "take":
            answers = jnp.split(totals[what], groups)
        elif kind == "after":
            early = {name: totals[name] for name in what[1]}
            answers = [value for _, (value, _) in asked]
            answers[-1], early = lax.optimization_barrier((answers[-1], early))
            totals.update(early)
        else:
            terms = [value for _, value in asked]
            if kind == "heads":
                terms = jax.tree.map(lambda *parts: jnp.concatenate(parts, axis=0), *terms)
            else:
                for value in terms[1:]:
                    terms[0] = add_trees(terms[0], value)
                terms = terms[0]
            if kind == "rows":
                terms = jax.tree.map(lambda value: value.astype(LOW), terms)
            if kind == "heads":
                totals.update({name: sum_heads(value) for name, value in terms.items()})
            else:
                before = {name: totals[name] for name in ahead}
                terms, before = lax.optimization_barrier((terms, before))
                totals.update(before)
                totals.update(lax.psum(terms, kind))
                ahead = list(terms)
        asked = [step.send(value) for step, value in zip(steps, answers)]
    outputs, input_grads, patch_grads = (
        jnp.concatenate([value[i] for _, value in asked], axis=0) for i in range(3)
    )
    patch_total, table_total, gains = jnp.split(
        totals["small"], [patch_width, patch_width + 2 * codes]
    )
    gradients = (
        table_total.reshape(codes, 2, cols),
        jnp.stack(totals["self"]),
        totals["self_output"],
        gains[1],
        totals["query"],
        jnp.stack(totals["pair"]),
        totals["cross_output"],
        patch_total,
        gains[0],
        totals["widen"],
        totals["narrow"],
    )
    return (outputs, input_grads, patch_grads) + tuple(value.astype(WIDE) for value in gradients)


def solution(mesh):
    sizes = mesh.shape
    paired = sizes["heads"] == 4 and sizes["rows"] == 8
    heads = ("far", "near") if paired else "heads"
    if paired:
        names = (*heads, "rows")
        mesh = jax.sharding.Mesh(mesh.devices.reshape(2, 2, sizes["rows"]), names)
    in_specs = (
        P(None, "rows", None),
        P(None, "rows"),
        P(None, "rows", None),
        P(),
        P(),
        P(None, None, heads),
        P(heads, None),
        P(),
        P(None, heads),
        P(None, None, heads),
        P(heads, None),
        P(),
        P(),
        P(None, heads),
        P(heads, None),
        P(None, "rows", None),
    )
    out_specs = (
        P(None, "rows", None),
        P(None, "rows", None),
        P(None, "rows", None),
        P(None, None, heads),
        P(None, None, heads),
        P(heads, None),
        P(heads),
        P(None, heads),
        P(None, None, heads),
        P(heads, None),
        P(None, heads),
        P(heads),
        P(None, heads),
        P(heads, None),
    )
    return jax.shard_map(
        paired_device if paired else per_device,
        mesh=mesh,
        in_specs=in_specs,
        out_specs=out_specs,
        check_vma=False,
    )
```

```python
import jax
import jax.numpy as jnp
from jax import lax
from jax.experimental import pallas as pl
from jax.experimental.pallas import tpu as pltpu
from jax.sharding import PartitionSpec as P

HEAD_DIM = 64
EPSILON = 1e-05
SCALE = HEAD_DIM ** (-0.5)
LOW = jnp.bfloat16
WIDE = jnp.float32

NN = (((1,), (0,)), ((), ()))
NT = (((1,), (1,)), ((), ()))
TN = (((0,), (0,)), ((), ()))
T_LAST = (((0,), (1,)), ((), ()))


def mul(left, right, dims=NN):
    return lax.dot_general(left, right, dims, preferred_element_type=WIDE)


def load_values(values, block, values_t):
    rows = values_t.shape[1]
    at = slice(block * rows, (block + 1) * rows)
    values[at, :HEAD_DIM] = values_t.T
    values[at, HEAD_DIM:] = jnp.ones((rows, HEAD_DIM), values.dtype)


def attend_block(queries, keys_t, values):
    scores = mul(queries, keys_t)
    peak = jnp.max(scores, axis=1, keepdims=True)
    both = mul(jnp.exp(scores - peak).astype(LOW), values).T
    total = both[HEAD_DIM : HEAD_DIM + 1]
    return both[:HEAD_DIM] / total, peak.T + jnp.log(total)


def attend_block_back(scaled_q, grad_t, keys, keys_t, values, log_total, spread):
    probs = jnp.exp(mul(keys, scaled_q) - log_total)
    grad_scores = (probs * (mul(values, grad_t) - spread)).astype(LOW)
    return (
        (mul(keys_t, grad_scores) * SCALE).astype(LOW),
        mul(grad_scores, scaled_q.T),
        mul(probs.astype(LOW), grad_t.T),
    )


def estimate(rows, cols, passes):
    return pl.CostEstimate(
        flops=int(rows * cols * 1200 * passes), transcendentals=int(rows * cols), bytes_accessed=int(rows * 2048)
    )


VMEM_LIMIT = 48 << 20


def by_length(length, full, blocks, run):
    @pl.when(length * 4 > full)
    def _():
        run(blocks)

    @pl.when(length * 4 <= full)
    def _():
        run(blocks // 4)


def cross_forward(queries_t, pair_t, lengths):
    blocks, _, cols, all_patches = pair_t.shape
    objects = lengths.shape[0]
    heads = cols // HEAD_DIM
    rows, patch_rows = queries_t.shape[1] // objects, all_patches // objects

    def kernel(len_ref, q_ref, pair_ref, mixed_ref, wide_ref, log_ref, keys_t, values):
        queries = (q_ref[...] * LOW(SCALE)).T

        def run(live):
            for c in range(live):
                keys_t[:, c * patch_rows : (c + 1) * patch_rows] = pair_ref[c, 0]
                load_values(values, c, pair_ref[c, 1])
            size = live * patch_rows
            mixed, log_total = attend_block(queries, keys_t[:, :size], values[:size])
            mixed_ref[...] = mixed.astype(LOW)
            wide_ref[...] = mixed
            log_ref[...] = log_total

        by_length(len_ref[pl.program_id(0)], blocks * patch_rows, blocks, run)

    block = pl.BlockSpec((HEAD_DIM, rows), lambda b, j, lens: (j, b))
    return pl.pallas_call(
        kernel,
        grid_spec=pltpu.PrefetchScalarGridSpec(
            num_scalar_prefetch=1,
            grid=(objects, heads),
            in_specs=[
                block,
                pl.BlockSpec((blocks, 2, HEAD_DIM, patch_rows), lambda b, j, lens: (0, 0, j, b)),
            ],
            out_specs=[block, block, pl.BlockSpec((None, 1, rows), lambda b, j, lens: (j, 0, b))],
            scratch_shapes=[
                pltpu.VMEM((HEAD_DIM, blocks * patch_rows), LOW),
                pltpu.VMEM((blocks * patch_rows, 2 * HEAD_DIM), LOW),
            ],
        ),
        out_shape=[
            jax.ShapeDtypeStruct(queries_t.shape, LOW),
            jax.ShapeDtypeStruct(queries_t.shape, WIDE),
            jax.ShapeDtypeStruct((heads, 1, queries_t.shape[1]), WIDE),
        ],
        name="cross_forward",
        cost_estimate=estimate(objects * rows, blocks * patch_rows * heads, 1.4),
        compiler_params=pltpu.CompilerParams(vmem_limit_bytes=VMEM_LIMIT),
    )(lengths, queries_t, pair_t)


def cross_backward(queries_t, pair_t, lengths, grad_t_all, wide, log_total):
    blocks, _, cols, all_patches = pair_t.shape
    objects = lengths.shape[0]
    heads = cols // HEAD_DIM
    rows, patch_rows = queries_t.shape[1] // objects, all_patches // objects

    def kernel(len_ref, q_ref, pair_ref, g_ref, wide_ref, log_ref, out_q, out_pair, keys, keys_t, values):
        grad_t = g_ref[...]
        spread = jnp.sum(grad_t.astype(WIDE) * wide_ref[...], axis=0, keepdims=True)

        def run(live):
            for c in range(live):
                at = slice(c * patch_rows, (c + 1) * patch_rows)
                keys[at] = pair_ref[c, 0].T
                keys_t[:, at] = pair_ref[c, 0]
                values[at] = pair_ref[c, 1].T
            size = live * patch_rows
            out_q[...], grad_k, grad_v = attend_block_back(
                q_ref[...] * LOW(SCALE),
                grad_t,
                keys[:size],
                keys_t[:, :size],
                values[:size],
                log_ref[...],
                spread,
            )
            for c in range(live):
                at = slice(c * patch_rows, (c + 1) * patch_rows)
                out_pair[c, 0] = grad_k[at].T.astype(LOW)
                out_pair[c, 1] = grad_v[at].T.astype(LOW)
            for c in range(live, blocks):
                out_pair[c] = jnp.zeros_like(out_pair[c])

        by_length(len_ref[pl.program_id(0)], blocks * patch_rows, blocks, run)

    block = pl.BlockSpec((HEAD_DIM, rows), lambda b, j, lens: (j, b))
    pair_block = pl.BlockSpec((blocks, 2, HEAD_DIM, patch_rows), lambda b, j, lens: (0, 0, j, b))
    return pl.pallas_call(
        kernel,
        grid_spec=pltpu.PrefetchScalarGridSpec(
            num_scalar_prefetch=1,
            grid=(objects, heads),
            in_specs=[
                block,
                pair_block,
                block,
                block,
                pl.BlockSpec((None, 1, rows), lambda b, j, lens: (j, 0, b)),
            ],
            out_specs=[block, pair_block],
            scratch_shapes=[
                pltpu.VMEM((blocks * patch_rows, HEAD_DIM), LOW),
                pltpu.VMEM((HEAD_DIM, blocks * patch_rows), LOW),
                pltpu.VMEM((blocks * patch_rows, HEAD_DIM), LOW),
            ],
        ),
        out_shape=[
            jax.ShapeDtypeStruct(queries_t.shape, LOW),
            jax.ShapeDtypeStruct(pair_t.shape, LOW),
        ],
        name="cross_backward",
        cost_estimate=estimate(objects * rows, blocks * patch_rows * heads, 2.5),
        compiler_params=pltpu.CompilerParams(vmem_limit_bytes=VMEM_LIMIT),
    )(lengths, queries_t, pair_t, grad_t_all, wide, log_total)


def shift(value, step):
    size = lax.axis_size("heads")
    return lax.ppermute(value, "heads", [((i + step) % size, i) for i in range(size)])


def gather_heads(value):
    size = lax.axis_size("heads")
    if size != 4:
        return [value] + [shift(value, step) for step in range(1, size)]
    after, before = shift(value, 1), shift(value, -1)
    inner = lax.ppermute(after, "heads", [(1, 0), (2, 1)]) + lax.ppermute(before, "heads", [(1, 2), (2, 3)])
    return [value, after, inner, before]


def scatter_heads(partial):
    size, me = lax.axis_size("heads"), lax.axis_index("heads")

    def part(step):
        return lax.dynamic_index_in_dim(partial, (me + step) % size, 0, keepdims=False)

    if size != 4:
        total = part(0)
        for step in range(1, size):
            total = total + shift(part(step).astype(LOW), -step).astype(WIDE)
        return total
    far = part(2).astype(LOW)
    up = lax.ppermute(far, "heads", [(0, 1), (1, 2)]).astype(WIDE)
    down = lax.ppermute(far, "heads", [(2, 1), (3, 2)]).astype(WIDE)
    from_below = shift((part(1) + up).astype(LOW), -1)
    from_above = shift((part(3) + down).astype(LOW), 1)
    return part(0) + from_below.astype(WIDE) + from_above.astype(WIDE)


def in_order(parts):
    size, me = lax.axis_size("heads"), lax.axis_index("heads")
    out = jnp.zeros((size,) + parts[0].shape, parts[0].dtype)
    for step, value in enumerate(parts):
        out = lax.dynamic_update_index_in_dim(out, value, (me + step) % size, 0)
    return out.reshape((-1,) + parts[0].shape[1:])


def sum_heads(partial):
    size = lax.axis_size("heads")
    split = partial.reshape((size, -1) + partial.shape[1:])
    return in_order(gather_heads(scatter_heads(split).astype(LOW)))


def exchange_rows(value):
    return lax.all_to_all(value, "rows", 0, 0, tiled=True)


def normed(value):
    centred = value - jnp.mean(value, axis=-1, keepdims=True)
    rate = lax.rsqrt(jnp.mean(centred * centred, axis=-1, keepdims=True) + EPSILON)
    return centred * rate, rate


def normed_back(grad, unit, rate):
    return rate * (
        grad
        - jnp.mean(grad, axis=-1, keepdims=True)
        - unit * jnp.mean(grad * unit, axis=-1, keepdims=True)
    )


def gelu_tanh(pre_act):
    return jax.nn.gelu(pre_act, approximate=True)


def add_trees(former, latter):
    return jax.tree.map(jnp.add, former, latter)


def pair_forward(queries, pair, key_at, length=None):
    blocks, objects, _, width, rows = queries.shape
    pair_rows = pair.shape[4]
    lengths = jnp.full((objects,), blocks * pair_rows, jnp.int32) if length is None else length

    def kernel(len_ref, q_ref, k_ref, v_ref, mixed_ref, wide_ref, log_ref, keys_t, values):
        def run(live):
            @pl.when(pl.program_id(1) == 0)
            def _():
                for c in range(live):
                    keys_t[:, c * pair_rows : (c + 1) * pair_rows] = k_ref[c]
                    load_values(values, c, v_ref[c])

            size = live * pair_rows
            mixed, log_total = attend_block(
                (q_ref[...] * LOW(SCALE)).T, keys_t[:, :size], values[:size]
            )
            mixed_ref[...] = mixed.astype(LOW)
            wide_ref[...] = mixed
            log_ref[...] = log_total

        if length is None:
            run(blocks)
        else:
            by_length(len_ref[pl.program_id(0)], blocks * pair_rows, blocks, run)

    block = pl.BlockSpec((None, None, width, rows), lambda o, i, lens: (i, o, 0, 0))
    return pl.pallas_call(
        kernel,
        grid_spec=pltpu.PrefetchScalarGridSpec(
            num_scalar_prefetch=1,
            grid=(objects, blocks),
            in_specs=[
                pl.BlockSpec((None, None, None, width, rows), lambda o, i, lens: (i, o, 0, 0, 0)),
                pl.BlockSpec((blocks, None, None, width, pair_rows), lambda o, i, lens: (0, o, key_at, 0, 0)),
                pl.BlockSpec((blocks, None, None, width, pair_rows), lambda o, i, lens: (0, o, key_at + 1, 0, 0)),
            ],
            out_specs=[block, block, pl.BlockSpec((None, None, 1, rows), lambda o, i, lens: (i, o, 0, 0))],
            scratch_shapes=[
                pltpu.VMEM((width, blocks * pair_rows), LOW),
                pltpu.VMEM((blocks * pair_rows, 2 * width), LOW),
            ],
        ),
        out_shape=[
            jax.ShapeDtypeStruct((blocks, objects, width, rows), LOW),
            jax.ShapeDtypeStruct((blocks, objects, width, rows), WIDE),
            jax.ShapeDtypeStruct((blocks, objects, 1, rows), WIDE),
        ],
        name="pair_forward",
        cost_estimate=estimate(objects * blocks * rows, blocks * pair_rows, 2 if length is None else 1.4),
        compiler_params=pltpu.CompilerParams(vmem_limit_bytes=VMEM_LIMIT),
    )(lengths, queries, pair, pair)


def pair_backward(queries, pair, key_at, length, grad_mixed, wide, log_total):
    blocks, objects, _, width, rows = queries.shape
    lengths = jnp.full((objects,), blocks * rows, jnp.int32) if length is None else length

    def kernel(len_ref, q_ref, k_ref, v_ref, g_ref, wide_ref, log_ref, out_ref, keys, keys_t, values, grad_k, grad_v):
        i = pl.program_id(1)

        def run(live):
            size = live * rows

            @pl.when(i == 0)
            def _():
                for c in range(live):
                    at = slice(c * rows, (c + 1) * rows)
                    keys[at] = k_ref[c].T
                    keys_t[:, at] = k_ref[c]
                    values[at] = v_ref[c].T

            grad_t = g_ref[...]
            spread = jnp.sum(grad_t.astype(WIDE) * wide_ref[...], axis=0, keepdims=True)
            out_ref[i, 0], term_k, term_v = attend_block_back(
                q_ref[...] * LOW(SCALE),
                grad_t,
                keys[:size],
                keys_t[:, :size],
                values[:size],
                log_ref[...],
                spread,
            )

            @pl.when(i == 0)
            def _():
                grad_k[:size] = term_k
                grad_v[:size] = term_v

            @pl.when(i > 0)
            def _():
                grad_k[:size] += term_k
                grad_v[:size] += term_v

            @pl.when(i == blocks - 1)
            def _():
                for c in range(live):
                    at = slice(c * rows, (c + 1) * rows)
                    out_ref[c, 1] = grad_k[at].T.astype(LOW)
                    out_ref[c, 2] = grad_v[at].T.astype(LOW)
                for c in range(live, blocks):
                    out_ref[c, 1:] = jnp.zeros_like(out_ref[c, 1:])

        if length is None:
            run(blocks)
        else:
            by_length(len_ref[pl.program_id(0)], blocks * rows, blocks, run)

    block = pl.BlockSpec((None, None, width, rows), lambda o, i, lens: (i, o, 0, 0))
    return pl.pallas_call(
        kernel,
        grid_spec=pltpu.PrefetchScalarGridSpec(
            num_scalar_prefetch=1,
            grid=(objects, blocks),
            in_specs=[
                pl.BlockSpec((None, None, None, width, rows), lambda o, i, lens: (i, o, 0, 0, 0)),
                pl.BlockSpec((blocks, None, None, width, rows), lambda o, i, lens: (0, o, key_at, 0, 0)),
                pl.BlockSpec((blocks, None, None, width, rows), lambda o, i, lens: (0, o, key_at + 1, 0, 0)),
                block,
                block,
                pl.BlockSpec((None, None, 1, rows), lambda o, i, lens: (i, o, 0, 0)),
            ],
            out_specs=pl.BlockSpec((blocks, None, 3, width, rows), lambda o, i, lens: (0, o, 0, 0, 0)),
            scratch_shapes=[
                pltpu.VMEM((blocks * rows, width), LOW),
                pltpu.VMEM((width, blocks * rows), LOW),
                pltpu.VMEM((blocks * rows, width), LOW),
                pltpu.VMEM((blocks * rows, width), WIDE),
                pltpu.VMEM((blocks * rows, width), WIDE),
            ],
        ),
        out_shape=jax.ShapeDtypeStruct((blocks, objects, 3, width, rows), LOW),
        name="pair_backward",
        cost_estimate=estimate(objects * blocks * rows, blocks * rows, 3 if length is None else 2),
        compiler_params=pltpu.CompilerParams(vmem_limit_bytes=VMEM_LIMIT),
    )(lengths, queries, pair, pair, grad_mixed, wide, log_total)


def swap(value, axis):
    return lax.ppermute(value, axis, [(0, 1), (1, 0)])


def sum_near(partial):
    low = partial.astype(LOW)
    return low.astype(WIDE) + swap(low, "near").astype(WIDE)


def tie(value, *others):
    return lax.optimization_barrier((value, *others))


def paired_device(
    tokens,
    cam_index,
    patches,
    patch_len,
    camera_table,
    self_weights,
    self_output,
    cross_gain,
    cross_query,
    cross_pair,
    cross_output,
    patch_weights,
    hidden_gain,
    widen_weights,
    narrow_weights,
    cotangent,
):
    objects = tokens.shape[0] // 2
    _, rows, width = tokens.shape
    cols = self_weights.shape[2]
    hidden = widen_weights.shape[1]
    heads = cols // HEAD_DIM
    codes = camera_table.shape[0]
    patch_width = patches.shape[2]
    count = objects * rows
    n_rows = lax.axis_size("rows")
    row_rank = lax.axis_index("rows")
    far, near = lax.axis_index("far"), lax.axis_index("near")

    def objects_of(value):
        return lax.dynamic_slice_in_dim(value, objects * far, objects, 0)

    def piece(value):
        size = value.shape[0] // n_rows
        return lax.dynamic_slice_in_dim(value, row_rank * size, size, 0)

    def join_rows(value):
        return lax.all_gather(value, "rows", axis=0, tiled=True)

    def both_columns(value):
        return [
            lax.dynamic_slice_in_dim(value, (2 * index + near) * cols, cols, value.ndim - 1)
            for index in range(2)
        ]

    def in_order(mine, away, axis=0):
        size = mine.shape[axis]
        shape = list(mine.shape)
        shape[axis] *= 2
        out = lax.dynamic_update_slice_in_dim(jnp.zeros(shape, mine.dtype), mine, far * size, axis)
        return lax.dynamic_update_slice_in_dim(out, away, (1 - far) * size, axis)

    def halves(value):
        value = value.reshape(objects, 2, rows // 2, -1)
        return [
            lax.dynamic_index_in_dim(value, index, 1, keepdims=False).reshape(count // 2, -1)
            for index in (near, 1 - near)
        ]

    def half_sum_near(partial):
        mine, away = halves(partial)
        return mine + swap(away.astype(LOW), "near").astype(WIDE)

    def over_heads(value):
        value = value.reshape(objects, rows // 2, -1)
        value = jnp.stack([value, swap(value, "far")])
        value = jnp.stack([value, swap(value, "near")])
        value = jnp.where(far == 0, value, jnp.flip(value, 1))
        value = jnp.where(near == 0, value, jnp.flip(value, 0))
        return value.transpose(1, 2, 0, 3, 4).reshape(2 * objects, rows, -1)

    def to_pairs(weights, value, slots):
        parts = [
            mul(weights, value[i * rows : (i + 1) * rows], NT)
            .astype(LOW)
            .reshape(n_rows, slots, HEAD_DIM, rows)
            for i in range(objects)
        ]
        return exchange_rows(jnp.stack(parts, axis=1))

    def from_pairs(value):
        return value.transpose(0, 2, 3, 1, 4).reshape(-1, count)

    def over_all_columns(value_t, weight):
        return mul(jnp.concatenate([value_t, swap(value_t, "near")]), weight, TN)

    qkv_rows = self_weights.reshape(3, width, heads, HEAD_DIM).transpose(2, 0, 3, 1)
    qkv_rows = qkv_rows.reshape(3 * cols, width)
    pair_rows = cross_pair.reshape(2, width, heads, HEAD_DIM).transpose(2, 0, 3, 1)
    pair_rows = pair_rows.reshape(2 * cols, width)
    query_rows = cross_query.T

    qkv_away = join_rows(swap(piece(qkv_rows), "far"))

    table_flat = camera_table.reshape(codes, -1)
    cross_gain_f = cross_gain.astype(WIDE)
    hidden_gain_f = hidden_gain.astype(WIDE)

    inputs = objects_of(tokens).reshape(count, width).astype(WIDE)
    patch_in = objects_of(patches).reshape(count, patch_width)
    length = objects_of(patch_len)
    grad_low = objects_of(cotangent).reshape(count, width)
    codes_of = objects_of(cam_index).reshape(count)
    onehot = (codes_of[:, None] == jnp.arange(codes)[None, :]).astype(LOW)
    shift_scale = mul(onehot, table_flat)
    gain_one = 1.0 + shift_scale[:, :width]
    unit_one, rate_one = normed(inputs)
    normed_one = (unit_one * gain_one + shift_scale[:, width:]).astype(LOW)

    mine = [piece(v) for v in (self_output, query_rows, cross_output, pair_rows)]
    normed_one, *mine = tie(normed_one, *mine)
    mine = jnp.concatenate(mine, axis=0)
    across = swap(mine, "far")
    size = cols // n_rows
    two = in_order(mine[None, : 3 * size], across[None, : 3 * size])
    four = jnp.concatenate([two, swap(two, "near")])
    sent = jnp.concatenate([four.reshape(-1, width), across[3 * size :]])
    sent = lax.all_gather(sent, "rows", axis=0)
    pair_away = sent[:, 12 * size :].reshape(2 * cols, width)
    whole = sent[:, : 12 * size].reshape(n_rows, 4, 3, size, width).transpose(2, 1, 0, 3, 4)
    self_whole, query_whole, cross_whole = whole.reshape(3, 4 * cols, width)

    qkv_both = in_order(qkv_rows, qkv_away)
    qkv = to_pairs(qkv_both, normed_one, 3)
    patch_mid = mul(patch_in, patch_weights).astype(LOW)
    pair_both = in_order(pair_rows, pair_away)
    pair = to_pairs(pair_both, patch_mid, 2)

    mine = [piece(widen_weights), piece(narrow_weights)]
    qkv, *mine = tie(qkv, *mine)
    size = width // n_rows
    sent = lax.all_gather(jnp.concatenate(mine, axis=0), ("far", "rows"), axis=0)
    sent = sent.reshape(2, n_rows, 2, size, width)
    widen = sent[:, :, 0].reshape(2, width, hidden)
    widen = jnp.concatenate([widen[0], widen[1]], axis=1)
    narrow = sent[:, :, 1].reshape(2 * hidden, width)

    mixed, self_wide, self_log = pair_forward(qkv, qkv, 1)
    self_mixed_t = from_pairs(exchange_rows(mixed)[:, :, None])
    after_self = inputs + over_all_columns(self_mixed_t, self_whole)
    unit_two, rate_two = normed(after_self)
    normed_two = (unit_two * cross_gain_f).astype(LOW)
    cross_q = to_pairs(query_whole[: 2 * cols], normed_two, 1)
    mixed, cross_wide, cross_log = pair_forward(cross_q, pair, 0, length)
    cross_mixed_t = from_pairs(exchange_rows(mixed)[:, :, None])
    after_cross = after_self + over_all_columns(cross_mixed_t, cross_whole)
    unit_three, rate_three = normed(after_cross)
    normed_three = (unit_three * hidden_gain_f).astype(LOW)
    activated, act_back = jax.vjp(gelu_tanh, mul(normed_three, widen))
    activated = activated.astype(LOW)
    grad_pre = act_back(mul(grad_low, narrow, NT))[0].astype(LOW)
    grad_three = sum_near(mul(grad_pre, widen, NT))
    hidden_half = half_sum_near(mul(activated, narrow))
    result = (halves(after_cross)[0] + hidden_half).astype(LOW)

    def part_rows(both):
        return lax.psum_scatter(both, "rows", scatter_dimension=1, tiled=True)

    def own_and_away(value):
        return [lax.dynamic_index_in_dim(value, index, 0, keepdims=False) for index in (far, 1 - far)]

    def add_far(mine, away):
        return (mine.astype(WIDE) + away.astype(WIDE)).astype(LOW)

    def by_shard(left, right):
        return mul(left, right, NN).astype(LOW).reshape(2, -1, right.shape[1])

    hidden_terms = jnp.concatenate(
        [
            mul(value, against, TN).astype(LOW).reshape(2, hidden, width)
            for value, against in ((activated, grad_low), (grad_pre, normed_three))
        ],
        axis=1,
    )
    hidden_part = lax.psum_scatter(
        hidden_terms.reshape(-1, width), ("far", "rows"), scatter_dimension=0, tiled=True
    )

    hidden_gain_term = jnp.sum(grad_three * unit_three, axis=0)
    grad_cross = grad_low.astype(WIDE) + normed_back(
        grad_three * hidden_gain_f, unit_three, rate_three
    )
    grad_cross_low = grad_cross.astype(LOW)
    grad_mixed = to_pairs(cross_whole[: 2 * cols], grad_cross_low, 1)[:, :, 0]
    grads = pair_backward(cross_q, pair, 0, length, grad_mixed, cross_wide, cross_log)
    grads, hidden_part = tie(grads, hidden_part)
    grads = exchange_rows(grads)
    hidden_total = join_rows(hidden_part)
    grad_cq_t = from_pairs(grads[:, :, :1])
    grad_pair_t = from_pairs(grads[:, :, 1:])
    grad_two = over_all_columns(grad_cq_t, query_whole)
    cross_gain_term = jnp.sum(grad_two * unit_two, axis=0)
    grad_self = grad_cross + normed_back(grad_two * cross_gain_f, unit_two, rate_two)
    grad_self_low = grad_self.astype(LOW)
    grad_mid = sum_near(
        mul(grad_pair_t, pair_both, TN)
    ).astype(LOW)
    patch_half = mul(halves(grad_mid)[0], patch_weights, NT).astype(LOW)
    patch_terms = jnp.stack([mul(value, patch_in, TN).astype(LOW) for value in both_columns(grad_mid)])
    patch_terms = jnp.pad(patch_terms, ((0, 0), (0, 0), (0, width - patch_width)))
    middle_part = part_rows(
        jnp.concatenate(
            [
                by_shard(cross_mixed_t, grad_cross_low),
                by_shard(self_mixed_t, grad_self_low),
                by_shard(grad_cq_t, normed_two),
                by_shard(grad_pair_t, patch_mid),
                patch_terms,
            ],
            axis=1,
        )
    )
    grad_mixed = to_pairs(self_whole[: 2 * cols], grad_self_low, 1)[:, :, 0]
    grads = pair_backward(qkv, qkv, 1, None, grad_mixed, self_wide, self_log)
    grads, hidden_total, middle_part = tie(grads, hidden_total, middle_part)
    grads = exchange_rows(grads)
    middle_own, middle_away = own_and_away(middle_part)
    middle_total = join_rows(add_far(middle_own, swap(middle_away, "far")))
    grad_qkv_t = from_pairs(grads)
    last_part = part_rows(by_shard(grad_qkv_t, normed_one))
    grad_one = half_sum_near(mul(grad_qkv_t, qkv_both, TN))
    gain_half, unit_half, rate_half, self_half = (
        halves(value)[0] for value in (gain_one, unit_one, rate_one, grad_self)
    )
    input_half = self_half + normed_back(grad_one * gain_half, unit_half, rate_half)
    input_half = input_half.astype(LOW)
    onehot_half = halves(onehot)[0].astype(WIDE)
    table_term = jnp.concatenate(
        [
            lax.dot_general(onehot_half, value, TN, precision=lax.Precision.HIGHEST)
            for value in (grad_one * unit_half, grad_one)
        ],
        axis=0,
    )
    small = [sum_near(table_term), hidden_gain_term[None], cross_gain_term[None], jnp.zeros((14, width), WIDE)]
    small = jnp.stack(both_columns(jnp.concatenate(small, axis=0).astype(LOW)))
    small = jnp.sum(lax.all_gather(small, "rows", axis=0).astype(WIDE), axis=0).astype(LOW)
    small_own, small_away = (
        lax.dynamic_index_in_dim(small, index, 0, keepdims=False) for index in (far, 1 - far)
    )
    small = small_own.astype(WIDE) + swap(small_away, "far").astype(WIDE)
    input_half, middle_total = tie(input_half, middle_total)
    input_grads = over_heads(input_half)
    outputs = over_heads(result)
    patch_grads = over_heads(patch_half)
    last_own, last_away = own_and_away(last_part)
    last_total = join_rows(add_far(last_own, swap(last_away, "far")))

    output_total = middle_total[: 2 * cols]
    query_total = middle_total[2 * cols : 3 * cols]
    pair_total = middle_total[3 * cols : 5 * cols].reshape(heads, 2, HEAD_DIM, width)
    patch_total = middle_total[5 * cols :, :patch_width]
    self_total = last_total.reshape(heads, 3, HEAD_DIM, width)
    gradients = (
        small[: 2 * codes].reshape(2, codes, cols).transpose(1, 0, 2),
        self_total.transpose(1, 3, 0, 2).reshape(3, width, cols),
        output_total[cols:],
        small[2 * codes + 1],
        query_total.T,
        pair_total.transpose(1, 3, 0, 2).reshape(2, width, cols),
        output_total[:cols],
        patch_total.T,
        small[2 * codes],
        hidden_total[hidden:].T,
        hidden_total[:hidden],
    )
    return (outputs, input_grads.astype(WIDE), patch_grads.astype(WIDE)) + tuple(
        value.astype(WIDE) for value in gradients
    )


def per_device(
    tokens,
    cam_index,
    patches,
    patch_len,
    camera_table,
    self_weights,
    self_output,
    cross_gain,
    cross_query,
    cross_pair,
    cross_output,
    patch_weights,
    hidden_gain,
    widen_weights,
    narrow_weights,
    cotangent,
):
    batches, rows, width = tokens.shape
    cols = self_weights.shape[2]
    heads = cols // HEAD_DIM
    codes = camera_table.shape[0]
    patch_rows, patch_width = patches.shape[1:]
    n_rows, n_heads = lax.axis_size("rows"), lax.axis_size("heads")
    row_rank, head_rank = lax.axis_index("rows"), lax.axis_index("heads")
    groups = 1
    objects = batches // groups
    full_lengths = jnp.full((objects,), n_rows * rows, jnp.int32)
    count = objects * rows

    def own_columns(value):
        return lax.dynamic_slice_in_dim(value, head_rank * cols, cols, value.ndim - 1)

    table_flat = camera_table.reshape(codes, -1)
    cross_gain_f = cross_gain.astype(WIDE)
    hidden_gain_f = hidden_gain.astype(WIDE)

    qkv_rows = (
        self_weights.reshape(3, width, heads, HEAD_DIM).transpose(2, 0, 3, 1).reshape(3 * cols, width)
    )
    qkv_rows_back = self_weights.transpose(0, 2, 1).reshape(3 * cols, width)
    pair_rows = cross_pair.transpose(0, 2, 1).reshape(2 * cols, width)
    query_rows = cross_query.T

    local = jnp.stack([self_output, cross_output, query_rows])
    piece = cols // n_rows
    local = lax.dynamic_slice_in_dim(local, row_rank * piece, piece, 1)
    whole = lax.all_gather(jnp.stack(gather_heads(local)), "rows", axis=0)
    whole = whole.transpose(2, 1, 0, 3, 4).reshape(3, n_heads * cols, width)
    self_whole, cross_whole, query_whole = whole[0], whole[1], whole[2]

    def over_all_columns(value_t, weight):
        return mul(jnp.concatenate(gather_heads(value_t), axis=0), weight, TN)

    def by_object(weight, value):
        return jnp.stack(
            [mul(weight, value[i * rows : (i + 1) * rows], NT).astype(LOW) for i in range(objects)]
        )

    def column_terms(value, grads_t):
        return [
            mul(value, grads_t[i : i + cols], (((0,), (1,)), ((), ())))
            for i in range(0, grads_t.shape[0], cols)
        ]

    def one_group(group):
        part = slice(group * objects, (group + 1) * objects)
        inputs = tokens[part].reshape(count, width).astype(WIDE)
        patch_in = patches[part].reshape(objects * patch_rows, patch_width)
        lengths = patch_len[part]
        grad_low = cotangent[part].reshape(count, width)
        onehot = (cam_index[part].reshape(count)[:, None] == jnp.arange(codes)[None, :]).astype(LOW)
        shift_scale = mul(onehot, table_flat)
        gain_one = 1.0 + shift_scale[:, :width]
        unit_one, rate_one = normed(inputs)
        normed_one = (unit_one * gain_one + shift_scale[:, width:]).astype(LOW)
        qkv_t = by_object(qkv_rows, normed_one)
        by_kind = qkv_t.reshape(objects, heads, 3, HEAD_DIM, rows).transpose(2, 1, 3, 0, 4)
        by_kind = by_kind.reshape(3, cols, count)
        self_pair = lax.all_gather(by_kind[1:], "rows", axis=0)
        patch_mid = mul(patch_in, patch_weights).astype(LOW)
        own_pair = mul(pair_rows, patch_mid, NT).astype(LOW).reshape(2, cols, -1)
        pair_t = lax.all_gather(own_pair, "rows", axis=0)
        self_mixed_t, self_wide, self_log = cross_forward(by_kind[0], self_pair, full_lengths)
        after_self = inputs + over_all_columns(self_mixed_t, self_whole)
        unit_two, rate_two = normed(after_self)
        normed_two = (unit_two * cross_gain_f).astype(LOW)
        cross_q_t = mul(query_rows, normed_two, NT).astype(LOW)
        cross_mixed_t, cross_wide, cross_log = cross_forward(cross_q_t, pair_t, lengths)
        after_cross = after_self + over_all_columns(cross_mixed_t, cross_whole)
        unit_three, rate_three = normed(after_cross)
        normed_three = (unit_three * hidden_gain_f).astype(LOW)
        pre_act = mul(normed_three, widen_weights)
        activated, act_back = jax.vjp(gelu_tanh, pre_act)
        activated = activated.astype(LOW)
        grad_pre = act_back(mul(grad_low, narrow_weights, NT))[0].astype(LOW)
        grad_three = sum_heads(mul(grad_pre, widen_weights, NT)).astype(WIDE)
        yield "heads", {"hidden": mul(activated, narrow_weights)}
        yield "rows", {
            "narrow": mul(activated, grad_low, TN),
            "widen": mul(normed_three, grad_pre, TN),
        }
        hidden_gain_term = jnp.sum(own_columns(grad_three * unit_three), axis=0)
        grad_cross = grad_low.astype(WIDE) + normed_back(
            grad_three * hidden_gain_f, unit_three, rate_three
        )
        grad_cross_low = grad_cross.astype(LOW)
        cross_output_term = mul(cross_mixed_t, grad_cross_low)
        grad_mixed_t = mul(cross_output, grad_cross_low, NT).astype(LOW)
        grad_cq_t, grad_pair_t = cross_backward(
            cross_q_t, pair_t, lengths, grad_mixed_t, cross_wide, cross_log
        )
        grad_two = over_all_columns(grad_cq_t, query_whole)
        grad_pair_t = lax.psum_scatter(grad_pair_t, "rows", scatter_dimension=0, tiled=False)
        grad_pair_t = grad_pair_t.reshape(2 * cols, -1)
        query_term = mul(normed_two, grad_cq_t, (((0,), (1,)), ((), ())))
        cross_gain_term = jnp.sum(own_columns(grad_two * unit_two), axis=0)
        grad_self = grad_cross + normed_back(grad_two * cross_gain_f, unit_two, rate_two)
        grad_self_low = grad_self.astype(LOW)
        self_output_term = mul(self_mixed_t, grad_self_low)
        yield "heads", {"patch": mul(grad_pair_t, pair_rows, TN)}
        yield "rows", {
            "query": query_term,
            "pair": column_terms(patch_mid, grad_pair_t),
            "cross_output": cross_output_term,
            "self_output": self_output_term,
        }
        grad_self_mixed_t = mul(self_output, grad_self_low, NT).astype(LOW)
        grad_q_t, grad_kv_t = cross_backward(
            by_kind[0], self_pair, full_lengths, grad_self_mixed_t, self_wide, self_log
        )
        grad_kv_t = lax.psum_scatter(grad_kv_t, "rows", scatter_dimension=0, tiled=False)
        grad_qkv_t = jnp.concatenate([grad_q_t[None], grad_kv_t]).reshape(3 * cols, count)
        grad_qkv_t = yield "after", (grad_qkv_t, ["patch", "narrow", "widen"])
        grad_mid = yield "take", "patch"
        patch_term = mul(patch_in, own_columns(grad_mid), TN)
        patch_grad = mul(grad_mid, patch_weights, NT)
        grad_one = sum_heads(mul(grad_qkv_t, qkv_rows_back, TN))
        grad_one = yield "after", (grad_one, ["query", "pair", "cross_output", "self_output"])
        grad_one = grad_one.astype(WIDE)
        input_grad = grad_self + normed_back(grad_one * gain_one, unit_one, rate_one)
        own_grad = own_columns(grad_one)
        table_term = jnp.stack(
            [
                lax.dot_general(onehot.astype(WIDE), v, TN, precision=lax.Precision.HIGHEST)
                for v in (own_grad * own_columns(unit_one), own_grad)
            ],
            axis=1,
        )
        small = [patch_term, table_term.reshape(2 * codes, cols)]
        small += [hidden_gain_term[None], cross_gain_term[None], jnp.zeros((14, cols), WIDE)]
        yield "rows", {
            "self": column_terms(normed_one, grad_qkv_t),
            "small": jnp.concatenate(small, axis=0),
        }
        hidden_sum = yield "take", "hidden"
        result = (after_cross + hidden_sum.astype(WIDE)).astype(LOW)
        yield (
            "done",
            (
                result.reshape(objects, rows, width),
                input_grad.reshape(objects, rows, width),
                patch_grad.reshape(objects, patch_rows, patch_width),
            ),
        )

    steps = [one_group(group) for group in range(groups)]
    asked = [next(step) for step in steps]
    totals, ahead = {}, []
    while asked[0][0] != "done":
        kind, what = asked[0]
        answers = [None] * groups
        if kind == "take":
            answers = jnp.split(totals[what], groups)
        elif kind == "after":
            early = {name: totals[name] for name in what[1]}
            answers = [value for _, (value, _) in asked]
            answers[-1], early = lax.optimization_barrier((answers[-1], early))
            totals.update(early)
        else:
            terms = [value for _, value in asked]
            if kind == "heads":
                terms = jax.tree.map(lambda *parts: jnp.concatenate(parts, axis=0), *terms)
            else:
                for value in terms[1:]:
                    terms[0] = add_trees(terms[0], value)
                terms = terms[0]
            if kind == "rows":
                terms = jax.tree.map(lambda value: value.astype(LOW), terms)
            if kind == "heads":
                totals.update({name: sum_heads(value) for name, value in terms.items()})
            else:
                before = {name: totals[name] for name in ahead}
                terms, before = lax.optimization_barrier((terms, before))
                totals.update(before)
                totals.update(lax.psum(terms, kind))
                ahead = list(terms)
        asked = [step.send(value) for step, value in zip(steps, answers)]
    outputs, input_grads, patch_grads = (
        jnp.concatenate([value[i] for _, value in asked], axis=0) for i in range(3)
    )
    patch_total, table_total, gains = jnp.split(
        totals["small"], [patch_width, patch_width + 2 * codes]
    )
    gradients = (
        table_total.reshape(codes, 2, cols),
        jnp.stack(totals["self"]),
        totals["self_output"],
        gains[1],
        totals["query"],
        jnp.stack(totals["pair"]),
        totals["cross_output"],
        patch_total,
        gains[0],
        totals["widen"],
        totals["narrow"],
    )
    return (outputs, input_grads, patch_grads) + tuple(value.astype(WIDE) for value in gradients)


def solution(mesh):
    sizes = mesh.shape
    paired = sizes["heads"] == 4 and sizes["rows"] == 8
    heads = ("far", "near") if paired else "heads"
    if paired:
        names = (*heads, "rows")
        mesh = jax.sharding.Mesh(mesh.devices.reshape(2, 2, sizes["rows"]), names)
    in_specs = (
        P(None, "rows", None),
        P(None, "rows"),
        P(None, "rows", None),
        P(),
        P(),
        P(None, None, heads),
        P(heads, None),
        P(),
        P(None, heads),
        P(None, None, heads),
        P(heads, None),
        P(),
        P(),
        P(None, heads),
        P(heads, None),
        P(None, "rows", None),
    )
    out_specs = (
        P(None, "rows", None),
        P(None, "rows", None),
        P(None, "rows", None),
        P(None, None, heads),
        P(None, None, heads),
        P(heads, None),
        P(heads),
        P(None, heads),
        P(None, None, heads),
        P(heads, None),
        P(None, heads),
        P(heads),
        P(None, heads),
        P(heads, None),
    )
    return jax.shard_map(
        paired_device if paired else per_device,
        mesh=mesh,
        in_specs=in_specs,
        out_specs=out_specs,
        check_vma=False,
    )
```

```python
import jax
import jax.numpy as jnp
from jax import lax
from jax.experimental import pallas as pl
from jax.experimental.pallas import tpu as pltpu
from jax.sharding import PartitionSpec as P

HEAD_DIM = 64
EPSILON = 1e-05
SCALE = HEAD_DIM ** (-0.5)
LOW = jnp.bfloat16
WIDE = jnp.float32

NN = (((1,), (0,)), ((), ()))
NT = (((1,), (1,)), ((), ()))
TN = (((0,), (0,)), ((), ()))
T_LAST = (((0,), (1,)), ((), ()))


def mul(left, right, dims=NN):
    return lax.dot_general(left, right, dims, preferred_element_type=WIDE)


def load_values(values, block, values_t):
    rows = values_t.shape[1]
    at = slice(block * rows, (block + 1) * rows)
    values[at, :HEAD_DIM] = values_t.T
    values[at, HEAD_DIM:] = jnp.ones((rows, HEAD_DIM), values.dtype)


def attend_block(queries, keys_t, values):
    scores = mul(queries, keys_t)
    peak = jnp.max(scores, axis=1, keepdims=True)
    both = mul(jnp.exp(scores - peak).astype(LOW), values).T
    total = both[HEAD_DIM : HEAD_DIM + 1]
    return both[:HEAD_DIM] / total, peak.T + jnp.log(total)


def attend_block_back(scaled_q, grad_t, keys, keys_t, values, log_total, spread):
    probs = jnp.exp(mul(keys, scaled_q) - log_total)
    grad_scores = (probs * (mul(values, grad_t) - spread)).astype(LOW)
    return (
        (mul(keys_t, grad_scores) * SCALE).astype(LOW),
        mul(grad_scores, scaled_q.T),
        mul(probs.astype(LOW), grad_t.T),
    )


def estimate(rows, cols, passes):
    return pl.CostEstimate(
        flops=int(rows * cols * 1200 * passes), transcendentals=int(rows * cols), bytes_accessed=int(rows * 2048)
    )


VMEM_LIMIT = 48 << 20


def by_length(length, full, blocks, run):
    @pl.when(length * 4 > full)
    def _():
        run(blocks)

    @pl.when(length * 4 <= full)
    def _():
        run(blocks // 4)


def cross_forward(queries_t, pair_t, lengths):
    blocks, _, cols, all_patches = pair_t.shape
    objects = lengths.shape[0]
    heads = cols // HEAD_DIM
    rows, patch_rows = queries_t.shape[1] // objects, all_patches // objects

    def kernel(len_ref, q_ref, pair_ref, mixed_ref, wide_ref, log_ref, keys_t, values):
        queries = (q_ref[...] * LOW(SCALE)).T

        def run(live):
            for c in range(live):
                keys_t[:, c * patch_rows : (c + 1) * patch_rows] = pair_ref[c, 0]
                load_values(values, c, pair_ref[c, 1])
            size = live * patch_rows
            mixed, log_total = attend_block(queries, keys_t[:, :size], values[:size])
            mixed_ref[...] = mixed.astype(LOW)
            wide_ref[...] = mixed
            log_ref[...] = log_total

        by_length(len_ref[pl.program_id(0)], blocks * patch_rows, blocks, run)

    block = pl.BlockSpec((HEAD_DIM, rows), lambda b, j, lens: (j, b))
    return pl.pallas_call(
        kernel,
        grid_spec=pltpu.PrefetchScalarGridSpec(
            num_scalar_prefetch=1,
            grid=(objects, heads),
            in_specs=[
                block,
                pl.BlockSpec((blocks, 2, HEAD_DIM, patch_rows), lambda b, j, lens: (0, 0, j, b)),
            ],
            out_specs=[block, block, pl.BlockSpec((None, 1, rows), lambda b, j, lens: (j, 0, b))],
            scratch_shapes=[
                pltpu.VMEM((HEAD_DIM, blocks * patch_rows), LOW),
                pltpu.VMEM((blocks * patch_rows, 2 * HEAD_DIM), LOW),
            ],
        ),
        out_shape=[
            jax.ShapeDtypeStruct(queries_t.shape, LOW),
            jax.ShapeDtypeStruct(queries_t.shape, WIDE),
            jax.ShapeDtypeStruct((heads, 1, queries_t.shape[1]), WIDE),
        ],
        name="cross_forward",
        cost_estimate=estimate(objects * rows, blocks * patch_rows * heads, 1.4),
        compiler_params=pltpu.CompilerParams(vmem_limit_bytes=VMEM_LIMIT),
    )(lengths, queries_t, pair_t)


def cross_backward(queries_t, pair_t, lengths, grad_t_all, wide, log_total):
    blocks, _, cols, all_patches = pair_t.shape
    objects = lengths.shape[0]
    heads = cols // HEAD_DIM
    rows, patch_rows = queries_t.shape[1] // objects, all_patches // objects

    def kernel(len_ref, q_ref, pair_ref, g_ref, wide_ref, log_ref, out_q, out_pair, keys, keys_t, values):
        grad_t = g_ref[...]
        spread = jnp.sum(grad_t.astype(WIDE) * wide_ref[...], axis=0, keepdims=True)

        def run(live):
            for c in range(live):
                at = slice(c * patch_rows, (c + 1) * patch_rows)
                keys[at] = pair_ref[c, 0].T
                keys_t[:, at] = pair_ref[c, 0]
                values[at] = pair_ref[c, 1].T
            size = live * patch_rows
            out_q[...], grad_k, grad_v = attend_block_back(
                q_ref[...] * LOW(SCALE),
                grad_t,
                keys[:size],
                keys_t[:, :size],
                values[:size],
                log_ref[...],
                spread,
            )
            for c in range(live):
                at = slice(c * patch_rows, (c + 1) * patch_rows)
                out_pair[c, 0] = grad_k[at].T.astype(LOW)
                out_pair[c, 1] = grad_v[at].T.astype(LOW)
            for c in range(live, blocks):
                out_pair[c] = jnp.zeros_like(out_pair[c])

        by_length(len_ref[pl.program_id(0)], blocks * patch_rows, blocks, run)

    block = pl.BlockSpec((HEAD_DIM, rows), lambda b, j, lens: (j, b))
    pair_block = pl.BlockSpec((blocks, 2, HEAD_DIM, patch_rows), lambda b, j, lens: (0, 0, j, b))
    return pl.pallas_call(
        kernel,
        grid_spec=pltpu.PrefetchScalarGridSpec(
            num_scalar_prefetch=1,
            grid=(objects, heads),
            in_specs=[
                block,
                pair_block,
                block,
                block,
                pl.BlockSpec((None, 1, rows), lambda b, j, lens: (j, 0, b)),
            ],
            out_specs=[block, pair_block],
            scratch_shapes=[
                pltpu.VMEM((blocks * patch_rows, HEAD_DIM), LOW),
                pltpu.VMEM((HEAD_DIM, blocks * patch_rows), LOW),
                pltpu.VMEM((blocks * patch_rows, HEAD_DIM), LOW),
            ],
        ),
        out_shape=[
            jax.ShapeDtypeStruct(queries_t.shape, LOW),
            jax.ShapeDtypeStruct(pair_t.shape, LOW),
        ],
        name="cross_backward",
        cost_estimate=estimate(objects * rows, blocks * patch_rows * heads, 2.5),
        compiler_params=pltpu.CompilerParams(vmem_limit_bytes=VMEM_LIMIT),
    )(lengths, queries_t, pair_t, grad_t_all, wide, log_total)


def shift(value, step):
    size = lax.axis_size("heads")
    return lax.ppermute(value, "heads", [((i + step) % size, i) for i in range(size)])


def gather_heads(value):
    size = lax.axis_size("heads")
    if size != 4:
        return [value] + [shift(value, step) for step in range(1, size)]
    after, before = shift(value, 1), shift(value, -1)
    inner = lax.ppermute(after, "heads", [(1, 0), (2, 1)]) + lax.ppermute(before, "heads", [(1, 2), (2, 3)])
    return [value, after, inner, before]


def scatter_heads(partial):
    size, me = lax.axis_size("heads"), lax.axis_index("heads")

    def part(step):
        return lax.dynamic_index_in_dim(partial, (me + step) % size, 0, keepdims=False)

    if size != 4:
        total = part(0)
        for step in range(1, size):
            total = total + shift(part(step).astype(LOW), -step).astype(WIDE)
        return total
    far = part(2).astype(LOW)
    up = lax.ppermute(far, "heads", [(0, 1), (1, 2)]).astype(WIDE)
    down = lax.ppermute(far, "heads", [(2, 1), (3, 2)]).astype(WIDE)
    from_below = shift((part(1) + up).astype(LOW), -1)
    from_above = shift((part(3) + down).astype(LOW), 1)
    return part(0) + from_below.astype(WIDE) + from_above.astype(WIDE)


def in_order(parts):
    size, me = lax.axis_size("heads"), lax.axis_index("heads")
    out = jnp.zeros((size,) + parts[0].shape, parts[0].dtype)
    for step, value in enumerate(parts):
        out = lax.dynamic_update_index_in_dim(out, value, (me + step) % size, 0)
    return out.reshape((-1,) + parts[0].shape[1:])


def sum_heads(partial):
    size = lax.axis_size("heads")
    split = partial.reshape((size, -1) + partial.shape[1:])
    return in_order(gather_heads(scatter_heads(split).astype(LOW)))


def exchange_rows(value):
    return lax.all_to_all(value, "rows", 0, 0, tiled=True)


def normed(value):
    centred = value - jnp.mean(value, axis=-1, keepdims=True)
    rate = lax.rsqrt(jnp.mean(centred * centred, axis=-1, keepdims=True) + EPSILON)
    return centred * rate, rate


def normed_back(grad, unit, rate):
    return rate * (
        grad
        - jnp.mean(grad, axis=-1, keepdims=True)
        - unit * jnp.mean(grad * unit, axis=-1, keepdims=True)
    )


def gelu_tanh(pre_act):
    return jax.nn.gelu(pre_act, approximate=True)


def add_trees(former, latter):
    return jax.tree.map(jnp.add, former, latter)


def pair_forward(queries, pair, key_at, length=None):
    blocks, objects, _, width, rows = queries.shape
    pair_rows = pair.shape[4]
    lengths = jnp.full((objects,), blocks * pair_rows, jnp.int32) if length is None else length

    def kernel(len_ref, q_ref, k_ref, v_ref, mixed_ref, wide_ref, log_ref, keys_t, values):
        def run(live):
            @pl.when(pl.program_id(1) == 0)
            def _():
                for c in range(live):
                    keys_t[:, c * pair_rows : (c + 1) * pair_rows] = k_ref[c]
                    load_values(values, c, v_ref[c])

            size = live * pair_rows
            mixed, log_total = attend_block(
                (q_ref[...] * LOW(SCALE)).T, keys_t[:, :size], values[:size]
            )
            mixed_ref[...] = mixed.astype(LOW)
            wide_ref[...] = mixed
            log_ref[...] = log_total

        if length is None:
            run(blocks)
        else:
            by_length(len_ref[pl.program_id(0)], blocks * pair_rows, blocks, run)

    block = pl.BlockSpec((None, None, width, rows), lambda o, i, lens: (i, o, 0, 0))
    return pl.pallas_call(
        kernel,
        grid_spec=pltpu.PrefetchScalarGridSpec(
            num_scalar_prefetch=1,
            grid=(objects, blocks),
            in_specs=[
                pl.BlockSpec((None, None, None, width, rows), lambda o, i, lens: (i, o, 0, 0, 0)),
                pl.BlockSpec((blocks, None, None, width, pair_rows), lambda o, i, lens: (0, o, key_at, 0, 0)),
                pl.BlockSpec((blocks, None, None, width, pair_rows), lambda o, i, lens: (0, o, key_at + 1, 0, 0)),
            ],
            out_specs=[block, block, pl.BlockSpec((None, None, 1, rows), lambda o, i, lens: (i, o, 0, 0))],
            scratch_shapes=[
                pltpu.VMEM((width, blocks * pair_rows), LOW),
                pltpu.VMEM((blocks * pair_rows, 2 * width), LOW),
            ],
        ),
        out_shape=[
            jax.ShapeDtypeStruct((blocks, objects, width, rows), LOW),
            jax.ShapeDtypeStruct((blocks, objects, width, rows), WIDE),
            jax.ShapeDtypeStruct((blocks, objects, 1, rows), WIDE),
        ],
        name="pair_forward",
        cost_estimate=estimate(objects * blocks * rows, blocks * pair_rows, 2 if length is None else 1.4),
        compiler_params=pltpu.CompilerParams(vmem_limit_bytes=VMEM_LIMIT),
    )(lengths, queries, pair, pair)


def pair_backward(queries, pair, key_at, length, grad_mixed, wide, log_total):
    blocks, objects, _, width, rows = queries.shape
    lengths = jnp.full((objects,), blocks * rows, jnp.int32) if length is None else length

    def kernel(len_ref, q_ref, k_ref, v_ref, g_ref, wide_ref, log_ref, out_ref, keys, keys_t, values, grad_k, grad_v):
        i = pl.program_id(1)

        def run(live):
            size = live * rows

            @pl.when(i == 0)
            def _():
                for c in range(live):
                    at = slice(c * rows, (c + 1) * rows)
                    keys[at] = k_ref[c].T
                    keys_t[:, at] = k_ref[c]
                    values[at] = v_ref[c].T

            grad_t = g_ref[...]
            spread = jnp.sum(grad_t.astype(WIDE) * wide_ref[...], axis=0, keepdims=True)
            out_ref[i, 0], term_k, term_v = attend_block_back(
                q_ref[...] * LOW(SCALE),
                grad_t,
                keys[:size],
                keys_t[:, :size],
                values[:size],
                log_ref[...],
                spread,
            )

            @pl.when(i == 0)
            def _():
                grad_k[:size] = term_k
                grad_v[:size] = term_v

            @pl.when(i > 0)
            def _():
                grad_k[:size] += term_k
                grad_v[:size] += term_v

            @pl.when(i == blocks - 1)
            def _():
                for c in range(live):
                    at = slice(c * rows, (c + 1) * rows)
                    out_ref[c, 1] = grad_k[at].T.astype(LOW)
                    out_ref[c, 2] = grad_v[at].T.astype(LOW)
                for c in range(live, blocks):
                    out_ref[c, 1:] = jnp.zeros_like(out_ref[c, 1:])

        if length is None:
            run(blocks)
        else:
            by_length(len_ref[pl.program_id(0)], blocks * rows, blocks, run)

    block = pl.BlockSpec((None, None, width, rows), lambda o, i, lens: (i, o, 0, 0))
    return pl.pallas_call(
        kernel,
        grid_spec=pltpu.PrefetchScalarGridSpec(
            num_scalar_prefetch=1,
            grid=(objects, blocks),
            in_specs=[
                pl.BlockSpec((None, None, None, width, rows), lambda o, i, lens: (i, o, 0, 0, 0)),
                pl.BlockSpec((blocks, None, None, width, rows), lambda o, i, lens: (0, o, key_at, 0, 0)),
                pl.BlockSpec((blocks, None, None, width, rows), lambda o, i, lens: (0, o, key_at + 1, 0, 0)),
                block,
                block,
                pl.BlockSpec((None, None, 1, rows), lambda o, i, lens: (i, o, 0, 0)),
            ],
            out_specs=pl.BlockSpec((blocks, None, 3, width, rows), lambda o, i, lens: (0, o, 0, 0, 0)),
            scratch_shapes=[
                pltpu.VMEM((blocks * rows, width), LOW),
                pltpu.VMEM((width, blocks * rows), LOW),
                pltpu.VMEM((blocks * rows, width), LOW),
                pltpu.VMEM((blocks * rows, width), WIDE),
                pltpu.VMEM((blocks * rows, width), WIDE),
            ],
        ),
        out_shape=jax.ShapeDtypeStruct((blocks, objects, 3, width, rows), LOW),
        name="pair_backward",
        cost_estimate=estimate(objects * blocks * rows, blocks * rows, 3 if length is None else 2),
        compiler_params=pltpu.CompilerParams(vmem_limit_bytes=VMEM_LIMIT),
    )(lengths, queries, pair, pair, grad_mixed, wide, log_total)


def swap(value, axis):
    return lax.ppermute(value, axis, [(0, 1), (1, 0)])


def sum_near(partial):
    low = partial.astype(LOW)
    return low.astype(WIDE) + swap(low, "near").astype(WIDE)


def tie(value, *others):
    return lax.optimization_barrier((value, *others))


def paired_device(
    tokens,
    cam_index,
    patches,
    patch_len,
    camera_table,
    self_weights,
    self_output,
    cross_gain,
    cross_query,
    cross_pair,
    cross_output,
    patch_weights,
    hidden_gain,
    widen_weights,
    narrow_weights,
    cotangent,
):
    objects = tokens.shape[0] // 2
    _, rows, width = tokens.shape
    cols = self_weights.shape[2]
    hidden = widen_weights.shape[1]
    heads = cols // HEAD_DIM
    codes = camera_table.shape[0]
    patch_width = patches.shape[2]
    count = objects * rows
    n_rows = lax.axis_size("rows")
    row_rank = lax.axis_index("rows")
    far, near = lax.axis_index("far"), lax.axis_index("near")

    def objects_of(value):
        return lax.dynamic_slice_in_dim(value, objects * far, objects, 0)

    def piece(value):
        size = value.shape[0] // n_rows
        return lax.dynamic_slice_in_dim(value, row_rank * size, size, 0)

    def join_rows(value):
        return lax.all_gather(value, "rows", axis=0, tiled=True)

    def both_columns(value):
        return [
            lax.dynamic_slice_in_dim(value, (2 * index + near) * cols, cols, value.ndim - 1)
            for index in range(2)
        ]

    def in_order(mine, away, axis=0):
        size = mine.shape[axis]
        shape = list(mine.shape)
        shape[axis] *= 2
        out = lax.dynamic_update_slice_in_dim(jnp.zeros(shape, mine.dtype), mine, far * size, axis)
        return lax.dynamic_update_slice_in_dim(out, away, (1 - far) * size, axis)

    def halves(value):
        value = value.reshape(objects, 2, rows // 2, -1)
        return [
            lax.dynamic_index_in_dim(value, index, 1, keepdims=False).reshape(count // 2, -1)
            for index in (near, 1 - near)
        ]

    def half_sum_near(partial):
        mine, away = halves(partial)
        return mine + swap(away.astype(LOW), "near").astype(WIDE)

    def over_heads(value):
        value = value.reshape(2, 2, objects, rows // 2, -1)
        value = jnp.where(far == 0, value, jnp.flip(value, 1))
        value = jnp.where(near == 0, value, jnp.flip(value, 0))
        return value.transpose(1, 2, 0, 3, 4).reshape(2 * objects, rows, -1)

    def to_pairs(weights, value, slots):
        parts = [
            mul(weights, value[i * rows : (i + 1) * rows], NT)
            .astype(LOW)
            .reshape(n_rows, slots, HEAD_DIM, rows)
            for i in range(objects)
        ]
        return jnp.stack(parts, axis=1)

    def from_pairs(value):
        return value.transpose(0, 2, 3, 1, 4).reshape(-1, count)

    def over_all_columns(value_t, weight):
        return mul(jnp.concatenate([value_t, swap(value_t, "near")]), weight, TN)

    qkv_rows = self_weights.reshape(3, width, heads, HEAD_DIM).transpose(2, 0, 3, 1)
    qkv_rows = qkv_rows.reshape(3 * cols, width)
    pair_rows = cross_pair.reshape(2, width, heads, HEAD_DIM).transpose(2, 0, 3, 1)
    pair_rows = pair_rows.reshape(2 * cols, width)
    query_rows = cross_query.T

    qkv_away = join_rows(swap(piece(qkv_rows), "far"))

    table_flat = camera_table.reshape(codes, -1)
    cross_gain_f = cross_gain.astype(WIDE)
    hidden_gain_f = hidden_gain.astype(WIDE)

    inputs = objects_of(tokens).reshape(count, width).astype(WIDE)
    patch_in = objects_of(patches).reshape(count, patch_width)
    length = objects_of(patch_len)
    grad_low = objects_of(cotangent).reshape(count, width)
    codes_of = objects_of(cam_index).reshape(count)
    onehot = (codes_of[:, None] == jnp.arange(codes)[None, :]).astype(LOW)
    shift_scale = mul(onehot, table_flat)
    gain_one = 1.0 + shift_scale[:, :width]
    unit_one, rate_one = normed(inputs)
    normed_one = (unit_one * gain_one + shift_scale[:, width:]).astype(LOW)

    mine = [piece(v) for v in (self_output, query_rows, cross_output, pair_rows)]
    normed_one, *mine = tie(normed_one, *mine)
    mine = jnp.concatenate(mine, axis=0)
    across = swap(mine, "far")
    size = cols // n_rows
    two = in_order(mine[None, : 3 * size], across[None, : 3 * size])
    four = jnp.concatenate([two, swap(two, "near")])
    sent = jnp.concatenate([four.reshape(-1, width), across[3 * size :]])
    sent = lax.all_gather(sent, "rows", axis=0)
    pair_away = sent[:, 12 * size :].reshape(2 * cols, width)
    whole = sent[:, : 12 * size].reshape(n_rows, 4, 3, size, width).transpose(2, 1, 0, 3, 4)
    self_whole, query_whole, cross_whole = whole.reshape(3, 4 * cols, width)

    qkv_both = in_order(qkv_rows, qkv_away)
    qkv = exchange_rows(to_pairs(qkv_both, normed_one, 3))
    patch_mid = mul(patch_in, patch_weights).astype(LOW)
    pair_both = in_order(pair_rows, pair_away)
    pair = exchange_rows(to_pairs(pair_both, patch_mid, 2))

    mine = [piece(widen_weights), piece(narrow_weights)]
    qkv, *mine = tie(qkv, *mine)
    size = width // n_rows
    sent = lax.all_gather(jnp.concatenate(mine, axis=0), ("far", "rows"), axis=0)
    sent = sent.reshape(2, n_rows, 2, size, width)
    widen = sent[:, :, 0].reshape(2, width, hidden)
    widen = jnp.concatenate([widen[0], widen[1]], axis=1)
    narrow = sent[:, :, 1].reshape(2 * hidden, width)

    mixed, self_wide, self_log = pair_forward(qkv, qkv, 1)
    self_mixed_t = from_pairs(exchange_rows(mixed)[:, :, None])
    after_self = inputs + over_all_columns(self_mixed_t, self_whole)
    unit_two, rate_two = normed(after_self)
    normed_two = (unit_two * cross_gain_f).astype(LOW)
    cross_q = exchange_rows(to_pairs(query_whole[: 2 * cols], normed_two, 1))
    mixed, cross_wide, cross_log = pair_forward(cross_q, pair, 0, length)
    cross_mixed_t = from_pairs(exchange_rows(mixed)[:, :, None])
    after_cross = after_self + over_all_columns(cross_mixed_t, cross_whole)
    unit_three, rate_three = normed(after_cross)
    normed_three = (unit_three * hidden_gain_f).astype(LOW)
    activated, act_back = jax.vjp(gelu_tanh, mul(normed_three, widen))
    activated = activated.astype(LOW)
    grad_pre = act_back(mul(grad_low, narrow, NT))[0].astype(LOW)
    third, activated, grad_pre = tie(mul(grad_pre, widen, NT).astype(LOW), activated, grad_pre)
    grad_three = third.astype(WIDE) + swap(third, "near").astype(WIDE)
    hidden_half = half_sum_near(mul(activated, narrow))
    result = (halves(after_cross)[0] + hidden_half).astype(LOW)

    def part_rows(both):
        return lax.psum_scatter(both, "rows", scatter_dimension=1, tiled=True)

    def own_and_away(value):
        return [lax.dynamic_index_in_dim(value, index, 0, keepdims=False) for index in (far, 1 - far)]

    def add_far(mine, away):
        return (mine.astype(WIDE) + away.astype(WIDE)).astype(LOW)

    def by_shard(left, right):
        return mul(left, right, NN).astype(LOW).reshape(2, -1, right.shape[1])

    hidden_terms = jnp.concatenate(
        [
            mul(value, against, TN).astype(LOW).reshape(2, hidden, width)
            for value, against in ((activated, grad_low), (grad_pre, normed_three))
        ],
        axis=1,
    )
    hidden_part = lax.psum_scatter(
        hidden_terms.reshape(-1, width), ("far", "rows"), scatter_dimension=0, tiled=True
    )

    hidden_gain_term = jnp.sum(grad_three * unit_three, axis=0)
    grad_cross = grad_low.astype(WIDE) + normed_back(
        grad_three * hidden_gain_f, unit_three, rate_three
    )
    grad_cross_low = grad_cross.astype(LOW)
    grad_mixed, result = tie(to_pairs(cross_whole[: 2 * cols], grad_cross_low, 1)[:, :, 0], result)
    result_two = jnp.stack([result, swap(result, "far")])
    grads = pair_backward(cross_q, pair, 0, length, exchange_rows(grad_mixed), cross_wide, cross_log)
    grads, result_two, hidden_part = tie(grads, result_two, hidden_part)
    result_four = jnp.stack([result_two, swap(result_two, "near")])
    grads = exchange_rows(grads)
    hidden_total = join_rows(hidden_part)
    grad_cq_t = from_pairs(grads[:, :, :1])
    grad_pair_t = from_pairs(grads[:, :, 1:])
    grad_two = over_all_columns(grad_cq_t, query_whole)
    cross_gain_term = jnp.sum(grad_two * unit_two, axis=0)
    grad_self = grad_cross + normed_back(grad_two * cross_gain_f, unit_two, rate_two)
    grad_self_low = grad_self.astype(LOW)
    grad_mid = sum_near(
        mul(grad_pair_t, pair_both, TN)
    ).astype(LOW)
    patch_half = mul(halves(grad_mid)[0], patch_weights, NT).astype(LOW)
    patch_terms = jnp.stack([mul(value, patch_in, TN).astype(LOW) for value in both_columns(grad_mid)])
    patch_terms = jnp.pad(patch_terms, ((0, 0), (0, 0), (0, width - patch_width)))
    middle_part = part_rows(
        jnp.concatenate(
            [
                by_shard(cross_mixed_t, grad_cross_low),
                by_shard(self_mixed_t, grad_self_low),
                by_shard(grad_cq_t, normed_two),
                by_shard(grad_pair_t, patch_mid),
            ],
            axis=1,
        )
    )
    grad_mixed, patch_half = tie(to_pairs(self_whole[: 2 * cols], grad_self_low, 1)[:, :, 0], patch_half)
    patch_two = jnp.stack([patch_half, swap(patch_half, "far")])
    grads = pair_backward(qkv, qkv, 1, None, exchange_rows(grad_mixed), self_wide, self_log)
    grads, patch_two, result_four, hidden_total, middle_part = tie(
        grads, patch_two, result_four, hidden_total, middle_part
    )
    middle_own, middle_away = own_and_away(middle_part)
    patch_four = jnp.stack([patch_two, swap(patch_two, "near")])
    grads, patch_four, middle_away = tie(exchange_rows(grads), patch_four, swap(middle_away, "far"))
    middle_total = join_rows(add_far(middle_own, middle_away))
    grad_qkv_t = from_pairs(grads)
    last_part = part_rows(jnp.concatenate([by_shard(grad_qkv_t, normed_one), patch_terms], axis=1))
    grad_one = half_sum_near(mul(grad_qkv_t, qkv_both, TN))
    gain_half, unit_half, rate_half, self_half = (
        halves(value)[0] for value in (gain_one, unit_one, rate_one, grad_self)
    )
    input_half = self_half + normed_back(grad_one * gain_half, unit_half, rate_half)
    input_half = input_half.astype(LOW)
    onehot_half = halves(onehot)[0].astype(WIDE)
    table_term = jnp.concatenate(
        [
            lax.dot_general(onehot_half, value, TN, precision=lax.Precision.HIGHEST)
            for value in (grad_one * unit_half, grad_one)
        ],
        axis=0,
    )
    small = [sum_near(table_term), hidden_gain_term[None], cross_gain_term[None], jnp.zeros((14, width), WIDE)]
    small = jnp.stack(both_columns(jnp.concatenate(small, axis=0).astype(LOW)))
    small = jnp.sum(lax.all_gather(small, "rows", axis=0).astype(WIDE), axis=0).astype(LOW)
    small_own, small_away = (
        lax.dynamic_index_in_dim(small, index, 0, keepdims=False) for index in (far, 1 - far)
    )
    small = small_own.astype(WIDE) + swap(small_away, "far").astype(WIDE)
    input_half, middle_total = tie(input_half, middle_total)
    input_two = jnp.stack([input_half, swap(input_half, "far")])
    last_part, input_two = tie(last_part, input_two)
    input_grads = over_heads(jnp.stack([input_two, swap(input_two, "near")]))
    outputs, patch_grads = over_heads(result_four), over_heads(patch_four)
    last_own, last_away = own_and_away(last_part)
    last_total = join_rows(add_far(last_own, swap(last_away, "far")))

    output_total = middle_total[: 2 * cols]
    query_total = middle_total[2 * cols : 3 * cols]
    pair_total = middle_total[3 * cols : 5 * cols].reshape(heads, 2, HEAD_DIM, width)
    patch_total = last_total[3 * cols :, :patch_width]
    self_total = last_total[: 3 * cols].reshape(heads, 3, HEAD_DIM, width)
    gradients = (
        small[: 2 * codes].reshape(2, codes, cols).transpose(1, 0, 2),
        self_total.transpose(1, 3, 0, 2).reshape(3, width, cols),
        output_total[cols:],
        small[2 * codes + 1],
        query_total.T,
        pair_total.transpose(1, 3, 0, 2).reshape(2, width, cols),
        output_total[:cols],
        patch_total.T,
        small[2 * codes],
        hidden_total[hidden:].T,
        hidden_total[:hidden],
    )
    return (outputs, input_grads.astype(WIDE), patch_grads.astype(WIDE)) + tuple(
        value.astype(WIDE) for value in gradients
    )


def per_device(
    tokens,
    cam_index,
    patches,
    patch_len,
    camera_table,
    self_weights,
    self_output,
    cross_gain,
    cross_query,
    cross_pair,
    cross_output,
    patch_weights,
    hidden_gain,
    widen_weights,
    narrow_weights,
    cotangent,
):
    batches, rows, width = tokens.shape
    cols = self_weights.shape[2]
    heads = cols // HEAD_DIM
    codes = camera_table.shape[0]
    patch_rows, patch_width = patches.shape[1:]
    n_rows, n_heads = lax.axis_size("rows"), lax.axis_size("heads")
    row_rank, head_rank = lax.axis_index("rows"), lax.axis_index("heads")
    groups = 1
    objects = batches // groups
    full_lengths = jnp.full((objects,), n_rows * rows, jnp.int32)
    count = objects * rows

    def own_columns(value):
        return lax.dynamic_slice_in_dim(value, head_rank * cols, cols, value.ndim - 1)

    table_flat = camera_table.reshape(codes, -1)
    cross_gain_f = cross_gain.astype(WIDE)
    hidden_gain_f = hidden_gain.astype(WIDE)

    qkv_rows = (
        self_weights.reshape(3, width, heads, HEAD_DIM).transpose(2, 0, 3, 1).reshape(3 * cols, width)
    )
    qkv_rows_back = self_weights.transpose(0, 2, 1).reshape(3 * cols, width)
    pair_rows = cross_pair.transpose(0, 2, 1).reshape(2 * cols, width)
    query_rows = cross_query.T

    local = jnp.stack([self_output, cross_output, query_rows])
    piece = cols // n_rows
    local = lax.dynamic_slice_in_dim(local, row_rank * piece, piece, 1)
    whole = lax.all_gather(jnp.stack(gather_heads(local)), "rows", axis=0)
    whole = whole.transpose(2, 1, 0, 3, 4).reshape(3, n_heads * cols, width)
    self_whole, cross_whole, query_whole = whole[0], whole[1], whole[2]

    def over_all_columns(value_t, weight):
        return mul(jnp.concatenate(gather_heads(value_t), axis=0), weight, TN)

    def by_object(weight, value):
        return jnp.stack(
            [mul(weight, value[i * rows : (i + 1) * rows], NT).astype(LOW) for i in range(objects)]
        )

    def column_terms(value, grads_t):
        return [
            mul(value, grads_t[i : i + cols], (((0,), (1,)), ((), ())))
            for i in range(0, grads_t.shape[0], cols)
        ]

    def one_group(group):
        part = slice(group * objects, (group + 1) * objects)
        inputs = tokens[part].reshape(count, width).astype(WIDE)
        patch_in = patches[part].reshape(objects * patch_rows, patch_width)
        lengths = patch_len[part]
        grad_low = cotangent[part].reshape(count, width)
        onehot = (cam_index[part].reshape(count)[:, None] == jnp.arange(codes)[None, :]).astype(LOW)
        shift_scale = mul(onehot, table_flat)
        gain_one = 1.0 + shift_scale[:, :width]
        unit_one, rate_one = normed(inputs)
        normed_one = (unit_one * gain_one + shift_scale[:, width:]).astype(LOW)
        qkv_t = by_object(qkv_rows, normed_one)
        by_kind = qkv_t.reshape(objects, heads, 3, HEAD_DIM, rows).transpose(2, 1, 3, 0, 4)
        by_kind = by_kind.reshape(3, cols, count)
        self_pair = lax.all_gather(by_kind[1:], "rows", axis=0)
        patch_mid = mul(patch_in, patch_weights).astype(LOW)
        own_pair = mul(pair_rows, patch_mid, NT).astype(LOW).reshape(2, cols, -1)
        pair_t = lax.all_gather(own_pair, "rows", axis=0)
        self_mixed_t, self_wide, self_log = cross_forward(by_kind[0], self_pair, full_lengths)
        after_self = inputs + over_all_columns(self_mixed_t, self_whole)
        unit_two, rate_two = normed(after_self)
        normed_two = (unit_two * cross_gain_f).astype(LOW)
        cross_q_t = mul(query_rows, normed_two, NT).astype(LOW)
        cross_mixed_t, cross_wide, cross_log = cross_forward(cross_q_t, pair_t, lengths)
        after_cross = after_self + over_all_columns(cross_mixed_t, cross_whole)
        unit_three, rate_three = normed(after_cross)
        normed_three = (unit_three * hidden_gain_f).astype(LOW)
        pre_act = mul(normed_three, widen_weights)
        activated, act_back = jax.vjp(gelu_tanh, pre_act)
        activated = activated.astype(LOW)
        grad_pre = act_back(mul(grad_low, narrow_weights, NT))[0].astype(LOW)
        grad_three = sum_heads(mul(grad_pre, widen_weights, NT)).astype(WIDE)
        yield "heads", {"hidden": mul(activated, narrow_weights)}
        yield "rows", {
            "narrow": mul(activated, grad_low, TN),
            "widen": mul(normed_three, grad_pre, TN),
        }
        hidden_gain_term = jnp.sum(own_columns(grad_three * unit_three), axis=0)
        grad_cross = grad_low.astype(WIDE) + normed_back(
            grad_three * hidden_gain_f, unit_three, rate_three
        )
        grad_cross_low = grad_cross.astype(LOW)
        cross_output_term = mul(cross_mixed_t, grad_cross_low)
        grad_mixed_t = mul(cross_output, grad_cross_low, NT).astype(LOW)
        grad_cq_t, grad_pair_t = cross_backward(
            cross_q_t, pair_t, lengths, grad_mixed_t, cross_wide, cross_log
        )
        grad_two = over_all_columns(grad_cq_t, query_whole)
        grad_pair_t = lax.psum_scatter(grad_pair_t, "rows", scatter_dimension=0, tiled=False)
        grad_pair_t = grad_pair_t.reshape(2 * cols, -1)
        query_term = mul(normed_two, grad_cq_t, (((0,), (1,)), ((), ())))
        cross_gain_term = jnp.sum(own_columns(grad_two * unit_two), axis=0)
        grad_self = grad_cross + normed_back(grad_two * cross_gain_f, unit_two, rate_two)
        grad_self_low = grad_self.astype(LOW)
        self_output_term = mul(self_mixed_t, grad_self_low)
        yield "heads", {"patch": mul(grad_pair_t, pair_rows, TN)}
        yield "rows", {
            "query": query_term,
            "pair": column_terms(patch_mid, grad_pair_t),
            "cross_output": cross_output_term,
            "self_output": self_output_term,
        }
        grad_self_mixed_t = mul(self_output, grad_self_low, NT).astype(LOW)
        grad_q_t, grad_kv_t = cross_backward(
            by_kind[0], self_pair, full_lengths, grad_self_mixed_t, self_wide, self_log
        )
        grad_kv_t = lax.psum_scatter(grad_kv_t, "rows", scatter_dimension=0, tiled=False)
        grad_qkv_t = jnp.concatenate([grad_q_t[None], grad_kv_t]).reshape(3 * cols, count)
        grad_qkv_t = yield "after", (grad_qkv_t, ["patch", "narrow", "widen"])
        grad_mid = yield "take", "patch"
        patch_term = mul(patch_in, own_columns(grad_mid), TN)
        patch_grad = mul(grad_mid, patch_weights, NT)
        grad_one = sum_heads(mul(grad_qkv_t, qkv_rows_back, TN))
        grad_one = yield "after", (grad_one, ["query", "pair", "cross_output", "self_output"])
        grad_one = grad_one.astype(WIDE)
        input_grad = grad_self + normed_back(grad_one * gain_one, unit_one, rate_one)
        own_grad = own_columns(grad_one)
        table_term = jnp.stack(
            [
                lax.dot_general(onehot.astype(WIDE), v, TN, precision=lax.Precision.HIGHEST)
                for v in (own_grad * own_columns(unit_one), own_grad)
            ],
            axis=1,
        )
        small = [patch_term, table_term.reshape(2 * codes, cols)]
        small += [hidden_gain_term[None], cross_gain_term[None], jnp.zeros((14, cols), WIDE)]
        yield "rows", {
            "self": column_terms(normed_one, grad_qkv_t),
            "small": jnp.concatenate(small, axis=0),
        }
        hidden_sum = yield "take", "hidden"
        result = (after_cross + hidden_sum.astype(WIDE)).astype(LOW)
        yield (
            "done",
            (
                result.reshape(objects, rows, width),
                input_grad.reshape(objects, rows, width),
                patch_grad.reshape(objects, patch_rows, patch_width),
            ),
        )

    steps = [one_group(group) for group in range(groups)]
    asked = [next(step) for step in steps]
    totals, ahead = {}, []
    while asked[0][0] != "done":
        kind, what = asked[0]
        answers = [None] * groups
        if kind == "take":
            answers = jnp.split(totals[what], groups)
        elif kind == "after":
            early = {name: totals[name] for name in what[1]}
            answers = [value for _, (value, _) in asked]
            answers[-1], early = lax.optimization_barrier((answers[-1], early))
            totals.update(early)
        else:
            terms = [value for _, value in asked]
            if kind == "heads":
                terms = jax.tree.map(lambda *parts: jnp.concatenate(parts, axis=0), *terms)
            else:
                for value in terms[1:]:
                    terms[0] = add_trees(terms[0], value)
                terms = terms[0]
            if kind == "rows":
                terms = jax.tree.map(lambda value: value.astype(LOW), terms)
            if kind == "heads":
                totals.update({name: sum_heads(value) for name, value in terms.items()})
            else:
                before = {name: totals[name] for name in ahead}
                terms, before = lax.optimization_barrier((terms, before))
                totals.update(before)
                totals.update(lax.psum(terms, kind))
                ahead = list(terms)
        asked = [step.send(value) for step, value in zip(steps, answers)]
    outputs, input_grads, patch_grads = (
        jnp.concatenate([value[i] for _, value in asked], axis=0) for i in range(3)
    )
    patch_total, table_total, gains = jnp.split(
        totals["small"], [patch_width, patch_width + 2 * codes]
    )
    gradients = (
        table_total.reshape(codes, 2, cols),
        jnp.stack(totals["self"]),
        totals["self_output"],
        gains[1],
        totals["query"],
        jnp.stack(totals["pair"]),
        totals["cross_output"],
        patch_total,
        gains[0],
        totals["widen"],
        totals["narrow"],
    )
    return (outputs, input_grads, patch_grads) + tuple(value.astype(WIDE) for value in gradients)


def solution(mesh):
    sizes = mesh.shape
    paired = sizes["heads"] == 4 and sizes["rows"] == 8
    heads = ("far", "near") if paired else "heads"
    if paired:
        names = (*heads, "rows")
        mesh = jax.sharding.Mesh(mesh.devices.reshape(2, 2, sizes["rows"]), names)
    in_specs = (
        P(None, "rows", None),
        P(None, "rows"),
        P(None, "rows", None),
        P(),
        P(),
        P(None, None, heads),
        P(heads, None),
        P(),
        P(None, heads),
        P(None, None, heads),
        P(heads, None),
        P(),
        P(),
        P(None, heads),
        P(heads, None),
        P(None, "rows", None),
    )
    out_specs = (
        P(None, "rows", None),
        P(None, "rows", None),
        P(None, "rows", None),
        P(None, None, heads),
        P(None, None, heads),
        P(heads, None),
        P(heads),
        P(None, heads),
        P(None, None, heads),
        P(heads, None),
        P(None, heads),
        P(heads),
        P(None, heads),
        P(heads, None),
    )
    return jax.shard_map(
        paired_device if paired else per_device,
        mesh=mesh,
        in_specs=in_specs,
        out_specs=out_specs,
        check_vma=False,
    )
```

```python
import jax
import jax.numpy as jnp
from jax import lax
from jax.experimental import pallas as pl
from jax.experimental.pallas import tpu as pltpu
from jax.sharding import PartitionSpec as P

HEAD_DIM = 64
EPSILON = 1e-05
SCALE = HEAD_DIM ** (-0.5)
LOW = jnp.bfloat16
WIDE = jnp.float32

NN = (((1,), (0,)), ((), ()))
NT = (((1,), (1,)), ((), ()))
TN = (((0,), (0,)), ((), ()))
T_LAST = (((0,), (1,)), ((), ()))


def mul(left, right, dims=NN):
    return lax.dot_general(left, right, dims, preferred_element_type=WIDE)


def load_values(values, block, values_t):
    rows = values_t.shape[1]
    at = slice(block * rows, (block + 1) * rows)
    values[at, :HEAD_DIM] = values_t.T
    values[at, HEAD_DIM:] = jnp.ones((rows, HEAD_DIM), values.dtype)


def attend_block(queries, keys_t, values):
    scores = mul(queries, keys_t)
    peak = jnp.max(scores, axis=1, keepdims=True)
    both = mul(jnp.exp(scores - peak).astype(LOW), values).T
    total = both[HEAD_DIM : HEAD_DIM + 1]
    return both[:HEAD_DIM] / total, peak.T + jnp.log(total)


def attend_block_back(scaled_q, grad_t, keys, keys_t, values, log_total, spread):
    probs = jnp.exp(mul(keys, scaled_q) - log_total)
    grad_scores = (probs * (mul(values, grad_t) - spread)).astype(LOW)
    return (
        (mul(keys_t, grad_scores) * SCALE).astype(LOW),
        mul(grad_scores, scaled_q.T),
        mul(probs.astype(LOW), grad_t.T),
    )


def estimate(rows, cols, passes):
    return pl.CostEstimate(
        flops=int(rows * cols * 1200 * passes), transcendentals=int(rows * cols), bytes_accessed=int(rows * 2048)
    )


VMEM_LIMIT = 48 << 20


def by_length(length, full, blocks, run):
    @pl.when(length * 4 > full)
    def _():
        run(blocks)

    @pl.when(length * 4 <= full)
    def _():
        run(blocks // 4)


def cross_forward(queries_t, pair_t, lengths):
    blocks, _, cols, all_patches = pair_t.shape
    objects = lengths.shape[0]
    heads = cols // HEAD_DIM
    rows, patch_rows = queries_t.shape[1] // objects, all_patches // objects

    def kernel(len_ref, q_ref, pair_ref, mixed_ref, wide_ref, log_ref, keys_t, values):
        queries = (q_ref[...] * LOW(SCALE)).T

        def run(live):
            for c in range(live):
                keys_t[:, c * patch_rows : (c + 1) * patch_rows] = pair_ref[c, 0]
                load_values(values, c, pair_ref[c, 1])
            size = live * patch_rows
            mixed, log_total = attend_block(queries, keys_t[:, :size], values[:size])
            mixed_ref[...] = mixed.astype(LOW)
            wide_ref[...] = mixed
            log_ref[...] = log_total

        by_length(len_ref[pl.program_id(0)], blocks * patch_rows, blocks, run)

    block = pl.BlockSpec((HEAD_DIM, rows), lambda b, j, lens: (j, b))
    return pl.pallas_call(
        kernel,
        grid_spec=pltpu.PrefetchScalarGridSpec(
            num_scalar_prefetch=1,
            grid=(objects, heads),
            in_specs=[
                block,
                pl.BlockSpec((blocks, 2, HEAD_DIM, patch_rows), lambda b, j, lens: (0, 0, j, b)),
            ],
            out_specs=[block, block, pl.BlockSpec((None, 1, rows), lambda b, j, lens: (j, 0, b))],
            scratch_shapes=[
                pltpu.VMEM((HEAD_DIM, blocks * patch_rows), LOW),
                pltpu.VMEM((blocks * patch_rows, 2 * HEAD_DIM), LOW),
            ],
        ),
        out_shape=[
            jax.ShapeDtypeStruct(queries_t.shape, LOW),
            jax.ShapeDtypeStruct(queries_t.shape, WIDE),
            jax.ShapeDtypeStruct((heads, 1, queries_t.shape[1]), WIDE),
        ],
        name="cross_forward",
        cost_estimate=estimate(objects * rows, blocks * patch_rows * heads, 1.4),
        compiler_params=pltpu.CompilerParams(vmem_limit_bytes=VMEM_LIMIT),
    )(lengths, queries_t, pair_t)


def cross_backward(queries_t, pair_t, lengths, grad_t_all, wide, log_total):
    blocks, _, cols, all_patches = pair_t.shape
    objects = lengths.shape[0]
    heads = cols // HEAD_DIM
    rows, patch_rows = queries_t.shape[1] // objects, all_patches // objects

    def kernel(len_ref, q_ref, pair_ref, g_ref, wide_ref, log_ref, out_q, out_pair, keys, keys_t, values):
        grad_t = g_ref[...]
        spread = jnp.sum(grad_t.astype(WIDE) * wide_ref[...], axis=0, keepdims=True)

        def run(live):
            for c in range(live):
                at = slice(c * patch_rows, (c + 1) * patch_rows)
                keys[at] = pair_ref[c, 0].T
                keys_t[:, at] = pair_ref[c, 0]
                values[at] = pair_ref[c, 1].T
            size = live * patch_rows
            out_q[...], grad_k, grad_v = attend_block_back(
                q_ref[...] * LOW(SCALE),
                grad_t,
                keys[:size],
                keys_t[:, :size],
                values[:size],
                log_ref[...],
                spread,
            )
            for c in range(live):
                at = slice(c * patch_rows, (c + 1) * patch_rows)
                out_pair[c, 0] = grad_k[at].T.astype(LOW)
                out_pair[c, 1] = grad_v[at].T.astype(LOW)
            for c in range(live, blocks):
                out_pair[c] = jnp.zeros_like(out_pair[c])

        by_length(len_ref[pl.program_id(0)], blocks * patch_rows, blocks, run)

    block = pl.BlockSpec((HEAD_DIM, rows), lambda b, j, lens: (j, b))
    pair_block = pl.BlockSpec((blocks, 2, HEAD_DIM, patch_rows), lambda b, j, lens: (0, 0, j, b))
    return pl.pallas_call(
        kernel,
        grid_spec=pltpu.PrefetchScalarGridSpec(
            num_scalar_prefetch=1,
            grid=(objects, heads),
            in_specs=[
                block,
                pair_block,
                block,
                block,
                pl.BlockSpec((None, 1, rows), lambda b, j, lens: (j, 0, b)),
            ],
            out_specs=[block, pair_block],
            scratch_shapes=[
                pltpu.VMEM((blocks * patch_rows, HEAD_DIM), LOW),
                pltpu.VMEM((HEAD_DIM, blocks * patch_rows), LOW),
                pltpu.VMEM((blocks * patch_rows, HEAD_DIM), LOW),
            ],
        ),
        out_shape=[
            jax.ShapeDtypeStruct(queries_t.shape, LOW),
            jax.ShapeDtypeStruct(pair_t.shape, LOW),
        ],
        name="cross_backward",
        cost_estimate=estimate(objects * rows, blocks * patch_rows * heads, 2.5),
        compiler_params=pltpu.CompilerParams(vmem_limit_bytes=VMEM_LIMIT),
    )(lengths, queries_t, pair_t, grad_t_all, wide, log_total)


def shift(value, step):
    size = lax.axis_size("heads")
    return lax.ppermute(value, "heads", [((i + step) % size, i) for i in range(size)])


def gather_heads(value):
    size = lax.axis_size("heads")
    if size != 4:
        return [value] + [shift(value, step) for step in range(1, size)]
    after, before = shift(value, 1), shift(value, -1)
    inner = lax.ppermute(after, "heads", [(1, 0), (2, 1)]) + lax.ppermute(before, "heads", [(1, 2), (2, 3)])
    return [value, after, inner, before]


def scatter_heads(partial):
    size, me = lax.axis_size("heads"), lax.axis_index("heads")

    def part(step):
        return lax.dynamic_index_in_dim(partial, (me + step) % size, 0, keepdims=False)

    if size != 4:
        total = part(0)
        for step in range(1, size):
            total = total + shift(part(step).astype(LOW), -step).astype(WIDE)
        return total
    far = part(2).astype(LOW)
    up = lax.ppermute(far, "heads", [(0, 1), (1, 2)]).astype(WIDE)
    down = lax.ppermute(far, "heads", [(2, 1), (3, 2)]).astype(WIDE)
    from_below = shift((part(1) + up).astype(LOW), -1)
    from_above = shift((part(3) + down).astype(LOW), 1)
    return part(0) + from_below.astype(WIDE) + from_above.astype(WIDE)


def in_order(parts):
    size, me = lax.axis_size("heads"), lax.axis_index("heads")
    out = jnp.zeros((size,) + parts[0].shape, parts[0].dtype)
    for step, value in enumerate(parts):
        out = lax.dynamic_update_index_in_dim(out, value, (me + step) % size, 0)
    return out.reshape((-1,) + parts[0].shape[1:])


def sum_heads(partial):
    size = lax.axis_size("heads")
    split = partial.reshape((size, -1) + partial.shape[1:])
    return in_order(gather_heads(scatter_heads(split).astype(LOW)))


def exchange_rows(value):
    return lax.all_to_all(value, "rows", 0, 0, tiled=True)


def normed(value):
    centred = value - jnp.mean(value, axis=-1, keepdims=True)
    rate = lax.rsqrt(jnp.mean(centred * centred, axis=-1, keepdims=True) + EPSILON)
    return centred * rate, rate


def normed_back(grad, unit, rate):
    return rate * (
        grad
        - jnp.mean(grad, axis=-1, keepdims=True)
        - unit * jnp.mean(grad * unit, axis=-1, keepdims=True)
    )


def gelu_tanh(pre_act):
    return jax.nn.gelu(pre_act, approximate=True)


def add_trees(former, latter):
    return jax.tree.map(jnp.add, former, latter)


def pair_forward(queries, pair, key_at, length=None):
    blocks, objects, _, width, rows = queries.shape
    pair_rows = pair.shape[4]
    lengths = jnp.full((objects,), blocks * pair_rows, jnp.int32) if length is None else length

    def kernel(len_ref, q_ref, k_ref, v_ref, mixed_ref, wide_ref, log_ref, keys_t, values):
        def run(live):
            @pl.when(pl.program_id(1) == 0)
            def _():
                for c in range(live):
                    keys_t[:, c * pair_rows : (c + 1) * pair_rows] = k_ref[c]
                    load_values(values, c, v_ref[c])

            size = live * pair_rows
            mixed, log_total = attend_block(
                (q_ref[...] * LOW(SCALE)).T, keys_t[:, :size], values[:size]
            )
            mixed_ref[...] = mixed.astype(LOW)
            wide_ref[...] = mixed
            log_ref[...] = log_total

        if length is None:
            run(blocks)
        else:
            by_length(len_ref[pl.program_id(0)], blocks * pair_rows, blocks, run)

    block = pl.BlockSpec((None, None, width, rows), lambda o, i, lens: (i, o, 0, 0))
    return pl.pallas_call(
        kernel,
        grid_spec=pltpu.PrefetchScalarGridSpec(
            num_scalar_prefetch=1,
            grid=(objects, blocks),
            in_specs=[
                pl.BlockSpec((None, None, None, width, rows), lambda o, i, lens: (i, o, 0, 0, 0)),
                pl.BlockSpec((blocks, None, None, width, pair_rows), lambda o, i, lens: (0, o, key_at, 0, 0)),
                pl.BlockSpec((blocks, None, None, width, pair_rows), lambda o, i, lens: (0, o, key_at + 1, 0, 0)),
            ],
            out_specs=[block, block, pl.BlockSpec((None, None, 1, rows), lambda o, i, lens: (i, o, 0, 0))],
            scratch_shapes=[
                pltpu.VMEM((width, blocks * pair_rows), LOW),
                pltpu.VMEM((blocks * pair_rows, 2 * width), LOW),
            ],
        ),
        out_shape=[
            jax.ShapeDtypeStruct((blocks, objects, width, rows), LOW),
            jax.ShapeDtypeStruct((blocks, objects, width, rows), WIDE),
            jax.ShapeDtypeStruct((blocks, objects, 1, rows), WIDE),
        ],
        name="pair_forward",
        cost_estimate=estimate(objects * blocks * rows, blocks * pair_rows, 2 if length is None else 1.4),
        compiler_params=pltpu.CompilerParams(vmem_limit_bytes=VMEM_LIMIT),
    )(lengths, queries, pair, pair)


def pair_backward(queries, pair, key_at, length, grad_mixed, wide, log_total):
    blocks, objects, _, width, rows = queries.shape
    lengths = jnp.full((objects,), blocks * rows, jnp.int32) if length is None else length

    def kernel(len_ref, q_ref, k_ref, v_ref, g_ref, wide_ref, log_ref, out_ref, keys, keys_t, values, grad_k, grad_v):
        i = pl.program_id(1)

        def run(live):
            size = live * rows

            @pl.when(i == 0)
            def _():
                for c in range(live):
                    at = slice(c * rows, (c + 1) * rows)
                    keys[at] = k_ref[c].T
                    keys_t[:, at] = k_ref[c]
                    values[at] = v_ref[c].T

            grad_t = g_ref[...]
            spread = jnp.sum(grad_t.astype(WIDE) * wide_ref[...], axis=0, keepdims=True)
            out_ref[i, 0], term_k, term_v = attend_block_back(
                q_ref[...] * LOW(SCALE),
                grad_t,
                keys[:size],
                keys_t[:, :size],
                values[:size],
                log_ref[...],
                spread,
            )

            @pl.when(i == 0)
            def _():
                grad_k[:size] = term_k
                grad_v[:size] = term_v

            @pl.when(i > 0)
            def _():
                grad_k[:size] += term_k
                grad_v[:size] += term_v

            @pl.when(i == blocks - 1)
            def _():
                for c in range(live):
                    at = slice(c * rows, (c + 1) * rows)
                    out_ref[c, 1] = grad_k[at].T.astype(LOW)
                    out_ref[c, 2] = grad_v[at].T.astype(LOW)
                for c in range(live, blocks):
                    out_ref[c, 1:] = jnp.zeros_like(out_ref[c, 1:])

        if length is None:
            run(blocks)
        else:
            by_length(len_ref[pl.program_id(0)], blocks * rows, blocks, run)

    block = pl.BlockSpec((None, None, width, rows), lambda o, i, lens: (i, o, 0, 0))
    return pl.pallas_call(
        kernel,
        grid_spec=pltpu.PrefetchScalarGridSpec(
            num_scalar_prefetch=1,
            grid=(objects, blocks),
            in_specs=[
                pl.BlockSpec((None, None, None, width, rows), lambda o, i, lens: (i, o, 0, 0, 0)),
                pl.BlockSpec((blocks, None, None, width, rows), lambda o, i, lens: (0, o, key_at, 0, 0)),
                pl.BlockSpec((blocks, None, None, width, rows), lambda o, i, lens: (0, o, key_at + 1, 0, 0)),
                block,
                block,
                pl.BlockSpec((None, None, 1, rows), lambda o, i, lens: (i, o, 0, 0)),
            ],
            out_specs=pl.BlockSpec((blocks, None, 3, width, rows), lambda o, i, lens: (0, o, 0, 0, 0)),
            scratch_shapes=[
                pltpu.VMEM((blocks * rows, width), LOW),
                pltpu.VMEM((width, blocks * rows), LOW),
                pltpu.VMEM((blocks * rows, width), LOW),
                pltpu.VMEM((blocks * rows, width), WIDE),
                pltpu.VMEM((blocks * rows, width), WIDE),
            ],
        ),
        out_shape=jax.ShapeDtypeStruct((blocks, objects, 3, width, rows), LOW),
        name="pair_backward",
        cost_estimate=estimate(objects * blocks * rows, blocks * rows, 3 if length is None else 2),
        compiler_params=pltpu.CompilerParams(vmem_limit_bytes=VMEM_LIMIT),
    )(lengths, queries, pair, pair, grad_mixed, wide, log_total)


def swap(value, axis):
    return lax.ppermute(value, axis, [(0, 1), (1, 0)])


def sum_near(partial):
    low = partial.astype(LOW)
    return low.astype(WIDE) + swap(low, "near").astype(WIDE)


def tie(value, *others):
    return lax.optimization_barrier((value, *others))


def paired_device(
    tokens,
    cam_index,
    patches,
    patch_len,
    camera_table,
    self_weights,
    self_output,
    cross_gain,
    cross_query,
    cross_pair,
    cross_output,
    patch_weights,
    hidden_gain,
    widen_weights,
    narrow_weights,
    cotangent,
):
    objects = tokens.shape[0] // 2
    _, rows, width = tokens.shape
    cols = self_weights.shape[2]
    hidden = widen_weights.shape[1]
    heads = cols // HEAD_DIM
    codes = camera_table.shape[0]
    patch_width = patches.shape[2]
    count = objects * rows
    n_rows = lax.axis_size("rows")
    row_rank = lax.axis_index("rows")
    far, near = lax.axis_index("far"), lax.axis_index("near")

    def objects_of(value):
        return lax.dynamic_slice_in_dim(value, objects * far, objects, 0)

    def piece(value):
        size = value.shape[0] // n_rows
        return lax.dynamic_slice_in_dim(value, row_rank * size, size, 0)

    def join_rows(value):
        return lax.all_gather(value, "rows", axis=0, tiled=True)

    def both_columns(value):
        return [
            lax.dynamic_slice_in_dim(value, (2 * index + near) * cols, cols, value.ndim - 1)
            for index in range(2)
        ]

    def in_order(mine, away, axis=0):
        size = mine.shape[axis]
        shape = list(mine.shape)
        shape[axis] *= 2
        out = lax.dynamic_update_slice_in_dim(jnp.zeros(shape, mine.dtype), mine, far * size, axis)
        return lax.dynamic_update_slice_in_dim(out, away, (1 - far) * size, axis)

    def halves(value):
        value = value.reshape(objects, 2, rows // 2, -1)
        return [
            lax.dynamic_index_in_dim(value, index, 1, keepdims=False).reshape(count // 2, -1)
            for index in (near, 1 - near)
        ]

    def half_sum_near(partial):
        mine, away = halves(partial)
        return mine + swap(away.astype(LOW), "near").astype(WIDE)

    def over_heads(value):
        value = value.reshape(2, 2, objects, rows // 2, -1)
        value = jnp.where(far == 0, value, jnp.flip(value, 1))
        value = jnp.where(near == 0, value, jnp.flip(value, 0))
        return value.transpose(1, 2, 0, 3, 4).reshape(2 * objects, rows, -1)

    def to_pairs(weights, value, slots):
        parts = [
            mul(weights, value[i * rows : (i + 1) * rows], NT)
            .astype(LOW)
            .reshape(n_rows, slots, HEAD_DIM, rows)
            for i in range(objects)
        ]
        return jnp.stack(parts, axis=1)

    def from_pairs(value):
        return value.transpose(0, 2, 3, 1, 4).reshape(-1, count)

    def over_all_columns(value_t, weight):
        return mul(jnp.concatenate([value_t, swap(value_t, "near")]), weight, TN)

    qkv_rows = self_weights.reshape(3, width, heads, HEAD_DIM).transpose(2, 0, 3, 1)
    qkv_rows = qkv_rows.reshape(3 * cols, width)
    pair_rows = cross_pair.reshape(2, width, heads, HEAD_DIM).transpose(2, 0, 3, 1)
    pair_rows = pair_rows.reshape(2 * cols, width)
    query_rows = cross_query.T

    qkv_away = join_rows(swap(piece(qkv_rows), "far"))

    table_flat = camera_table.reshape(codes, -1)
    cross_gain_f = cross_gain.astype(WIDE)
    hidden_gain_f = hidden_gain.astype(WIDE)

    inputs = objects_of(tokens).reshape(count, width).astype(WIDE)
    patch_in = objects_of(patches).reshape(count, patch_width)
    length = objects_of(patch_len)
    grad_low = objects_of(cotangent).reshape(count, width)
    codes_of = objects_of(cam_index).reshape(count)
    onehot = (codes_of[:, None] == jnp.arange(codes)[None, :]).astype(LOW)
    shift_scale = mul(onehot, table_flat)
    gain_one = 1.0 + shift_scale[:, :width]
    unit_one, rate_one = normed(inputs)
    normed_one = (unit_one * gain_one + shift_scale[:, width:]).astype(LOW)

    mine = [piece(v) for v in (self_output, query_rows, cross_output, pair_rows)]
    normed_one, *mine = tie(normed_one, *mine)
    mine = jnp.concatenate(mine, axis=0)
    across = swap(mine, "far")
    size = cols // n_rows
    two = in_order(mine[None, : 3 * size], across[None, : 3 * size])
    four = jnp.concatenate([two, swap(two, "near")])
    sent = jnp.concatenate([four.reshape(-1, width), across[3 * size :]])
    sent = lax.all_gather(sent, "rows", axis=0)
    pair_away = sent[:, 12 * size :].reshape(2 * cols, width)
    whole = sent[:, : 12 * size].reshape(n_rows, 4, 3, size, width).transpose(2, 1, 0, 3, 4)
    self_whole, query_whole, cross_whole = whole.reshape(3, 4 * cols, width)

    qkv_both = in_order(qkv_rows, qkv_away)
    qkv = exchange_rows(to_pairs(qkv_both, normed_one, 3))
    patch_mid = mul(patch_in, patch_weights).astype(LOW)
    pair_both = in_order(pair_rows, pair_away)
    pair = exchange_rows(to_pairs(pair_both, patch_mid, 2))

    mine = [piece(widen_weights), piece(narrow_weights)]
    qkv, *mine = tie(qkv, *mine)
    size = width // n_rows
    sent = lax.all_gather(jnp.concatenate(mine, axis=0), ("far", "rows"), axis=0)
    sent = sent.reshape(2, n_rows, 2, size, width)
    widen = sent[:, :, 0].reshape(2, width, hidden)
    widen = jnp.concatenate([widen[0], widen[1]], axis=1)
    narrow = sent[:, :, 1].reshape(2 * hidden, width)

    mixed, self_wide, self_log = pair_forward(qkv, qkv, 1)
    self_mixed_t = from_pairs(exchange_rows(mixed)[:, :, None])
    after_self = inputs + over_all_columns(self_mixed_t, self_whole)
    unit_two, rate_two = normed(after_self)
    normed_two = (unit_two * cross_gain_f).astype(LOW)
    cross_q = exchange_rows(to_pairs(query_whole[: 2 * cols], normed_two, 1))
    mixed, cross_wide, cross_log = pair_forward(cross_q, pair, 0, length)
    cross_mixed_t = from_pairs(exchange_rows(mixed)[:, :, None])
    after_cross = after_self + over_all_columns(cross_mixed_t, cross_whole)
    unit_three, rate_three = normed(after_cross)
    normed_three = (unit_three * hidden_gain_f).astype(LOW)
    activated, act_back = jax.vjp(gelu_tanh, mul(normed_three, widen))
    activated = activated.astype(LOW)
    grad_pre = act_back(mul(grad_low, narrow, NT))[0].astype(LOW)
    third, activated, grad_pre = tie(mul(grad_pre, widen, NT).astype(LOW), activated, grad_pre)
    grad_three = third.astype(WIDE) + swap(third, "near").astype(WIDE)
    hidden_mine, hidden_away = halves(mul(activated, narrow))
    hidden_away, grad_three = tie(hidden_away.astype(LOW), grad_three)
    hidden_half = hidden_mine + swap(hidden_away, "near").astype(WIDE)
    result = (halves(after_cross)[0] + hidden_half).astype(LOW)

    def part_rows(both):
        return lax.psum_scatter(both, "rows", scatter_dimension=1, tiled=True)

    def own_and_away(value):
        return [lax.dynamic_index_in_dim(value, index, 0, keepdims=False) for index in (far, 1 - far)]

    def add_far(mine, away):
        return (mine.astype(WIDE) + away.astype(WIDE)).astype(LOW)

    def by_shard(left, right):
        return mul(left, right, NN).astype(LOW).reshape(2, -1, right.shape[1])

    hidden_terms = jnp.concatenate(
        [
            mul(value, against, TN).astype(LOW).reshape(2, hidden, width)
            for value, against in ((activated, grad_low), (grad_pre, normed_three))
        ],
        axis=1,
    )
    hidden_part = lax.psum_scatter(
        hidden_terms.reshape(-1, width), ("far", "rows"), scatter_dimension=0, tiled=True
    )

    hidden_gain_term = jnp.sum(grad_three * unit_three, axis=0)
    grad_cross = grad_low.astype(WIDE) + normed_back(
        grad_three * hidden_gain_f, unit_three, rate_three
    )
    grad_cross_low = grad_cross.astype(LOW)
    grad_mixed = exchange_rows(to_pairs(cross_whole[: 2 * cols], grad_cross_low, 1)[:, :, 0])
    grad_mixed, result = tie(grad_mixed, result)
    result_two = jnp.stack([result, swap(result, "far")])
    grads = pair_backward(cross_q, pair, 0, length, grad_mixed, cross_wide, cross_log)
    grads, result_two = tie(grads, result_two)
    result_four = jnp.stack([result_two, swap(result_two, "near")])
    grads, result_four, hidden_part = tie(exchange_rows(grads), result_four, hidden_part)
    hidden_total = join_rows(hidden_part)
    grad_cq_t = from_pairs(grads[:, :, :1])
    grad_pair_t = from_pairs(grads[:, :, 1:])
    grad_two = over_all_columns(grad_cq_t, query_whole)
    cross_gain_term = jnp.sum(grad_two * unit_two, axis=0)
    grad_self = grad_cross + normed_back(grad_two * cross_gain_f, unit_two, rate_two)
    grad_self_low = grad_self.astype(LOW)
    grad_mid = sum_near(
        mul(grad_pair_t, pair_both, TN)
    ).astype(LOW)
    patch_half = mul(halves(grad_mid)[0], patch_weights, NT).astype(LOW)
    patch_terms = jnp.stack([mul(value, patch_in, TN).astype(LOW) for value in both_columns(grad_mid)])
    patch_terms = jnp.pad(patch_terms, ((0, 0), (0, 0), (0, width - patch_width)))
    grad_mixed, grad_self_low = tie(to_pairs(self_whole[: 2 * cols], grad_self_low, 1)[:, :, 0], grad_self_low)
    middle_part = part_rows(
        jnp.concatenate(
            [
                by_shard(cross_mixed_t, grad_cross_low),
                by_shard(self_mixed_t, grad_self_low),
                by_shard(grad_cq_t, normed_two),
                by_shard(grad_pair_t, patch_mid),
            ],
            axis=1,
        )
    )
    grad_mixed, patch_half = tie(exchange_rows(grad_mixed), patch_half)
    patch_two = jnp.stack([patch_half, swap(patch_half, "far")])
    grads = pair_backward(qkv, qkv, 1, None, grad_mixed, self_wide, self_log)
    grads, patch_two, hidden_total, middle_part = tie(grads, patch_two, hidden_total, middle_part)
    middle_own, middle_away = own_and_away(middle_part)
    patch_four = jnp.stack([patch_two, swap(patch_two, "near")])
    grads, patch_four, middle_away = tie(exchange_rows(grads), patch_four, swap(middle_away, "far"))
    grad_qkv_t = from_pairs(grads)
    last_terms = jnp.concatenate([by_shard(grad_qkv_t, normed_one), patch_terms], axis=1)
    last_part = part_rows(last_terms)
    grad_one = half_sum_near(mul(grad_qkv_t, qkv_both, TN))
    grad_one, middle_own = tie(grad_one, middle_own)
    middle_total = join_rows(add_far(middle_own, middle_away))
    gain_half, unit_half, rate_half, self_half = (
        halves(value)[0] for value in (gain_one, unit_one, rate_one, grad_self)
    )
    input_half = self_half + normed_back(grad_one * gain_half, unit_half, rate_half)
    input_half = input_half.astype(LOW)
    onehot_half = halves(onehot)[0].astype(WIDE)
    table_term = jnp.concatenate(
        [
            lax.dot_general(onehot_half, value, TN, precision=lax.Precision.HIGHEST)
            for value in (grad_one * unit_half, grad_one)
        ],
        axis=0,
    )
    small = [sum_near(table_term), hidden_gain_term[None], cross_gain_term[None], jnp.zeros((14, width), WIDE)]
    small = jnp.stack(both_columns(jnp.concatenate(small, axis=0).astype(LOW)))
    small = jnp.sum(lax.all_gather(small, "rows", axis=0).astype(WIDE), axis=0).astype(LOW)
    small_own, small_away = (
        lax.dynamic_index_in_dim(small, index, 0, keepdims=False) for index in (far, 1 - far)
    )
    small = small_own.astype(WIDE) + swap(small_away, "far").astype(WIDE)
    input_two = jnp.stack([input_half, swap(input_half, "far")])
    last_part, input_two = tie(last_part, input_two)
    input_grads = over_heads(jnp.stack([input_two, swap(input_two, "near")]))
    outputs, patch_grads = over_heads(result_four), over_heads(patch_four)
    last_own, last_away = own_and_away(last_part)
    last_total = join_rows(add_far(last_own, swap(last_away, "far")))

    output_total = middle_total[: 2 * cols]
    query_total = middle_total[2 * cols : 3 * cols]
    pair_total = middle_total[3 * cols : 5 * cols].reshape(heads, 2, HEAD_DIM, width)
    patch_total = last_total[3 * cols :, :patch_width]
    self_total = last_total[: 3 * cols].reshape(heads, 3, HEAD_DIM, width)
    gradients = (
        small[: 2 * codes].reshape(2, codes, cols).transpose(1, 0, 2),
        self_total.transpose(1, 3, 0, 2).reshape(3, width, cols),
        output_total[cols:],
        small[2 * codes + 1],
        query_total.T,
        pair_total.transpose(1, 3, 0, 2).reshape(2, width, cols),
        output_total[:cols],
        patch_total.T,
        small[2 * codes],
        hidden_total[hidden:].T,
        hidden_total[:hidden],
    )
    return (outputs, input_grads.astype(WIDE), patch_grads.astype(WIDE)) + tuple(
        value.astype(WIDE) for value in gradients
    )


def per_device(
    tokens,
    cam_index,
    patches,
    patch_len,
    camera_table,
    self_weights,
    self_output,
    cross_gain,
    cross_query,
    cross_pair,
    cross_output,
    patch_weights,
    hidden_gain,
    widen_weights,
    narrow_weights,
    cotangent,
):
    batches, rows, width = tokens.shape
    cols = self_weights.shape[2]
    heads = cols // HEAD_DIM
    codes = camera_table.shape[0]
    patch_rows, patch_width = patches.shape[1:]
    n_rows, n_heads = lax.axis_size("rows"), lax.axis_size("heads")
    row_rank, head_rank = lax.axis_index("rows"), lax.axis_index("heads")
    groups = 1
    objects = batches // groups
    full_lengths = jnp.full((objects,), n_rows * rows, jnp.int32)
    count = objects * rows

    def own_columns(value):
        return lax.dynamic_slice_in_dim(value, head_rank * cols, cols, value.ndim - 1)

    table_flat = camera_table.reshape(codes, -1)
    cross_gain_f = cross_gain.astype(WIDE)
    hidden_gain_f = hidden_gain.astype(WIDE)

    qkv_rows = (
        self_weights.reshape(3, width, heads, HEAD_DIM).transpose(2, 0, 3, 1).reshape(3 * cols, width)
    )
    qkv_rows_back = self_weights.transpose(0, 2, 1).reshape(3 * cols, width)
    pair_rows = cross_pair.transpose(0, 2, 1).reshape(2 * cols, width)
    query_rows = cross_query.T

    local = jnp.stack([self_output, cross_output, query_rows])
    piece = cols // n_rows
    local = lax.dynamic_slice_in_dim(local, row_rank * piece, piece, 1)
    whole = lax.all_gather(jnp.stack(gather_heads(local)), "rows", axis=0)
    whole = whole.transpose(2, 1, 0, 3, 4).reshape(3, n_heads * cols, width)
    self_whole, cross_whole, query_whole = whole[0], whole[1], whole[2]

    def over_all_columns(value_t, weight):
        return mul(jnp.concatenate(gather_heads(value_t), axis=0), weight, TN)

    def by_object(weight, value):
        return jnp.stack(
            [mul(weight, value[i * rows : (i + 1) * rows], NT).astype(LOW) for i in range(objects)]
        )

    def column_terms(value, grads_t):
        return [
            mul(value, grads_t[i : i + cols], (((0,), (1,)), ((), ())))
            for i in range(0, grads_t.shape[0], cols)
        ]

    def one_group(group):
        part = slice(group * objects, (group + 1) * objects)
        inputs = tokens[part].reshape(count, width).astype(WIDE)
        patch_in = patches[part].reshape(objects * patch_rows, patch_width)
        lengths = patch_len[part]
        grad_low = cotangent[part].reshape(count, width)
        onehot = (cam_index[part].reshape(count)[:, None] == jnp.arange(codes)[None, :]).astype(LOW)
        shift_scale = mul(onehot, table_flat)
        gain_one = 1.0 + shift_scale[:, :width]
        unit_one, rate_one = normed(inputs)
        normed_one = (unit_one * gain_one + shift_scale[:, width:]).astype(LOW)
        qkv_t = by_object(qkv_rows, normed_one)
        by_kind = qkv_t.reshape(objects, heads, 3, HEAD_DIM, rows).transpose(2, 1, 3, 0, 4)
        by_kind = by_kind.reshape(3, cols, count)
        self_pair = lax.all_gather(by_kind[1:], "rows", axis=0)
        patch_mid = mul(patch_in, patch_weights).astype(LOW)
        own_pair = mul(pair_rows, patch_mid, NT).astype(LOW).reshape(2, cols, -1)
        pair_t = lax.all_gather(own_pair, "rows", axis=0)
        self_mixed_t, self_wide, self_log = cross_forward(by_kind[0], self_pair, full_lengths)
        after_self = inputs + over_all_columns(self_mixed_t, self_whole)
        unit_two, rate_two = normed(after_self)
        normed_two = (unit_two * cross_gain_f).astype(LOW)
        cross_q_t = mul(query_rows, normed_two, NT).astype(LOW)
        cross_mixed_t, cross_wide, cross_log = cross_forward(cross_q_t, pair_t, lengths)
        after_cross = after_self + over_all_columns(cross_mixed_t, cross_whole)
        unit_three, rate_three = normed(after_cross)
        normed_three = (unit_three * hidden_gain_f).astype(LOW)
        pre_act = mul(normed_three, widen_weights)
        activated, act_back = jax.vjp(gelu_tanh, pre_act)
        activated = activated.astype(LOW)
        grad_pre = act_back(mul(grad_low, narrow_weights, NT))[0].astype(LOW)
        grad_three = sum_heads(mul(grad_pre, widen_weights, NT)).astype(WIDE)
        yield "heads", {"hidden": mul(activated, narrow_weights)}
        yield "rows", {
            "narrow": mul(activated, grad_low, TN),
            "widen": mul(normed_three, grad_pre, TN),
        }
        hidden_gain_term = jnp.sum(own_columns(grad_three * unit_three), axis=0)
        grad_cross = grad_low.astype(WIDE) + normed_back(
            grad_three * hidden_gain_f, unit_three, rate_three
        )
        grad_cross_low = grad_cross.astype(LOW)
        cross_output_term = mul(cross_mixed_t, grad_cross_low)
        grad_mixed_t = mul(cross_output, grad_cross_low, NT).astype(LOW)
        grad_cq_t, grad_pair_t = cross_backward(
            cross_q_t, pair_t, lengths, grad_mixed_t, cross_wide, cross_log
        )
        grad_two = over_all_columns(grad_cq_t, query_whole)
        grad_pair_t = lax.psum_scatter(grad_pair_t, "rows", scatter_dimension=0, tiled=False)
        grad_pair_t = grad_pair_t.reshape(2 * cols, -1)
        query_term = mul(normed_two, grad_cq_t, (((0,), (1,)), ((), ())))
        cross_gain_term = jnp.sum(own_columns(grad_two * unit_two), axis=0)
        grad_self = grad_cross + normed_back(grad_two * cross_gain_f, unit_two, rate_two)
        grad_self_low = grad_self.astype(LOW)
        self_output_term = mul(self_mixed_t, grad_self_low)
        yield "heads", {"patch": mul(grad_pair_t, pair_rows, TN)}
        yield "rows", {
            "query": query_term,
            "pair": column_terms(patch_mid, grad_pair_t),
            "cross_output": cross_output_term,
            "self_output": self_output_term,
        }
        grad_self_mixed_t = mul(self_output, grad_self_low, NT).astype(LOW)
        grad_q_t, grad_kv_t = cross_backward(
            by_kind[0], self_pair, full_lengths, grad_self_mixed_t, self_wide, self_log
        )
        grad_kv_t = lax.psum_scatter(grad_kv_t, "rows", scatter_dimension=0, tiled=False)
        grad_qkv_t = jnp.concatenate([grad_q_t[None], grad_kv_t]).reshape(3 * cols, count)
        grad_qkv_t = yield "after", (grad_qkv_t, ["patch", "narrow", "widen"])
        grad_mid = yield "take", "patch"
        patch_term = mul(patch_in, own_columns(grad_mid), TN)
        patch_grad = mul(grad_mid, patch_weights, NT)
        grad_one = sum_heads(mul(grad_qkv_t, qkv_rows_back, TN))
        grad_one = yield "after", (grad_one, ["query", "pair", "cross_output", "self_output"])
        grad_one = grad_one.astype(WIDE)
        input_grad = grad_self + normed_back(grad_one * gain_one, unit_one, rate_one)
        own_grad = own_columns(grad_one)
        table_term = jnp.stack(
            [
                lax.dot_general(onehot.astype(WIDE), v, TN, precision=lax.Precision.HIGHEST)
                for v in (own_grad * own_columns(unit_one), own_grad)
            ],
            axis=1,
        )
        small = [patch_term, table_term.reshape(2 * codes, cols)]
        small += [hidden_gain_term[None], cross_gain_term[None], jnp.zeros((14, cols), WIDE)]
        yield "rows", {
            "self": column_terms(normed_one, grad_qkv_t),
            "small": jnp.concatenate(small, axis=0),
        }
        hidden_sum = yield "take", "hidden"
        result = (after_cross + hidden_sum.astype(WIDE)).astype(LOW)
        yield (
            "done",
            (
                result.reshape(objects, rows, width),
                input_grad.reshape(objects, rows, width),
                patch_grad.reshape(objects, patch_rows, patch_width),
            ),
        )

    steps = [one_group(group) for group in range(groups)]
    asked = [next(step) for step in steps]
    totals, ahead = {}, []
    while asked[0][0] != "done":
        kind, what = asked[0]
        answers = [None] * groups
        if kind == "take":
            answers = jnp.split(totals[what], groups)
        elif kind == "after":
            early = {name: totals[name] for name in what[1]}
            answers = [value for _, (value, _) in asked]
            answers[-1], early = lax.optimization_barrier((answers[-1], early))
            totals.update(early)
        else:
            terms = [value for _, value in asked]
            if kind == "heads":
                terms = jax.tree.map(lambda *parts: jnp.concatenate(parts, axis=0), *terms)
            else:
                for value in terms[1:]:
                    terms[0] = add_trees(terms[0], value)
                terms = terms[0]
            if kind == "rows":
                terms = jax.tree.map(lambda value: value.astype(LOW), terms)
            if kind == "heads":
                totals.update({name: sum_heads(value) for name, value in terms.items()})
            else:
                before = {name: totals[name] for name in ahead}
                terms, before = lax.optimization_barrier((terms, before))
                totals.update(before)
                totals.update(lax.psum(terms, kind))
                ahead = list(terms)
        asked = [step.send(value) for step, value in zip(steps, answers)]
    outputs, input_grads, patch_grads = (
        jnp.concatenate([value[i] for _, value in asked], axis=0) for i in range(3)
    )
    patch_total, table_total, gains = jnp.split(
        totals["small"], [patch_width, patch_width + 2 * codes]
    )
    gradients = (
        table_total.reshape(codes, 2, cols),
        jnp.stack(totals["self"]),
        totals["self_output"],
        gains[1],
        totals["query"],
        jnp.stack(totals["pair"]),
        totals["cross_output"],
        patch_total,
        gains[0],
        totals["widen"],
        totals["narrow"],
    )
    return (outputs, input_grads, patch_grads) + tuple(value.astype(WIDE) for value in gradients)


def solution(mesh):
    sizes = mesh.shape
    paired = sizes["heads"] == 4 and sizes["rows"] == 8
    heads = ("far", "near") if paired else "heads"
    if paired:
        names = (*heads, "rows")
        mesh = jax.sharding.Mesh(mesh.devices.reshape(2, 2, sizes["rows"]), names)
    in_specs = (
        P(None, "rows", None),
        P(None, "rows"),
        P(None, "rows", None),
        P(),
        P(),
        P(None, None, heads),
        P(heads, None),
        P(),
        P(None, heads),
        P(None, None, heads),
        P(heads, None),
        P(),
        P(),
        P(None, heads),
        P(heads, None),
        P(None, "rows", None),
    )
    out_specs = (
        P(None, "rows", None),
        P(None, "rows", None),
        P(None, "rows", None),
        P(None, None, heads),
        P(None, None, heads),
        P(heads, None),
        P(heads),
        P(None, heads),
        P(None, None, heads),
        P(heads, None),
        P(None, heads),
        P(heads),
        P(None, heads),
        P(heads, None),
    )
    return jax.shard_map(
        paired_device if paired else per_device,
        mesh=mesh,
        in_specs=in_specs,
        out_specs=out_specs,
        check_vma=False,
    )
```

```python
import jax
import jax.numpy as jnp
from jax import lax
from jax.experimental import pallas as pl
from jax.experimental.pallas import tpu as pltpu
from jax.sharding import PartitionSpec as P

HEAD_DIM = 64
EPSILON = 1e-05
SCALE = HEAD_DIM ** (-0.5)
LOW = jnp.bfloat16
WIDE = jnp.float32

NN = (((1,), (0,)), ((), ()))
NT = (((1,), (1,)), ((), ()))
TN = (((0,), (0,)), ((), ()))
T_LAST = (((0,), (1,)), ((), ()))


def mul(left, right, dims=NN):
    return lax.dot_general(left, right, dims, preferred_element_type=WIDE)


def load_values(values, block, values_t):
    rows = values_t.shape[1]
    at = slice(block * rows, (block + 1) * rows)
    values[at, :HEAD_DIM] = values_t.T
    values[at, HEAD_DIM:] = jnp.ones((rows, HEAD_DIM), values.dtype)


def attend_block(queries, keys_t, values):
    scores = mul(queries, keys_t)
    peak = jnp.max(scores, axis=1, keepdims=True)
    both = mul(jnp.exp(scores - peak).astype(LOW), values).T
    total = both[HEAD_DIM : HEAD_DIM + 1]
    return both[:HEAD_DIM] / total, peak.T + jnp.log(total)


def attend_block_back(scaled_q, grad_t, keys, keys_t, values, log_total, spread):
    probs = jnp.exp(mul(keys, scaled_q) - log_total)
    grad_scores = (probs * (mul(values, grad_t) - spread)).astype(LOW)
    return (
        (mul(keys_t, grad_scores) * SCALE).astype(LOW),
        mul(grad_scores, scaled_q.T),
        mul(probs.astype(LOW), grad_t.T),
    )


def estimate(rows, cols, passes):
    return pl.CostEstimate(
        flops=int(rows * cols * 1200 * passes), transcendentals=int(rows * cols), bytes_accessed=int(rows * 2048)
    )


VMEM_LIMIT = 48 << 20


def by_length(length, full, blocks, run):
    @pl.when(length * 4 > full)
    def _():
        run(blocks)

    @pl.when(length * 4 <= full)
    def _():
        run(blocks // 4)


def cross_forward(queries_t, pair_t, lengths):
    blocks, _, cols, all_patches = pair_t.shape
    objects = lengths.shape[0]
    heads = cols // HEAD_DIM
    rows, patch_rows = queries_t.shape[1] // objects, all_patches // objects

    def kernel(len_ref, q_ref, pair_ref, mixed_ref, wide_ref, log_ref, keys_t, values):
        queries = (q_ref[...] * LOW(SCALE)).T

        def run(live):
            for c in range(live):
                keys_t[:, c * patch_rows : (c + 1) * patch_rows] = pair_ref[c, 0]
                load_values(values, c, pair_ref[c, 1])
            size = live * patch_rows
            mixed, log_total = attend_block(queries, keys_t[:, :size], values[:size])
            mixed_ref[...] = mixed.astype(LOW)
            wide_ref[...] = mixed
            log_ref[...] = log_total

        by_length(len_ref[pl.program_id(0)], blocks * patch_rows, blocks, run)

    block = pl.BlockSpec((HEAD_DIM, rows), lambda b, j, lens: (j, b))
    return pl.pallas_call(
        kernel,
        grid_spec=pltpu.PrefetchScalarGridSpec(
            num_scalar_prefetch=1,
            grid=(objects, heads),
            in_specs=[
                block,
                pl.BlockSpec((blocks, 2, HEAD_DIM, patch_rows), lambda b, j, lens: (0, 0, j, b)),
            ],
            out_specs=[block, block, pl.BlockSpec((None, 1, rows), lambda b, j, lens: (j, 0, b))],
            scratch_shapes=[
                pltpu.VMEM((HEAD_DIM, blocks * patch_rows), LOW),
                pltpu.VMEM((blocks * patch_rows, 2 * HEAD_DIM), LOW),
            ],
        ),
        out_shape=[
            jax.ShapeDtypeStruct(queries_t.shape, LOW),
            jax.ShapeDtypeStruct(queries_t.shape, WIDE),
            jax.ShapeDtypeStruct((heads, 1, queries_t.shape[1]), WIDE),
        ],
        name="cross_forward",
        cost_estimate=estimate(objects * rows, blocks * patch_rows * heads, 1.4),
        compiler_params=pltpu.CompilerParams(vmem_limit_bytes=VMEM_LIMIT),
    )(lengths, queries_t, pair_t)


def cross_backward(queries_t, pair_t, lengths, grad_t_all, wide, log_total):
    blocks, _, cols, all_patches = pair_t.shape
    objects = lengths.shape[0]
    heads = cols // HEAD_DIM
    rows, patch_rows = queries_t.shape[1] // objects, all_patches // objects

    def kernel(len_ref, q_ref, pair_ref, g_ref, wide_ref, log_ref, out_q, out_pair, keys, keys_t, values):
        grad_t = g_ref[...]
        spread = jnp.sum(grad_t.astype(WIDE) * wide_ref[...], axis=0, keepdims=True)

        def run(live):
            for c in range(live):
                at = slice(c * patch_rows, (c + 1) * patch_rows)
                keys[at] = pair_ref[c, 0].T
                keys_t[:, at] = pair_ref[c, 0]
                values[at] = pair_ref[c, 1].T
            size = live * patch_rows
            out_q[...], grad_k, grad_v = attend_block_back(
                q_ref[...] * LOW(SCALE),
                grad_t,
                keys[:size],
                keys_t[:, :size],
                values[:size],
                log_ref[...],
                spread,
            )
            for c in range(live):
                at = slice(c * patch_rows, (c + 1) * patch_rows)
                out_pair[c, 0] = grad_k[at].T.astype(LOW)
                out_pair[c, 1] = grad_v[at].T.astype(LOW)
            for c in range(live, blocks):
                out_pair[c] = jnp.zeros_like(out_pair[c])

        by_length(len_ref[pl.program_id(0)], blocks * patch_rows, blocks, run)

    block = pl.BlockSpec((HEAD_DIM, rows), lambda b, j, lens: (j, b))
    pair_block = pl.BlockSpec((blocks, 2, HEAD_DIM, patch_rows), lambda b, j, lens: (0, 0, j, b))
    return pl.pallas_call(
        kernel,
        grid_spec=pltpu.PrefetchScalarGridSpec(
            num_scalar_prefetch=1,
            grid=(objects, heads),
            in_specs=[
                block,
                pair_block,
                block,
                block,
                pl.BlockSpec((None, 1, rows), lambda b, j, lens: (j, 0, b)),
            ],
            out_specs=[block, pair_block],
            scratch_shapes=[
                pltpu.VMEM((blocks * patch_rows, HEAD_DIM), LOW),
                pltpu.VMEM((HEAD_DIM, blocks * patch_rows), LOW),
                pltpu.VMEM((blocks * patch_rows, HEAD_DIM), LOW),
            ],
        ),
        out_shape=[
            jax.ShapeDtypeStruct(queries_t.shape, LOW),
            jax.ShapeDtypeStruct(pair_t.shape, LOW),
        ],
        name="cross_backward",
        cost_estimate=estimate(objects * rows, blocks * patch_rows * heads, 2.5),
        compiler_params=pltpu.CompilerParams(vmem_limit_bytes=VMEM_LIMIT),
    )(lengths, queries_t, pair_t, grad_t_all, wide, log_total)


def shift(value, step):
    size = lax.axis_size("heads")
    return lax.ppermute(value, "heads", [((i + step) % size, i) for i in range(size)])


def gather_heads(value):
    size = lax.axis_size("heads")
    if size != 4:
        return [value] + [shift(value, step) for step in range(1, size)]
    after, before = shift(value, 1), shift(value, -1)
    inner = lax.ppermute(after, "heads", [(1, 0), (2, 1)]) + lax.ppermute(before, "heads", [(1, 2), (2, 3)])
    return [value, after, inner, before]


def scatter_heads(partial):
    size, me = lax.axis_size("heads"), lax.axis_index("heads")

    def part(step):
        return lax.dynamic_index_in_dim(partial, (me + step) % size, 0, keepdims=False)

    if size != 4:
        total = part(0)
        for step in range(1, size):
            total = total + shift(part(step).astype(LOW), -step).astype(WIDE)
        return total
    far = part(2).astype(LOW)
    up = lax.ppermute(far, "heads", [(0, 1), (1, 2)]).astype(WIDE)
    down = lax.ppermute(far, "heads", [(2, 1), (3, 2)]).astype(WIDE)
    from_below = shift((part(1) + up).astype(LOW), -1)
    from_above = shift((part(3) + down).astype(LOW), 1)
    return part(0) + from_below.astype(WIDE) + from_above.astype(WIDE)


def in_order(parts):
    size, me = lax.axis_size("heads"), lax.axis_index("heads")
    out = jnp.zeros((size,) + parts[0].shape, parts[0].dtype)
    for step, value in enumerate(parts):
        out = lax.dynamic_update_index_in_dim(out, value, (me + step) % size, 0)
    return out.reshape((-1,) + parts[0].shape[1:])


def sum_heads(partial):
    size = lax.axis_size("heads")
    split = partial.reshape((size, -1) + partial.shape[1:])
    return in_order(gather_heads(scatter_heads(split).astype(LOW)))


def exchange_rows(value):
    return lax.all_to_all(value, "rows", 0, 0, tiled=True)


def normed(value):
    centred = value - jnp.mean(value, axis=-1, keepdims=True)
    rate = lax.rsqrt(jnp.mean(centred * centred, axis=-1, keepdims=True) + EPSILON)
    return centred * rate, rate


def normed_back(grad, unit, rate):
    return rate * (
        grad
        - jnp.mean(grad, axis=-1, keepdims=True)
        - unit * jnp.mean(grad * unit, axis=-1, keepdims=True)
    )


def gelu_tanh(pre_act):
    return jax.nn.gelu(pre_act, approximate=True)


def add_trees(former, latter):
    return jax.tree.map(jnp.add, former, latter)


def pair_forward(queries, pair, key_at, length=None):
    blocks, objects, _, width, rows = queries.shape
    pair_rows = pair.shape[4]
    lengths = jnp.full((objects,), blocks * pair_rows, jnp.int32) if length is None else length

    def kernel(len_ref, q_ref, k_ref, v_ref, mixed_ref, wide_ref, log_ref, keys_t, values):
        def run(live):
            @pl.when(pl.program_id(1) == 0)
            def _():
                for c in range(live):
                    keys_t[:, c * pair_rows : (c + 1) * pair_rows] = k_ref[c]
                    load_values(values, c, v_ref[c])

            size = live * pair_rows
            mixed, log_total = attend_block(
                (q_ref[...] * LOW(SCALE)).T, keys_t[:, :size], values[:size]
            )
            mixed_ref[...] = mixed.astype(LOW)
            wide_ref[...] = mixed
            log_ref[...] = log_total

        if length is None:
            run(blocks)
        else:
            by_length(len_ref[pl.program_id(0)], blocks * pair_rows, blocks, run)

    block = pl.BlockSpec((None, None, width, rows), lambda o, i, lens: (i, o, 0, 0))
    return pl.pallas_call(
        kernel,
        grid_spec=pltpu.PrefetchScalarGridSpec(
            num_scalar_prefetch=1,
            grid=(objects, blocks),
            in_specs=[
                pl.BlockSpec((None, None, None, width, rows), lambda o, i, lens: (i, o, 0, 0, 0)),
                pl.BlockSpec((blocks, None, None, width, pair_rows), lambda o, i, lens: (0, o, key_at, 0, 0)),
                pl.BlockSpec((blocks, None, None, width, pair_rows), lambda o, i, lens: (0, o, key_at + 1, 0, 0)),
            ],
            out_specs=[block, block, pl.BlockSpec((None, None, 1, rows), lambda o, i, lens: (i, o, 0, 0))],
            scratch_shapes=[
                pltpu.VMEM((width, blocks * pair_rows), LOW),
                pltpu.VMEM((blocks * pair_rows, 2 * width), LOW),
            ],
        ),
        out_shape=[
            jax.ShapeDtypeStruct((blocks, objects, width, rows), LOW),
            jax.ShapeDtypeStruct((blocks, objects, width, rows), WIDE),
            jax.ShapeDtypeStruct((blocks, objects, 1, rows), WIDE),
        ],
        name="pair_forward",
        cost_estimate=estimate(objects * blocks * rows, blocks * pair_rows, 2 if length is None else 1.4),
        compiler_params=pltpu.CompilerParams(vmem_limit_bytes=VMEM_LIMIT),
    )(lengths, queries, pair, pair)


def pair_backward(queries, pair, key_at, length, grad_mixed, wide, log_total):
    blocks, objects, _, width, rows = queries.shape
    lengths = jnp.full((objects,), blocks * rows, jnp.int32) if length is None else length

    def kernel(len_ref, q_ref, k_ref, v_ref, g_ref, wide_ref, log_ref, out_ref, keys, keys_t, values, grad_k, grad_v):
        i = pl.program_id(1)

        def run(live):
            size = live * rows

            @pl.when(i == 0)
            def _():
                for c in range(live):
                    at = slice(c * rows, (c + 1) * rows)
                    keys[at] = k_ref[c].T
                    keys_t[:, at] = k_ref[c]
                    values[at] = v_ref[c].T

            grad_t = g_ref[...]
            spread = jnp.sum(grad_t.astype(WIDE) * wide_ref[...], axis=0, keepdims=True)
            out_ref[i, 0], term_k, term_v = attend_block_back(
                q_ref[...] * LOW(SCALE),
                grad_t,
                keys[:size],
                keys_t[:, :size],
                values[:size],
                log_ref[...],
                spread,
            )

            @pl.when(i == 0)
            def _():
                grad_k[:size] = term_k
                grad_v[:size] = term_v

            @pl.when(i > 0)
            def _():
                grad_k[:size] += term_k
                grad_v[:size] += term_v

            @pl.when(i == blocks - 1)
            def _():
                for c in range(live):
                    at = slice(c * rows, (c + 1) * rows)
                    out_ref[c, 1] = grad_k[at].T.astype(LOW)
                    out_ref[c, 2] = grad_v[at].T.astype(LOW)
                for c in range(live, blocks):
                    out_ref[c, 1:] = jnp.zeros_like(out_ref[c, 1:])

        if length is None:
            run(blocks)
        else:
            by_length(len_ref[pl.program_id(0)], blocks * rows, blocks, run)

    block = pl.BlockSpec((None, None, width, rows), lambda o, i, lens: (i, o, 0, 0))
    return pl.pallas_call(
        kernel,
        grid_spec=pltpu.PrefetchScalarGridSpec(
            num_scalar_prefetch=1,
            grid=(objects, blocks),
            in_specs=[
                pl.BlockSpec((None, None, None, width, rows), lambda o, i, lens: (i, o, 0, 0, 0)),
                pl.BlockSpec((blocks, None, None, width, rows), lambda o, i, lens: (0, o, key_at, 0, 0)),
                pl.BlockSpec((blocks, None, None, width, rows), lambda o, i, lens: (0, o, key_at + 1, 0, 0)),
                block,
                block,
                pl.BlockSpec((None, None, 1, rows), lambda o, i, lens: (i, o, 0, 0)),
            ],
            out_specs=pl.BlockSpec((blocks, None, 3, width, rows), lambda o, i, lens: (0, o, 0, 0, 0)),
            scratch_shapes=[
                pltpu.VMEM((blocks * rows, width), LOW),
                pltpu.VMEM((width, blocks * rows), LOW),
                pltpu.VMEM((blocks * rows, width), LOW),
                pltpu.VMEM((blocks * rows, width), WIDE),
                pltpu.VMEM((blocks * rows, width), WIDE),
            ],
        ),
        out_shape=jax.ShapeDtypeStruct((blocks, objects, 3, width, rows), LOW),
        name="pair_backward",
        cost_estimate=estimate(objects * blocks * rows, blocks * rows, 3 if length is None else 2),
        compiler_params=pltpu.CompilerParams(vmem_limit_bytes=VMEM_LIMIT),
    )(lengths, queries, pair, pair, grad_mixed, wide, log_total)


def swap(value, axis):
    return lax.ppermute(value, axis, [(0, 1), (1, 0)])


def sum_near(partial):
    low = partial.astype(LOW)
    return low.astype(WIDE) + swap(low, "near").astype(WIDE)


def tie(value, *others):
    return lax.optimization_barrier((value, *others))


def paired_device(
    tokens,
    cam_index,
    patches,
    patch_len,
    camera_table,
    self_weights,
    self_output,
    cross_gain,
    cross_query,
    cross_pair,
    cross_output,
    patch_weights,
    hidden_gain,
    widen_weights,
    narrow_weights,
    cotangent,
):
    objects = tokens.shape[0] // 2
    _, rows, width = tokens.shape
    cols = self_weights.shape[2]
    hidden = widen_weights.shape[1]
    heads = cols // HEAD_DIM
    codes = camera_table.shape[0]
    patch_width = patches.shape[2]
    count = objects * rows
    n_rows = lax.axis_size("rows")
    row_rank = lax.axis_index("rows")
    far, near = lax.axis_index("far"), lax.axis_index("near")

    def objects_of(value):
        return lax.dynamic_slice_in_dim(value, objects * far, objects, 0)

    def piece(value):
        size = value.shape[0] // n_rows
        return lax.dynamic_slice_in_dim(value, row_rank * size, size, 0)

    def join_rows(value):
        return lax.all_gather(value, "rows", axis=0, tiled=True)

    def both_columns(value):
        return [
            lax.dynamic_slice_in_dim(value, (2 * index + near) * cols, cols, value.ndim - 1)
            for index in range(2)
        ]

    def in_order(mine, away, axis=0):
        size = mine.shape[axis]
        shape = list(mine.shape)
        shape[axis] *= 2
        out = lax.dynamic_update_slice_in_dim(jnp.zeros(shape, mine.dtype), mine, far * size, axis)
        return lax.dynamic_update_slice_in_dim(out, away, (1 - far) * size, axis)

    def halves(value):
        value = value.reshape(objects, 2, rows // 2, -1)
        return [
            lax.dynamic_index_in_dim(value, index, 1, keepdims=False).reshape(count // 2, -1)
            for index in (near, 1 - near)
        ]

    def half_sum_near(partial):
        mine, away = halves(partial)
        return mine + swap(away.astype(LOW), "near").astype(WIDE)

    def over_heads(value):
        value = value.reshape(2, 2, objects, rows // 2, -1)
        value = jnp.where(far == 0, value, jnp.flip(value, 1))
        value = jnp.where(near == 0, value, jnp.flip(value, 0))
        return value.transpose(1, 2, 0, 3, 4).reshape(2 * objects, rows, -1)

    def to_pairs(weights, value, slots):
        parts = [
            mul(weights, value[i * rows : (i + 1) * rows], NT)
            .astype(LOW)
            .reshape(n_rows, slots, HEAD_DIM, rows)
            for i in range(objects)
        ]
        return jnp.stack(parts, axis=1)

    def from_pairs(value):
        return value.transpose(0, 2, 3, 1, 4).reshape(-1, count)

    def over_all_columns(value_t, weight):
        return mul(jnp.concatenate([value_t, swap(value_t, "near")]), weight, TN)

    qkv_rows = self_weights.reshape(3, width, heads, HEAD_DIM).transpose(2, 0, 3, 1)
    qkv_rows = qkv_rows.reshape(3 * cols, width)
    pair_rows = cross_pair.reshape(2, width, heads, HEAD_DIM).transpose(2, 0, 3, 1)
    pair_rows = pair_rows.reshape(2 * cols, width)
    query_rows = cross_query.T

    qkv_away = join_rows(swap(piece(qkv_rows), "far"))

    table_flat = camera_table.reshape(codes, -1)
    cross_gain_f = cross_gain.astype(WIDE)
    hidden_gain_f = hidden_gain.astype(WIDE)

    inputs = objects_of(tokens).reshape(count, width).astype(WIDE)
    patch_in = objects_of(patches).reshape(count, patch_width)
    length = objects_of(patch_len)
    grad_low = objects_of(cotangent).reshape(count, width)
    codes_of = objects_of(cam_index).reshape(count)
    onehot = (codes_of[:, None] == jnp.arange(codes)[None, :]).astype(LOW)
    shift_scale = mul(onehot, table_flat)
    gain_one = 1.0 + shift_scale[:, :width]
    unit_one, rate_one = normed(inputs)
    normed_one = (unit_one * gain_one + shift_scale[:, width:]).astype(LOW)

    mine = [piece(v) for v in (self_output, query_rows, cross_output, pair_rows)]
    normed_one, *mine = tie(normed_one, *mine)
    mine = jnp.concatenate(mine, axis=0)
    across = swap(mine, "far")
    size = cols // n_rows
    two = in_order(mine[None, : 3 * size], across[None, : 3 * size])
    four = jnp.concatenate([two, swap(two, "near")])
    sent = jnp.concatenate([four.reshape(-1, width), across[3 * size :]])
    sent = lax.all_gather(sent, "rows", axis=0)
    pair_away = sent[:, 12 * size :].reshape(2 * cols, width)
    whole = sent[:, : 12 * size].reshape(n_rows, 4, 3, size, width).transpose(2, 1, 0, 3, 4)
    self_whole, query_whole, cross_whole = whole.reshape(3, 4 * cols, width)

    qkv_both = in_order(qkv_rows, qkv_away)
    qkv = exchange_rows(to_pairs(qkv_both, normed_one, 3))
    patch_mid = mul(patch_in, patch_weights).astype(LOW)
    pair_both = in_order(pair_rows, pair_away)
    pair = to_pairs(pair_both, patch_mid, 2)

    mine = [piece(widen_weights), piece(narrow_weights)]
    qkv, *mine = tie(qkv, *mine)
    size = width // n_rows
    sent = lax.all_gather(jnp.concatenate(mine, axis=0), ("far", "rows"), axis=0)
    sent = sent.reshape(2, n_rows, 2, size, width)
    widen = sent[:, :, 0].reshape(2, width, hidden)
    widen = jnp.concatenate([widen[0], widen[1]], axis=1)
    narrow = sent[:, :, 1].reshape(2 * hidden, width)

    mixed, self_wide, self_log = pair_forward(qkv, qkv, 1)
    mixed, pair = tie(exchange_rows(mixed), pair)
    pair = exchange_rows(pair)
    self_mixed_t = from_pairs(mixed[:, :, None])
    after_self = inputs + over_all_columns(self_mixed_t, self_whole)
    unit_two, rate_two = normed(after_self)
    normed_two = (unit_two * cross_gain_f).astype(LOW)
    cross_q, pair = tie(to_pairs(query_whole[: 2 * cols], normed_two, 1), pair)
    cross_q = exchange_rows(cross_q)
    mixed, cross_wide, cross_log = pair_forward(cross_q, pair, 0, length)
    cross_mixed_t = from_pairs(exchange_rows(mixed)[:, :, None])
    after_cross = after_self + over_all_columns(cross_mixed_t, cross_whole)
    unit_three, rate_three = normed(after_cross)
    normed_three = (unit_three * hidden_gain_f).astype(LOW)
    activated, act_back = jax.vjp(gelu_tanh, mul(normed_three, widen))
    activated = activated.astype(LOW)
    grad_pre = act_back(mul(grad_low, narrow, NT))[0].astype(LOW)
    third, activated, grad_pre = tie(mul(grad_pre, widen, NT).astype(LOW), activated, grad_pre)
    grad_three = third.astype(WIDE) + swap(third, "near").astype(WIDE)
    hidden_mine, hidden_away = halves(mul(activated, narrow))
    hidden_away, grad_three = tie(hidden_away.astype(LOW), grad_three)
    hidden_half = hidden_mine + swap(hidden_away, "near").astype(WIDE)
    result = (halves(after_cross)[0] + hidden_half).astype(LOW)

    def part_rows(both):
        return lax.psum_scatter(both, "rows", scatter_dimension=1, tiled=True)

    def own_and_away(value):
        return [lax.dynamic_index_in_dim(value, index, 0, keepdims=False) for index in (far, 1 - far)]

    def add_far(mine, away):
        return (mine.astype(WIDE) + away.astype(WIDE)).astype(LOW)

    def by_shard(left, right):
        return mul(left, right, NN).astype(LOW).reshape(2, -1, right.shape[1])

    hidden_terms = jnp.concatenate(
        [
            mul(value, against, TN).astype(LOW).reshape(2, hidden, width)
            for value, against in ((activated, grad_low), (grad_pre, normed_three))
        ],
        axis=1,
    )
    hidden_part = lax.psum_scatter(
        hidden_terms.reshape(-1, width), ("far", "rows"), scatter_dimension=0, tiled=True
    )

    hidden_gain_term = jnp.sum(grad_three * unit_three, axis=0)
    grad_cross = grad_low.astype(WIDE) + normed_back(
        grad_three * hidden_gain_f, unit_three, rate_three
    )
    grad_cross_low = grad_cross.astype(LOW)
    grad_mixed = exchange_rows(to_pairs(cross_whole[: 2 * cols], grad_cross_low, 1)[:, :, 0])
    grad_mixed, result = tie(grad_mixed, result)
    result_two = jnp.stack([result, swap(result, "far")])
    grads = pair_backward(cross_q, pair, 0, length, grad_mixed, cross_wide, cross_log)
    grads, result_two = tie(grads, result_two)
    grads = exchange_rows(grads)
    grad_cq_t = from_pairs(grads[:, :, :1])
    grad_pair_t = from_pairs(grads[:, :, 1:])
    middle_terms = jnp.concatenate(
        [
            by_shard(cross_mixed_t, grad_cross_low),
            by_shard(grad_cq_t, normed_two),
            by_shard(grad_pair_t, patch_mid),
        ],
        axis=1,
    )
    grad_cq_away, middle_terms = tie(swap(grad_cq_t, "near"), middle_terms)
    middle_part = part_rows(middle_terms)
    grad_two = mul(jnp.concatenate([grad_cq_t, grad_cq_away]), query_whole, TN)
    grad_two, result_two, hidden_part = tie(grad_two, result_two, hidden_part)
    result_four = jnp.stack([result_two, swap(result_two, "near")])
    hidden_total = join_rows(hidden_part)
    cross_gain_term = jnp.sum(grad_two * unit_two, axis=0)
    grad_self = grad_cross + normed_back(grad_two * cross_gain_f, unit_two, rate_two)
    grad_self_low = grad_self.astype(LOW)
    grad_mid = sum_near(
        mul(grad_pair_t, pair_both, TN)
    ).astype(LOW)
    patch_half = mul(halves(grad_mid)[0], patch_weights, NT).astype(LOW)
    patch_terms = jnp.stack([mul(value, patch_in, TN).astype(LOW) for value in both_columns(grad_mid)])
    patch_terms = jnp.pad(patch_terms, ((0, 0), (0, 0), (0, width - patch_width)))
    grad_mixed, grad_self_low = tie(to_pairs(self_whole[: 2 * cols], grad_self_low, 1)[:, :, 0], grad_self_low)
    output_terms = by_shard(self_mixed_t, grad_self_low)
    grad_mixed, patch_half, middle_part = tie(exchange_rows(grad_mixed), patch_half, middle_part)
    patch_two = jnp.stack([patch_half, swap(patch_half, "far")])
    middle_own, middle_away = own_and_away(middle_part)
    middle_away = swap(middle_away, "far")
    grads = pair_backward(qkv, qkv, 1, None, grad_mixed, self_wide, self_log)
    grads, patch_two, hidden_total, middle_away, result_four = tie(
        grads, patch_two, hidden_total, middle_away, result_four
    )
    patch_four = jnp.stack([patch_two, swap(patch_two, "near")])
    middle_total = join_rows(add_far(middle_own, middle_away))
    grads, patch_four = tie(exchange_rows(grads), patch_four)
    grad_qkv_t = from_pairs(grads)
    last_terms = jnp.concatenate([by_shard(grad_qkv_t, normed_one), output_terms, patch_terms], axis=1)
    last_part = part_rows(last_terms)
    grad_one = half_sum_near(mul(grad_qkv_t, qkv_both, TN))
    gain_half, unit_half, rate_half, self_half = (
        halves(value)[0] for value in (gain_one, unit_one, rate_one, grad_self)
    )
    input_half = self_half + normed_back(grad_one * gain_half, unit_half, rate_half)
    input_half = input_half.astype(LOW)
    onehot_half = halves(onehot)[0].astype(WIDE)
    table_term = jnp.concatenate(
        [
            lax.dot_general(onehot_half, value, TN, precision=lax.Precision.HIGHEST)
            for value in (grad_one * unit_half, grad_one)
        ],
        axis=0,
    )
    input_two = jnp.stack([input_half, swap(input_half, "far")])
    last_part, input_two, table_term = tie(last_part, input_two, table_term)
    small = [sum_near(table_term), hidden_gain_term[None], cross_gain_term[None], jnp.zeros((14, width), WIDE)]
    small = jnp.stack(both_columns(jnp.concatenate(small, axis=0).astype(LOW)))
    small = jnp.sum(lax.all_gather(small, "rows", axis=0).astype(WIDE), axis=0).astype(LOW)
    small_own, small_away = (
        lax.dynamic_index_in_dim(small, index, 0, keepdims=False) for index in (far, 1 - far)
    )
    small = small_own.astype(WIDE) + swap(small_away, "far").astype(WIDE)
    input_grads = over_heads(jnp.stack([input_two, swap(input_two, "near")]))
    outputs, patch_grads = over_heads(result_four), over_heads(patch_four)
    last_own, last_away = own_and_away(last_part)
    last_total = join_rows(add_far(last_own, swap(last_away, "far")))

    cross_output_total, query_total = middle_total[:cols], middle_total[cols : 2 * cols]
    pair_total = middle_total[2 * cols :].reshape(heads, 2, HEAD_DIM, width)
    self_total = last_total[: 3 * cols].reshape(heads, 3, HEAD_DIM, width)
    self_output_total = last_total[3 * cols : 4 * cols]
    patch_total = last_total[4 * cols :, :patch_width]
    gradients = (
        small[: 2 * codes].reshape(2, codes, cols).transpose(1, 0, 2),
        self_total.transpose(1, 3, 0, 2).reshape(3, width, cols),
        self_output_total,
        small[2 * codes + 1],
        query_total.T,
        pair_total.transpose(1, 3, 0, 2).reshape(2, width, cols),
        cross_output_total,
        patch_total.T,
        small[2 * codes],
        hidden_total[hidden:].T,
        hidden_total[:hidden],
    )
    return (outputs, input_grads.astype(WIDE), patch_grads.astype(WIDE)) + tuple(
        value.astype(WIDE) for value in gradients
    )


def per_device(
    tokens,
    cam_index,
    patches,
    patch_len,
    camera_table,
    self_weights,
    self_output,
    cross_gain,
    cross_query,
    cross_pair,
    cross_output,
    patch_weights,
    hidden_gain,
    widen_weights,
    narrow_weights,
    cotangent,
):
    batches, rows, width = tokens.shape
    cols = self_weights.shape[2]
    heads = cols // HEAD_DIM
    codes = camera_table.shape[0]
    patch_rows, patch_width = patches.shape[1:]
    n_rows, n_heads = lax.axis_size("rows"), lax.axis_size("heads")
    row_rank, head_rank = lax.axis_index("rows"), lax.axis_index("heads")
    groups = 1
    objects = batches // groups
    full_lengths = jnp.full((objects,), n_rows * rows, jnp.int32)
    count = objects * rows

    def own_columns(value):
        return lax.dynamic_slice_in_dim(value, head_rank * cols, cols, value.ndim - 1)

    table_flat = camera_table.reshape(codes, -1)
    cross_gain_f = cross_gain.astype(WIDE)
    hidden_gain_f = hidden_gain.astype(WIDE)

    qkv_rows = (
        self_weights.reshape(3, width, heads, HEAD_DIM).transpose(2, 0, 3, 1).reshape(3 * cols, width)
    )
    qkv_rows_back = self_weights.transpose(0, 2, 1).reshape(3 * cols, width)
    pair_rows = cross_pair.transpose(0, 2, 1).reshape(2 * cols, width)
    query_rows = cross_query.T

    local = jnp.stack([self_output, cross_output, query_rows])
    piece = cols // n_rows
    local = lax.dynamic_slice_in_dim(local, row_rank * piece, piece, 1)
    whole = lax.all_gather(jnp.stack(gather_heads(local)), "rows", axis=0)
    whole = whole.transpose(2, 1, 0, 3, 4).reshape(3, n_heads * cols, width)
    self_whole, cross_whole, query_whole = whole[0], whole[1], whole[2]

    def over_all_columns(value_t, weight):
        return mul(jnp.concatenate(gather_heads(value_t), axis=0), weight, TN)

    def by_object(weight, value):
        return jnp.stack(
            [mul(weight, value[i * rows : (i + 1) * rows], NT).astype(LOW) for i in range(objects)]
        )

    def column_terms(value, grads_t):
        return [
            mul(value, grads_t[i : i + cols], (((0,), (1,)), ((), ())))
            for i in range(0, grads_t.shape[0], cols)
        ]

    def one_group(group):
        part = slice(group * objects, (group + 1) * objects)
        inputs = tokens[part].reshape(count, width).astype(WIDE)
        patch_in = patches[part].reshape(objects * patch_rows, patch_width)
        lengths = patch_len[part]
        grad_low = cotangent[part].reshape(count, width)
        onehot = (cam_index[part].reshape(count)[:, None] == jnp.arange(codes)[None, :]).astype(LOW)
        shift_scale = mul(onehot, table_flat)
        gain_one = 1.0 + shift_scale[:, :width]
        unit_one, rate_one = normed(inputs)
        normed_one = (unit_one * gain_one + shift_scale[:, width:]).astype(LOW)
        qkv_t = by_object(qkv_rows, normed_one)
        by_kind = qkv_t.reshape(objects, heads, 3, HEAD_DIM, rows).transpose(2, 1, 3, 0, 4)
        by_kind = by_kind.reshape(3, cols, count)
        self_pair = lax.all_gather(by_kind[1:], "rows", axis=0)
        patch_mid = mul(patch_in, patch_weights).astype(LOW)
        own_pair = mul(pair_rows, patch_mid, NT).astype(LOW).reshape(2, cols, -1)
        pair_t = lax.all_gather(own_pair, "rows", axis=0)
        self_mixed_t, self_wide, self_log = cross_forward(by_kind[0], self_pair, full_lengths)
        after_self = inputs + over_all_columns(self_mixed_t, self_whole)
        unit_two, rate_two = normed(after_self)
        normed_two = (unit_two * cross_gain_f).astype(LOW)
        cross_q_t = mul(query_rows, normed_two, NT).astype(LOW)
        cross_mixed_t, cross_wide, cross_log = cross_forward(cross_q_t, pair_t, lengths)
        after_cross = after_self + over_all_columns(cross_mixed_t, cross_whole)
        unit_three, rate_three = normed(after_cross)
        normed_three = (unit_three * hidden_gain_f).astype(LOW)
        pre_act = mul(normed_three, widen_weights)
        activated, act_back = jax.vjp(gelu_tanh, pre_act)
        activated = activated.astype(LOW)
        grad_pre = act_back(mul(grad_low, narrow_weights, NT))[0].astype(LOW)
        grad_three = sum_heads(mul(grad_pre, widen_weights, NT)).astype(WIDE)
        yield "heads", {"hidden": mul(activated, narrow_weights)}
        yield "rows", {
            "narrow": mul(activated, grad_low, TN),
            "widen": mul(normed_three, grad_pre, TN),
        }
        hidden_gain_term = jnp.sum(own_columns(grad_three * unit_three), axis=0)
        grad_cross = grad_low.astype(WIDE) + normed_back(
            grad_three * hidden_gain_f, unit_three, rate_three
        )
        grad_cross_low = grad_cross.astype(LOW)
        cross_output_term = mul(cross_mixed_t, grad_cross_low)
        grad_mixed_t = mul(cross_output, grad_cross_low, NT).astype(LOW)
        grad_cq_t, grad_pair_t = cross_backward(
            cross_q_t, pair_t, lengths, grad_mixed_t, cross_wide, cross_log
        )
        grad_two = over_all_columns(grad_cq_t, query_whole)
        grad_pair_t = lax.psum_scatter(grad_pair_t, "rows", scatter_dimension=0, tiled=False)
        grad_pair_t = grad_pair_t.reshape(2 * cols, -1)
        query_term = mul(normed_two, grad_cq_t, (((0,), (1,)), ((), ())))
        cross_gain_term = jnp.sum(own_columns(grad_two * unit_two), axis=0)
        grad_self = grad_cross + normed_back(grad_two * cross_gain_f, unit_two, rate_two)
        grad_self_low = grad_self.astype(LOW)
        self_output_term = mul(self_mixed_t, grad_self_low)
        yield "heads", {"patch": mul(grad_pair_t, pair_rows, TN)}
        yield "rows", {
            "query": query_term,
            "pair": column_terms(patch_mid, grad_pair_t),
            "cross_output": cross_output_term,
            "self_output": self_output_term,
        }
        grad_self_mixed_t = mul(self_output, grad_self_low, NT).astype(LOW)
        grad_q_t, grad_kv_t = cross_backward(
            by_kind[0], self_pair, full_lengths, grad_self_mixed_t, self_wide, self_log
        )
        grad_kv_t = lax.psum_scatter(grad_kv_t, "rows", scatter_dimension=0, tiled=False)
        grad_qkv_t = jnp.concatenate([grad_q_t[None], grad_kv_t]).reshape(3 * cols, count)
        grad_qkv_t = yield "after", (grad_qkv_t, ["patch", "narrow", "widen"])
        grad_mid = yield "take", "patch"
        patch_term = mul(patch_in, own_columns(grad_mid), TN)
        patch_grad = mul(grad_mid, patch_weights, NT)
        grad_one = sum_heads(mul(grad_qkv_t, qkv_rows_back, TN))
        grad_one = yield "after", (grad_one, ["query", "pair", "cross_output", "self_output"])
        grad_one = grad_one.astype(WIDE)
        input_grad = grad_self + normed_back(grad_one * gain_one, unit_one, rate_one)
        own_grad = own_columns(grad_one)
        table_term = jnp.stack(
            [
                lax.dot_general(onehot.astype(WIDE), v, TN, precision=lax.Precision.HIGHEST)
                for v in (own_grad * own_columns(unit_one), own_grad)
            ],
            axis=1,
        )
        small = [patch_term, table_term.reshape(2 * codes, cols)]
        small += [hidden_gain_term[None], cross_gain_term[None], jnp.zeros((14, cols), WIDE)]
        yield "rows", {
            "self": column_terms(normed_one, grad_qkv_t),
            "small": jnp.concatenate(small, axis=0),
        }
        hidden_sum = yield "take", "hidden"
        result = (after_cross + hidden_sum.astype(WIDE)).astype(LOW)
        yield (
            "done",
            (
                result.reshape(objects, rows, width),
                input_grad.reshape(objects, rows, width),
                patch_grad.reshape(objects, patch_rows, patch_width),
            ),
        )

    steps = [one_group(group) for group in range(groups)]
    asked = [next(step) for step in steps]
    totals, ahead = {}, []
    while asked[0][0] != "done":
        kind, what = asked[0]
        answers = [None] * groups
        if kind == "take":
            answers = jnp.split(totals[what], groups)
        elif kind == "after":
            early = {name: totals[name] for name in what[1]}
            answers = [value for _, (value, _) in asked]
            answers[-1], early = lax.optimization_barrier((answers[-1], early))
            totals.update(early)
        else:
            terms = [value for _, value in asked]
            if kind == "heads":
                terms = jax.tree.map(lambda *parts: jnp.concatenate(parts, axis=0), *terms)
            else:
                for value in terms[1:]:
                    terms[0] = add_trees(terms[0], value)
                terms = terms[0]
            if kind == "rows":
                terms = jax.tree.map(lambda value: value.astype(LOW), terms)
            if kind == "heads":
                totals.update({name: sum_heads(value) for name, value in terms.items()})
            else:
                before = {name: totals[name] for name in ahead}
                terms, before = lax.optimization_barrier((terms, before))
                totals.update(before)
                totals.update(lax.psum(terms, kind))
                ahead = list(terms)
        asked = [step.send(value) for step, value in zip(steps, answers)]
    outputs, input_grads, patch_grads = (
        jnp.concatenate([value[i] for _, value in asked], axis=0) for i in range(3)
    )
    patch_total, table_total, gains = jnp.split(
        totals["small"], [patch_width, patch_width + 2 * codes]
    )
    gradients = (
        table_total.reshape(codes, 2, cols),
        jnp.stack(totals["self"]),
        totals["self_output"],
        gains[1],
        totals["query"],
        jnp.stack(totals["pair"]),
        totals["cross_output"],
        patch_total,
        gains[0],
        totals["widen"],
        totals["narrow"],
    )
    return (outputs, input_grads, patch_grads) + tuple(value.astype(WIDE) for value in gradients)


def solution(mesh):
    sizes = mesh.shape
    paired = sizes["heads"] == 4 and sizes["rows"] == 8
    heads = ("far", "near") if paired else "heads"
    if paired:
        names = (*heads, "rows")
        mesh = jax.sharding.Mesh(mesh.devices.reshape(2, 2, sizes["rows"]), names)
    in_specs = (
        P(None, "rows", None),
        P(None, "rows"),
        P(None, "rows", None),
        P(),
        P(),
        P(None, None, heads),
        P(heads, None),
        P(),
        P(None, heads),
        P(None, None, heads),
        P(heads, None),
        P(),
        P(),
        P(None, heads),
        P(heads, None),
        P(None, "rows", None),
    )
    out_specs = (
        P(None, "rows", None),
        P(None, "rows", None),
        P(None, "rows", None),
        P(None, None, heads),
        P(None, None, heads),
        P(heads, None),
        P(heads),
        P(None, heads),
        P(None, None, heads),
        P(heads, None),
        P(None, heads),
        P(heads),
        P(None, heads),
        P(heads, None),
    )
    return jax.shard_map(
        paired_device if paired else per_device,
        mesh=mesh,
        in_specs=in_specs,
        out_specs=out_specs,
        check_vma=False,
    )
```

```python
import jax
import jax.numpy as jnp
from jax import lax
from jax.experimental import pallas as pl
from jax.experimental.pallas import tpu as pltpu
from jax.sharding import PartitionSpec as P

HEAD_DIM = 64
EPSILON = 1e-05
SCALE = HEAD_DIM ** (-0.5)
LOW = jnp.bfloat16
WIDE = jnp.float32

NN = (((1,), (0,)), ((), ()))
NT = (((1,), (1,)), ((), ()))
TN = (((0,), (0,)), ((), ()))
T_LAST = (((0,), (1,)), ((), ()))


def mul(left, right, dims=NN):
    return lax.dot_general(left, right, dims, preferred_element_type=WIDE)


def load_values(values, block, values_t):
    rows = values_t.shape[1]
    at = slice(block * rows, (block + 1) * rows)
    values[at, :HEAD_DIM] = values_t.T
    values[at, HEAD_DIM:] = jnp.ones((rows, HEAD_DIM), values.dtype)


def attend_block(queries, keys_t, values):
    scores = mul(queries, keys_t)
    peak = jnp.max(scores, axis=1, keepdims=True)
    both = mul(jnp.exp(scores - peak).astype(LOW), values).T
    total = both[HEAD_DIM : HEAD_DIM + 1]
    return both[:HEAD_DIM] / total, peak.T + jnp.log(total)


def attend_block_back(scaled_q, grad_t, keys, keys_t, values, log_total, spread):
    probs = jnp.exp(mul(keys, scaled_q) - log_total)
    grad_scores = (probs * (mul(values, grad_t) - spread)).astype(LOW)
    return (
        (mul(keys_t, grad_scores) * SCALE).astype(LOW),
        mul(grad_scores, scaled_q.T),
        mul(probs.astype(LOW), grad_t.T),
    )


def estimate(rows, cols, passes):
    return pl.CostEstimate(
        flops=int(rows * cols * 1200 * passes), transcendentals=int(rows * cols), bytes_accessed=int(rows * 2048)
    )


VMEM_LIMIT = 48 << 20


def by_length(length, full, blocks, run):
    @pl.when(length * 4 > full)
    def _():
        run(blocks)

    @pl.when(length * 4 <= full)
    def _():
        run(blocks // 4)


def cross_forward(queries_t, pair_t, lengths):
    blocks, _, cols, all_patches = pair_t.shape
    objects = lengths.shape[0]
    heads = cols // HEAD_DIM
    rows, patch_rows = queries_t.shape[1] // objects, all_patches // objects

    def kernel(len_ref, q_ref, pair_ref, mixed_ref, wide_ref, log_ref, keys_t, values):
        queries = (q_ref[...] * LOW(SCALE)).T

        def run(live):
            for c in range(live):
                keys_t[:, c * patch_rows : (c + 1) * patch_rows] = pair_ref[c, 0]
                load_values(values, c, pair_ref[c, 1])
            size = live * patch_rows
            mixed, log_total = attend_block(queries, keys_t[:, :size], values[:size])
            mixed_ref[...] = mixed.astype(LOW)
            wide_ref[...] = mixed
            log_ref[...] = log_total

        by_length(len_ref[pl.program_id(0)], blocks * patch_rows, blocks, run)

    block = pl.BlockSpec((HEAD_DIM, rows), lambda b, j, lens: (j, b))
    return pl.pallas_call(
        kernel,
        grid_spec=pltpu.PrefetchScalarGridSpec(
            num_scalar_prefetch=1,
            grid=(objects, heads),
            in_specs=[
                block,
                pl.BlockSpec((blocks, 2, HEAD_DIM, patch_rows), lambda b, j, lens: (0, 0, j, b)),
            ],
            out_specs=[block, block, pl.BlockSpec((None, 1, rows), lambda b, j, lens: (j, 0, b))],
            scratch_shapes=[
                pltpu.VMEM((HEAD_DIM, blocks * patch_rows), LOW),
                pltpu.VMEM((blocks * patch_rows, 2 * HEAD_DIM), LOW),
            ],
        ),
        out_shape=[
            jax.ShapeDtypeStruct(queries_t.shape, LOW),
            jax.ShapeDtypeStruct(queries_t.shape, WIDE),
            jax.ShapeDtypeStruct((heads, 1, queries_t.shape[1]), WIDE),
        ],
        name="cross_forward",
        cost_estimate=estimate(objects * rows, blocks * patch_rows * heads, 1.4),
        compiler_params=pltpu.CompilerParams(vmem_limit_bytes=VMEM_LIMIT),
    )(lengths, queries_t, pair_t)


def cross_backward(queries_t, pair_t, lengths, grad_t_all, wide, log_total):
    blocks, _, cols, all_patches = pair_t.shape
    objects = lengths.shape[0]
    heads = cols // HEAD_DIM
    rows, patch_rows = queries_t.shape[1] // objects, all_patches // objects

    def kernel(len_ref, q_ref, pair_ref, g_ref, wide_ref, log_ref, out_q, out_pair, keys, keys_t, values):
        grad_t = g_ref[...]
        spread = jnp.sum(grad_t.astype(WIDE) * wide_ref[...], axis=0, keepdims=True)

        def run(live):
            for c in range(live):
                at = slice(c * patch_rows, (c + 1) * patch_rows)
                keys[at] = pair_ref[c, 0].T
                keys_t[:, at] = pair_ref[c, 0]
                values[at] = pair_ref[c, 1].T
            size = live * patch_rows
            out_q[...], grad_k, grad_v = attend_block_back(
                q_ref[...] * LOW(SCALE),
                grad_t,
                keys[:size],
                keys_t[:, :size],
                values[:size],
                log_ref[...],
                spread,
            )
            for c in range(live):
                at = slice(c * patch_rows, (c + 1) * patch_rows)
                out_pair[c, 0] = grad_k[at].T.astype(LOW)
                out_pair[c, 1] = grad_v[at].T.astype(LOW)
            for c in range(live, blocks):
                out_pair[c] = jnp.zeros_like(out_pair[c])

        by_length(len_ref[pl.program_id(0)], blocks * patch_rows, blocks, run)

    block = pl.BlockSpec((HEAD_DIM, rows), lambda b, j, lens: (j, b))
    pair_block = pl.BlockSpec((blocks, 2, HEAD_DIM, patch_rows), lambda b, j, lens: (0, 0, j, b))
    return pl.pallas_call(
        kernel,
        grid_spec=pltpu.PrefetchScalarGridSpec(
            num_scalar_prefetch=1,
            grid=(objects, heads),
            in_specs=[
                block,
                pair_block,
                block,
                block,
                pl.BlockSpec((None, 1, rows), lambda b, j, lens: (j, 0, b)),
            ],
            out_specs=[block, pair_block],
            scratch_shapes=[
                pltpu.VMEM((blocks * patch_rows, HEAD_DIM), LOW),
                pltpu.VMEM((HEAD_DIM, blocks * patch_rows), LOW),
                pltpu.VMEM((blocks * patch_rows, HEAD_DIM), LOW),
            ],
        ),
        out_shape=[
            jax.ShapeDtypeStruct(queries_t.shape, LOW),
            jax.ShapeDtypeStruct(pair_t.shape, LOW),
        ],
        name="cross_backward",
        cost_estimate=estimate(objects * rows, blocks * patch_rows * heads, 2.5),
        compiler_params=pltpu.CompilerParams(vmem_limit_bytes=VMEM_LIMIT),
    )(lengths, queries_t, pair_t, grad_t_all, wide, log_total)


def shift(value, step):
    size = lax.axis_size("heads")
    return lax.ppermute(value, "heads", [((i + step) % size, i) for i in range(size)])


def gather_heads(value):
    size = lax.axis_size("heads")
    if size != 4:
        return [value] + [shift(value, step) for step in range(1, size)]
    after, before = shift(value, 1), shift(value, -1)
    inner = lax.ppermute(after, "heads", [(1, 0), (2, 1)]) + lax.ppermute(before, "heads", [(1, 2), (2, 3)])
    return [value, after, inner, before]


def scatter_heads(partial):
    size, me = lax.axis_size("heads"), lax.axis_index("heads")

    def part(step):
        return lax.dynamic_index_in_dim(partial, (me + step) % size, 0, keepdims=False)

    if size != 4:
        total = part(0)
        for step in range(1, size):
            total = total + shift(part(step).astype(LOW), -step).astype(WIDE)
        return total
    far = part(2).astype(LOW)
    up = lax.ppermute(far, "heads", [(0, 1), (1, 2)]).astype(WIDE)
    down = lax.ppermute(far, "heads", [(2, 1), (3, 2)]).astype(WIDE)
    from_below = shift((part(1) + up).astype(LOW), -1)
    from_above = shift((part(3) + down).astype(LOW), 1)
    return part(0) + from_below.astype(WIDE) + from_above.astype(WIDE)


def in_order(parts):
    size, me = lax.axis_size("heads"), lax.axis_index("heads")
    out = jnp.zeros((size,) + parts[0].shape, parts[0].dtype)
    for step, value in enumerate(parts):
        out = lax.dynamic_update_index_in_dim(out, value, (me + step) % size, 0)
    return out.reshape((-1,) + parts[0].shape[1:])


def sum_heads(partial):
    size = lax.axis_size("heads")
    split = partial.reshape((size, -1) + partial.shape[1:])
    return in_order(gather_heads(scatter_heads(split).astype(LOW)))


def exchange_rows(value):
    return lax.all_to_all(value, "rows", 0, 0, tiled=True)


def normed(value):
    centred = value - jnp.mean(value, axis=-1, keepdims=True)
    rate = lax.rsqrt(jnp.mean(centred * centred, axis=-1, keepdims=True) + EPSILON)
    return centred * rate, rate


def normed_back(grad, unit, rate):
    return rate * (
        grad
        - jnp.mean(grad, axis=-1, keepdims=True)
        - unit * jnp.mean(grad * unit, axis=-1, keepdims=True)
    )


def gelu_tanh(pre_act):
    return jax.nn.gelu(pre_act, approximate=True)


def add_trees(former, latter):
    return jax.tree.map(jnp.add, former, latter)


def pair_forward(queries, pair, key_at, length=None):
    blocks, objects, _, width, rows = queries.shape
    pair_rows = pair.shape[4]
    lengths = jnp.full((objects,), blocks * pair_rows, jnp.int32) if length is None else length

    def kernel(len_ref, q_ref, k_ref, v_ref, mixed_ref, wide_ref, log_ref, keys_t, values):
        def run(live):
            @pl.when(pl.program_id(1) == 0)
            def _():
                for c in range(live):
                    keys_t[:, c * pair_rows : (c + 1) * pair_rows] = k_ref[c]
                    load_values(values, c, v_ref[c])

            size = live * pair_rows
            mixed, log_total = attend_block(
                (q_ref[...] * LOW(SCALE)).T, keys_t[:, :size], values[:size]
            )
            mixed_ref[...] = mixed.astype(LOW)
            wide_ref[...] = mixed
            log_ref[...] = log_total

        if length is None:
            run(blocks)
        else:
            by_length(len_ref[pl.program_id(0)], blocks * pair_rows, blocks, run)

    block = pl.BlockSpec((None, None, width, rows), lambda o, i, lens: (i, o, 0, 0))
    return pl.pallas_call(
        kernel,
        grid_spec=pltpu.PrefetchScalarGridSpec(
            num_scalar_prefetch=1,
            grid=(objects, blocks),
            in_specs=[
                pl.BlockSpec((None, None, None, width, rows), lambda o, i, lens: (i, o, 0, 0, 0)),
                pl.BlockSpec((blocks, None, None, width, pair_rows), lambda o, i, lens: (0, o, key_at, 0, 0)),
                pl.BlockSpec((blocks, None, None, width, pair_rows), lambda o, i, lens: (0, o, key_at + 1, 0, 0)),
            ],
            out_specs=[block, block, pl.BlockSpec((None, None, 1, rows), lambda o, i, lens: (i, o, 0, 0))],
            scratch_shapes=[
                pltpu.VMEM((width, blocks * pair_rows), LOW),
                pltpu.VMEM((blocks * pair_rows, 2 * width), LOW),
            ],
        ),
        out_shape=[
            jax.ShapeDtypeStruct((blocks, objects, width, rows), LOW),
            jax.ShapeDtypeStruct((blocks, objects, width, rows), WIDE),
            jax.ShapeDtypeStruct((blocks, objects, 1, rows), WIDE),
        ],
        name="pair_forward",
        cost_estimate=estimate(objects * blocks * rows, blocks * pair_rows, 2 if length is None else 1.4),
        compiler_params=pltpu.CompilerParams(vmem_limit_bytes=VMEM_LIMIT),
    )(lengths, queries, pair, pair)


def pair_backward(queries, pair, key_at, length, grad_mixed, wide, log_total):
    blocks, objects, _, width, rows = queries.shape
    lengths = jnp.full((objects,), blocks * rows, jnp.int32) if length is None else length

    def kernel(len_ref, q_ref, k_ref, v_ref, g_ref, wide_ref, log_ref, out_ref, keys, keys_t, values, grad_k, grad_v):
        i = pl.program_id(1)

        def run(live):
            size = live * rows

            @pl.when(i == 0)
            def _():
                for c in range(live):
                    at = slice(c * rows, (c + 1) * rows)
                    keys[at] = k_ref[c].T
                    keys_t[:, at] = k_ref[c]
                    values[at] = v_ref[c].T

            grad_t = g_ref[...]
            spread = jnp.sum(grad_t.astype(WIDE) * wide_ref[...], axis=0, keepdims=True)
            out_ref[i, 0], term_k, term_v = attend_block_back(
                q_ref[...] * LOW(SCALE),
                grad_t,
                keys[:size],
                keys_t[:, :size],
                values[:size],
                log_ref[...],
                spread,
            )

            @pl.when(i == 0)
            def _():
                grad_k[:size] = term_k
                grad_v[:size] = term_v

            @pl.when(i > 0)
            def _():
                grad_k[:size] += term_k
                grad_v[:size] += term_v

            @pl.when(i == blocks - 1)
            def _():
                for c in range(live):
                    at = slice(c * rows, (c + 1) * rows)
                    out_ref[c, 1] = grad_k[at].T.astype(LOW)
                    out_ref[c, 2] = grad_v[at].T.astype(LOW)
                for c in range(live, blocks):
                    out_ref[c, 1:] = jnp.zeros_like(out_ref[c, 1:])

        if length is None:
            run(blocks)
        else:
            by_length(len_ref[pl.program_id(0)], blocks * rows, blocks, run)

    block = pl.BlockSpec((None, None, width, rows), lambda o, i, lens: (i, o, 0, 0))
    return pl.pallas_call(
        kernel,
        grid_spec=pltpu.PrefetchScalarGridSpec(
            num_scalar_prefetch=1,
            grid=(objects, blocks),
            in_specs=[
                pl.BlockSpec((None, None, None, width, rows), lambda o, i, lens: (i, o, 0, 0, 0)),
                pl.BlockSpec((blocks, None, None, width, rows), lambda o, i, lens: (0, o, key_at, 0, 0)),
                pl.BlockSpec((blocks, None, None, width, rows), lambda o, i, lens: (0, o, key_at + 1, 0, 0)),
                block,
                block,
                pl.BlockSpec((None, None, 1, rows), lambda o, i, lens: (i, o, 0, 0)),
            ],
            out_specs=pl.BlockSpec((blocks, None, 3, width, rows), lambda o, i, lens: (0, o, 0, 0, 0)),
            scratch_shapes=[
                pltpu.VMEM((blocks * rows, width), LOW),
                pltpu.VMEM((width, blocks * rows), LOW),
                pltpu.VMEM((blocks * rows, width), LOW),
                pltpu.VMEM((blocks * rows, width), WIDE),
                pltpu.VMEM((blocks * rows, width), WIDE),
            ],
        ),
        out_shape=jax.ShapeDtypeStruct((blocks, objects, 3, width, rows), LOW),
        name="pair_backward",
        cost_estimate=estimate(objects * blocks * rows, blocks * rows, 3 if length is None else 2),
        compiler_params=pltpu.CompilerParams(vmem_limit_bytes=VMEM_LIMIT),
    )(lengths, queries, pair, pair, grad_mixed, wide, log_total)


def swap(value, axis):
    return lax.ppermute(value, axis, [(0, 1), (1, 0)])


def sum_near(partial):
    low = partial.astype(LOW)
    return low.astype(WIDE) + swap(low, "near").astype(WIDE)


def tie(value, *others):
    return lax.optimization_barrier((value, *others))


def paired_device(
    tokens,
    cam_index,
    patches,
    patch_len,
    camera_table,
    self_weights,
    self_output,
    cross_gain,
    cross_query,
    cross_pair,
    cross_output,
    patch_weights,
    hidden_gain,
    widen_weights,
    narrow_weights,
    cotangent,
):
    objects = tokens.shape[0] // 2
    _, rows, width = tokens.shape
    cols = self_weights.shape[2]
    hidden = widen_weights.shape[1]
    heads = cols // HEAD_DIM
    codes = camera_table.shape[0]
    patch_width = patches.shape[2]
    count = objects * rows
    n_rows = lax.axis_size("rows")
    row_rank = lax.axis_index("rows")
    far, near = lax.axis_index("far"), lax.axis_index("near")

    def objects_of(value):
        return lax.dynamic_slice_in_dim(value, objects * far, objects, 0)

    def piece(value):
        size = value.shape[0] // n_rows
        return lax.dynamic_slice_in_dim(value, row_rank * size, size, 0)

    def join_rows(value):
        return lax.all_gather(value, "rows", axis=0, tiled=True)

    def both_columns(value):
        return [
            lax.dynamic_slice_in_dim(value, (2 * index + near) * cols, cols, value.ndim - 1)
            for index in range(2)
        ]

    def in_order(mine, away, axis=0):
        size = mine.shape[axis]
        shape = list(mine.shape)
        shape[axis] *= 2
        out = lax.dynamic_update_slice_in_dim(jnp.zeros(shape, mine.dtype), mine, far * size, axis)
        return lax.dynamic_update_slice_in_dim(out, away, (1 - far) * size, axis)

    def halves(value):
        value = value.reshape(objects, 2, rows // 2, -1)
        return [
            lax.dynamic_index_in_dim(value, index, 1, keepdims=False).reshape(count // 2, -1)
            for index in (near, 1 - near)
        ]

    def half_sum_near(partial):
        mine, away = halves(partial)
        return mine + swap(away.astype(LOW), "near").astype(WIDE)

    def over_heads(value):
        value = value.reshape(2, 2, objects, rows // 2, -1)
        value = jnp.where(far == 0, value, jnp.flip(value, 1))
        value = jnp.where(near == 0, value, jnp.flip(value, 0))
        return value.transpose(1, 2, 0, 3, 4).reshape(2 * objects, rows, -1)

    def to_pairs(weights, value, slots):
        parts = [
            mul(weights, value[i * rows : (i + 1) * rows], NT)
            .astype(LOW)
            .reshape(n_rows, slots, HEAD_DIM, rows)
            for i in range(objects)
        ]
        return jnp.stack(parts, axis=1)

    def from_pairs(value):
        return value.transpose(0, 2, 3, 1, 4).reshape(-1, count)

    def over_all_columns(value_t, weight):
        return mul(jnp.concatenate([value_t, swap(value_t, "near")]), weight, TN)

    qkv_rows = self_weights.reshape(3, width, heads, HEAD_DIM).transpose(2, 0, 3, 1)
    qkv_rows = qkv_rows.reshape(3 * cols, width)
    pair_rows = cross_pair.reshape(2, width, heads, HEAD_DIM).transpose(2, 0, 3, 1)
    pair_rows = pair_rows.reshape(2 * cols, width)
    query_rows = cross_query.T

    qkv_away = join_rows(swap(piece(qkv_rows), "far"))

    table_flat = camera_table.reshape(codes, -1)
    cross_gain_f = cross_gain.astype(WIDE)
    hidden_gain_f = hidden_gain.astype(WIDE)

    inputs = objects_of(tokens).reshape(count, width).astype(WIDE)
    patch_in = objects_of(patches).reshape(count, patch_width)
    length = objects_of(patch_len)
    grad_low = objects_of(cotangent).reshape(count, width)
    codes_of = objects_of(cam_index).reshape(count)
    onehot = (codes_of[:, None] == jnp.arange(codes)[None, :]).astype(LOW)
    shift_scale = mul(onehot, table_flat)
    gain_one = 1.0 + shift_scale[:, :width]
    unit_one, rate_one = normed(inputs)
    normed_one = (unit_one * gain_one + shift_scale[:, width:]).astype(LOW)

    mine = [piece(v) for v in (self_output, query_rows, cross_output, pair_rows)]
    normed_one, *mine = tie(normed_one, *mine)
    mine = jnp.concatenate(mine, axis=0)
    across = swap(mine, "far")
    size = cols // n_rows
    two = in_order(mine[None, : 3 * size], across[None, : 3 * size])
    four = jnp.concatenate([two, swap(two, "near")])
    sent = jnp.concatenate([four.reshape(-1, width), across[3 * size :]])
    sent = lax.all_gather(sent, "rows", axis=0)
    pair_away = sent[:, 12 * size :].reshape(2 * cols, width)
    whole = sent[:, : 12 * size].reshape(n_rows, 4, 3, size, width).transpose(2, 1, 0, 3, 4)
    self_whole, query_whole, cross_whole = whole.reshape(3, 4 * cols, width)

    qkv_both = in_order(qkv_rows, qkv_away)
    qkv = exchange_rows(to_pairs(qkv_both, normed_one, 3))
    patch_mid = mul(patch_in, patch_weights).astype(LOW)
    pair_both = in_order(pair_rows, pair_away)
    pair = to_pairs(pair_both, patch_mid, 2)

    mine = [piece(widen_weights), piece(narrow_weights)]
    qkv, *mine = tie(qkv, *mine)
    size = width // n_rows
    sent = lax.all_gather(jnp.concatenate(mine, axis=0), ("far", "rows"), axis=0)
    sent = sent.reshape(2, n_rows, 2, size, width)
    widen = sent[:, :, 0].reshape(2, width, hidden)
    widen = jnp.concatenate([widen[0], widen[1]], axis=1)
    narrow = sent[:, :, 1].reshape(2 * hidden, width)

    mixed, self_wide, self_log = pair_forward(qkv, qkv, 1)
    mixed, pair = tie(exchange_rows(mixed), pair)
    pair = exchange_rows(pair)
    self_mixed_t = from_pairs(mixed[:, :, None])
    after_self = inputs + over_all_columns(self_mixed_t, self_whole)
    unit_two, rate_two = normed(after_self)
    normed_two = (unit_two * cross_gain_f).astype(LOW)
    cross_q, pair = tie(to_pairs(query_whole[: 2 * cols], normed_two, 1), pair)
    cross_q = exchange_rows(cross_q)
    mixed, cross_wide, cross_log = pair_forward(cross_q, pair, 0, length)
    cross_mixed_t = from_pairs(exchange_rows(mixed)[:, :, None])
    after_cross = after_self + over_all_columns(cross_mixed_t, cross_whole)
    unit_three, rate_three = normed(after_cross)
    normed_three = (unit_three * hidden_gain_f).astype(LOW)
    activated, act_back = jax.vjp(gelu_tanh, mul(normed_three, widen))
    activated = activated.astype(LOW)
    grad_pre = act_back(mul(grad_low, narrow, NT))[0].astype(LOW)
    third, activated, grad_pre = tie(mul(grad_pre, widen, NT).astype(LOW), activated, grad_pre)
    grad_three = third.astype(WIDE) + swap(third, "near").astype(WIDE)
    hidden_mine, hidden_away = halves(mul(activated, narrow))
    hidden_away, grad_three = tie(hidden_away.astype(LOW), grad_three)
    hidden_half = hidden_mine + swap(hidden_away, "near").astype(WIDE)
    result = (halves(after_cross)[0] + hidden_half).astype(LOW)

    def part_rows(both):
        return lax.psum_scatter(both, "rows", scatter_dimension=1, tiled=True)

    def own_and_away(value):
        return [lax.dynamic_index_in_dim(value, index, 0, keepdims=False) for index in (far, 1 - far)]

    def add_far(mine, away):
        return (mine.astype(WIDE) + away.astype(WIDE)).astype(LOW)

    def by_shard(left, right):
        return mul(left, right, NN).astype(LOW).reshape(2, -1, right.shape[1])

    hidden_terms = jnp.concatenate(
        [
            mul(value, against, TN).astype(LOW).reshape(2, hidden, width)
            for value, against in ((activated, grad_low), (grad_pre, normed_three))
        ],
        axis=1,
    )
    hidden_part = lax.psum_scatter(
        hidden_terms.reshape(-1, width), ("far", "rows"), scatter_dimension=0, tiled=True
    )

    hidden_gain_term = jnp.sum(grad_three * unit_three, axis=0)
    grad_cross = grad_low.astype(WIDE) + normed_back(
        grad_three * hidden_gain_f, unit_three, rate_three
    )
    grad_cross_low = grad_cross.astype(LOW)
    grad_mixed = exchange_rows(to_pairs(cross_whole[: 2 * cols], grad_cross_low, 1)[:, :, 0])
    grad_mixed, result = tie(grad_mixed, result)
    result_two = jnp.stack([result, swap(result, "far")])
    grads = pair_backward(cross_q, pair, 0, length, grad_mixed, cross_wide, cross_log)
    grads, result_two = tie(grads, result_two)
    grads = exchange_rows(grads)
    grad_cq_t = from_pairs(grads[:, :, :1])
    grad_pair_t = from_pairs(grads[:, :, 1:])
    middle_terms = jnp.concatenate(
        [
            by_shard(cross_mixed_t, grad_cross_low),
            by_shard(grad_cq_t, normed_two),
            by_shard(grad_pair_t, patch_mid),
        ],
        axis=1,
    )
    grad_cq_away, middle_terms = tie(swap(grad_cq_t, "near"), middle_terms)
    middle_part = part_rows(middle_terms)
    grad_two = mul(jnp.concatenate([grad_cq_t, grad_cq_away]), query_whole, TN)
    grad_two, result_two, hidden_part = tie(grad_two, result_two, hidden_part)
    result_four = jnp.stack([result_two, swap(result_two, "near")])
    hidden_total = join_rows(hidden_part)
    cross_gain_term = jnp.sum(grad_two * unit_two, axis=0)
    grad_self = grad_cross + normed_back(grad_two * cross_gain_f, unit_two, rate_two)
    grad_self_low = grad_self.astype(LOW)
    grad_mid = sum_near(
        mul(grad_pair_t, pair_both, TN)
    ).astype(LOW)
    patch_half = mul(halves(grad_mid)[0], patch_weights, NT).astype(LOW)
    patch_terms = jnp.stack([mul(value, patch_in, TN).astype(LOW) for value in both_columns(grad_mid)])
    patch_terms = jnp.pad(patch_terms, ((0, 0), (0, 0), (0, width - patch_width)))
    grad_mixed, grad_self_low = tie(to_pairs(self_whole[: 2 * cols], grad_self_low, 1)[:, :, 0], grad_self_low)
    output_terms = by_shard(self_mixed_t, grad_self_low)
    grad_mixed, patch_half = tie(exchange_rows(grad_mixed), patch_half)
    patch_two = jnp.stack([patch_half, swap(patch_half, "far")])
    last_terms = jnp.pad(
        jnp.concatenate([output_terms, patch_terms], axis=1), ((0, 0), (3 * cols, 0), (0, 0))
    )
    grads = pair_backward(qkv, qkv, 1, None, grad_mixed, self_wide, self_log)
    grads, patch_two, middle_part, result_four, last_terms = tie(
        grads, patch_two, middle_part, result_four, last_terms
    )
    middle_own, middle_away = own_and_away(middle_part)
    patch_four = jnp.stack([patch_two, swap(patch_two, "near")])
    grads, patch_four, middle_away, hidden_total = tie(
        exchange_rows(grads), patch_four, swap(middle_away, "far"), hidden_total
    )
    middle_total = join_rows(add_far(middle_own, middle_away))
    grad_qkv_t = from_pairs(grads)
    last_terms = lax.dynamic_update_slice_in_dim(last_terms, by_shard(grad_qkv_t, normed_one), 0, 1)
    last_part = part_rows(last_terms)
    grad_one = half_sum_near(mul(grad_qkv_t, qkv_both, TN))
    gain_half, unit_half, rate_half, self_half = (
        halves(value)[0] for value in (gain_one, unit_one, rate_one, grad_self)
    )
    input_half = self_half + normed_back(grad_one * gain_half, unit_half, rate_half)
    input_half = input_half.astype(LOW)
    onehot_half = halves(onehot)[0].astype(WIDE)
    table_term = jnp.concatenate(
        [
            lax.dot_general(onehot_half, value, TN, precision=lax.Precision.HIGHEST)
            for value in (grad_one * unit_half, grad_one)
        ],
        axis=0,
    )
    input_two = jnp.stack([input_half, swap(input_half, "far")])
    last_part, input_two = tie(last_part, input_two)
    input_four = jnp.stack([input_two, swap(input_two, "near")])
    input_four, table_term = tie(input_four, table_term)
    small = [sum_near(table_term), hidden_gain_term[None], cross_gain_term[None], jnp.zeros((14, width), WIDE)]
    small = jnp.stack(both_columns(jnp.concatenate(small, axis=0).astype(LOW)))
    small = jnp.sum(lax.all_gather(small, "rows", axis=0).astype(WIDE), axis=0).astype(LOW)
    small_own, small_away = (
        lax.dynamic_index_in_dim(small, index, 0, keepdims=False) for index in (far, 1 - far)
    )
    small = small_own.astype(WIDE) + swap(small_away, "far").astype(WIDE)
    input_grads = over_heads(input_four)
    outputs, patch_grads = over_heads(result_four), over_heads(patch_four)
    last_own, last_away = own_and_away(last_part)
    last_total = join_rows(add_far(last_own, swap(last_away, "far")))

    cross_output_total, query_total = middle_total[:cols], middle_total[cols : 2 * cols]
    pair_total = middle_total[2 * cols :].reshape(heads, 2, HEAD_DIM, width)
    self_total = last_total[: 3 * cols].reshape(heads, 3, HEAD_DIM, width)
    self_output_total = last_total[3 * cols : 4 * cols]
    patch_total = last_total[4 * cols :, :patch_width]
    gradients = (
        small[: 2 * codes].reshape(2, codes, cols).transpose(1, 0, 2),
        self_total.transpose(1, 3, 0, 2).reshape(3, width, cols),
        self_output_total,
        small[2 * codes + 1],
        query_total.T,
        pair_total.transpose(1, 3, 0, 2).reshape(2, width, cols),
        cross_output_total,
        patch_total.T,
        small[2 * codes],
        hidden_total[hidden:].T,
        hidden_total[:hidden],
    )
    return (outputs, input_grads.astype(WIDE), patch_grads.astype(WIDE)) + tuple(
        value.astype(WIDE) for value in gradients
    )


def per_device(
    tokens,
    cam_index,
    patches,
    patch_len,
    camera_table,
    self_weights,
    self_output,
    cross_gain,
    cross_query,
    cross_pair,
    cross_output,
    patch_weights,
    hidden_gain,
    widen_weights,
    narrow_weights,
    cotangent,
):
    batches, rows, width = tokens.shape
    cols = self_weights.shape[2]
    heads = cols // HEAD_DIM
    codes = camera_table.shape[0]
    patch_rows, patch_width = patches.shape[1:]
    n_rows, n_heads = lax.axis_size("rows"), lax.axis_size("heads")
    row_rank, head_rank = lax.axis_index("rows"), lax.axis_index("heads")
    groups = 1
    objects = batches // groups
    full_lengths = jnp.full((objects,), n_rows * rows, jnp.int32)
    count = objects * rows

    def own_columns(value):
        return lax.dynamic_slice_in_dim(value, head_rank * cols, cols, value.ndim - 1)

    table_flat = camera_table.reshape(codes, -1)
    cross_gain_f = cross_gain.astype(WIDE)
    hidden_gain_f = hidden_gain.astype(WIDE)

    qkv_rows = (
        self_weights.reshape(3, width, heads, HEAD_DIM).transpose(2, 0, 3, 1).reshape(3 * cols, width)
    )
    qkv_rows_back = self_weights.transpose(0, 2, 1).reshape(3 * cols, width)
    pair_rows = cross_pair.transpose(0, 2, 1).reshape(2 * cols, width)
    query_rows = cross_query.T

    local = jnp.stack([self_output, cross_output, query_rows])
    piece = cols // n_rows
    local = lax.dynamic_slice_in_dim(local, row_rank * piece, piece, 1)
    whole = lax.all_gather(jnp.stack(gather_heads(local)), "rows", axis=0)
    whole = whole.transpose(2, 1, 0, 3, 4).reshape(3, n_heads * cols, width)
    self_whole, cross_whole, query_whole = whole[0], whole[1], whole[2]

    def over_all_columns(value_t, weight):
        return mul(jnp.concatenate(gather_heads(value_t), axis=0), weight, TN)

    def by_object(weight, value):
        return jnp.stack(
            [mul(weight, value[i * rows : (i + 1) * rows], NT).astype(LOW) for i in range(objects)]
        )

    def column_terms(value, grads_t):
        return [
            mul(value, grads_t[i : i + cols], (((0,), (1,)), ((), ())))
            for i in range(0, grads_t.shape[0], cols)
        ]

    def one_group(group):
        part = slice(group * objects, (group + 1) * objects)
        inputs = tokens[part].reshape(count, width).astype(WIDE)
        patch_in = patches[part].reshape(objects * patch_rows, patch_width)
        lengths = patch_len[part]
        grad_low = cotangent[part].reshape(count, width)
        onehot = (cam_index[part].reshape(count)[:, None] == jnp.arange(codes)[None, :]).astype(LOW)
        shift_scale = mul(onehot, table_flat)
        gain_one = 1.0 + shift_scale[:, :width]
        unit_one, rate_one = normed(inputs)
        normed_one = (unit_one * gain_one + shift_scale[:, width:]).astype(LOW)
        qkv_t = by_object(qkv_rows, normed_one)
        by_kind = qkv_t.reshape(objects, heads, 3, HEAD_DIM, rows).transpose(2, 1, 3, 0, 4)
        by_kind = by_kind.reshape(3, cols, count)
        self_pair = lax.all_gather(by_kind[1:], "rows", axis=0)
        patch_mid = mul(patch_in, patch_weights).astype(LOW)
        own_pair = mul(pair_rows, patch_mid, NT).astype(LOW).reshape(2, cols, -1)
        pair_t = lax.all_gather(own_pair, "rows", axis=0)
        self_mixed_t, self_wide, self_log = cross_forward(by_kind[0], self_pair, full_lengths)
        after_self = inputs + over_all_columns(self_mixed_t, self_whole)
        unit_two, rate_two = normed(after_self)
        normed_two = (unit_two * cross_gain_f).astype(LOW)
        cross_q_t = mul(query_rows, normed_two, NT).astype(LOW)
        cross_mixed_t, cross_wide, cross_log = cross_forward(cross_q_t, pair_t, lengths)
        after_cross = after_self + over_all_columns(cross_mixed_t, cross_whole)
        unit_three, rate_three = normed(after_cross)
        normed_three = (unit_three * hidden_gain_f).astype(LOW)
        pre_act = mul(normed_three, widen_weights)
        activated, act_back = jax.vjp(gelu_tanh, pre_act)
        activated = activated.astype(LOW)
        grad_pre = act_back(mul(grad_low, narrow_weights, NT))[0].astype(LOW)
        grad_three = sum_heads(mul(grad_pre, widen_weights, NT)).astype(WIDE)
        yield "heads", {"hidden": mul(activated, narrow_weights)}
        yield "rows", {
            "narrow": mul(activated, grad_low, TN),
            "widen": mul(normed_three, grad_pre, TN),
        }
        hidden_gain_term = jnp.sum(own_columns(grad_three * unit_three), axis=0)
        grad_cross = grad_low.astype(WIDE) + normed_back(
            grad_three * hidden_gain_f, unit_three, rate_three
        )
        grad_cross_low = grad_cross.astype(LOW)
        cross_output_term = mul(cross_mixed_t, grad_cross_low)
        grad_mixed_t = mul(cross_output, grad_cross_low, NT).astype(LOW)
        grad_cq_t, grad_pair_t = cross_backward(
            cross_q_t, pair_t, lengths, grad_mixed_t, cross_wide, cross_log
        )
        grad_two = over_all_columns(grad_cq_t, query_whole)
        grad_pair_t = lax.psum_scatter(grad_pair_t, "rows", scatter_dimension=0, tiled=False)
        grad_pair_t = grad_pair_t.reshape(2 * cols, -1)
        query_term = mul(normed_two, grad_cq_t, (((0,), (1,)), ((), ())))
        cross_gain_term = jnp.sum(own_columns(grad_two * unit_two), axis=0)
        grad_self = grad_cross + normed_back(grad_two * cross_gain_f, unit_two, rate_two)
        grad_self_low = grad_self.astype(LOW)
        self_output_term = mul(self_mixed_t, grad_self_low)
        yield "heads", {"patch": mul(grad_pair_t, pair_rows, TN)}
        yield "rows", {
            "query": query_term,
            "pair": column_terms(patch_mid, grad_pair_t),
            "cross_output": cross_output_term,
            "self_output": self_output_term,
        }
        grad_self_mixed_t = mul(self_output, grad_self_low, NT).astype(LOW)
        grad_q_t, grad_kv_t = cross_backward(
            by_kind[0], self_pair, full_lengths, grad_self_mixed_t, self_wide, self_log
        )
        grad_kv_t = lax.psum_scatter(grad_kv_t, "rows", scatter_dimension=0, tiled=False)
        grad_qkv_t = jnp.concatenate([grad_q_t[None], grad_kv_t]).reshape(3 * cols, count)
        grad_qkv_t = yield "after", (grad_qkv_t, ["patch", "narrow", "widen"])
        grad_mid = yield "take", "patch"
        patch_term = mul(patch_in, own_columns(grad_mid), TN)
        patch_grad = mul(grad_mid, patch_weights, NT)
        grad_one = sum_heads(mul(grad_qkv_t, qkv_rows_back, TN))
        grad_one = yield "after", (grad_one, ["query", "pair", "cross_output", "self_output"])
        grad_one = grad_one.astype(WIDE)
        input_grad = grad_self + normed_back(grad_one * gain_one, unit_one, rate_one)
        own_grad = own_columns(grad_one)
        table_term = jnp.stack(
            [
                lax.dot_general(onehot.astype(WIDE), v, TN, precision=lax.Precision.HIGHEST)
                for v in (own_grad * own_columns(unit_one), own_grad)
            ],
            axis=1,
        )
        small = [patch_term, table_term.reshape(2 * codes, cols)]
        small += [hidden_gain_term[None], cross_gain_term[None], jnp.zeros((14, cols), WIDE)]
        yield "rows", {
            "self": column_terms(normed_one, grad_qkv_t),
            "small": jnp.concatenate(small, axis=0),
        }
        hidden_sum = yield "take", "hidden"
        result = (after_cross + hidden_sum.astype(WIDE)).astype(LOW)
        yield (
            "done",
            (
                result.reshape(objects, rows, width),
                input_grad.reshape(objects, rows, width),
                patch_grad.reshape(objects, patch_rows, patch_width),
            ),
        )

    steps = [one_group(group) for group in range(groups)]
    asked = [next(step) for step in steps]
    totals, ahead = {}, []
    while asked[0][0] != "done":
        kind, what = asked[0]
        answers = [None] * groups
        if kind == "take":
            answers = jnp.split(totals[what], groups)
        elif kind == "after":
            early = {name: totals[name] for name in what[1]}
            answers = [value for _, (value, _) in asked]
            answers[-1], early = lax.optimization_barrier((answers[-1], early))
            totals.update(early)
        else:
            terms = [value for _, value in asked]
            if kind == "heads":
                terms = jax.tree.map(lambda *parts: jnp.concatenate(parts, axis=0), *terms)
            else:
                for value in terms[1:]:
                    terms[0] = add_trees(terms[0], value)
                terms = terms[0]
            if kind == "rows":
                terms = jax.tree.map(lambda value: value.astype(LOW), terms)
            if kind == "heads":
                totals.update({name: sum_heads(value) for name, value in terms.items()})
            else:
                before = {name: totals[name] for name in ahead}
                terms, before = lax.optimization_barrier((terms, before))
                totals.update(before)
                totals.update(lax.psum(terms, kind))
                ahead = list(terms)
        asked = [step.send(value) for step, value in zip(steps, answers)]
    outputs, input_grads, patch_grads = (
        jnp.concatenate([value[i] for _, value in asked], axis=0) for i in range(3)
    )
    patch_total, table_total, gains = jnp.split(
        totals["small"], [patch_width, patch_width + 2 * codes]
    )
    gradients = (
        table_total.reshape(codes, 2, cols),
        jnp.stack(totals["self"]),
        totals["self_output"],
        gains[1],
        totals["query"],
        jnp.stack(totals["pair"]),
        totals["cross_output"],
        patch_total,
        gains[0],
        totals["widen"],
        totals["narrow"],
    )
    return (outputs, input_grads, patch_grads) + tuple(value.astype(WIDE) for value in gradients)


def solution(mesh):
    sizes = mesh.shape
    paired = sizes["heads"] == 4 and sizes["rows"] == 8
    heads = ("far", "near") if paired else "heads"
    if paired:
        names = (*heads, "rows")
        mesh = jax.sharding.Mesh(mesh.devices.reshape(2, 2, sizes["rows"]), names)
    in_specs = (
        P(None, "rows", None),
        P(None, "rows"),
        P(None, "rows", None),
        P(),
        P(),
        P(None, None, heads),
        P(heads, None),
        P(),
        P(None, heads),
        P(None, None, heads),
        P(heads, None),
        P(),
        P(),
        P(None, heads),
        P(heads, None),
        P(None, "rows", None),
    )
    out_specs = (
        P(None, "rows", None),
        P(None, "rows", None),
        P(None, "rows", None),
        P(None, None, heads),
        P(None, None, heads),
        P(heads, None),
        P(heads),
        P(None, heads),
        P(None, None, heads),
        P(heads, None),
        P(None, heads),
        P(heads),
        P(None, heads),
        P(heads, None),
    )
    return jax.shard_map(
        paired_device if paired else per_device,
        mesh=mesh,
        in_specs=in_specs,
        out_specs=out_specs,
        check_vma=False,
    )
```

```python
import jax
import jax.numpy as jnp
from jax import lax
from jax.experimental import pallas as pl
from jax.experimental.pallas import tpu as pltpu
from jax.sharding import PartitionSpec as P

HEAD_DIM = 64
EPSILON = 1e-05
SCALE = HEAD_DIM ** (-0.5)
LOW = jnp.bfloat16
WIDE = jnp.float32

NN = (((1,), (0,)), ((), ()))
NT = (((1,), (1,)), ((), ()))
TN = (((0,), (0,)), ((), ()))
T_LAST = (((0,), (1,)), ((), ()))


def mul(left, right, dims=NN):
    return lax.dot_general(left, right, dims, preferred_element_type=WIDE)


def load_values(values, block, values_t):
    rows = values_t.shape[1]
    at = slice(block * rows, (block + 1) * rows)
    values[at, :HEAD_DIM] = values_t.T
    values[at, HEAD_DIM:] = jnp.ones((rows, HEAD_DIM), values.dtype)


def attend_block(queries, keys_t, values):
    scores = mul(queries, keys_t)
    peak = jnp.max(scores, axis=1, keepdims=True)
    both = mul(jnp.exp(scores - peak).astype(LOW), values).T
    total = both[HEAD_DIM : HEAD_DIM + 1]
    return both[:HEAD_DIM] / total, peak.T + jnp.log(total)


def attend_block_back(scaled_q, grad_t, keys, keys_t, values, log_total, spread):
    probs = jnp.exp(mul(keys, scaled_q) - log_total)
    grad_scores = (probs * (mul(values, grad_t) - spread)).astype(LOW)
    return (
        (mul(keys_t, grad_scores) * SCALE).astype(LOW),
        mul(grad_scores, scaled_q.T),
        mul(probs.astype(LOW), grad_t.T),
    )


def estimate(rows, cols, passes):
    return pl.CostEstimate(
        flops=int(rows * cols * 1200 * passes), transcendentals=int(rows * cols), bytes_accessed=int(rows * 2048)
    )


VMEM_LIMIT = 48 << 20


def by_length(length, full, blocks, run):
    @pl.when(length * 4 > full)
    def _():
        run(blocks)

    @pl.when(length * 4 <= full)
    def _():
        run(blocks // 4)


def cross_forward(queries_t, pair_t, lengths):
    blocks, _, cols, all_patches = pair_t.shape
    objects = lengths.shape[0]
    heads = cols // HEAD_DIM
    rows, patch_rows = queries_t.shape[1] // objects, all_patches // objects

    def kernel(len_ref, q_ref, pair_ref, mixed_ref, wide_ref, log_ref, keys_t, values):
        queries = (q_ref[...] * LOW(SCALE)).T

        def run(live):
            for c in range(live):
                keys_t[:, c * patch_rows : (c + 1) * patch_rows] = pair_ref[c, 0]
                load_values(values, c, pair_ref[c, 1])
            size = live * patch_rows
            mixed, log_total = attend_block(queries, keys_t[:, :size], values[:size])
            mixed_ref[...] = mixed.astype(LOW)
            wide_ref[...] = mixed
            log_ref[...] = log_total

        by_length(len_ref[pl.program_id(0)], blocks * patch_rows, blocks, run)

    block = pl.BlockSpec((HEAD_DIM, rows), lambda b, j, lens: (j, b))
    return pl.pallas_call(
        kernel,
        grid_spec=pltpu.PrefetchScalarGridSpec(
            num_scalar_prefetch=1,
            grid=(objects, heads),
            in_specs=[
                block,
                pl.BlockSpec((blocks, 2, HEAD_DIM, patch_rows), lambda b, j, lens: (0, 0, j, b)),
            ],
            out_specs=[block, block, pl.BlockSpec((None, 1, rows), lambda b, j, lens: (j, 0, b))],
            scratch_shapes=[
                pltpu.VMEM((HEAD_DIM, blocks * patch_rows), LOW),
                pltpu.VMEM((blocks * patch_rows, 2 * HEAD_DIM), LOW),
            ],
        ),
        out_shape=[
            jax.ShapeDtypeStruct(queries_t.shape, LOW),
            jax.ShapeDtypeStruct(queries_t.shape, WIDE),
            jax.ShapeDtypeStruct((heads, 1, queries_t.shape[1]), WIDE),
        ],
        name="cross_forward",
        cost_estimate=estimate(objects * rows, blocks * patch_rows * heads, 1.4),
        compiler_params=pltpu.CompilerParams(vmem_limit_bytes=VMEM_LIMIT),
    )(lengths, queries_t, pair_t)


def cross_backward(queries_t, pair_t, lengths, grad_t_all, wide, log_total):
    blocks, _, cols, all_patches = pair_t.shape
    objects = lengths.shape[0]
    heads = cols // HEAD_DIM
    rows, patch_rows = queries_t.shape[1] // objects, all_patches // objects

    def kernel(len_ref, q_ref, pair_ref, g_ref, wide_ref, log_ref, out_q, out_pair, keys, keys_t, values):
        grad_t = g_ref[...]
        spread = jnp.sum(grad_t.astype(WIDE) * wide_ref[...], axis=0, keepdims=True)

        def run(live):
            for c in range(live):
                at = slice(c * patch_rows, (c + 1) * patch_rows)
                keys[at] = pair_ref[c, 0].T
                keys_t[:, at] = pair_ref[c, 0]
                values[at] = pair_ref[c, 1].T
            size = live * patch_rows
            out_q[...], grad_k, grad_v = attend_block_back(
                q_ref[...] * LOW(SCALE),
                grad_t,
                keys[:size],
                keys_t[:, :size],
                values[:size],
                log_ref[...],
                spread,
            )
            for c in range(live):
                at = slice(c * patch_rows, (c + 1) * patch_rows)
                out_pair[c, 0] = grad_k[at].T.astype(LOW)
                out_pair[c, 1] = grad_v[at].T.astype(LOW)
            for c in range(live, blocks):
                out_pair[c] = jnp.zeros_like(out_pair[c])

        by_length(len_ref[pl.program_id(0)], blocks * patch_rows, blocks, run)

    block = pl.BlockSpec((HEAD_DIM, rows), lambda b, j, lens: (j, b))
    pair_block = pl.BlockSpec((blocks, 2, HEAD_DIM, patch_rows), lambda b, j, lens: (0, 0, j, b))
    return pl.pallas_call(
        kernel,
        grid_spec=pltpu.PrefetchScalarGridSpec(
            num_scalar_prefetch=1,
            grid=(objects, heads),
            in_specs=[
                block,
                pair_block,
                block,
                block,
                pl.BlockSpec((None, 1, rows), lambda b, j, lens: (j, 0, b)),
            ],
            out_specs=[block, pair_block],
            scratch_shapes=[
                pltpu.VMEM((blocks * patch_rows, HEAD_DIM), LOW),
                pltpu.VMEM((HEAD_DIM, blocks * patch_rows), LOW),
                pltpu.VMEM((blocks * patch_rows, HEAD_DIM), LOW),
            ],
        ),
        out_shape=[
            jax.ShapeDtypeStruct(queries_t.shape, LOW),
            jax.ShapeDtypeStruct(pair_t.shape, LOW),
        ],
        name="cross_backward",
        cost_estimate=estimate(objects * rows, blocks * patch_rows * heads, 2.5),
        compiler_params=pltpu.CompilerParams(vmem_limit_bytes=VMEM_LIMIT),
    )(lengths, queries_t, pair_t, grad_t_all, wide, log_total)


def shift(value, step):
    size = lax.axis_size("heads")
    return lax.ppermute(value, "heads", [((i + step) % size, i) for i in range(size)])


def gather_heads(value):
    size = lax.axis_size("heads")
    if size != 4:
        return [value] + [shift(value, step) for step in range(1, size)]
    after, before = shift(value, 1), shift(value, -1)
    inner = lax.ppermute(after, "heads", [(1, 0), (2, 1)]) + lax.ppermute(before, "heads", [(1, 2), (2, 3)])
    return [value, after, inner, before]


def scatter_heads(partial):
    size, me = lax.axis_size("heads"), lax.axis_index("heads")

    def part(step):
        return lax.dynamic_index_in_dim(partial, (me + step) % size, 0, keepdims=False)

    if size != 4:
        total = part(0)
        for step in range(1, size):
            total = total + shift(part(step).astype(LOW), -step).astype(WIDE)
        return total
    far = part(2).astype(LOW)
    up = lax.ppermute(far, "heads", [(0, 1), (1, 2)]).astype(WIDE)
    down = lax.ppermute(far, "heads", [(2, 1), (3, 2)]).astype(WIDE)
    from_below = shift((part(1) + up).astype(LOW), -1)
    from_above = shift((part(3) + down).astype(LOW), 1)
    return part(0) + from_below.astype(WIDE) + from_above.astype(WIDE)


def in_order(parts):
    size, me = lax.axis_size("heads"), lax.axis_index("heads")
    out = jnp.zeros((size,) + parts[0].shape, parts[0].dtype)
    for step, value in enumerate(parts):
        out = lax.dynamic_update_index_in_dim(out, value, (me + step) % size, 0)
    return out.reshape((-1,) + parts[0].shape[1:])


def sum_heads(partial):
    size = lax.axis_size("heads")
    split = partial.reshape((size, -1) + partial.shape[1:])
    return in_order(gather_heads(scatter_heads(split).astype(LOW)))


def exchange_rows(value):
    return lax.all_to_all(value, "rows", 0, 0, tiled=True)


def normed(value):
    centred = value - jnp.mean(value, axis=-1, keepdims=True)
    rate = lax.rsqrt(jnp.mean(centred * centred, axis=-1, keepdims=True) + EPSILON)
    return centred * rate, rate


def normed_back(grad, unit, rate):
    return rate * (
        grad
        - jnp.mean(grad, axis=-1, keepdims=True)
        - unit * jnp.mean(grad * unit, axis=-1, keepdims=True)
    )


def gelu_tanh(pre_act):
    return jax.nn.gelu(pre_act, approximate=True)


def add_trees(former, latter):
    return jax.tree.map(jnp.add, former, latter)


def pair_forward(queries, pair, key_at, length=None):
    blocks, objects, _, width, rows = queries.shape
    pair_rows = pair.shape[4]
    lengths = jnp.full((objects,), blocks * pair_rows, jnp.int32) if length is None else length

    def kernel(len_ref, q_ref, k_ref, v_ref, mixed_ref, wide_ref, log_ref, keys_t, values):
        def run(live):
            @pl.when(pl.program_id(1) == 0)
            def _():
                for c in range(live):
                    keys_t[:, c * pair_rows : (c + 1) * pair_rows] = k_ref[c]
                    load_values(values, c, v_ref[c])

            size = live * pair_rows
            mixed, log_total = attend_block(
                (q_ref[...] * LOW(SCALE)).T, keys_t[:, :size], values[:size]
            )
            mixed_ref[...] = mixed.astype(LOW)
            wide_ref[...] = mixed
            log_ref[...] = log_total

        if length is None:
            run(blocks)
        else:
            by_length(len_ref[pl.program_id(0)], blocks * pair_rows, blocks, run)

    block = pl.BlockSpec((None, None, width, rows), lambda o, i, lens: (i, o, 0, 0))
    return pl.pallas_call(
        kernel,
        grid_spec=pltpu.PrefetchScalarGridSpec(
            num_scalar_prefetch=1,
            grid=(objects, blocks),
            in_specs=[
                pl.BlockSpec((None, None, None, width, rows), lambda o, i, lens: (i, o, 0, 0, 0)),
                pl.BlockSpec((blocks, None, None, width, pair_rows), lambda o, i, lens: (0, o, key_at, 0, 0)),
                pl.BlockSpec((blocks, None, None, width, pair_rows), lambda o, i, lens: (0, o, key_at + 1, 0, 0)),
            ],
            out_specs=[block, block, pl.BlockSpec((None, None, 1, rows), lambda o, i, lens: (i, o, 0, 0))],
            scratch_shapes=[
                pltpu.VMEM((width, blocks * pair_rows), LOW),
                pltpu.VMEM((blocks * pair_rows, 2 * width), LOW),
            ],
        ),
        out_shape=[
            jax.ShapeDtypeStruct((blocks, objects, width, rows), LOW),
            jax.ShapeDtypeStruct((blocks, objects, width, rows), WIDE),
            jax.ShapeDtypeStruct((blocks, objects, 1, rows), WIDE),
        ],
        name="pair_forward",
        cost_estimate=estimate(objects * blocks * rows, blocks * pair_rows, 2 if length is None else 1.4),
        compiler_params=pltpu.CompilerParams(vmem_limit_bytes=VMEM_LIMIT),
    )(lengths, queries, pair, pair)


def pair_backward(queries, pair, key_at, length, grad_mixed, wide, log_total):
    blocks, objects, _, width, rows = queries.shape
    lengths = jnp.full((objects,), blocks * rows, jnp.int32) if length is None else length

    def kernel(len_ref, q_ref, k_ref, v_ref, g_ref, wide_ref, log_ref, out_ref, keys, keys_t, values, grad_k, grad_v):
        i = pl.program_id(1)

        def run(live):
            size = live * rows

            @pl.when(i == 0)
            def _():
                for c in range(live):
                    at = slice(c * rows, (c + 1) * rows)
                    keys[at] = k_ref[c].T
                    keys_t[:, at] = k_ref[c]
                    values[at] = v_ref[c].T

            grad_t = g_ref[...]
            spread = jnp.sum(grad_t.astype(WIDE) * wide_ref[...], axis=0, keepdims=True)
            out_ref[i, 0], term_k, term_v = attend_block_back(
                q_ref[...] * LOW(SCALE),
                grad_t,
                keys[:size],
                keys_t[:, :size],
                values[:size],
                log_ref[...],
                spread,
            )

            @pl.when(i == 0)
            def _():
                grad_k[:size] = term_k
                grad_v[:size] = term_v

            @pl.when(i > 0)
            def _():
                grad_k[:size] += term_k
                grad_v[:size] += term_v

            @pl.when(i == blocks - 1)
            def _():
                for c in range(live):
                    at = slice(c * rows, (c + 1) * rows)
                    out_ref[c, 1] = grad_k[at].T.astype(LOW)
                    out_ref[c, 2] = grad_v[at].T.astype(LOW)
                for c in range(live, blocks):
                    out_ref[c, 1:] = jnp.zeros_like(out_ref[c, 1:])

        if length is None:
            run(blocks)
        else:
            by_length(len_ref[pl.program_id(0)], blocks * rows, blocks, run)

    block = pl.BlockSpec((None, None, width, rows), lambda o, i, lens: (i, o, 0, 0))
    return pl.pallas_call(
        kernel,
        grid_spec=pltpu.PrefetchScalarGridSpec(
            num_scalar_prefetch=1,
            grid=(objects, blocks),
            in_specs=[
                pl.BlockSpec((None, None, None, width, rows), lambda o, i, lens: (i, o, 0, 0, 0)),
                pl.BlockSpec((blocks, None, None, width, rows), lambda o, i, lens: (0, o, key_at, 0, 0)),
                pl.BlockSpec((blocks, None, None, width, rows), lambda o, i, lens: (0, o, key_at + 1, 0, 0)),
                block,
                block,
                pl.BlockSpec((None, None, 1, rows), lambda o, i, lens: (i, o, 0, 0)),
            ],
            out_specs=pl.BlockSpec((blocks, None, 3, width, rows), lambda o, i, lens: (0, o, 0, 0, 0)),
            scratch_shapes=[
                pltpu.VMEM((blocks * rows, width), LOW),
                pltpu.VMEM((width, blocks * rows), LOW),
                pltpu.VMEM((blocks * rows, width), LOW),
                pltpu.VMEM((blocks * rows, width), WIDE),
                pltpu.VMEM((blocks * rows, width), WIDE),
            ],
        ),
        out_shape=jax.ShapeDtypeStruct((blocks, objects, 3, width, rows), LOW),
        name="pair_backward",
        cost_estimate=estimate(objects * blocks * rows, blocks * rows, 3 if length is None else 2),
        compiler_params=pltpu.CompilerParams(vmem_limit_bytes=VMEM_LIMIT),
    )(lengths, queries, pair, pair, grad_mixed, wide, log_total)


def swap(value, axis):
    return lax.ppermute(value, axis, [(0, 1), (1, 0)])


def sum_near(partial):
    low = partial.astype(LOW)
    return low.astype(WIDE) + swap(low, "near").astype(WIDE)


def tie(value, *others):
    return lax.optimization_barrier((value, *others))


def paired_device(
    tokens,
    cam_index,
    patches,
    patch_len,
    camera_table,
    self_weights,
    self_output,
    cross_gain,
    cross_query,
    cross_pair,
    cross_output,
    patch_weights,
    hidden_gain,
    widen_weights,
    narrow_weights,
    cotangent,
):
    objects = tokens.shape[0] // 2
    _, rows, width = tokens.shape
    cols = self_weights.shape[2]
    hidden = widen_weights.shape[1]
    heads = cols // HEAD_DIM
    codes = camera_table.shape[0]
    patch_width = patches.shape[2]
    count = objects * rows
    n_rows = lax.axis_size("rows")
    row_rank = lax.axis_index("rows")
    far, near = lax.axis_index("far"), lax.axis_index("near")

    def objects_of(value):
        return lax.dynamic_slice_in_dim(value, objects * far, objects, 0)

    def piece(value):
        size = value.shape[0] // n_rows
        return lax.dynamic_slice_in_dim(value, row_rank * size, size, 0)

    def join_rows(value):
        return lax.all_gather(value, "rows", axis=0, tiled=True)

    def both_columns(value):
        return [
            lax.dynamic_slice_in_dim(value, (2 * index + near) * cols, cols, value.ndim - 1)
            for index in range(2)
        ]

    def in_order(mine, away, axis=0):
        size = mine.shape[axis]
        shape = list(mine.shape)
        shape[axis] *= 2
        out = lax.dynamic_update_slice_in_dim(jnp.zeros(shape, mine.dtype), mine, far * size, axis)
        return lax.dynamic_update_slice_in_dim(out, away, (1 - far) * size, axis)

    def halves(value):
        value = value.reshape(objects, 2, rows // 2, -1)
        return [
            lax.dynamic_index_in_dim(value, index, 1, keepdims=False).reshape(count // 2, -1)
            for index in (near, 1 - near)
        ]

    def half_sum_near(partial):
        mine, away = halves(partial)
        return mine + swap(away.astype(LOW), "near").astype(WIDE)

    def over_heads(value):
        value = value.reshape(2, 2, objects, rows // 2, -1)
        value = jnp.where(far == 0, value, jnp.flip(value, 1))
        value = jnp.where(near == 0, value, jnp.flip(value, 0))
        return value.transpose(1, 2, 0, 3, 4).reshape(2 * objects, rows, -1)

    def to_pairs(weights, value, slots):
        parts = [
            mul(weights, value[i * rows : (i + 1) * rows], NT)
            .astype(LOW)
            .reshape(n_rows, slots, HEAD_DIM, rows)
            for i in range(objects)
        ]
        return jnp.stack(parts, axis=1)

    def from_pairs(value):
        return value.transpose(0, 2, 3, 1, 4).reshape(-1, count)

    def over_all_columns(value_t, weight):
        return mul(jnp.concatenate([value_t, swap(value_t, "near")]), weight, TN)

    qkv_rows = self_weights.reshape(3, width, heads, HEAD_DIM).transpose(2, 0, 3, 1)
    qkv_rows = qkv_rows.reshape(3 * cols, width)
    pair_rows = cross_pair.reshape(2, width, heads, HEAD_DIM).transpose(2, 0, 3, 1)
    pair_rows = pair_rows.reshape(2 * cols, width)
    query_rows = cross_query.T

    qkv_away = join_rows(swap(piece(qkv_rows), "far"))

    table_flat = camera_table.reshape(codes, -1)
    cross_gain_f = cross_gain.astype(WIDE)
    hidden_gain_f = hidden_gain.astype(WIDE)

    inputs = objects_of(tokens).reshape(count, width).astype(WIDE)
    patch_in = objects_of(patches).reshape(count, patch_width)
    length = objects_of(patch_len)
    grad_low = objects_of(cotangent).reshape(count, width)
    codes_of = objects_of(cam_index).reshape(count)
    onehot = (codes_of[:, None] == jnp.arange(codes)[None, :]).astype(LOW)
    shift_scale = mul(onehot, table_flat)
    gain_one = 1.0 + shift_scale[:, :width]
    unit_one, rate_one = normed(inputs)
    normed_one = (unit_one * gain_one + shift_scale[:, width:]).astype(LOW)

    mine = [piece(v) for v in (self_output, query_rows, cross_output, pair_rows)]
    normed_one, *mine = tie(normed_one, *mine)
    mine = jnp.concatenate(mine, axis=0)
    across = swap(mine, "far")
    size = cols // n_rows
    two = in_order(mine[None, : 3 * size], across[None, : 3 * size])
    four = jnp.concatenate([two, swap(two, "near")])
    sent = jnp.concatenate([four.reshape(-1, width), across[3 * size :]])
    sent = lax.all_gather(sent, "rows", axis=0)
    pair_away = sent[:, 12 * size :].reshape(2 * cols, width)
    whole = sent[:, : 12 * size].reshape(n_rows, 4, 3, size, width).transpose(2, 1, 0, 3, 4)
    self_whole, query_whole, cross_whole = whole.reshape(3, 4 * cols, width)

    qkv_both = in_order(qkv_rows, qkv_away)
    qkv = exchange_rows(to_pairs(qkv_both, normed_one, 3))
    patch_mid = mul(patch_in, patch_weights).astype(LOW)
    pair_both = in_order(pair_rows, pair_away)
    pair = to_pairs(pair_both, patch_mid, 2)

    mine = [piece(widen_weights), piece(narrow_weights)]
    qkv, *mine = tie(qkv, *mine)
    size = width // n_rows
    sent = lax.all_gather(jnp.concatenate(mine, axis=0), ("far", "rows"), axis=0)
    sent = sent.reshape(2, n_rows, 2, size, width)
    widen = sent[:, :, 0].reshape(2, width, hidden)
    widen = jnp.concatenate([widen[0], widen[1]], axis=1)
    narrow = sent[:, :, 1].reshape(2 * hidden, width)

    mixed, self_wide, self_log = pair_forward(qkv, qkv, 1)
    mixed, pair = tie(exchange_rows(mixed), pair)
    pair = exchange_rows(pair)
    self_mixed_t = from_pairs(mixed[:, :, None])
    after_self = inputs + over_all_columns(self_mixed_t, self_whole)
    unit_two, rate_two = normed(after_self)
    normed_two = (unit_two * cross_gain_f).astype(LOW)
    cross_q, pair = tie(to_pairs(query_whole[: 2 * cols], normed_two, 1), pair)
    cross_q = exchange_rows(cross_q)
    mixed, cross_wide, cross_log = pair_forward(cross_q, pair, 0, length)
    cross_mixed_t = from_pairs(exchange_rows(mixed)[:, :, None])
    after_cross = after_self + over_all_columns(cross_mixed_t, cross_whole)
    unit_three, rate_three = normed(after_cross)
    normed_three = (unit_three * hidden_gain_f).astype(LOW)
    activated, act_back = jax.vjp(gelu_tanh, mul(normed_three, widen))
    activated = activated.astype(LOW)
    grad_pre = act_back(mul(grad_low, narrow, NT))[0].astype(LOW)
    third, activated, grad_pre = tie(mul(grad_pre, widen, NT).astype(LOW), activated, grad_pre)
    grad_three = third.astype(WIDE) + swap(third, "near").astype(WIDE)
    hidden_mine, hidden_away = halves(mul(activated, narrow))
    hidden_away, grad_three = tie(hidden_away.astype(LOW), grad_three)
    hidden_half = hidden_mine + swap(hidden_away, "near").astype(WIDE)
    result = (halves(after_cross)[0] + hidden_half).astype(LOW)

    def part_rows(both):
        return lax.psum_scatter(both, "rows", scatter_dimension=1, tiled=True)

    def own_and_away(value):
        return [lax.dynamic_index_in_dim(value, index, 0, keepdims=False) for index in (far, 1 - far)]

    def add_far(mine, away):
        return (mine.astype(WIDE) + away.astype(WIDE)).astype(LOW)

    def by_shard(left, right):
        return mul(left, right, NN).astype(LOW).reshape(2, -1, right.shape[1])

    hidden_terms = jnp.concatenate(
        [
            mul(value, against, TN).astype(LOW).reshape(2, hidden, width)
            for value, against in ((activated, grad_low), (grad_pre, normed_three))
        ],
        axis=1,
    )
    hidden_part = lax.psum_scatter(
        hidden_terms.reshape(-1, width), ("far", "rows"), scatter_dimension=0, tiled=True
    )

    hidden_gain_term = jnp.sum(grad_three * unit_three, axis=0)
    grad_cross = grad_low.astype(WIDE) + normed_back(
        grad_three * hidden_gain_f, unit_three, rate_three
    )
    grad_cross_low = grad_cross.astype(LOW)
    grad_mixed = exchange_rows(to_pairs(cross_whole[: 2 * cols], grad_cross_low, 1)[:, :, 0])
    grad_mixed, result = tie(grad_mixed, result)
    result_two = jnp.stack([result, swap(result, "far")])
    grads = pair_backward(cross_q, pair, 0, length, grad_mixed, cross_wide, cross_log)
    grads, result_two = tie(grads, result_two)
    grads = exchange_rows(grads)
    grad_cq_t = from_pairs(grads[:, :, :1])
    grad_pair_t = from_pairs(grads[:, :, 1:])
    middle_terms = jnp.concatenate(
        [
            by_shard(cross_mixed_t, grad_cross_low),
            by_shard(grad_cq_t, normed_two),
            by_shard(grad_pair_t, patch_mid),
        ],
        axis=1,
    )
    grad_cq_away, middle_terms = tie(swap(grad_cq_t, "near"), middle_terms)
    middle_part = part_rows(middle_terms)
    grad_two = mul(jnp.concatenate([grad_cq_t, grad_cq_away]), query_whole, TN)
    grad_two, result_two, hidden_part = tie(grad_two, result_two, hidden_part)
    result_four = jnp.stack([result_two, swap(result_two, "near")])
    hidden_total = join_rows(hidden_part)
    cross_gain_term = jnp.sum(grad_two * unit_two, axis=0)
    grad_self = grad_cross + normed_back(grad_two * cross_gain_f, unit_two, rate_two)
    grad_self_low = grad_self.astype(LOW)
    grad_mixed, grad_self_low, grad_mid = tie(
        to_pairs(self_whole[: 2 * cols], grad_self_low, 1)[:, :, 0],
        grad_self_low,
        mul(grad_pair_t, pair_both, TN).astype(LOW),
    )
    grad_mid_away = swap(grad_mid, "near")
    output_terms = by_shard(self_mixed_t, grad_self_low)
    grads = pair_backward(qkv, qkv, 1, None, exchange_rows(grad_mixed), self_wide, self_log)
    grads, grad_mid_away, result_four = tie(grads, grad_mid_away, result_four)
    grad_mid = (grad_mid.astype(WIDE) + grad_mid_away.astype(WIDE)).astype(LOW)
    patch_half = mul(halves(grad_mid)[0], patch_weights, NT).astype(LOW)
    patch_two = jnp.stack([patch_half, swap(patch_half, "far")])
    patch_terms = jnp.stack([mul(value, patch_in, TN).astype(LOW) for value in both_columns(grad_mid)])
    patch_terms = jnp.pad(patch_terms, ((0, 0), (0, 0), (0, width - patch_width)))
    last_terms = jnp.pad(
        jnp.concatenate([output_terms, patch_terms], axis=1), ((0, 0), (3 * cols, 0), (0, 0))
    )
    grads, patch_two, last_terms, hidden_total, middle_part = tie(
        exchange_rows(grads), patch_two, last_terms, hidden_total, middle_part
    )
    grad_qkv_t = from_pairs(grads)
    last_terms = lax.dynamic_update_slice_in_dim(last_terms, by_shard(grad_qkv_t, normed_one), 0, 1)
    last_part = part_rows(last_terms)
    middle_own, middle_away = own_and_away(middle_part)
    middle_total = join_rows(add_far(middle_own, swap(middle_away, "far")))
    grad_one = half_sum_near(mul(grad_qkv_t, qkv_both, TN))
    gain_half, unit_half, rate_half, self_half = (
        halves(value)[0] for value in (gain_one, unit_one, rate_one, grad_self)
    )
    input_half = self_half + normed_back(grad_one * gain_half, unit_half, rate_half)
    input_half = input_half.astype(LOW)
    input_two = jnp.stack([input_half, swap(input_half, "far")])
    input_two, patch_two = tie(input_two, patch_two)
    input_four = jnp.stack([input_two, swap(input_two, "near")])
    patch_four = jnp.stack([patch_two, swap(patch_two, "near")])
    last_part, input_four = tie(last_part, input_four)
    onehot_half = halves(onehot)[0].astype(WIDE)
    table_term = jnp.concatenate(
        [
            lax.dot_general(onehot_half, value, TN, precision=lax.Precision.HIGHEST)
            for value in (grad_one * unit_half, grad_one)
        ],
        axis=0,
    )
    small = [sum_near(table_term), hidden_gain_term[None], cross_gain_term[None], jnp.zeros((14, width), WIDE)]
    small = jnp.stack(both_columns(jnp.concatenate(small, axis=0).astype(LOW)))
    small = jnp.sum(lax.all_gather(small, "rows", axis=0).astype(WIDE), axis=0).astype(LOW)
    small_own, small_away = own_and_away(small)
    small = small_own.astype(WIDE) + swap(small_away, "far").astype(WIDE)
    input_grads = over_heads(input_four)
    outputs, patch_grads = over_heads(result_four), over_heads(patch_four)
    last_own, last_away = own_and_away(last_part)
    last_total = join_rows(add_far(last_own, swap(last_away, "far")))

    cross_output_total, query_total = middle_total[:cols], middle_total[cols : 2 * cols]
    pair_total = middle_total[2 * cols :].reshape(heads, 2, HEAD_DIM, width)
    self_total = last_total[: 3 * cols].reshape(heads, 3, HEAD_DIM, width)
    self_output_total = last_total[3 * cols : 4 * cols]
    patch_total = last_total[4 * cols :, :patch_width]
    gradients = (
        small[: 2 * codes].reshape(2, codes, cols).transpose(1, 0, 2),
        self_total.transpose(1, 3, 0, 2).reshape(3, width, cols),
        self_output_total,
        small[2 * codes + 1],
        query_total.T,
        pair_total.transpose(1, 3, 0, 2).reshape(2, width, cols),
        cross_output_total,
        patch_total.T,
        small[2 * codes],
        hidden_total[hidden:].T,
        hidden_total[:hidden],
    )
    return (outputs, input_grads.astype(WIDE), patch_grads.astype(WIDE)) + tuple(
        value.astype(WIDE) for value in gradients
    )


def per_device(
    tokens,
    cam_index,
    patches,
    patch_len,
    camera_table,
    self_weights,
    self_output,
    cross_gain,
    cross_query,
    cross_pair,
    cross_output,
    patch_weights,
    hidden_gain,
    widen_weights,
    narrow_weights,
    cotangent,
):
    batches, rows, width = tokens.shape
    cols = self_weights.shape[2]
    heads = cols // HEAD_DIM
    codes = camera_table.shape[0]
    patch_rows, patch_width = patches.shape[1:]
    n_rows, n_heads = lax.axis_size("rows"), lax.axis_size("heads")
    row_rank, head_rank = lax.axis_index("rows"), lax.axis_index("heads")
    groups = 1
    objects = batches // groups
    full_lengths = jnp.full((objects,), n_rows * rows, jnp.int32)
    count = objects * rows

    def own_columns(value):
        return lax.dynamic_slice_in_dim(value, head_rank * cols, cols, value.ndim - 1)

    table_flat = camera_table.reshape(codes, -1)
    cross_gain_f = cross_gain.astype(WIDE)
    hidden_gain_f = hidden_gain.astype(WIDE)

    qkv_rows = (
        self_weights.reshape(3, width, heads, HEAD_DIM).transpose(2, 0, 3, 1).reshape(3 * cols, width)
    )
    qkv_rows_back = self_weights.transpose(0, 2, 1).reshape(3 * cols, width)
    pair_rows = cross_pair.transpose(0, 2, 1).reshape(2 * cols, width)
    query_rows = cross_query.T

    local = jnp.stack([self_output, cross_output, query_rows])
    piece = cols // n_rows
    local = lax.dynamic_slice_in_dim(local, row_rank * piece, piece, 1)
    whole = lax.all_gather(jnp.stack(gather_heads(local)), "rows", axis=0)
    whole = whole.transpose(2, 1, 0, 3, 4).reshape(3, n_heads * cols, width)
    self_whole, cross_whole, query_whole = whole[0], whole[1], whole[2]

    def over_all_columns(value_t, weight):
        return mul(jnp.concatenate(gather_heads(value_t), axis=0), weight, TN)

    def by_object(weight, value):
        return jnp.stack(
            [mul(weight, value[i * rows : (i + 1) * rows], NT).astype(LOW) for i in range(objects)]
        )

    def column_terms(value, grads_t):
        return [
            mul(value, grads_t[i : i + cols], (((0,), (1,)), ((), ())))
            for i in range(0, grads_t.shape[0], cols)
        ]

    def one_group(group):
        part = slice(group * objects, (group + 1) * objects)
        inputs = tokens[part].reshape(count, width).astype(WIDE)
        patch_in = patches[part].reshape(objects * patch_rows, patch_width)
        lengths = patch_len[part]
        grad_low = cotangent[part].reshape(count, width)
        onehot = (cam_index[part].reshape(count)[:, None] == jnp.arange(codes)[None, :]).astype(LOW)
        shift_scale = mul(onehot, table_flat)
        gain_one = 1.0 + shift_scale[:, :width]
        unit_one, rate_one = normed(inputs)
        normed_one = (unit_one * gain_one + shift_scale[:, width:]).astype(LOW)
        qkv_t = by_object(qkv_rows, normed_one)
        by_kind = qkv_t.reshape(objects, heads, 3, HEAD_DIM, rows).transpose(2, 1, 3, 0, 4)
        by_kind = by_kind.reshape(3, cols, count)
        self_pair = lax.all_gather(by_kind[1:], "rows", axis=0)
        patch_mid = mul(patch_in, patch_weights).astype(LOW)
        own_pair = mul(pair_rows, patch_mid, NT).astype(LOW).reshape(2, cols, -1)
        pair_t = lax.all_gather(own_pair, "rows", axis=0)
        self_mixed_t, self_wide, self_log = cross_forward(by_kind[0], self_pair, full_lengths)
        after_self = inputs + over_all_columns(self_mixed_t, self_whole)
        unit_two, rate_two = normed(after_self)
        normed_two = (unit_two * cross_gain_f).astype(LOW)
        cross_q_t = mul(query_rows, normed_two, NT).astype(LOW)
        cross_mixed_t, cross_wide, cross_log = cross_forward(cross_q_t, pair_t, lengths)
        after_cross = after_self + over_all_columns(cross_mixed_t, cross_whole)
        unit_three, rate_three = normed(after_cross)
        normed_three = (unit_three * hidden_gain_f).astype(LOW)
        pre_act = mul(normed_three, widen_weights)
        activated, act_back = jax.vjp(gelu_tanh, pre_act)
        activated = activated.astype(LOW)
        grad_pre = act_back(mul(grad_low, narrow_weights, NT))[0].astype(LOW)
        grad_three = sum_heads(mul(grad_pre, widen_weights, NT)).astype(WIDE)
        yield "heads", {"hidden": mul(activated, narrow_weights)}
        yield "rows", {
            "narrow": mul(activated, grad_low, TN),
            "widen": mul(normed_three, grad_pre, TN),
        }
        hidden_gain_term = jnp.sum(own_columns(grad_three * unit_three), axis=0)
        grad_cross = grad_low.astype(WIDE) + normed_back(
            grad_three * hidden_gain_f, unit_three, rate_three
        )
        grad_cross_low = grad_cross.astype(LOW)
        cross_output_term = mul(cross_mixed_t, grad_cross_low)
        grad_mixed_t = mul(cross_output, grad_cross_low, NT).astype(LOW)
        grad_cq_t, grad_pair_t = cross_backward(
            cross_q_t, pair_t, lengths, grad_mixed_t, cross_wide, cross_log
        )
        grad_two = over_all_columns(grad_cq_t, query_whole)
        grad_pair_t = lax.psum_scatter(grad_pair_t, "rows", scatter_dimension=0, tiled=False)
        grad_pair_t = grad_pair_t.reshape(2 * cols, -1)
        query_term = mul(normed_two, grad_cq_t, (((0,), (1,)), ((), ())))
        cross_gain_term = jnp.sum(own_columns(grad_two * unit_two), axis=0)
        grad_self = grad_cross + normed_back(grad_two * cross_gain_f, unit_two, rate_two)
        grad_self_low = grad_self.astype(LOW)
        self_output_term = mul(self_mixed_t, grad_self_low)
        yield "heads", {"patch": mul(grad_pair_t, pair_rows, TN)}
        yield "rows", {
            "query": query_term,
            "pair": column_terms(patch_mid, grad_pair_t),
            "cross_output": cross_output_term,
            "self_output": self_output_term,
        }
        grad_self_mixed_t = mul(self_output, grad_self_low, NT).astype(LOW)
        grad_q_t, grad_kv_t = cross_backward(
            by_kind[0], self_pair, full_lengths, grad_self_mixed_t, self_wide, self_log
        )
        grad_kv_t = lax.psum_scatter(grad_kv_t, "rows", scatter_dimension=0, tiled=False)
        grad_qkv_t = jnp.concatenate([grad_q_t[None], grad_kv_t]).reshape(3 * cols, count)
        grad_qkv_t = yield "after", (grad_qkv_t, ["patch", "narrow", "widen"])
        grad_mid = yield "take", "patch"
        patch_term = mul(patch_in, own_columns(grad_mid), TN)
        patch_grad = mul(grad_mid, patch_weights, NT)
        grad_one = sum_heads(mul(grad_qkv_t, qkv_rows_back, TN))
        grad_one = yield "after", (grad_one, ["query", "pair", "cross_output", "self_output"])
        grad_one = grad_one.astype(WIDE)
        input_grad = grad_self + normed_back(grad_one * gain_one, unit_one, rate_one)
        own_grad = own_columns(grad_one)
        table_term = jnp.stack(
            [
                lax.dot_general(onehot.astype(WIDE), v, TN, precision=lax.Precision.HIGHEST)
                for v in (own_grad * own_columns(unit_one), own_grad)
            ],
            axis=1,
        )
        small = [patch_term, table_term.reshape(2 * codes, cols)]
        small += [hidden_gain_term[None], cross_gain_term[None], jnp.zeros((14, cols), WIDE)]
        yield "rows", {
            "self": column_terms(normed_one, grad_qkv_t),
            "small": jnp.concatenate(small, axis=0),
        }
        hidden_sum = yield "take", "hidden"
        result = (after_cross + hidden_sum.astype(WIDE)).astype(LOW)
        yield (
            "done",
            (
                result.reshape(objects, rows, width),
                input_grad.reshape(objects, rows, width),
                patch_grad.reshape(objects, patch_rows, patch_width),
            ),
        )

    steps = [one_group(group) for group in range(groups)]
    asked = [next(step) for step in steps]
    totals, ahead = {}, []
    while asked[0][0] != "done":
        kind, what = asked[0]
        answers = [None] * groups
        if kind == "take":
            answers = jnp.split(totals[what], groups)
        elif kind == "after":
            early = {name: totals[name] for name in what[1]}
            answers = [value for _, (value, _) in asked]
            answers[-1], early = lax.optimization_barrier((answers[-1], early))
            totals.update(early)
        else:
            terms = [value for _, value in asked]
            if kind == "heads":
                terms = jax.tree.map(lambda *parts: jnp.concatenate(parts, axis=0), *terms)
            else:
                for value in terms[1:]:
                    terms[0] = add_trees(terms[0], value)
                terms = terms[0]
            if kind == "rows":
                terms = jax.tree.map(lambda value: value.astype(LOW), terms)
            if kind == "heads":
                totals.update({name: sum_heads(value) for name, value in terms.items()})
            else:
                before = {name: totals[name] for name in ahead}
                terms, before = lax.optimization_barrier((terms, before))
                totals.update(before)
                totals.update(lax.psum(terms, kind))
                ahead = list(terms)
        asked = [step.send(value) for step, value in zip(steps, answers)]
    outputs, input_grads, patch_grads = (
        jnp.concatenate([value[i] for _, value in asked], axis=0) for i in range(3)
    )
    patch_total, table_total, gains = jnp.split(
        totals["small"], [patch_width, patch_width + 2 * codes]
    )
    gradients = (
        table_total.reshape(codes, 2, cols),
        jnp.stack(totals["self"]),
        totals["self_output"],
        gains[1],
        totals["query"],
        jnp.stack(totals["pair"]),
        totals["cross_output"],
        patch_total,
        gains[0],
        totals["widen"],
        totals["narrow"],
    )
    return (outputs, input_grads, patch_grads) + tuple(value.astype(WIDE) for value in gradients)


def solution(mesh):
    sizes = mesh.shape
    paired = sizes["heads"] == 4 and sizes["rows"] == 8
    heads = ("far", "near") if paired else "heads"
    if paired:
        names = (*heads, "rows")
        mesh = jax.sharding.Mesh(mesh.devices.reshape(2, 2, sizes["rows"]), names)
    in_specs = (
        P(None, "rows", None),
        P(None, "rows"),
        P(None, "rows", None),
        P(),
        P(),
        P(None, None, heads),
        P(heads, None),
        P(),
        P(None, heads),
        P(None, None, heads),
        P(heads, None),
        P(),
        P(),
        P(None, heads),
        P(heads, None),
        P(None, "rows", None),
    )
    out_specs = (
        P(None, "rows", None),
        P(None, "rows", None),
        P(None, "rows", None),
        P(None, None, heads),
        P(None, None, heads),
        P(heads, None),
        P(heads),
        P(None, heads),
        P(None, None, heads),
        P(heads, None),
        P(None, heads),
        P(heads),
        P(None, heads),
        P(heads, None),
    )
    return jax.shard_map(
        paired_device if paired else per_device,
        mesh=mesh,
        in_specs=in_specs,
        out_specs=out_specs,
        check_vma=False,
    )
```

```python
import jax
import jax.numpy as jnp
from jax import lax
from jax.experimental import pallas as pl
from jax.experimental.pallas import tpu as pltpu
from jax.sharding import PartitionSpec as P

HEAD_DIM = 64
EPSILON = 1e-05
SCALE = HEAD_DIM ** (-0.5)
LOW = jnp.bfloat16
WIDE = jnp.float32

NN = (((1,), (0,)), ((), ()))
NT = (((1,), (1,)), ((), ()))
TN = (((0,), (0,)), ((), ()))
T_LAST = (((0,), (1,)), ((), ()))


def mul(left, right, dims=NN):
    return lax.dot_general(left, right, dims, preferred_element_type=WIDE)


def load_values(values, block, values_t):
    rows = values_t.shape[1]
    at = slice(block * rows, (block + 1) * rows)
    values[at, :HEAD_DIM] = values_t.T
    values[at, HEAD_DIM:] = jnp.ones((rows, HEAD_DIM), values.dtype)


def attend_block(queries, keys_t, values):
    scores = mul(queries, keys_t)
    peak = jnp.max(scores, axis=1, keepdims=True)
    both = mul(jnp.exp(scores - peak).astype(LOW), values).T
    total = both[HEAD_DIM : HEAD_DIM + 1]
    return both[:HEAD_DIM] / total, peak.T + jnp.log(total)


def attend_block_back(scaled_q, grad_t, keys, keys_t, values, log_total, spread):
    probs = jnp.exp(mul(keys, scaled_q) - log_total)
    grad_scores = (probs * (mul(values, grad_t) - spread)).astype(LOW)
    return (
        (mul(keys_t, grad_scores) * SCALE).astype(LOW),
        mul(grad_scores, scaled_q.T),
        mul(probs.astype(LOW), grad_t.T),
    )


def estimate(rows, cols, passes):
    return pl.CostEstimate(
        flops=int(rows * cols * 1200 * passes), transcendentals=int(rows * cols), bytes_accessed=int(rows * 2048)
    )


VMEM_LIMIT = 48 << 20


def by_length(length, full, blocks, run):
    @pl.when(length * 4 > full)
    def _():
        run(blocks)

    @pl.when(length * 4 <= full)
    def _():
        run(blocks // 4)


def cross_forward(queries_t, pair_t, lengths):
    blocks, _, cols, all_patches = pair_t.shape
    objects = lengths.shape[0]
    heads = cols // HEAD_DIM
    rows, patch_rows = queries_t.shape[1] // objects, all_patches // objects

    def kernel(len_ref, q_ref, pair_ref, mixed_ref, wide_ref, log_ref, keys_t, values):
        queries = (q_ref[...] * LOW(SCALE)).T

        def run(live):
            for c in range(live):
                keys_t[:, c * patch_rows : (c + 1) * patch_rows] = pair_ref[c, 0]
                load_values(values, c, pair_ref[c, 1])
            size = live * patch_rows
            mixed, log_total = attend_block(queries, keys_t[:, :size], values[:size])
            mixed_ref[...] = mixed.astype(LOW)
            wide_ref[...] = mixed
            log_ref[...] = log_total

        by_length(len_ref[pl.program_id(0)], blocks * patch_rows, blocks, run)

    block = pl.BlockSpec((HEAD_DIM, rows), lambda b, j, lens: (j, b))
    return pl.pallas_call(
        kernel,
        grid_spec=pltpu.PrefetchScalarGridSpec(
            num_scalar_prefetch=1,
            grid=(objects, heads),
            in_specs=[
                block,
                pl.BlockSpec((blocks, 2, HEAD_DIM, patch_rows), lambda b, j, lens: (0, 0, j, b)),
            ],
            out_specs=[block, block, pl.BlockSpec((None, 1, rows), lambda b, j, lens: (j, 0, b))],
            scratch_shapes=[
                pltpu.VMEM((HEAD_DIM, blocks * patch_rows), LOW),
                pltpu.VMEM((blocks * patch_rows, 2 * HEAD_DIM), LOW),
            ],
        ),
        out_shape=[
            jax.ShapeDtypeStruct(queries_t.shape, LOW),
            jax.ShapeDtypeStruct(queries_t.shape, WIDE),
            jax.ShapeDtypeStruct((heads, 1, queries_t.shape[1]), WIDE),
        ],
        name="cross_forward",
        cost_estimate=estimate(objects * rows, blocks * patch_rows * heads, 1.4),
        compiler_params=pltpu.CompilerParams(vmem_limit_bytes=VMEM_LIMIT),
    )(lengths, queries_t, pair_t)


def cross_backward(queries_t, pair_t, lengths, grad_t_all, wide, log_total):
    blocks, _, cols, all_patches = pair_t.shape
    objects = lengths.shape[0]
    heads = cols // HEAD_DIM
    rows, patch_rows = queries_t.shape[1] // objects, all_patches // objects

    def kernel(len_ref, q_ref, pair_ref, g_ref, wide_ref, log_ref, out_q, out_pair, keys, keys_t, values):
        grad_t = g_ref[...]
        spread = jnp.sum(grad_t.astype(WIDE) * wide_ref[...], axis=0, keepdims=True)

        def run(live):
            for c in range(live):
                at = slice(c * patch_rows, (c + 1) * patch_rows)
                keys[at] = pair_ref[c, 0].T
                keys_t[:, at] = pair_ref[c, 0]
                values[at] = pair_ref[c, 1].T
            size = live * patch_rows
            out_q[...], grad_k, grad_v = attend_block_back(
                q_ref[...] * LOW(SCALE),
                grad_t,
                keys[:size],
                keys_t[:, :size],
                values[:size],
                log_ref[...],
                spread,
            )
            for c in range(live):
                at = slice(c * patch_rows, (c + 1) * patch_rows)
                out_pair[c, 0] = grad_k[at].T.astype(LOW)
                out_pair[c, 1] = grad_v[at].T.astype(LOW)
            for c in range(live, blocks):
                out_pair[c] = jnp.zeros_like(out_pair[c])

        by_length(len_ref[pl.program_id(0)], blocks * patch_rows, blocks, run)

    block = pl.BlockSpec((HEAD_DIM, rows), lambda b, j, lens: (j, b))
    pair_block = pl.BlockSpec((blocks, 2, HEAD_DIM, patch_rows), lambda b, j, lens: (0, 0, j, b))
    return pl.pallas_call(
        kernel,
        grid_spec=pltpu.PrefetchScalarGridSpec(
            num_scalar_prefetch=1,
            grid=(objects, heads),
            in_specs=[
                block,
                pair_block,
                block,
                block,
                pl.BlockSpec((None, 1, rows), lambda b, j, lens: (j, 0, b)),
            ],
            out_specs=[block, pair_block],
            scratch_shapes=[
                pltpu.VMEM((blocks * patch_rows, HEAD_DIM), LOW),
                pltpu.VMEM((HEAD_DIM, blocks * patch_rows), LOW),
                pltpu.VMEM((blocks * patch_rows, HEAD_DIM), LOW),
            ],
        ),
        out_shape=[
            jax.ShapeDtypeStruct(queries_t.shape, LOW),
            jax.ShapeDtypeStruct(pair_t.shape, LOW),
        ],
        name="cross_backward",
        cost_estimate=estimate(objects * rows, blocks * patch_rows * heads, 2.5),
        compiler_params=pltpu.CompilerParams(vmem_limit_bytes=VMEM_LIMIT),
    )(lengths, queries_t, pair_t, grad_t_all, wide, log_total)


def shift(value, step):
    size = lax.axis_size("heads")
    return lax.ppermute(value, "heads", [((i + step) % size, i) for i in range(size)])


def gather_heads(value):
    size = lax.axis_size("heads")
    if size != 4:
        return [value] + [shift(value, step) for step in range(1, size)]
    after, before = shift(value, 1), shift(value, -1)
    inner = lax.ppermute(after, "heads", [(1, 0), (2, 1)]) + lax.ppermute(before, "heads", [(1, 2), (2, 3)])
    return [value, after, inner, before]


def scatter_heads(partial):
    size, me = lax.axis_size("heads"), lax.axis_index("heads")

    def part(step):
        return lax.dynamic_index_in_dim(partial, (me + step) % size, 0, keepdims=False)

    if size != 4:
        total = part(0)
        for step in range(1, size):
            total = total + shift(part(step).astype(LOW), -step).astype(WIDE)
        return total
    far = part(2).astype(LOW)
    up = lax.ppermute(far, "heads", [(0, 1), (1, 2)]).astype(WIDE)
    down = lax.ppermute(far, "heads", [(2, 1), (3, 2)]).astype(WIDE)
    from_below = shift((part(1) + up).astype(LOW), -1)
    from_above = shift((part(3) + down).astype(LOW), 1)
    return part(0) + from_below.astype(WIDE) + from_above.astype(WIDE)


def in_order(parts):
    size, me = lax.axis_size("heads"), lax.axis_index("heads")
    out = jnp.zeros((size,) + parts[0].shape, parts[0].dtype)
    for step, value in enumerate(parts):
        out = lax.dynamic_update_index_in_dim(out, value, (me + step) % size, 0)
    return out.reshape((-1,) + parts[0].shape[1:])


def sum_heads(partial):
    size = lax.axis_size("heads")
    split = partial.reshape((size, -1) + partial.shape[1:])
    return in_order(gather_heads(scatter_heads(split).astype(LOW)))


def exchange_rows(value):
    return lax.all_to_all(value, "rows", 0, 0, tiled=True)


def normed(value):
    centred = value - jnp.mean(value, axis=-1, keepdims=True)
    rate = lax.rsqrt(jnp.mean(centred * centred, axis=-1, keepdims=True) + EPSILON)
    return centred * rate, rate


def normed_back(grad, unit, rate):
    return rate * (
        grad
        - jnp.mean(grad, axis=-1, keepdims=True)
        - unit * jnp.mean(grad * unit, axis=-1, keepdims=True)
    )


def gelu_tanh(pre_act):
    return jax.nn.gelu(pre_act, approximate=True)


def add_trees(former, latter):
    return jax.tree.map(jnp.add, former, latter)


def pair_forward(queries, pair, key_at, length=None):
    blocks, objects, _, width, rows = queries.shape
    pair_rows = pair.shape[4]
    lengths = jnp.full((objects,), blocks * pair_rows, jnp.int32) if length is None else length

    def kernel(len_ref, q_ref, k_ref, v_ref, mixed_ref, wide_ref, log_ref, keys_t, values):
        def run(live):
            @pl.when(pl.program_id(1) == 0)
            def _():
                for c in range(live):
                    keys_t[:, c * pair_rows : (c + 1) * pair_rows] = k_ref[c]
                    load_values(values, c, v_ref[c])

            size = live * pair_rows
            mixed, log_total = attend_block(
                (q_ref[...] * LOW(SCALE)).T, keys_t[:, :size], values[:size]
            )
            mixed_ref[...] = mixed.astype(LOW)
            wide_ref[...] = mixed
            log_ref[...] = log_total

        if length is None:
            run(blocks)
        else:
            by_length(len_ref[pl.program_id(0)], blocks * pair_rows, blocks, run)

    block = pl.BlockSpec((None, None, width, rows), lambda o, i, lens: (i, o, 0, 0))
    return pl.pallas_call(
        kernel,
        grid_spec=pltpu.PrefetchScalarGridSpec(
            num_scalar_prefetch=1,
            grid=(objects, blocks),
            in_specs=[
                pl.BlockSpec((None, None, None, width, rows), lambda o, i, lens: (i, o, 0, 0, 0)),
                pl.BlockSpec((blocks, None, None, width, pair_rows), lambda o, i, lens: (0, o, key_at, 0, 0)),
                pl.BlockSpec((blocks, None, None, width, pair_rows), lambda o, i, lens: (0, o, key_at + 1, 0, 0)),
            ],
            out_specs=[block, block, pl.BlockSpec((None, None, 1, rows), lambda o, i, lens: (i, o, 0, 0))],
            scratch_shapes=[
                pltpu.VMEM((width, blocks * pair_rows), LOW),
                pltpu.VMEM((blocks * pair_rows, 2 * width), LOW),
            ],
        ),
        out_shape=[
            jax.ShapeDtypeStruct((blocks, objects, width, rows), LOW),
            jax.ShapeDtypeStruct((blocks, objects, width, rows), WIDE),
            jax.ShapeDtypeStruct((blocks, objects, 1, rows), WIDE),
        ],
        name="pair_forward",
        cost_estimate=estimate(objects * blocks * rows, blocks * pair_rows, 2 if length is None else 1.4),
        compiler_params=pltpu.CompilerParams(vmem_limit_bytes=VMEM_LIMIT),
    )(lengths, queries, pair, pair)


def pair_backward(queries, pair, key_at, length, grad_mixed, wide, log_total):
    blocks, objects, _, width, rows = queries.shape
    lengths = jnp.full((objects,), blocks * rows, jnp.int32) if length is None else length

    def kernel(len_ref, q_ref, k_ref, v_ref, g_ref, wide_ref, log_ref, out_ref, keys, keys_t, values, grad_k, grad_v):
        i = pl.program_id(1)

        def run(live):
            size = live * rows

            @pl.when(i == 0)
            def _():
                for c in range(live):
                    at = slice(c * rows, (c + 1) * rows)
                    keys[at] = k_ref[c].T
                    keys_t[:, at] = k_ref[c]
                    values[at] = v_ref[c].T

            grad_t = g_ref[...]
            spread = jnp.sum(grad_t.astype(WIDE) * wide_ref[...], axis=0, keepdims=True)
            out_ref[i, 0], term_k, term_v = attend_block_back(
                q_ref[...] * LOW(SCALE),
                grad_t,
                keys[:size],
                keys_t[:, :size],
                values[:size],
                log_ref[...],
                spread,
            )

            @pl.when(i == 0)
            def _():
                grad_k[:size] = term_k
                grad_v[:size] = term_v

            @pl.when(i > 0)
            def _():
                grad_k[:size] += term_k
                grad_v[:size] += term_v

            @pl.when(i == blocks - 1)
            def _():
                for c in range(live):
                    at = slice(c * rows, (c + 1) * rows)
                    out_ref[c, 1] = grad_k[at].T.astype(LOW)
                    out_ref[c, 2] = grad_v[at].T.astype(LOW)
                for c in range(live, blocks):
                    out_ref[c, 1:] = jnp.zeros_like(out_ref[c, 1:])

        if length is None:
            run(blocks)
        else:
            by_length(len_ref[pl.program_id(0)], blocks * rows, blocks, run)

    block = pl.BlockSpec((None, None, width, rows), lambda o, i, lens: (i, o, 0, 0))
    return pl.pallas_call(
        kernel,
        grid_spec=pltpu.PrefetchScalarGridSpec(
            num_scalar_prefetch=1,
            grid=(objects, blocks),
            in_specs=[
                pl.BlockSpec((None, None, None, width, rows), lambda o, i, lens: (i, o, 0, 0, 0)),
                pl.BlockSpec((blocks, None, None, width, rows), lambda o, i, lens: (0, o, key_at, 0, 0)),
                pl.BlockSpec((blocks, None, None, width, rows), lambda o, i, lens: (0, o, key_at + 1, 0, 0)),
                block,
                block,
                pl.BlockSpec((None, None, 1, rows), lambda o, i, lens: (i, o, 0, 0)),
            ],
            out_specs=pl.BlockSpec((blocks, None, 3, width, rows), lambda o, i, lens: (0, o, 0, 0, 0)),
            scratch_shapes=[
                pltpu.VMEM((blocks * rows, width), LOW),
                pltpu.VMEM((width, blocks * rows), LOW),
                pltpu.VMEM((blocks * rows, width), LOW),
                pltpu.VMEM((blocks * rows, width), WIDE),
                pltpu.VMEM((blocks * rows, width), WIDE),
            ],
        ),
        out_shape=jax.ShapeDtypeStruct((blocks, objects, 3, width, rows), LOW),
        name="pair_backward",
        cost_estimate=estimate(objects * blocks * rows, blocks * rows, 3 if length is None else 2),
        compiler_params=pltpu.CompilerParams(vmem_limit_bytes=VMEM_LIMIT),
    )(lengths, queries, pair, pair, grad_mixed, wide, log_total)


def swap(value, axis):
    return lax.ppermute(value, axis, [(0, 1), (1, 0)])


def sum_near(partial):
    low = partial.astype(LOW)
    return low.astype(WIDE) + swap(low, "near").astype(WIDE)


def tie(value, *others):
    return lax.optimization_barrier((value, *others))


def paired_device(
    tokens,
    cam_index,
    patches,
    patch_len,
    camera_table,
    self_weights,
    self_output,
    cross_gain,
    cross_query,
    cross_pair,
    cross_output,
    patch_weights,
    hidden_gain,
    widen_weights,
    narrow_weights,
    cotangent,
):
    objects = tokens.shape[0] // 2
    _, rows, width = tokens.shape
    cols = self_weights.shape[2]
    hidden = widen_weights.shape[1]
    heads = cols // HEAD_DIM
    codes = camera_table.shape[0]
    patch_width = patches.shape[2]
    count = objects * rows
    n_rows = lax.axis_size("rows")
    row_rank = lax.axis_index("rows")
    far, near = lax.axis_index("far"), lax.axis_index("near")

    def objects_of(value):
        return lax.dynamic_slice_in_dim(value, objects * far, objects, 0)

    def piece(value):
        size = value.shape[0] // n_rows
        return lax.dynamic_slice_in_dim(value, row_rank * size, size, 0)

    def join_rows(value):
        return lax.all_gather(value, "rows", axis=0, tiled=True)

    def both_columns(value):
        return [
            lax.dynamic_slice_in_dim(value, (2 * index + near) * cols, cols, value.ndim - 1)
            for index in range(2)
        ]

    def in_order(mine, away, axis=0):
        size = mine.shape[axis]
        shape = list(mine.shape)
        shape[axis] *= 2
        out = lax.dynamic_update_slice_in_dim(jnp.zeros(shape, mine.dtype), mine, far * size, axis)
        return lax.dynamic_update_slice_in_dim(out, away, (1 - far) * size, axis)

    def halves(value):
        value = value.reshape(objects, 2, rows // 2, -1)
        return [
            lax.dynamic_index_in_dim(value, index, 1, keepdims=False).reshape(count // 2, -1)
            for index in (near, 1 - near)
        ]

    def half_sum_near(partial):
        mine, away = halves(partial)
        return mine + swap(away.astype(LOW), "near").astype(WIDE)

    def over_heads(value):
        value = value.reshape(2, 2, objects, rows // 2, -1)
        value = jnp.where(far == 0, value, jnp.flip(value, 1))
        value = jnp.where(near == 0, value, jnp.flip(value, 0))
        return value.transpose(1, 2, 0, 3, 4).reshape(2 * objects, rows, -1)

    def to_pairs(weights, value, slots):
        parts = [
            mul(weights, value[i * rows : (i + 1) * rows], NT)
            .astype(LOW)
            .reshape(n_rows, slots, HEAD_DIM, rows)
            for i in range(objects)
        ]
        return jnp.stack(parts, axis=1)

    def from_pairs(value):
        return value.transpose(0, 2, 3, 1, 4).reshape(-1, count)

    def over_all_columns(value_t, weight):
        return mul(jnp.concatenate([value_t, swap(value_t, "near")]), weight, TN)

    qkv_rows = self_weights.reshape(3, width, heads, HEAD_DIM).transpose(2, 0, 3, 1)
    qkv_rows = qkv_rows.reshape(3 * cols, width)
    pair_rows = cross_pair.reshape(2, width, heads, HEAD_DIM).transpose(2, 0, 3, 1)
    pair_rows = pair_rows.reshape(2 * cols, width)
    query_rows = cross_query.T

    qkv_away = join_rows(swap(piece(qkv_rows), "far"))

    table_flat = camera_table.reshape(codes, -1)
    cross_gain_f = cross_gain.astype(WIDE)
    hidden_gain_f = hidden_gain.astype(WIDE)

    inputs = objects_of(tokens).reshape(count, width).astype(WIDE)
    patch_in = objects_of(patches).reshape(count, patch_width)
    length = objects_of(patch_len)
    grad_low = objects_of(cotangent).reshape(count, width)
    codes_of = objects_of(cam_index).reshape(count)
    onehot = (codes_of[:, None] == jnp.arange(codes)[None, :]).astype(LOW)
    shift_scale = mul(onehot, table_flat)
    gain_one = 1.0 + shift_scale[:, :width]
    unit_one, rate_one = normed(inputs)
    normed_one = (unit_one * gain_one + shift_scale[:, width:]).astype(LOW)

    mine = [piece(v) for v in (self_output, query_rows, cross_output, pair_rows)]
    normed_one, *mine = tie(normed_one, *mine)
    mine = jnp.concatenate(mine, axis=0)
    across = swap(mine, "far")
    size = cols // n_rows
    two = in_order(mine[None, : 3 * size], across[None, : 3 * size])
    four = jnp.concatenate([two, swap(two, "near")])
    sent = jnp.concatenate([four.reshape(-1, width), across[3 * size :]])
    sent = lax.all_gather(sent, "rows", axis=0)
    pair_away = sent[:, 12 * size :].reshape(2 * cols, width)
    whole = sent[:, : 12 * size].reshape(n_rows, 4, 3, size, width).transpose(2, 1, 0, 3, 4)
    self_whole, query_whole, cross_whole = whole.reshape(3, 4 * cols, width)

    qkv_both = in_order(qkv_rows, qkv_away)
    qkv = exchange_rows(to_pairs(qkv_both, normed_one, 3))
    patch_mid = mul(patch_in, patch_weights).astype(LOW)
    pair_both = in_order(pair_rows, pair_away)
    pair = to_pairs(pair_both, patch_mid, 2)

    mine = [piece(widen_weights), piece(narrow_weights)]
    qkv, *mine = tie(qkv, *mine)
    size = width // n_rows
    sent = lax.all_gather(jnp.concatenate(mine, axis=0), ("far", "rows"), axis=0)
    sent = sent.reshape(2, n_rows, 2, size, width)
    widen = sent[:, :, 0].reshape(2, width, hidden)
    widen = jnp.concatenate([widen[0], widen[1]], axis=1)
    narrow = sent[:, :, 1].reshape(2 * hidden, width)

    mixed, self_wide, self_log = pair_forward(qkv, qkv, 1)
    mixed, pair = tie(exchange_rows(mixed), pair)
    pair = exchange_rows(pair)
    self_mixed_t = from_pairs(mixed[:, :, None])
    after_self = inputs + over_all_columns(self_mixed_t, self_whole)
    unit_two, rate_two = normed(after_self)
    normed_two = (unit_two * cross_gain_f).astype(LOW)
    cross_q, pair = tie(to_pairs(query_whole[: 2 * cols], normed_two, 1), pair)
    cross_q = exchange_rows(cross_q)
    mixed, cross_wide, cross_log = pair_forward(cross_q, pair, 0, length)
    cross_mixed_t = from_pairs(exchange_rows(mixed)[:, :, None])
    after_cross = after_self + over_all_columns(cross_mixed_t, cross_whole)
    unit_three, rate_three = normed(after_cross)
    normed_three = (unit_three * hidden_gain_f).astype(LOW)
    activated, act_back = jax.vjp(gelu_tanh, mul(normed_three, widen))
    activated = activated.astype(LOW)
    grad_pre = act_back(mul(grad_low, narrow, NT))[0].astype(LOW)
    third, activated, grad_pre = tie(mul(grad_pre, widen, NT).astype(LOW), activated, grad_pre)
    grad_three = third.astype(WIDE) + swap(third, "near").astype(WIDE)
    hidden_mine, hidden_away = halves(mul(activated, narrow))
    hidden_away, grad_three = tie(hidden_away.astype(LOW), grad_three)
    hidden_half = hidden_mine + swap(hidden_away, "near").astype(WIDE)
    result = (halves(after_cross)[0] + hidden_half).astype(LOW)

    def part_rows(both):
        return lax.psum_scatter(both, "rows", scatter_dimension=1, tiled=True)

    def own_and_away(value):
        return [lax.dynamic_index_in_dim(value, index, 0, keepdims=False) for index in (far, 1 - far)]

    def add_far(mine, away):
        return (mine.astype(WIDE) + away.astype(WIDE)).astype(LOW)

    def by_shard(left, right):
        return mul(left, right, NN).astype(LOW).reshape(2, -1, right.shape[1])

    hidden_terms = jnp.concatenate(
        [
            mul(value, against, TN).astype(LOW).reshape(2, hidden, width)
            for value, against in ((activated, grad_low), (grad_pre, normed_three))
        ],
        axis=1,
    )
    hidden_part = part_rows(hidden_terms)

    hidden_gain_term = jnp.sum(grad_three * unit_three, axis=0)
    grad_cross = grad_low.astype(WIDE) + normed_back(
        grad_three * hidden_gain_f, unit_three, rate_three
    )
    grad_cross_low = grad_cross.astype(LOW)
    grad_mixed = exchange_rows(to_pairs(cross_whole[: 2 * cols], grad_cross_low, 1)[:, :, 0])
    grad_mixed, hidden_part = tie(grad_mixed, hidden_part)
    hidden_own, hidden_away = own_and_away(hidden_part)
    hidden_away = swap(hidden_away, "far")
    grads = pair_backward(cross_q, pair, 0, length, grad_mixed, cross_wide, cross_log)
    grads, hidden_away, result = tie(grads, hidden_away, result)
    hidden_total = join_rows(add_far(hidden_own, hidden_away))
    result_two = jnp.stack([result, swap(result, "far")])
    grads, result_two = tie(exchange_rows(grads), result_two)
    grad_cq_t = from_pairs(grads[:, :, :1])
    grad_pair_t = from_pairs(grads[:, :, 1:])
    middle_terms = jnp.concatenate(
        [
            by_shard(cross_mixed_t, grad_cross_low),
            by_shard(grad_cq_t, normed_two),
            by_shard(grad_pair_t, patch_mid),
        ],
        axis=1,
    )
    grad_cq_away, middle_terms = tie(swap(grad_cq_t, "near"), middle_terms)
    middle_part = part_rows(middle_terms)
    grad_two = mul(jnp.concatenate([grad_cq_t, grad_cq_away]), query_whole, TN)
    grad_two, result_two = tie(grad_two, result_two)
    result_four = jnp.stack([result_two, swap(result_two, "near")])
    cross_gain_term = jnp.sum(grad_two * unit_two, axis=0)
    grad_self = grad_cross + normed_back(grad_two * cross_gain_f, unit_two, rate_two)
    grad_self_low = grad_self.astype(LOW)
    grad_mixed, grad_self_low, grad_mid = tie(
        to_pairs(self_whole[: 2 * cols], grad_self_low, 1)[:, :, 0],
        grad_self_low,
        mul(grad_pair_t, pair_both, TN).astype(LOW),
    )
    grad_mid_away = swap(grad_mid, "near")
    output_terms = by_shard(self_mixed_t, grad_self_low)
    grads = pair_backward(qkv, qkv, 1, None, exchange_rows(grad_mixed), self_wide, self_log)
    grads, grad_mid_away, result_four = tie(grads, grad_mid_away, result_four)
    grad_mid = (grad_mid.astype(WIDE) + grad_mid_away.astype(WIDE)).astype(LOW)
    patch_half = mul(halves(grad_mid)[0], patch_weights, NT).astype(LOW)
    patch_two = jnp.stack([patch_half, swap(patch_half, "far")])
    patch_terms = jnp.stack([mul(value, patch_in, TN).astype(LOW) for value in both_columns(grad_mid)])
    patch_terms = jnp.pad(patch_terms, ((0, 0), (0, 0), (0, width - patch_width)))
    last_terms = jnp.pad(
        jnp.concatenate([output_terms, patch_terms], axis=1), ((0, 0), (3 * cols, 0), (0, 0))
    )
    hidden_gradients = [hidden_total[hidden:].T.astype(WIDE), hidden_total[:hidden].astype(WIDE)]
    grads, patch_two, last_terms, hidden_gradients, middle_part = tie(
        exchange_rows(grads), patch_two, last_terms, hidden_gradients, middle_part
    )
    grad_qkv_t = from_pairs(grads)
    last_terms = lax.dynamic_update_slice_in_dim(last_terms, by_shard(grad_qkv_t, normed_one), 0, 1)
    last_part = part_rows(last_terms)
    middle_own, middle_away = own_and_away(middle_part)
    middle_total = join_rows(add_far(middle_own, swap(middle_away, "far")))
    grad_one = half_sum_near(mul(grad_qkv_t, qkv_both, TN))
    gain_half, unit_half, rate_half, self_half = (
        halves(value)[0] for value in (gain_one, unit_one, rate_one, grad_self)
    )
    input_half = self_half + normed_back(grad_one * gain_half, unit_half, rate_half)
    input_half = input_half.astype(LOW)
    input_two = jnp.stack([input_half, swap(input_half, "far")])
    last_part, input_two, patch_two = tie(last_part, input_two, patch_two)
    input_four = jnp.stack([input_two, swap(input_two, "near")])
    patch_four = jnp.stack([patch_two, swap(patch_two, "near")])
    onehot_half = halves(onehot)[0].astype(WIDE)
    table_term = jnp.concatenate(
        [
            lax.dot_general(onehot_half, value, TN, precision=lax.Precision.HIGHEST)
            for value in (grad_one * unit_half, grad_one)
        ],
        axis=0,
    )
    small = [sum_near(table_term), hidden_gain_term[None], cross_gain_term[None], jnp.zeros((14, width), WIDE)]
    small = jnp.stack(both_columns(jnp.concatenate(small, axis=0).astype(LOW)))
    small = jnp.sum(lax.all_gather(small, "rows", axis=0).astype(WIDE), axis=0).astype(LOW)
    small_own, small_away = own_and_away(small)
    small = small_own.astype(WIDE) + swap(small_away, "far").astype(WIDE)
    input_grads = over_heads(input_four)
    outputs, patch_grads = over_heads(result_four), over_heads(patch_four)
    last_own, last_away = own_and_away(last_part)
    last_total = join_rows(add_far(last_own, swap(last_away, "far")))

    cross_output_total, query_total = middle_total[:cols], middle_total[cols : 2 * cols]
    pair_total = middle_total[2 * cols :].reshape(heads, 2, HEAD_DIM, width)
    self_total = last_total[: 3 * cols].reshape(heads, 3, HEAD_DIM, width)
    self_output_total = last_total[3 * cols : 4 * cols]
    patch_total = last_total[4 * cols :, :patch_width]
    gradients = (
        small[: 2 * codes].reshape(2, codes, cols).transpose(1, 0, 2),
        self_total.transpose(1, 3, 0, 2).reshape(3, width, cols),
        self_output_total,
        small[2 * codes + 1],
        query_total.T,
        pair_total.transpose(1, 3, 0, 2).reshape(2, width, cols),
        cross_output_total,
        patch_total.T,
        small[2 * codes],
        *hidden_gradients,
    )
    return (outputs, input_grads.astype(WIDE), patch_grads.astype(WIDE)) + tuple(
        value.astype(WIDE) for value in gradients
    )


def per_device(
    tokens,
    cam_index,
    patches,
    patch_len,
    camera_table,
    self_weights,
    self_output,
    cross_gain,
    cross_query,
    cross_pair,
    cross_output,
    patch_weights,
    hidden_gain,
    widen_weights,
    narrow_weights,
    cotangent,
):
    batches, rows, width = tokens.shape
    cols = self_weights.shape[2]
    heads = cols // HEAD_DIM
    codes = camera_table.shape[0]
    patch_rows, patch_width = patches.shape[1:]
    n_rows, n_heads = lax.axis_size("rows"), lax.axis_size("heads")
    row_rank, head_rank = lax.axis_index("rows"), lax.axis_index("heads")
    groups = 1
    objects = batches // groups
    full_lengths = jnp.full((objects,), n_rows * rows, jnp.int32)
    count = objects * rows

    def own_columns(value):
        return lax.dynamic_slice_in_dim(value, head_rank * cols, cols, value.ndim - 1)

    table_flat = camera_table.reshape(codes, -1)
    cross_gain_f = cross_gain.astype(WIDE)
    hidden_gain_f = hidden_gain.astype(WIDE)

    qkv_rows = (
        self_weights.reshape(3, width, heads, HEAD_DIM).transpose(2, 0, 3, 1).reshape(3 * cols, width)
    )
    qkv_rows_back = self_weights.transpose(0, 2, 1).reshape(3 * cols, width)
    pair_rows = cross_pair.transpose(0, 2, 1).reshape(2 * cols, width)
    query_rows = cross_query.T

    local = jnp.stack([self_output, cross_output, query_rows])
    piece = cols // n_rows
    local = lax.dynamic_slice_in_dim(local, row_rank * piece, piece, 1)
    whole = lax.all_gather(jnp.stack(gather_heads(local)), "rows", axis=0)
    whole = whole.transpose(2, 1, 0, 3, 4).reshape(3, n_heads * cols, width)
    self_whole, cross_whole, query_whole = whole[0], whole[1], whole[2]

    def over_all_columns(value_t, weight):
        return mul(jnp.concatenate(gather_heads(value_t), axis=0), weight, TN)

    def by_object(weight, value):
        return jnp.stack(
            [mul(weight, value[i * rows : (i + 1) * rows], NT).astype(LOW) for i in range(objects)]
        )

    def column_terms(value, grads_t):
        return [
            mul(value, grads_t[i : i + cols], (((0,), (1,)), ((), ())))
            for i in range(0, grads_t.shape[0], cols)
        ]

    def one_group(group):
        part = slice(group * objects, (group + 1) * objects)
        inputs = tokens[part].reshape(count, width).astype(WIDE)
        patch_in = patches[part].reshape(objects * patch_rows, patch_width)
        lengths = patch_len[part]
        grad_low = cotangent[part].reshape(count, width)
        onehot = (cam_index[part].reshape(count)[:, None] == jnp.arange(codes)[None, :]).astype(LOW)
        shift_scale = mul(onehot, table_flat)
        gain_one = 1.0 + shift_scale[:, :width]
        unit_one, rate_one = normed(inputs)
        normed_one = (unit_one * gain_one + shift_scale[:, width:]).astype(LOW)
        qkv_t = by_object(qkv_rows, normed_one)
        by_kind = qkv_t.reshape(objects, heads, 3, HEAD_DIM, rows).transpose(2, 1, 3, 0, 4)
        by_kind = by_kind.reshape(3, cols, count)
        self_pair = lax.all_gather(by_kind[1:], "rows", axis=0)
        patch_mid = mul(patch_in, patch_weights).astype(LOW)
        own_pair = mul(pair_rows, patch_mid, NT).astype(LOW).reshape(2, cols, -1)
        pair_t = lax.all_gather(own_pair, "rows", axis=0)
        self_mixed_t, self_wide, self_log = cross_forward(by_kind[0], self_pair, full_lengths)
        after_self = inputs + over_all_columns(self_mixed_t, self_whole)
        unit_two, rate_two = normed(after_self)
        normed_two = (unit_two * cross_gain_f).astype(LOW)
        cross_q_t = mul(query_rows, normed_two, NT).astype(LOW)
        cross_mixed_t, cross_wide, cross_log = cross_forward(cross_q_t, pair_t, lengths)
        after_cross = after_self + over_all_columns(cross_mixed_t, cross_whole)
        unit_three, rate_three = normed(after_cross)
        normed_three = (unit_three * hidden_gain_f).astype(LOW)
        pre_act = mul(normed_three, widen_weights)
        activated, act_back = jax.vjp(gelu_tanh, pre_act)
        activated = activated.astype(LOW)
        grad_pre = act_back(mul(grad_low, narrow_weights, NT))[0].astype(LOW)
        grad_three = sum_heads(mul(grad_pre, widen_weights, NT)).astype(WIDE)
        yield "heads", {"hidden": mul(activated, narrow_weights)}
        yield "rows", {
            "narrow": mul(activated, grad_low, TN),
            "widen": mul(normed_three, grad_pre, TN),
        }
        hidden_gain_term = jnp.sum(own_columns(grad_three * unit_three), axis=0)
        grad_cross = grad_low.astype(WIDE) + normed_back(
            grad_three * hidden_gain_f, unit_three, rate_three
        )
        grad_cross_low = grad_cross.astype(LOW)
        cross_output_term = mul(cross_mixed_t, grad_cross_low)
        grad_mixed_t = mul(cross_output, grad_cross_low, NT).astype(LOW)
        grad_cq_t, grad_pair_t = cross_backward(
            cross_q_t, pair_t, lengths, grad_mixed_t, cross_wide, cross_log
        )
        grad_two = over_all_columns(grad_cq_t, query_whole)
        grad_pair_t = lax.psum_scatter(grad_pair_t, "rows", scatter_dimension=0, tiled=False)
        grad_pair_t = grad_pair_t.reshape(2 * cols, -1)
        query_term = mul(normed_two, grad_cq_t, (((0,), (1,)), ((), ())))
        cross_gain_term = jnp.sum(own_columns(grad_two * unit_two), axis=0)
        grad_self = grad_cross + normed_back(grad_two * cross_gain_f, unit_two, rate_two)
        grad_self_low = grad_self.astype(LOW)
        self_output_term = mul(self_mixed_t, grad_self_low)
        yield "heads", {"patch": mul(grad_pair_t, pair_rows, TN)}
        yield "rows", {
            "query": query_term,
            "pair": column_terms(patch_mid, grad_pair_t),
            "cross_output": cross_output_term,
            "self_output": self_output_term,
        }
        grad_self_mixed_t = mul(self_output, grad_self_low, NT).astype(LOW)
        grad_q_t, grad_kv_t = cross_backward(
            by_kind[0], self_pair, full_lengths, grad_self_mixed_t, self_wide, self_log
        )
        grad_kv_t = lax.psum_scatter(grad_kv_t, "rows", scatter_dimension=0, tiled=False)
        grad_qkv_t = jnp.concatenate([grad_q_t[None], grad_kv_t]).reshape(3 * cols, count)
        grad_qkv_t = yield "after", (grad_qkv_t, ["patch", "narrow", "widen"])
        grad_mid = yield "take", "patch"
        patch_term = mul(patch_in, own_columns(grad_mid), TN)
        patch_grad = mul(grad_mid, patch_weights, NT)
        grad_one = sum_heads(mul(grad_qkv_t, qkv_rows_back, TN))
        grad_one = yield "after", (grad_one, ["query", "pair", "cross_output", "self_output"])
        grad_one = grad_one.astype(WIDE)
        input_grad = grad_self + normed_back(grad_one * gain_one, unit_one, rate_one)
        own_grad = own_columns(grad_one)
        table_term = jnp.stack(
            [
                lax.dot_general(onehot.astype(WIDE), v, TN, precision=lax.Precision.HIGHEST)
                for v in (own_grad * own_columns(unit_one), own_grad)
            ],
            axis=1,
        )
        small = [patch_term, table_term.reshape(2 * codes, cols)]
        small += [hidden_gain_term[None], cross_gain_term[None], jnp.zeros((14, cols), WIDE)]
        yield "rows", {
            "self": column_terms(normed_one, grad_qkv_t),
            "small": jnp.concatenate(small, axis=0),
        }
        hidden_sum = yield "take", "hidden"
        result = (after_cross + hidden_sum.astype(WIDE)).astype(LOW)
        yield (
            "done",
            (
                result.reshape(objects, rows, width),
                input_grad.reshape(objects, rows, width),
                patch_grad.reshape(objects, patch_rows, patch_width),
            ),
        )

    steps = [one_group(group) for group in range(groups)]
    asked = [next(step) for step in steps]
    totals, ahead = {}, []
    while asked[0][0] != "done":
        kind, what = asked[0]
        answers = [None] * groups
        if kind == "take":
            answers = jnp.split(totals[what], groups)
        elif kind == "after":
            early = {name: totals[name] for name in what[1]}
            answers = [value for _, (value, _) in asked]
            answers[-1], early = lax.optimization_barrier((answers[-1], early))
            totals.update(early)
        else:
            terms = [value for _, value in asked]
            if kind == "heads":
                terms = jax.tree.map(lambda *parts: jnp.concatenate(parts, axis=0), *terms)
            else:
                for value in terms[1:]:
                    terms[0] = add_trees(terms[0], value)
                terms = terms[0]
            if kind == "rows":
                terms = jax.tree.map(lambda value: value.astype(LOW), terms)
            if kind == "heads":
                totals.update({name: sum_heads(value) for name, value in terms.items()})
            else:
                before = {name: totals[name] for name in ahead}
                terms, before = lax.optimization_barrier((terms, before))
                totals.update(before)
                totals.update(lax.psum(terms, kind))
                ahead = list(terms)
        asked = [step.send(value) for step, value in zip(steps, answers)]
    outputs, input_grads, patch_grads = (
        jnp.concatenate([value[i] for _, value in asked], axis=0) for i in range(3)
    )
    patch_total, table_total, gains = jnp.split(
        totals["small"], [patch_width, patch_width + 2 * codes]
    )
    gradients = (
        table_total.reshape(codes, 2, cols),
        jnp.stack(totals["self"]),
        totals["self_output"],
        gains[1],
        totals["query"],
        jnp.stack(totals["pair"]),
        totals["cross_output"],
        patch_total,
        gains[0],
        totals["widen"],
        totals["narrow"],
    )
    return (outputs, input_grads, patch_grads) + tuple(value.astype(WIDE) for value in gradients)


def solution(mesh):
    sizes = mesh.shape
    paired = sizes["heads"] == 4 and sizes["rows"] == 8
    heads = ("far", "near") if paired else "heads"
    if paired:
        names = (*heads, "rows")
        mesh = jax.sharding.Mesh(mesh.devices.reshape(2, 2, sizes["rows"]), names)
    in_specs = (
        P(None, "rows", None),
        P(None, "rows"),
        P(None, "rows", None),
        P(),
        P(),
        P(None, None, heads),
        P(heads, None),
        P(),
        P(None, heads),
        P(None, None, heads),
        P(heads, None),
        P(),
        P(),
        P(None, heads),
        P(heads, None),
        P(None, "rows", None),
    )
    out_specs = (
        P(None, "rows", None),
        P(None, "rows", None),
        P(None, "rows", None),
        P(None, None, heads),
        P(None, None, heads),
        P(heads, None),
        P(heads),
        P(None, heads),
        P(None, None, heads),
        P(heads, None),
        P(None, heads),
        P(heads),
        P(None, heads),
        P(heads, None),
    )
    return jax.shard_map(
        paired_device if paired else per_device,
        mesh=mesh,
        in_specs=in_specs,
        out_specs=out_specs,
        check_vma=False,
    )
```

```python
import jax
import jax.numpy as jnp
from jax import lax
from jax.experimental import pallas as pl
from jax.experimental.pallas import tpu as pltpu
from jax.sharding import PartitionSpec as P

HEAD_DIM = 64
EPSILON = 1e-05
SCALE = HEAD_DIM ** (-0.5)
LOW = jnp.bfloat16
WIDE = jnp.float32

NN = (((1,), (0,)), ((), ()))
NT = (((1,), (1,)), ((), ()))
TN = (((0,), (0,)), ((), ()))
T_LAST = (((0,), (1,)), ((), ()))


def mul(left, right, dims=NN):
    return lax.dot_general(left, right, dims, preferred_element_type=WIDE)


def load_values(values, block, values_t):
    rows = values_t.shape[1]
    at = slice(block * rows, (block + 1) * rows)
    values[at, :HEAD_DIM] = values_t.T
    values[at, HEAD_DIM:] = jnp.ones((rows, HEAD_DIM), values.dtype)


def attend_block(queries, keys_t, values):
    scores = mul(queries, keys_t)
    peak = jnp.max(scores, axis=1, keepdims=True)
    both = mul(jnp.exp(scores - peak).astype(LOW), values).T
    total = both[HEAD_DIM : HEAD_DIM + 1]
    return both[:HEAD_DIM] / total, peak.T + jnp.log(total)


def attend_block_back(scaled_q, grad_t, keys, keys_t, values, log_total, spread):
    probs = jnp.exp(mul(keys, scaled_q) - log_total)
    grad_scores = (probs * (mul(values, grad_t) - spread)).astype(LOW)
    return (
        (mul(keys_t, grad_scores) * SCALE).astype(LOW),
        mul(grad_scores, scaled_q.T),
        mul(probs.astype(LOW), grad_t.T),
    )


def estimate(rows, cols, passes):
    return pl.CostEstimate(
        flops=int(rows * cols * 1200 * passes), transcendentals=int(rows * cols), bytes_accessed=int(rows * 2048)
    )


VMEM_LIMIT = 48 << 20


def by_length(length, full, blocks, run):
    @pl.when(length * 4 > full)
    def _():
        run(blocks)

    @pl.when(length * 4 <= full)
    def _():
        run(blocks // 4)


def cross_forward(queries_t, pair_t, lengths):
    blocks, _, cols, all_patches = pair_t.shape
    objects = lengths.shape[0]
    heads = cols // HEAD_DIM
    rows, patch_rows = queries_t.shape[1] // objects, all_patches // objects

    def kernel(len_ref, q_ref, pair_ref, mixed_ref, wide_ref, log_ref, keys_t, values):
        queries = (q_ref[...] * LOW(SCALE)).T

        def run(live):
            for c in range(live):
                keys_t[:, c * patch_rows : (c + 1) * patch_rows] = pair_ref[c, 0]
                load_values(values, c, pair_ref[c, 1])
            size = live * patch_rows
            mixed, log_total = attend_block(queries, keys_t[:, :size], values[:size])
            mixed_ref[...] = mixed.astype(LOW)
            wide_ref[...] = mixed
            log_ref[...] = log_total

        by_length(len_ref[pl.program_id(0)], blocks * patch_rows, blocks, run)

    block = pl.BlockSpec((HEAD_DIM, rows), lambda b, j, lens: (j, b))
    return pl.pallas_call(
        kernel,
        grid_spec=pltpu.PrefetchScalarGridSpec(
            num_scalar_prefetch=1,
            grid=(objects, heads),
            in_specs=[
                block,
                pl.BlockSpec((blocks, 2, HEAD_DIM, patch_rows), lambda b, j, lens: (0, 0, j, b)),
            ],
            out_specs=[block, block, pl.BlockSpec((None, 1, rows), lambda b, j, lens: (j, 0, b))],
            scratch_shapes=[
                pltpu.VMEM((HEAD_DIM, blocks * patch_rows), LOW),
                pltpu.VMEM((blocks * patch_rows, 2 * HEAD_DIM), LOW),
            ],
        ),
        out_shape=[
            jax.ShapeDtypeStruct(queries_t.shape, LOW),
            jax.ShapeDtypeStruct(queries_t.shape, WIDE),
            jax.ShapeDtypeStruct((heads, 1, queries_t.shape[1]), WIDE),
        ],
        name="cross_forward",
        cost_estimate=estimate(objects * rows, blocks * patch_rows * heads, 1.4),
        compiler_params=pltpu.CompilerParams(vmem_limit_bytes=VMEM_LIMIT),
    )(lengths, queries_t, pair_t)


def cross_backward(queries_t, pair_t, lengths, grad_t_all, wide, log_total):
    blocks, _, cols, all_patches = pair_t.shape
    objects = lengths.shape[0]
    heads = cols // HEAD_DIM
    rows, patch_rows = queries_t.shape[1] // objects, all_patches // objects

    def kernel(len_ref, q_ref, pair_ref, g_ref, wide_ref, log_ref, out_q, out_pair, keys, keys_t, values):
        grad_t = g_ref[...]
        spread = jnp.sum(grad_t.astype(WIDE) * wide_ref[...], axis=0, keepdims=True)

        def run(live):
            for c in range(live):
                at = slice(c * patch_rows, (c + 1) * patch_rows)
                keys[at] = pair_ref[c, 0].T
                keys_t[:, at] = pair_ref[c, 0]
                values[at] = pair_ref[c, 1].T
            size = live * patch_rows
            out_q[...], grad_k, grad_v = attend_block_back(
                q_ref[...] * LOW(SCALE),
                grad_t,
                keys[:size],
                keys_t[:, :size],
                values[:size],
                log_ref[...],
                spread,
            )
            for c in range(live):
                at = slice(c * patch_rows, (c + 1) * patch_rows)
                out_pair[c, 0] = grad_k[at].T.astype(LOW)
                out_pair[c, 1] = grad_v[at].T.astype(LOW)
            for c in range(live, blocks):
                out_pair[c] = jnp.zeros_like(out_pair[c])

        by_length(len_ref[pl.program_id(0)], blocks * patch_rows, blocks, run)

    block = pl.BlockSpec((HEAD_DIM, rows), lambda b, j, lens: (j, b))
    pair_block = pl.BlockSpec((blocks, 2, HEAD_DIM, patch_rows), lambda b, j, lens: (0, 0, j, b))
    return pl.pallas_call(
        kernel,
        grid_spec=pltpu.PrefetchScalarGridSpec(
            num_scalar_prefetch=1,
            grid=(objects, heads),
            in_specs=[
                block,
                pair_block,
                block,
                block,
                pl.BlockSpec((None, 1, rows), lambda b, j, lens: (j, 0, b)),
            ],
            out_specs=[block, pair_block],
            scratch_shapes=[
                pltpu.VMEM((blocks * patch_rows, HEAD_DIM), LOW),
                pltpu.VMEM((HEAD_DIM, blocks * patch_rows), LOW),
                pltpu.VMEM((blocks * patch_rows, HEAD_DIM), LOW),
            ],
        ),
        out_shape=[
            jax.ShapeDtypeStruct(queries_t.shape, LOW),
            jax.ShapeDtypeStruct(pair_t.shape, LOW),
        ],
        name="cross_backward",
        cost_estimate=estimate(objects * rows, blocks * patch_rows * heads, 2.5),
        compiler_params=pltpu.CompilerParams(vmem_limit_bytes=VMEM_LIMIT),
    )(lengths, queries_t, pair_t, grad_t_all, wide, log_total)


def shift(value, step):
    size = lax.axis_size("heads")
    return lax.ppermute(value, "heads", [((i + step) % size, i) for i in range(size)])


def gather_heads(value):
    size = lax.axis_size("heads")
    if size != 4:
        return [value] + [shift(value, step) for step in range(1, size)]
    after, before = shift(value, 1), shift(value, -1)
    inner = lax.ppermute(after, "heads", [(1, 0), (2, 1)]) + lax.ppermute(before, "heads", [(1, 2), (2, 3)])
    return [value, after, inner, before]


def scatter_heads(partial):
    size, me = lax.axis_size("heads"), lax.axis_index("heads")

    def part(step):
        return lax.dynamic_index_in_dim(partial, (me + step) % size, 0, keepdims=False)

    if size != 4:
        total = part(0)
        for step in range(1, size):
            total = total + shift(part(step).astype(LOW), -step).astype(WIDE)
        return total
    far = part(2).astype(LOW)
    up = lax.ppermute(far, "heads", [(0, 1), (1, 2)]).astype(WIDE)
    down = lax.ppermute(far, "heads", [(2, 1), (3, 2)]).astype(WIDE)
    from_below = shift((part(1) + up).astype(LOW), -1)
    from_above = shift((part(3) + down).astype(LOW), 1)
    return part(0) + from_below.astype(WIDE) + from_above.astype(WIDE)


def in_order(parts):
    size, me = lax.axis_size("heads"), lax.axis_index("heads")
    out = jnp.zeros((size,) + parts[0].shape, parts[0].dtype)
    for step, value in enumerate(parts):
        out = lax.dynamic_update_index_in_dim(out, value, (me + step) % size, 0)
    return out.reshape((-1,) + parts[0].shape[1:])


def sum_heads(partial):
    size = lax.axis_size("heads")
    split = partial.reshape((size, -1) + partial.shape[1:])
    return in_order(gather_heads(scatter_heads(split).astype(LOW)))


def exchange_rows(value):
    return lax.all_to_all(value, "rows", 0, 0, tiled=True)


def normed(value):
    centred = value - jnp.mean(value, axis=-1, keepdims=True)
    rate = lax.rsqrt(jnp.mean(centred * centred, axis=-1, keepdims=True) + EPSILON)
    return centred * rate, rate


def normed_back(grad, unit, rate):
    return rate * (
        grad
        - jnp.mean(grad, axis=-1, keepdims=True)
        - unit * jnp.mean(grad * unit, axis=-1, keepdims=True)
    )


def gelu_tanh(pre_act):
    return jax.nn.gelu(pre_act, approximate=True)


def add_trees(former, latter):
    return jax.tree.map(jnp.add, former, latter)


def pair_forward(queries, pair, key_at, length=None):
    blocks, objects, _, width, rows = queries.shape
    pair_rows = pair.shape[4]
    lengths = jnp.full((objects,), blocks * pair_rows, jnp.int32) if length is None else length

    def kernel(len_ref, q_ref, k_ref, v_ref, mixed_ref, wide_ref, log_ref, keys_t, values):
        def run(live):
            @pl.when(pl.program_id(1) == 0)
            def _():
                for c in range(live):
                    keys_t[:, c * pair_rows : (c + 1) * pair_rows] = k_ref[c]
                    load_values(values, c, v_ref[c])

            size = live * pair_rows
            mixed, log_total = attend_block(
                (q_ref[...] * LOW(SCALE)).T, keys_t[:, :size], values[:size]
            )
            mixed_ref[...] = mixed.astype(LOW)
            wide_ref[...] = mixed
            log_ref[...] = log_total

        if length is None:
            run(blocks)
        else:
            by_length(len_ref[pl.program_id(0)], blocks * pair_rows, blocks, run)

    block = pl.BlockSpec((None, None, width, rows), lambda o, i, lens: (i, o, 0, 0))
    return pl.pallas_call(
        kernel,
        grid_spec=pltpu.PrefetchScalarGridSpec(
            num_scalar_prefetch=1,
            grid=(objects, blocks),
            in_specs=[
                pl.BlockSpec((None, None, None, width, rows), lambda o, i, lens: (i, o, 0, 0, 0)),
                pl.BlockSpec((blocks, None, None, width, pair_rows), lambda o, i, lens: (0, o, key_at, 0, 0)),
                pl.BlockSpec((blocks, None, None, width, pair_rows), lambda o, i, lens: (0, o, key_at + 1, 0, 0)),
            ],
            out_specs=[block, block, pl.BlockSpec((None, None, 1, rows), lambda o, i, lens: (i, o, 0, 0))],
            scratch_shapes=[
                pltpu.VMEM((width, blocks * pair_rows), LOW),
                pltpu.VMEM((blocks * pair_rows, 2 * width), LOW),
            ],
        ),
        out_shape=[
            jax.ShapeDtypeStruct((blocks, objects, width, rows), LOW),
            jax.ShapeDtypeStruct((blocks, objects, width, rows), WIDE),
            jax.ShapeDtypeStruct((blocks, objects, 1, rows), WIDE),
        ],
        name="pair_forward",
        cost_estimate=estimate(objects * blocks * rows, blocks * pair_rows, 2 if length is None else 1.4),
        compiler_params=pltpu.CompilerParams(vmem_limit_bytes=VMEM_LIMIT),
    )(lengths, queries, pair, pair)


def pair_backward(queries, pair, key_at, length, grad_mixed, wide, log_total):
    blocks, objects, _, width, rows = queries.shape
    lengths = jnp.full((objects,), blocks * rows, jnp.int32) if length is None else length

    def kernel(len_ref, q_ref, k_ref, v_ref, g_ref, wide_ref, log_ref, out_ref, keys, keys_t, values, grad_k, grad_v):
        i = pl.program_id(1)

        def run(live):
            size = live * rows

            @pl.when(i == 0)
            def _():
                for c in range(live):
                    at = slice(c * rows, (c + 1) * rows)
                    keys[at] = k_ref[c].T
                    keys_t[:, at] = k_ref[c]
                    values[at] = v_ref[c].T

            grad_t = g_ref[...]
            spread = jnp.sum(grad_t.astype(WIDE) * wide_ref[...], axis=0, keepdims=True)
            out_ref[i, 0], term_k, term_v = attend_block_back(
                q_ref[...] * LOW(SCALE),
                grad_t,
                keys[:size],
                keys_t[:, :size],
                values[:size],
                log_ref[...],
                spread,
            )

            @pl.when(i == 0)
            def _():
                grad_k[:size] = term_k
                grad_v[:size] = term_v

            @pl.when(i > 0)
            def _():
                grad_k[:size] += term_k
                grad_v[:size] += term_v

            @pl.when(i == blocks - 1)
            def _():
                for c in range(live):
                    at = slice(c * rows, (c + 1) * rows)
                    out_ref[c, 1] = grad_k[at].T.astype(LOW)
                    out_ref[c, 2] = grad_v[at].T.astype(LOW)
                for c in range(live, blocks):
                    out_ref[c, 1:] = jnp.zeros_like(out_ref[c, 1:])

        if length is None:
            run(blocks)
        else:
            by_length(len_ref[pl.program_id(0)], blocks * rows, blocks, run)

    block = pl.BlockSpec((None, None, width, rows), lambda o, i, lens: (i, o, 0, 0))
    return pl.pallas_call(
        kernel,
        grid_spec=pltpu.PrefetchScalarGridSpec(
            num_scalar_prefetch=1,
            grid=(objects, blocks),
            in_specs=[
                pl.BlockSpec((None, None, None, width, rows), lambda o, i, lens: (i, o, 0, 0, 0)),
                pl.BlockSpec((blocks, None, None, width, rows), lambda o, i, lens: (0, o, key_at, 0, 0)),
                pl.BlockSpec((blocks, None, None, width, rows), lambda o, i, lens: (0, o, key_at + 1, 0, 0)),
                block,
                block,
                pl.BlockSpec((None, None, 1, rows), lambda o, i, lens: (i, o, 0, 0)),
            ],
            out_specs=pl.BlockSpec((blocks, None, 3, width, rows), lambda o, i, lens: (0, o, 0, 0, 0)),
            scratch_shapes=[
                pltpu.VMEM((blocks * rows, width), LOW),
                pltpu.VMEM((width, blocks * rows), LOW),
                pltpu.VMEM((blocks * rows, width), LOW),
                pltpu.VMEM((blocks * rows, width), WIDE),
                pltpu.VMEM((blocks * rows, width), WIDE),
            ],
        ),
        out_shape=jax.ShapeDtypeStruct((blocks, objects, 3, width, rows), LOW),
        name="pair_backward",
        cost_estimate=estimate(objects * blocks * rows, blocks * rows, 3 if length is None else 2),
        compiler_params=pltpu.CompilerParams(vmem_limit_bytes=VMEM_LIMIT),
    )(lengths, queries, pair, pair, grad_mixed, wide, log_total)


def swap(value, axis):
    return lax.ppermute(value, axis, [(0, 1), (1, 0)])


def sum_near(partial):
    low = partial.astype(LOW)
    return low.astype(WIDE) + swap(low, "near").astype(WIDE)


def tie(value, *others):
    return lax.optimization_barrier((value, *others))


def paired_device(
    tokens,
    cam_index,
    patches,
    patch_len,
    camera_table,
    self_weights,
    self_output,
    cross_gain,
    cross_query,
    cross_pair,
    cross_output,
    patch_weights,
    hidden_gain,
    widen_weights,
    narrow_weights,
    cotangent,
):
    objects = tokens.shape[0] // 2
    _, rows, width = tokens.shape
    cols = self_weights.shape[2]
    hidden = widen_weights.shape[1]
    heads = cols // HEAD_DIM
    codes = camera_table.shape[0]
    patch_width = patches.shape[2]
    count = objects * rows
    n_rows = lax.axis_size("rows")
    row_rank = lax.axis_index("rows")
    far, near = lax.axis_index("far"), lax.axis_index("near")

    def objects_of(value):
        return lax.dynamic_slice_in_dim(value, objects * far, objects, 0)

    def piece(value):
        size = value.shape[0] // n_rows
        return lax.dynamic_slice_in_dim(value, row_rank * size, size, 0)

    def join_rows(value):
        return lax.all_gather(value, "rows", axis=0, tiled=True)

    def both_columns(value):
        return [
            lax.dynamic_slice_in_dim(value, (2 * index + near) * cols, cols, value.ndim - 1)
            for index in range(2)
        ]

    def in_order(mine, away, axis=0):
        size = mine.shape[axis]
        shape = list(mine.shape)
        shape[axis] *= 2
        out = lax.dynamic_update_slice_in_dim(jnp.zeros(shape, mine.dtype), mine, far * size, axis)
        return lax.dynamic_update_slice_in_dim(out, away, (1 - far) * size, axis)

    def halves(value):
        value = value.reshape(objects, 2, rows // 2, -1)
        return [
            lax.dynamic_index_in_dim(value, index, 1, keepdims=False).reshape(count // 2, -1)
            for index in (near, 1 - near)
        ]

    def half_sum_near(partial):
        mine, away = halves(partial)
        return mine + swap(away.astype(LOW), "near").astype(WIDE)

    def over_heads(value):
        value = value.reshape(2, 2, objects, rows // 2, -1)
        value = jnp.where(far == 0, value, jnp.flip(value, 1))
        value = jnp.where(near == 0, value, jnp.flip(value, 0))
        return value.transpose(1, 2, 0, 3, 4).reshape(2 * objects, rows, -1)

    def to_pairs(weights, value, slots):
        parts = [
            mul(weights, value[i * rows : (i + 1) * rows], NT)
            .astype(LOW)
            .reshape(n_rows, slots, HEAD_DIM, rows)
            for i in range(objects)
        ]
        return jnp.stack(parts, axis=1)

    def from_pairs(value):
        return value.transpose(0, 2, 3, 1, 4).reshape(-1, count)

    def over_all_columns(value_t, weight):
        return mul(jnp.concatenate([value_t, swap(value_t, "near")]), weight, TN)

    qkv_rows = self_weights.reshape(3, width, heads, HEAD_DIM).transpose(2, 0, 3, 1)
    qkv_rows = qkv_rows.reshape(3 * cols, width)
    pair_rows = cross_pair.reshape(2, width, heads, HEAD_DIM).transpose(2, 0, 3, 1)
    pair_rows = pair_rows.reshape(2 * cols, width)
    query_rows = cross_query.T

    qkv_away = join_rows(swap(piece(qkv_rows), "far"))

    table_flat = camera_table.reshape(codes, -1)
    cross_gain_f = cross_gain.astype(WIDE)
    hidden_gain_f = hidden_gain.astype(WIDE)

    inputs = objects_of(tokens).reshape(count, width).astype(WIDE)
    patch_in = objects_of(patches).reshape(count, patch_width)
    length = objects_of(patch_len)
    grad_low = objects_of(cotangent).reshape(count, width)
    codes_of = objects_of(cam_index).reshape(count)
    onehot = (codes_of[:, None] == jnp.arange(codes)[None, :]).astype(LOW)
    shift_scale = mul(onehot, table_flat)
    gain_one = 1.0 + shift_scale[:, :width]
    unit_one, rate_one = normed(inputs)
    normed_one = (unit_one * gain_one + shift_scale[:, width:]).astype(LOW)

    mine = [piece(v) for v in (self_output, query_rows, cross_output, pair_rows)]
    normed_one, *mine = tie(normed_one, *mine)
    mine = jnp.concatenate(mine, axis=0)
    across = swap(mine, "far")
    size = cols // n_rows
    two = in_order(mine[None, : 3 * size], across[None, : 3 * size])
    four = jnp.concatenate([two, swap(two, "near")])
    sent = jnp.concatenate([four.reshape(-1, width), across[3 * size :]])
    sent = lax.all_gather(sent, "rows", axis=0)
    pair_away = sent[:, 12 * size :].reshape(2 * cols, width)
    whole = sent[:, : 12 * size].reshape(n_rows, 4, 3, size, width).transpose(2, 1, 0, 3, 4)
    self_whole, query_whole, cross_whole = whole.reshape(3, 4 * cols, width)

    qkv_both = in_order(qkv_rows, qkv_away)
    qkv = exchange_rows(to_pairs(qkv_both, normed_one, 3))
    patch_mid = mul(patch_in, patch_weights).astype(LOW)
    pair_both = in_order(pair_rows, pair_away)
    pair = to_pairs(pair_both, patch_mid, 2)

    mine = [piece(widen_weights), piece(narrow_weights)]
    qkv, *mine = tie(qkv, *mine)
    size = width // n_rows
    sent = lax.all_gather(jnp.concatenate(mine, axis=0), ("far", "rows"), axis=0)
    sent = sent.reshape(2, n_rows, 2, size, width)
    widen = sent[:, :, 0].reshape(2, width, hidden)
    widen = jnp.concatenate([widen[0], widen[1]], axis=1)
    narrow = sent[:, :, 1].reshape(2 * hidden, width)

    mixed, self_wide, self_log = pair_forward(qkv, qkv, 1)
    mixed, pair = tie(exchange_rows(mixed), pair)
    pair = exchange_rows(pair)
    self_mixed_t = from_pairs(mixed[:, :, None])
    after_self = inputs + over_all_columns(self_mixed_t, self_whole)
    unit_two, rate_two = normed(after_self)
    normed_two = (unit_two * cross_gain_f).astype(LOW)
    cross_q, pair = tie(to_pairs(query_whole[: 2 * cols], normed_two, 1), pair)
    cross_q = exchange_rows(cross_q)
    mixed, cross_wide, cross_log = pair_forward(cross_q, pair, 0, length)
    cross_mixed_t = from_pairs(exchange_rows(mixed)[:, :, None])
    after_cross = after_self + over_all_columns(cross_mixed_t, cross_whole)
    unit_three, rate_three = normed(after_cross)
    normed_three = (unit_three * hidden_gain_f).astype(LOW)
    activated, act_back = jax.vjp(gelu_tanh, mul(normed_three, widen))
    activated = activated.astype(LOW)
    grad_pre = act_back(mul(grad_low, narrow, NT))[0].astype(LOW)
    third, activated, grad_pre = tie(mul(grad_pre, widen, NT).astype(LOW), activated, grad_pre)
    grad_three = third.astype(WIDE) + swap(third, "near").astype(WIDE)
    hidden_mine, hidden_away = halves(mul(activated, narrow))
    hidden_away, grad_three = tie(hidden_away.astype(LOW), grad_three)
    hidden_half = hidden_mine + swap(hidden_away, "near").astype(WIDE)
    result = (halves(after_cross)[0] + hidden_half).astype(LOW)

    def part_rows(both):
        return lax.psum_scatter(both, "rows", scatter_dimension=1, tiled=True)

    def own_and_away(value):
        return [lax.dynamic_index_in_dim(value, index, 0, keepdims=False) for index in (far, 1 - far)]

    def add_far(mine, away):
        return (mine.astype(WIDE) + away.astype(WIDE)).astype(LOW)

    def by_shard(left, right):
        return mul(left, right, NN).astype(LOW).reshape(2, -1, right.shape[1])

    hidden_terms = jnp.concatenate(
        [
            mul(value, against, TN).astype(LOW).reshape(2, hidden, width)
            for value, against in ((activated, grad_low), (grad_pre, normed_three))
        ],
        axis=1,
    )
    hidden_part = part_rows(hidden_terms)

    hidden_gain_term = jnp.sum(grad_three * unit_three, axis=0)
    grad_cross = grad_low.astype(WIDE) + normed_back(
        grad_three * hidden_gain_f, unit_three, rate_three
    )
    grad_cross_low = grad_cross.astype(LOW)
    grad_mixed = exchange_rows(to_pairs(cross_whole[: 2 * cols], grad_cross_low, 1)[:, :, 0])
    grad_mixed, result = tie(grad_mixed, result)
    result_two = jnp.stack([result, swap(result, "far")])
    grads = pair_backward(cross_q, pair, 0, length, grad_mixed, cross_wide, cross_log)
    grads, result_two, hidden_part = tie(grads, result_two, hidden_part)
    hidden_own, hidden_away = own_and_away(hidden_part)
    grads, hidden_away = tie(exchange_rows(grads), swap(hidden_away, "far"))
    hidden_total = join_rows(add_far(hidden_own, hidden_away))
    grad_cq_t = from_pairs(grads[:, :, :1])
    grad_pair_t = from_pairs(grads[:, :, 1:])
    middle_terms = jnp.concatenate(
        [
            by_shard(cross_mixed_t, grad_cross_low),
            by_shard(grad_cq_t, normed_two),
            by_shard(grad_pair_t, patch_mid),
        ],
        axis=1,
    )
    grad_cq_away, middle_terms = tie(swap(grad_cq_t, "near"), middle_terms)
    middle_part = part_rows(middle_terms)
    grad_two = mul(jnp.concatenate([grad_cq_t, grad_cq_away]), query_whole, TN)
    grad_two, result_two = tie(grad_two, result_two)
    result_four = jnp.stack([result_two, swap(result_two, "near")])
    cross_gain_term = jnp.sum(grad_two * unit_two, axis=0)
    grad_self = grad_cross + normed_back(grad_two * cross_gain_f, unit_two, rate_two)
    grad_self_low = grad_self.astype(LOW)
    grad_mixed, grad_self_low, grad_mid = tie(
        to_pairs(self_whole[: 2 * cols], grad_self_low, 1)[:, :, 0],
        grad_self_low,
        mul(grad_pair_t, pair_both, TN).astype(LOW),
    )
    grad_mid_away = swap(grad_mid, "near")
    output_terms = by_shard(self_mixed_t, grad_self_low)
    grads = pair_backward(qkv, qkv, 1, None, exchange_rows(grad_mixed), self_wide, self_log)
    grads, grad_mid_away, result_four = tie(grads, grad_mid_away, result_four)
    grad_mid = (grad_mid.astype(WIDE) + grad_mid_away.astype(WIDE)).astype(LOW)
    patch_half = mul(halves(grad_mid)[0], patch_weights, NT).astype(LOW)
    patch_two = jnp.stack([patch_half, swap(patch_half, "far")])
    patch_terms = jnp.stack([mul(value, patch_in, TN).astype(LOW) for value in both_columns(grad_mid)])
    patch_terms = jnp.pad(patch_terms, ((0, 0), (0, 0), (0, width - patch_width)))
    last_terms = jnp.pad(
        jnp.concatenate([output_terms, patch_terms], axis=1), ((0, 0), (3 * cols, 0), (0, 0))
    )
    hidden_gradients = [hidden_total[hidden:].T.astype(WIDE), hidden_total[:hidden].astype(WIDE)]
    grads, patch_two, last_terms, hidden_gradients, middle_part = tie(
        exchange_rows(grads), patch_two, last_terms, hidden_gradients, middle_part
    )
    grad_qkv_t = from_pairs(grads)
    last_terms = lax.dynamic_update_slice_in_dim(last_terms, by_shard(grad_qkv_t, normed_one), 0, 1)
    last_part = part_rows(last_terms)
    middle_own, middle_away = own_and_away(middle_part)
    first_mine, first_away = halves(mul(grad_qkv_t, qkv_both, TN))
    first_away, middle_away = tie(first_away.astype(LOW), middle_away)
    middle_total = join_rows(add_far(middle_own, swap(middle_away, "far")))
    grad_one = first_mine + swap(first_away, "near").astype(WIDE)
    gain_half, unit_half, rate_half, self_half = (
        halves(value)[0] for value in (gain_one, unit_one, rate_one, grad_self)
    )
    input_half = self_half + normed_back(grad_one * gain_half, unit_half, rate_half)
    input_half = input_half.astype(LOW)
    input_two = jnp.stack([input_half, swap(input_half, "far")])
    last_part, input_two, patch_two = tie(last_part, input_two, patch_two)
    input_four = jnp.stack([input_two, swap(input_two, "near")])
    patch_four = jnp.stack([patch_two, swap(patch_two, "near")])
    onehot_half = halves(onehot)[0].astype(WIDE)
    table_term = jnp.concatenate(
        [
            lax.dot_general(onehot_half, value, TN, precision=lax.Precision.HIGHEST)
            for value in (grad_one * unit_half, grad_one)
        ],
        axis=0,
    )
    small = [sum_near(table_term), hidden_gain_term[None], cross_gain_term[None], jnp.zeros((14, width), WIDE)]
    small = jnp.stack(both_columns(jnp.concatenate(small, axis=0).astype(LOW)))
    small = jnp.sum(lax.all_gather(small, "rows", axis=0).astype(WIDE), axis=0).astype(LOW)
    small_own, small_away = own_and_away(small)
    small_away, patch_four = tie(small_away, patch_four)
    small = small_own.astype(WIDE) + swap(small_away, "far").astype(WIDE)
    last_own, last_away = own_and_away(last_part)
    last_sum, input_four = tie(add_far(last_own, swap(last_away, "far")), input_four)
    last_total = join_rows(last_sum)
    input_grads = over_heads(input_four)
    outputs, patch_grads = over_heads(result_four), over_heads(patch_four)

    cross_output_total, query_total = middle_total[:cols], middle_total[cols : 2 * cols]
    pair_total = middle_total[2 * cols :].reshape(heads, 2, HEAD_DIM, width)
    self_total = last_total[: 3 * cols].reshape(heads, 3, HEAD_DIM, width)
    self_output_total = last_total[3 * cols : 4 * cols]
    patch_total = last_total[4 * cols :, :patch_width]
    gradients = (
        small[: 2 * codes].reshape(2, codes, cols).transpose(1, 0, 2),
        self_total.transpose(1, 3, 0, 2).reshape(3, width, cols),
        self_output_total,
        small[2 * codes + 1],
        query_total.T,
        pair_total.transpose(1, 3, 0, 2).reshape(2, width, cols),
        cross_output_total,
        patch_total.T,
        small[2 * codes],
        *hidden_gradients,
    )
    return (outputs, input_grads.astype(WIDE), patch_grads.astype(WIDE)) + tuple(
        value.astype(WIDE) for value in gradients
    )


def per_device(
    tokens,
    cam_index,
    patches,
    patch_len,
    camera_table,
    self_weights,
    self_output,
    cross_gain,
    cross_query,
    cross_pair,
    cross_output,
    patch_weights,
    hidden_gain,
    widen_weights,
    narrow_weights,
    cotangent,
):
    batches, rows, width = tokens.shape
    cols = self_weights.shape[2]
    heads = cols // HEAD_DIM
    codes = camera_table.shape[0]
    patch_rows, patch_width = patches.shape[1:]
    n_rows, n_heads = lax.axis_size("rows"), lax.axis_size("heads")
    row_rank, head_rank = lax.axis_index("rows"), lax.axis_index("heads")
    groups = 1
    objects = batches // groups
    full_lengths = jnp.full((objects,), n_rows * rows, jnp.int32)
    count = objects * rows

    def own_columns(value):
        return lax.dynamic_slice_in_dim(value, head_rank * cols, cols, value.ndim - 1)

    table_flat = camera_table.reshape(codes, -1)
    cross_gain_f = cross_gain.astype(WIDE)
    hidden_gain_f = hidden_gain.astype(WIDE)

    qkv_rows = (
        self_weights.reshape(3, width, heads, HEAD_DIM).transpose(2, 0, 3, 1).reshape(3 * cols, width)
    )
    qkv_rows_back = self_weights.transpose(0, 2, 1).reshape(3 * cols, width)
    pair_rows = cross_pair.transpose(0, 2, 1).reshape(2 * cols, width)
    query_rows = cross_query.T

    local = jnp.stack([self_output, cross_output, query_rows])
    piece = cols // n_rows
    local = lax.dynamic_slice_in_dim(local, row_rank * piece, piece, 1)
    whole = lax.all_gather(jnp.stack(gather_heads(local)), "rows", axis=0)
    whole = whole.transpose(2, 1, 0, 3, 4).reshape(3, n_heads * cols, width)
    self_whole, cross_whole, query_whole = whole[0], whole[1], whole[2]

    def over_all_columns(value_t, weight):
        return mul(jnp.concatenate(gather_heads(value_t), axis=0), weight, TN)

    def by_object(weight, value):
        return jnp.stack(
            [mul(weight, value[i * rows : (i + 1) * rows], NT).astype(LOW) for i in range(objects)]
        )

    def column_terms(value, grads_t):
        return [
            mul(value, grads_t[i : i + cols], (((0,), (1,)), ((), ())))
            for i in range(0, grads_t.shape[0], cols)
        ]

    def one_group(group):
        part = slice(group * objects, (group + 1) * objects)
        inputs = tokens[part].reshape(count, width).astype(WIDE)
        patch_in = patches[part].reshape(objects * patch_rows, patch_width)
        lengths = patch_len[part]
        grad_low = cotangent[part].reshape(count, width)
        onehot = (cam_index[part].reshape(count)[:, None] == jnp.arange(codes)[None, :]).astype(LOW)
        shift_scale = mul(onehot, table_flat)
        gain_one = 1.0 + shift_scale[:, :width]
        unit_one, rate_one = normed(inputs)
        normed_one = (unit_one * gain_one + shift_scale[:, width:]).astype(LOW)
        qkv_t = by_object(qkv_rows, normed_one)
        by_kind = qkv_t.reshape(objects, heads, 3, HEAD_DIM, rows).transpose(2, 1, 3, 0, 4)
        by_kind = by_kind.reshape(3, cols, count)
        self_pair = lax.all_gather(by_kind[1:], "rows", axis=0)
        patch_mid = mul(patch_in, patch_weights).astype(LOW)
        own_pair = mul(pair_rows, patch_mid, NT).astype(LOW).reshape(2, cols, -1)
        pair_t = lax.all_gather(own_pair, "rows", axis=0)
        self_mixed_t, self_wide, self_log = cross_forward(by_kind[0], self_pair, full_lengths)
        after_self = inputs + over_all_columns(self_mixed_t, self_whole)
        unit_two, rate_two = normed(after_self)
        normed_two = (unit_two * cross_gain_f).astype(LOW)
        cross_q_t = mul(query_rows, normed_two, NT).astype(LOW)
        cross_mixed_t, cross_wide, cross_log = cross_forward(cross_q_t, pair_t, lengths)
        after_cross = after_self + over_all_columns(cross_mixed_t, cross_whole)
        unit_three, rate_three = normed(after_cross)
        normed_three = (unit_three * hidden_gain_f).astype(LOW)
        pre_act = mul(normed_three, widen_weights)
        activated, act_back = jax.vjp(gelu_tanh, pre_act)
        activated = activated.astype(LOW)
        grad_pre = act_back(mul(grad_low, narrow_weights, NT))[0].astype(LOW)
        grad_three = sum_heads(mul(grad_pre, widen_weights, NT)).astype(WIDE)
        yield "heads", {"hidden": mul(activated, narrow_weights)}
        yield "rows", {
            "narrow": mul(activated, grad_low, TN),
            "widen": mul(normed_three, grad_pre, TN),
        }
        hidden_gain_term = jnp.sum(own_columns(grad_three * unit_three), axis=0)
        grad_cross = grad_low.astype(WIDE) + normed_back(
            grad_three * hidden_gain_f, unit_three, rate_three
        )
        grad_cross_low = grad_cross.astype(LOW)
        cross_output_term = mul(cross_mixed_t, grad_cross_low)
        grad_mixed_t = mul(cross_output, grad_cross_low, NT).astype(LOW)
        grad_cq_t, grad_pair_t = cross_backward(
            cross_q_t, pair_t, lengths, grad_mixed_t, cross_wide, cross_log
        )
        grad_two = over_all_columns(grad_cq_t, query_whole)
        grad_pair_t = lax.psum_scatter(grad_pair_t, "rows", scatter_dimension=0, tiled=False)
        grad_pair_t = grad_pair_t.reshape(2 * cols, -1)
        query_term = mul(normed_two, grad_cq_t, (((0,), (1,)), ((), ())))
        cross_gain_term = jnp.sum(own_columns(grad_two * unit_two), axis=0)
        grad_self = grad_cross + normed_back(grad_two * cross_gain_f, unit_two, rate_two)
        grad_self_low = grad_self.astype(LOW)
        self_output_term = mul(self_mixed_t, grad_self_low)
        yield "heads", {"patch": mul(grad_pair_t, pair_rows, TN)}
        yield "rows", {
            "query": query_term,
            "pair": column_terms(patch_mid, grad_pair_t),
            "cross_output": cross_output_term,
            "self_output": self_output_term,
        }
        grad_self_mixed_t = mul(self_output, grad_self_low, NT).astype(LOW)
        grad_q_t, grad_kv_t = cross_backward(
            by_kind[0], self_pair, full_lengths, grad_self_mixed_t, self_wide, self_log
        )
        grad_kv_t = lax.psum_scatter(grad_kv_t, "rows", scatter_dimension=0, tiled=False)
        grad_qkv_t = jnp.concatenate([grad_q_t[None], grad_kv_t]).reshape(3 * cols, count)
        grad_qkv_t = yield "after", (grad_qkv_t, ["patch", "narrow", "widen"])
        grad_mid = yield "take", "patch"
        patch_term = mul(patch_in, own_columns(grad_mid), TN)
        patch_grad = mul(grad_mid, patch_weights, NT)
        grad_one = sum_heads(mul(grad_qkv_t, qkv_rows_back, TN))
        grad_one = yield "after", (grad_one, ["query", "pair", "cross_output", "self_output"])
        grad_one = grad_one.astype(WIDE)
        input_grad = grad_self + normed_back(grad_one * gain_one, unit_one, rate_one)
        own_grad = own_columns(grad_one)
        table_term = jnp.stack(
            [
                lax.dot_general(onehot.astype(WIDE), v, TN, precision=lax.Precision.HIGHEST)
                for v in (own_grad * own_columns(unit_one), own_grad)
            ],
            axis=1,
        )
        small = [patch_term, table_term.reshape(2 * codes, cols)]
        small += [hidden_gain_term[None], cross_gain_term[None], jnp.zeros((14, cols), WIDE)]
        yield "rows", {
            "self": column_terms(normed_one, grad_qkv_t),
            "small": jnp.concatenate(small, axis=0),
        }
        hidden_sum = yield "take", "hidden"
        result = (after_cross + hidden_sum.astype(WIDE)).astype(LOW)
        yield (
            "done",
            (
                result.reshape(objects, rows, width),
                input_grad.reshape(objects, rows, width),
                patch_grad.reshape(objects, patch_rows, patch_width),
            ),
        )

    steps = [one_group(group) for group in range(groups)]
    asked = [next(step) for step in steps]
    totals, ahead = {}, []
    while asked[0][0] != "done":
        kind, what = asked[0]
        answers = [None] * groups
        if kind == "take":
            answers = jnp.split(totals[what], groups)
        elif kind == "after":
            early = {name: totals[name] for name in what[1]}
            answers = [value for _, (value, _) in asked]
            answers[-1], early = lax.optimization_barrier((answers[-1], early))
            totals.update(early)
        else:
            terms = [value for _, value in asked]
            if kind == "heads":
                terms = jax.tree.map(lambda *parts: jnp.concatenate(parts, axis=0), *terms)
            else:
                for value in terms[1:]:
                    terms[0] = add_trees(terms[0], value)
                terms = terms[0]
            if kind == "rows":
                terms = jax.tree.map(lambda value: value.astype(LOW), terms)
            if kind == "heads":
                totals.update({name: sum_heads(value) for name, value in terms.items()})
            else:
                before = {name: totals[name] for name in ahead}
                terms, before = lax.optimization_barrier((terms, before))
                totals.update(before)
                totals.update(lax.psum(terms, kind))
                ahead = list(terms)
        asked = [step.send(value) for step, value in zip(steps, answers)]
    outputs, input_grads, patch_grads = (
        jnp.concatenate([value[i] for _, value in asked], axis=0) for i in range(3)
    )
    patch_total, table_total, gains = jnp.split(
        totals["small"], [patch_width, patch_width + 2 * codes]
    )
    gradients = (
        table_total.reshape(codes, 2, cols),
        jnp.stack(totals["self"]),
        totals["self_output"],
        gains[1],
        totals["query"],
        jnp.stack(totals["pair"]),
        totals["cross_output"],
        patch_total,
        gains[0],
        totals["widen"],
        totals["narrow"],
    )
    return (outputs, input_grads, patch_grads) + tuple(value.astype(WIDE) for value in gradients)


def solution(mesh):
    sizes = mesh.shape
    paired = sizes["heads"] == 4 and sizes["rows"] == 8
    heads = ("far", "near") if paired else "heads"
    if paired:
        names = (*heads, "rows")
        mesh = jax.sharding.Mesh(mesh.devices.reshape(2, 2, sizes["rows"]), names)
    in_specs = (
        P(None, "rows", None),
        P(None, "rows"),
        P(None, "rows", None),
        P(),
        P(),
        P(None, None, heads),
        P(heads, None),
        P(),
        P(None, heads),
        P(None, None, heads),
        P(heads, None),
        P(),
        P(),
        P(None, heads),
        P(heads, None),
        P(None, "rows", None),
    )
    out_specs = (
        P(None, "rows", None),
        P(None, "rows", None),
        P(None, "rows", None),
        P(None, None, heads),
        P(None, None, heads),
        P(heads, None),
        P(heads),
        P(None, heads),
        P(None, None, heads),
        P(heads, None),
        P(None, heads),
        P(heads),
        P(None, heads),
        P(heads, None),
    )
    return jax.shard_map(
        paired_device if paired else per_device,
        mesh=mesh,
        in_specs=in_specs,
        out_specs=out_specs,
        check_vma=False,
    )
```

```python
import jax
import jax.numpy as jnp
from jax import lax
from jax.experimental import pallas as pl
from jax.experimental.pallas import tpu as pltpu
from jax.sharding import PartitionSpec as P

HEAD_DIM = 64
EPSILON = 1e-05
SCALE = HEAD_DIM ** (-0.5)
LOW = jnp.bfloat16
WIDE = jnp.float32

NN = (((1,), (0,)), ((), ()))
NT = (((1,), (1,)), ((), ()))
TN = (((0,), (0,)), ((), ()))
T_LAST = (((0,), (1,)), ((), ()))


def mul(left, right, dims=NN):
    return lax.dot_general(left, right, dims, preferred_element_type=WIDE)


def load_values(values, block, values_t):
    rows = values_t.shape[1]
    at = slice(block * rows, (block + 1) * rows)
    values[at, :HEAD_DIM] = values_t.T
    values[at, HEAD_DIM:] = jnp.ones((rows, HEAD_DIM), values.dtype)


def attend_block(queries, keys_t, values):
    scores = mul(queries, keys_t)
    peak = jnp.max(scores, axis=1, keepdims=True)
    both = mul(jnp.exp(scores - peak).astype(LOW), values).T
    total = both[HEAD_DIM : HEAD_DIM + 1]
    return both[:HEAD_DIM] / total, peak.T + jnp.log(total)


def attend_block_back(scaled_q, grad_t, keys, keys_t, values, log_total, spread):
    probs = jnp.exp(mul(keys, scaled_q) - log_total)
    grad_scores = (probs * (mul(values, grad_t) - spread)).astype(LOW)
    return (
        (mul(keys_t, grad_scores) * SCALE).astype(LOW),
        mul(grad_scores, scaled_q.T),
        mul(probs.astype(LOW), grad_t.T),
    )


def estimate(rows, cols, passes):
    return pl.CostEstimate(
        flops=int(rows * cols * 1200 * passes), transcendentals=int(rows * cols), bytes_accessed=int(rows * 2048)
    )


VMEM_LIMIT = 48 << 20


def by_length(length, full, blocks, run):
    @pl.when(length * 4 > full)
    def _():
        run(blocks)

    @pl.when(length * 4 <= full)
    def _():
        run(blocks // 4)


def cross_forward(queries_t, pair_t, lengths):
    blocks, _, cols, all_patches = pair_t.shape
    objects = lengths.shape[0]
    heads = cols // HEAD_DIM
    rows, patch_rows = queries_t.shape[1] // objects, all_patches // objects

    def kernel(len_ref, q_ref, pair_ref, mixed_ref, wide_ref, log_ref, keys_t, values):
        queries = (q_ref[...] * LOW(SCALE)).T

        def run(live):
            for c in range(live):
                keys_t[:, c * patch_rows : (c + 1) * patch_rows] = pair_ref[c, 0]
                load_values(values, c, pair_ref[c, 1])
            size = live * patch_rows
            mixed, log_total = attend_block(queries, keys_t[:, :size], values[:size])
            mixed_ref[...] = mixed.astype(LOW)
            wide_ref[...] = mixed
            log_ref[...] = log_total

        by_length(len_ref[pl.program_id(0)], blocks * patch_rows, blocks, run)

    block = pl.BlockSpec((HEAD_DIM, rows), lambda b, j, lens: (j, b))
    return pl.pallas_call(
        kernel,
        grid_spec=pltpu.PrefetchScalarGridSpec(
            num_scalar_prefetch=1,
            grid=(objects, heads),
            in_specs=[
                block,
                pl.BlockSpec((blocks, 2, HEAD_DIM, patch_rows), lambda b, j, lens: (0, 0, j, b)),
            ],
            out_specs=[block, block, pl.BlockSpec((None, 1, rows), lambda b, j, lens: (j, 0, b))],
            scratch_shapes=[
                pltpu.VMEM((HEAD_DIM, blocks * patch_rows), LOW),
                pltpu.VMEM((blocks * patch_rows, 2 * HEAD_DIM), LOW),
            ],
        ),
        out_shape=[
            jax.ShapeDtypeStruct(queries_t.shape, LOW),
            jax.ShapeDtypeStruct(queries_t.shape, WIDE),
            jax.ShapeDtypeStruct((heads, 1, queries_t.shape[1]), WIDE),
        ],
        name="cross_forward",
        cost_estimate=estimate(objects * rows, blocks * patch_rows * heads, 1.4),
        compiler_params=pltpu.CompilerParams(vmem_limit_bytes=VMEM_LIMIT),
    )(lengths, queries_t, pair_t)


def cross_backward(queries_t, pair_t, lengths, grad_t_all, wide, log_total):
    blocks, _, cols, all_patches = pair_t.shape
    objects = lengths.shape[0]
    heads = cols // HEAD_DIM
    rows, patch_rows = queries_t.shape[1] // objects, all_patches // objects

    def kernel(len_ref, q_ref, pair_ref, g_ref, wide_ref, log_ref, out_q, out_pair, keys, keys_t, values):
        grad_t = g_ref[...]
        spread = jnp.sum(grad_t.astype(WIDE) * wide_ref[...], axis=0, keepdims=True)

        def run(live):
            for c in range(live):
                at = slice(c * patch_rows, (c + 1) * patch_rows)
                keys[at] = pair_ref[c, 0].T
                keys_t[:, at] = pair_ref[c, 0]
                values[at] = pair_ref[c, 1].T
            size = live * patch_rows
            out_q[...], grad_k, grad_v = attend_block_back(
                q_ref[...] * LOW(SCALE),
                grad_t,
                keys[:size],
                keys_t[:, :size],
                values[:size],
                log_ref[...],
                spread,
            )
            for c in range(live):
                at = slice(c * patch_rows, (c + 1) * patch_rows)
                out_pair[c, 0] = grad_k[at].T.astype(LOW)
                out_pair[c, 1] = grad_v[at].T.astype(LOW)
            for c in range(live, blocks):
                out_pair[c] = jnp.zeros_like(out_pair[c])

        by_length(len_ref[pl.program_id(0)], blocks * patch_rows, blocks, run)

    block = pl.BlockSpec((HEAD_DIM, rows), lambda b, j, lens: (j, b))
    pair_block = pl.BlockSpec((blocks, 2, HEAD_DIM, patch_rows), lambda b, j, lens: (0, 0, j, b))
    return pl.pallas_call(
        kernel,
        grid_spec=pltpu.PrefetchScalarGridSpec(
            num_scalar_prefetch=1,
            grid=(objects, heads),
            in_specs=[
                block,
                pair_block,
                block,
                block,
                pl.BlockSpec((None, 1, rows), lambda b, j, lens: (j, 0, b)),
            ],
            out_specs=[block, pair_block],
            scratch_shapes=[
                pltpu.VMEM((blocks * patch_rows, HEAD_DIM), LOW),
                pltpu.VMEM((HEAD_DIM, blocks * patch_rows), LOW),
                pltpu.VMEM((blocks * patch_rows, HEAD_DIM), LOW),
            ],
        ),
        out_shape=[
            jax.ShapeDtypeStruct(queries_t.shape, LOW),
            jax.ShapeDtypeStruct(pair_t.shape, LOW),
        ],
        name="cross_backward",
        cost_estimate=estimate(objects * rows, blocks * patch_rows * heads, 2.5),
        compiler_params=pltpu.CompilerParams(vmem_limit_bytes=VMEM_LIMIT),
    )(lengths, queries_t, pair_t, grad_t_all, wide, log_total)


def shift(value, step):
    size = lax.axis_size("heads")
    return lax.ppermute(value, "heads", [((i + step) % size, i) for i in range(size)])


def gather_heads(value):
    size = lax.axis_size("heads")
    if size != 4:
        return [value] + [shift(value, step) for step in range(1, size)]
    after, before = shift(value, 1), shift(value, -1)
    inner = lax.ppermute(after, "heads", [(1, 0), (2, 1)]) + lax.ppermute(before, "heads", [(1, 2), (2, 3)])
    return [value, after, inner, before]


def scatter_heads(partial):
    size, me = lax.axis_size("heads"), lax.axis_index("heads")

    def part(step):
        return lax.dynamic_index_in_dim(partial, (me + step) % size, 0, keepdims=False)

    if size != 4:
        total = part(0)
        for step in range(1, size):
            total = total + shift(part(step).astype(LOW), -step).astype(WIDE)
        return total
    far = part(2).astype(LOW)
    up = lax.ppermute(far, "heads", [(0, 1), (1, 2)]).astype(WIDE)
    down = lax.ppermute(far, "heads", [(2, 1), (3, 2)]).astype(WIDE)
    from_below = shift((part(1) + up).astype(LOW), -1)
    from_above = shift((part(3) + down).astype(LOW), 1)
    return part(0) + from_below.astype(WIDE) + from_above.astype(WIDE)


def in_order(parts):
    size, me = lax.axis_size("heads"), lax.axis_index("heads")
    out = jnp.zeros((size,) + parts[0].shape, parts[0].dtype)
    for step, value in enumerate(parts):
        out = lax.dynamic_update_index_in_dim(out, value, (me + step) % size, 0)
    return out.reshape((-1,) + parts[0].shape[1:])


def sum_heads(partial):
    size = lax.axis_size("heads")
    split = partial.reshape((size, -1) + partial.shape[1:])
    return in_order(gather_heads(scatter_heads(split).astype(LOW)))


def exchange_rows(value):
    return lax.all_to_all(value, "rows", 0, 0, tiled=True)


def normed(value):
    centred = value - jnp.mean(value, axis=-1, keepdims=True)
    rate = lax.rsqrt(jnp.mean(centred * centred, axis=-1, keepdims=True) + EPSILON)
    return centred * rate, rate


def normed_back(grad, unit, rate):
    return rate * (
        grad
        - jnp.mean(grad, axis=-1, keepdims=True)
        - unit * jnp.mean(grad * unit, axis=-1, keepdims=True)
    )


def gelu_tanh(pre_act):
    return jax.nn.gelu(pre_act, approximate=True)


def add_trees(former, latter):
    return jax.tree.map(jnp.add, former, latter)


def pair_forward(queries, pair, key_at, objects, length=None):
    blocks, _, width, count = queries.shape
    rows, pair_rows = count // objects, pair.shape[3] // objects
    lengths = jnp.full((objects,), blocks * pair_rows, jnp.int32) if length is None else length

    def kernel(len_ref, q_ref, k_ref, v_ref, mixed_ref, wide_ref, log_ref, keys_t, values):
        def run(live):
            @pl.when(pl.program_id(1) == 0)
            def _():
                for c in range(live):
                    keys_t[:, c * pair_rows : (c + 1) * pair_rows] = k_ref[c]
                    load_values(values, c, v_ref[c])

            size = live * pair_rows
            mixed, log_total = attend_block(
                (q_ref[...] * LOW(SCALE)).T, keys_t[:, :size], values[:size]
            )
            mixed_ref[...] = mixed.astype(LOW)
            wide_ref[...] = mixed
            log_ref[...] = log_total

        if length is None:
            run(blocks)
        else:
            by_length(len_ref[pl.program_id(0)], blocks * pair_rows, blocks, run)

    block = pl.BlockSpec((None, width, rows), lambda o, i, lens: (i, 0, o))
    return pl.pallas_call(
        kernel,
        grid_spec=pltpu.PrefetchScalarGridSpec(
            num_scalar_prefetch=1,
            grid=(objects, blocks),
            in_specs=[
                pl.BlockSpec((None, None, width, rows), lambda o, i, lens: (i, 0, 0, o)),
                pl.BlockSpec((blocks, None, width, pair_rows), lambda o, i, lens: (0, key_at, 0, o)),
                pl.BlockSpec((blocks, None, width, pair_rows), lambda o, i, lens: (0, key_at + 1, 0, o)),
            ],
            out_specs=[block, block, pl.BlockSpec((None, 1, rows), lambda o, i, lens: (i, 0, o))],
            scratch_shapes=[
                pltpu.VMEM((width, blocks * pair_rows), LOW),
                pltpu.VMEM((blocks * pair_rows, 2 * width), LOW),
            ],
        ),
        out_shape=[
            jax.ShapeDtypeStruct((blocks, width, count), LOW),
            jax.ShapeDtypeStruct((blocks, width, count), WIDE),
            jax.ShapeDtypeStruct((blocks, 1, count), WIDE),
        ],
        name="pair_forward",
        cost_estimate=estimate(objects * blocks * rows, blocks * pair_rows, 2 if length is None else 1.4),
        compiler_params=pltpu.CompilerParams(vmem_limit_bytes=VMEM_LIMIT),
    )(lengths, queries, pair, pair)


def pair_backward(queries, pair, key_at, objects, length, grad_mixed, wide, log_total):
    blocks, _, width, count = queries.shape
    rows = count // objects
    lengths = jnp.full((objects,), blocks * rows, jnp.int32) if length is None else length

    def kernel(len_ref, q_ref, k_ref, v_ref, g_ref, wide_ref, log_ref, out_ref, keys, keys_t, values, grad_k, grad_v):
        i = pl.program_id(1)

        def run(live):
            size = live * rows

            @pl.when(i == 0)
            def _():
                for c in range(live):
                    at = slice(c * rows, (c + 1) * rows)
                    keys[at] = k_ref[c].T
                    keys_t[:, at] = k_ref[c]
                    values[at] = v_ref[c].T

            grad_t = g_ref[...]
            spread = jnp.sum(grad_t.astype(WIDE) * wide_ref[...], axis=0, keepdims=True)
            out_ref[i, 0], term_k, term_v = attend_block_back(
                q_ref[...] * LOW(SCALE),
                grad_t,
                keys[:size],
                keys_t[:, :size],
                values[:size],
                log_ref[...],
                spread,
            )

            @pl.when(i == 0)
            def _():
                grad_k[:size] = term_k
                grad_v[:size] = term_v

            @pl.when(i > 0)
            def _():
                grad_k[:size] += term_k
                grad_v[:size] += term_v

            @pl.when(i == blocks - 1)
            def _():
                for c in range(live):
                    at = slice(c * rows, (c + 1) * rows)
                    out_ref[c, 1] = grad_k[at].T.astype(LOW)
                    out_ref[c, 2] = grad_v[at].T.astype(LOW)
                for c in range(live, blocks):
                    out_ref[c, 1:] = jnp.zeros_like(out_ref[c, 1:])

        if length is None:
            run(blocks)
        else:
            by_length(len_ref[pl.program_id(0)], blocks * rows, blocks, run)

    block = pl.BlockSpec((None, width, rows), lambda o, i, lens: (i, 0, o))
    return pl.pallas_call(
        kernel,
        grid_spec=pltpu.PrefetchScalarGridSpec(
            num_scalar_prefetch=1,
            grid=(objects, blocks),
            in_specs=[
                pl.BlockSpec((None, None, width, rows), lambda o, i, lens: (i, 0, 0, o)),
                pl.BlockSpec((blocks, None, width, rows), lambda o, i, lens: (0, key_at, 0, o)),
                pl.BlockSpec((blocks, None, width, rows), lambda o, i, lens: (0, key_at + 1, 0, o)),
                block,
                block,
                pl.BlockSpec((None, 1, rows), lambda o, i, lens: (i, 0, o)),
            ],
            out_specs=pl.BlockSpec((blocks, 3, width, rows), lambda o, i, lens: (0, 0, 0, o)),
            scratch_shapes=[
                pltpu.VMEM((blocks * rows, width), LOW),
                pltpu.VMEM((width, blocks * rows), LOW),
                pltpu.VMEM((blocks * rows, width), LOW),
                pltpu.VMEM((blocks * rows, width), WIDE),
                pltpu.VMEM((blocks * rows, width), WIDE),
            ],
        ),
        out_shape=jax.ShapeDtypeStruct((blocks, 3, width, count), LOW),
        name="pair_backward",
        cost_estimate=estimate(objects * blocks * rows, blocks * rows, 3 if length is None else 2),
        compiler_params=pltpu.CompilerParams(vmem_limit_bytes=VMEM_LIMIT),
    )(lengths, queries, pair, pair, grad_mixed, wide, log_total)


def swap(value, axis):
    return lax.ppermute(value, axis, [(0, 1), (1, 0)])


def sum_near(partial):
    low = partial.astype(LOW)
    return low.astype(WIDE) + swap(low, "near").astype(WIDE)


def tie(value, *others):
    return lax.optimization_barrier((value, *others))


def paired_device(
    tokens,
    cam_index,
    patches,
    patch_len,
    camera_table,
    self_weights,
    self_output,
    cross_gain,
    cross_query,
    cross_pair,
    cross_output,
    patch_weights,
    hidden_gain,
    widen_weights,
    narrow_weights,
    cotangent,
):
    objects = tokens.shape[0] // 2
    _, rows, width = tokens.shape
    cols = self_weights.shape[2]
    hidden = widen_weights.shape[1]
    heads = cols // HEAD_DIM
    codes = camera_table.shape[0]
    patch_width = patches.shape[2]
    count = objects * rows
    n_rows = lax.axis_size("rows")
    row_rank = lax.axis_index("rows")
    far, near = lax.axis_index("far"), lax.axis_index("near")

    def objects_of(value):
        return lax.dynamic_slice_in_dim(value, objects * far, objects, 0)

    def piece(value):
        size = value.shape[0] // n_rows
        return lax.dynamic_slice_in_dim(value, row_rank * size, size, 0)

    def join_rows(value):
        return lax.all_gather(value, "rows", axis=0, tiled=True)

    def both_columns(value):
        return [
            lax.dynamic_slice_in_dim(value, (2 * index + near) * cols, cols, value.ndim - 1)
            for index in range(2)
        ]

    def in_order(mine, away, axis=0):
        size = mine.shape[axis]
        shape = list(mine.shape)
        shape[axis] *= 2
        out = lax.dynamic_update_slice_in_dim(jnp.zeros(shape, mine.dtype), mine, far * size, axis)
        return lax.dynamic_update_slice_in_dim(out, away, (1 - far) * size, axis)

    def halves(value):
        value = value.reshape(objects, 2, rows // 2, -1)
        return [
            lax.dynamic_index_in_dim(value, index, 1, keepdims=False).reshape(count // 2, -1)
            for index in (near, 1 - near)
        ]

    def half_sum_near(partial):
        mine, away = halves(partial)
        return mine + swap(away.astype(LOW), "near").astype(WIDE)

    def over_heads(value):
        value = value.reshape(2, 2, objects, rows // 2, -1)
        value = jnp.where(far == 0, value, jnp.flip(value, 1))
        value = jnp.where(near == 0, value, jnp.flip(value, 0))
        return value.transpose(1, 2, 0, 3, 4).reshape(2 * objects, rows, -1)

    def to_pairs(value_t, slots):
        return value_t.reshape(n_rows, slots, HEAD_DIM, count)

    def times(weights, value):
        return mul(weights, value, NT).astype(LOW)

    def from_pairs(value):
        return value.reshape(-1, count)

    def over_all_columns(value_t, weight):
        return mul(jnp.concatenate([value_t, swap(value_t, "near")]), weight, TN)

    qkv_rows = self_weights.reshape(3, width, heads, HEAD_DIM).transpose(2, 0, 3, 1)
    qkv_rows = qkv_rows.reshape(3 * cols, width)
    pair_rows = cross_pair.reshape(2, width, heads, HEAD_DIM).transpose(2, 0, 3, 1)
    pair_rows = pair_rows.reshape(2 * cols, width)
    query_rows = cross_query.T

    qkv_away = join_rows(swap(piece(qkv_rows), "far"))

    table_flat = camera_table.reshape(codes, -1)
    cross_gain_f = cross_gain.astype(WIDE)
    hidden_gain_f = hidden_gain.astype(WIDE)

    inputs = objects_of(tokens).reshape(count, width).astype(WIDE)
    patch_in = objects_of(patches).reshape(count, patch_width)
    length = objects_of(patch_len)
    grad_low = objects_of(cotangent).reshape(count, width)
    codes_of = objects_of(cam_index).reshape(count)
    onehot = (codes_of[:, None] == jnp.arange(codes)[None, :]).astype(LOW)
    shift_scale = mul(onehot, table_flat)
    gain_one = 1.0 + shift_scale[:, :width]
    unit_one, rate_one = normed(inputs)
    normed_one = (unit_one * gain_one + shift_scale[:, width:]).astype(LOW)

    mine = [piece(v) for v in (self_output, query_rows, cross_output, pair_rows)]
    normed_one, *mine = tie(normed_one, *mine)
    mine = jnp.concatenate(mine, axis=0)
    across = swap(mine, "far")
    size = cols // n_rows
    two = in_order(mine[None, : 3 * size], across[None, : 3 * size])
    four = jnp.concatenate([two, swap(two, "near")])
    sent = jnp.concatenate([four.reshape(-1, width), across[3 * size :]])
    sent = lax.all_gather(sent, "rows", axis=0)
    pair_away = sent[:, 12 * size :].reshape(2 * cols, width)
    whole = sent[:, : 12 * size].reshape(n_rows, 4, 3, size, width).transpose(2, 1, 0, 3, 4)
    self_whole, query_whole, cross_whole = whole.reshape(3, 4 * cols, width)

    qkv_both = in_order(qkv_rows, qkv_away)
    qkv = in_order(times(qkv_rows, normed_one), times(qkv_away, normed_one))
    qkv = exchange_rows(to_pairs(qkv, 3))
    patch_mid = mul(patch_in, patch_weights).astype(LOW)
    pair_both = in_order(pair_rows, pair_away)
    pair = to_pairs(times(pair_both, patch_mid), 2)

    mine = [piece(widen_weights), piece(narrow_weights)]
    qkv, *mine = tie(qkv, *mine)
    size = width // n_rows
    sent = lax.all_gather(jnp.concatenate(mine, axis=0), ("far", "rows"), axis=0)
    sent = sent.reshape(2, n_rows, 2, size, width)
    widen = sent[:, :, 0].reshape(2, width, hidden)
    widen = jnp.concatenate([widen[0], widen[1]], axis=1)
    narrow = sent[:, :, 1].reshape(2 * hidden, width)

    mixed, self_wide, self_log = pair_forward(qkv, qkv, 1, objects)
    mixed, pair = tie(exchange_rows(mixed), pair)
    pair = exchange_rows(pair)
    self_mixed_t = from_pairs(mixed)
    after_self = inputs + over_all_columns(self_mixed_t, self_whole)
    unit_two, rate_two = normed(after_self)
    normed_two = (unit_two * cross_gain_f).astype(LOW)
    cross_q, pair = tie(to_pairs(times(query_whole[: 2 * cols], normed_two), 1), pair)
    cross_q = exchange_rows(cross_q)
    mixed, cross_wide, cross_log = pair_forward(cross_q, pair, 0, objects, length)
    cross_mixed_t = from_pairs(exchange_rows(mixed))
    after_cross = after_self + over_all_columns(cross_mixed_t, cross_whole)
    unit_three, rate_three = normed(after_cross)
    normed_three = (unit_three * hidden_gain_f).astype(LOW)
    activated, act_back = jax.vjp(gelu_tanh, mul(normed_three, widen))
    activated = activated.astype(LOW)
    grad_pre = act_back(mul(grad_low, narrow, NT))[0].astype(LOW)
    third, activated, grad_pre = tie(mul(grad_pre, widen, NT).astype(LOW), activated, grad_pre)
    grad_three = third.astype(WIDE) + swap(third, "near").astype(WIDE)
    hidden_mine, hidden_away = halves(mul(activated, narrow))
    hidden_away, grad_three = tie(hidden_away.astype(LOW), grad_three)
    hidden_half = hidden_mine + swap(hidden_away, "near").astype(WIDE)
    result = (halves(after_cross)[0] + hidden_half).astype(LOW)

    def part_rows(both):
        return lax.psum_scatter(both, "rows", scatter_dimension=1, tiled=True)

    def own_and_away(value):
        return [lax.dynamic_index_in_dim(value, index, 0, keepdims=False) for index in (far, 1 - far)]

    def add_far(mine, away):
        return (mine.astype(WIDE) + away.astype(WIDE)).astype(LOW)

    def by_shard(left, right):
        return mul(left, right, NN).astype(LOW).reshape(2, -1, right.shape[1])

    hidden_terms = jnp.concatenate(
        [
            mul(value, against, TN).astype(LOW).reshape(2, hidden, width)
            for value, against in ((activated, grad_low), (grad_pre, normed_three))
        ],
        axis=1,
    )
    hidden_part = part_rows(hidden_terms)

    hidden_gain_term = jnp.sum(grad_three * unit_three, axis=0)
    grad_cross = grad_low.astype(WIDE) + normed_back(
        grad_three * hidden_gain_f, unit_three, rate_three
    )
    grad_cross_low = grad_cross.astype(LOW)
    grad_mixed = exchange_rows(to_pairs(times(cross_whole[: 2 * cols], grad_cross_low), 1)[:, 0])
    grad_mixed, result = tie(grad_mixed, result)
    result_two = jnp.stack([result, swap(result, "far")])
    grads = pair_backward(cross_q, pair, 0, objects, length, grad_mixed, cross_wide, cross_log)
    grads, result_two, hidden_part = tie(grads, result_two, hidden_part)
    hidden_own, hidden_away = own_and_away(hidden_part)
    grads, hidden_away = tie(exchange_rows(grads), swap(hidden_away, "far"))
    hidden_total = join_rows(add_far(hidden_own, hidden_away))
    grad_cq_t = from_pairs(grads[:, :1])
    grad_pair_t = from_pairs(grads[:, 1:])
    middle_terms = jnp.concatenate(
        [
            by_shard(cross_mixed_t, grad_cross_low),
            by_shard(grad_cq_t, normed_two),
            by_shard(grad_pair_t, patch_mid),
        ],
        axis=1,
    )
    grad_cq_away, middle_terms = tie(swap(grad_cq_t, "near"), middle_terms)
    middle_part = part_rows(middle_terms)
    grad_two = mul(jnp.concatenate([grad_cq_t, grad_cq_away]), query_whole, TN)
    grad_two, result_two = tie(grad_two, result_two)
    result_four = jnp.stack([result_two, swap(result_two, "near")])
    cross_gain_term = jnp.sum(grad_two * unit_two, axis=0)
    grad_self = grad_cross + normed_back(grad_two * cross_gain_f, unit_two, rate_two)
    grad_self_low = grad_self.astype(LOW)
    grad_mixed, grad_self_low, grad_mid = tie(
        to_pairs(times(self_whole[: 2 * cols], grad_self_low), 1)[:, 0],
        grad_self_low,
        mul(grad_pair_t, pair_both, TN).astype(LOW),
    )
    grad_mid_away = swap(grad_mid, "near")
    output_terms = by_shard(self_mixed_t, grad_self_low)
    grads = pair_backward(qkv, qkv, 1, objects, None, exchange_rows(grad_mixed), self_wide, self_log)
    grads, grad_mid_away, result_four = tie(grads, grad_mid_away, result_four)
    grad_mid = (grad_mid.astype(WIDE) + grad_mid_away.astype(WIDE)).astype(LOW)
    patch_half = mul(halves(grad_mid)[0], patch_weights, NT).astype(LOW)
    patch_two = jnp.stack([patch_half, swap(patch_half, "far")])
    patch_terms = jnp.stack([mul(value, patch_in, TN).astype(LOW) for value in both_columns(grad_mid)])
    patch_terms = jnp.pad(patch_terms, ((0, 0), (0, 0), (0, width - patch_width)))
    last_terms = jnp.pad(
        jnp.concatenate([output_terms, patch_terms], axis=1), ((0, 0), (3 * cols, 0), (0, 0))
    )
    hidden_gradients = [hidden_total[hidden:].T.astype(WIDE), hidden_total[:hidden].astype(WIDE)]
    grads, patch_two, last_terms, middle_part = tie(exchange_rows(grads), patch_two, last_terms, middle_part)
    grad_qkv_t = from_pairs(grads)
    last_terms = lax.dynamic_update_slice_in_dim(last_terms, by_shard(grad_qkv_t, normed_one), 0, 1)
    last_part = part_rows(last_terms)
    middle_own, middle_away = own_and_away(middle_part)
    first_mine, first_away = halves(mul(grad_qkv_t, qkv_both, TN))
    first_away, middle_away = tie(first_away.astype(LOW), middle_away)
    middle_total = join_rows(add_far(middle_own, swap(middle_away, "far")))
    grad_one = first_mine + swap(first_away, "near").astype(WIDE)
    gain_half, unit_half, rate_half, self_half = (
        halves(value)[0] for value in (gain_one, unit_one, rate_one, grad_self)
    )
    input_half = self_half + normed_back(grad_one * gain_half, unit_half, rate_half)
    input_half = input_half.astype(LOW)
    input_two = jnp.stack([input_half, swap(input_half, "far")])
    last_part, input_two, patch_two, hidden_gradients = tie(last_part, input_two, patch_two, hidden_gradients)
    input_four = jnp.stack([input_two, swap(input_two, "near")])
    patch_four = jnp.stack([patch_two, swap(patch_two, "near")])
    onehot_half = halves(onehot)[0].astype(WIDE)
    table_term = jnp.concatenate(
        [
            lax.dot_general(onehot_half, value, TN, precision=lax.Precision.HIGHEST)
            for value in (grad_one * unit_half, grad_one)
        ],
        axis=0,
    )
    small = [sum_near(table_term), hidden_gain_term[None], cross_gain_term[None], jnp.zeros((14, width), WIDE)]
    small = jnp.stack(both_columns(jnp.concatenate(small, axis=0).astype(LOW)))
    small = jnp.sum(lax.all_gather(small, "rows", axis=0).astype(WIDE), axis=0).astype(LOW)
    small_own, small_away = own_and_away(small)
    small_away, patch_four = tie(small_away, patch_four)
    small = small_own.astype(WIDE) + swap(small_away, "far").astype(WIDE)
    last_own, last_away = own_and_away(last_part)
    last_sum, input_four = tie(add_far(last_own, swap(last_away, "far")), input_four)
    last_total = join_rows(last_sum)
    input_grads = over_heads(input_four)
    outputs, patch_grads = over_heads(result_four), over_heads(patch_four)

    cross_output_total, query_total = middle_total[:cols], middle_total[cols : 2 * cols]
    pair_total = middle_total[2 * cols :].reshape(heads, 2, HEAD_DIM, width)
    self_total = last_total[: 3 * cols].reshape(heads, 3, HEAD_DIM, width)
    self_output_total = last_total[3 * cols : 4 * cols]
    patch_total = last_total[4 * cols :, :patch_width]
    gradients = (
        small[: 2 * codes].reshape(2, codes, cols).transpose(1, 0, 2),
        self_total.transpose(1, 3, 0, 2).reshape(3, width, cols),
        self_output_total,
        small[2 * codes + 1],
        query_total.T,
        pair_total.transpose(1, 3, 0, 2).reshape(2, width, cols),
        cross_output_total,
        patch_total.T,
        small[2 * codes],
        *hidden_gradients,
    )
    return (outputs, input_grads.astype(WIDE), patch_grads.astype(WIDE)) + tuple(
        value.astype(WIDE) for value in gradients
    )


def per_device(
    tokens,
    cam_index,
    patches,
    patch_len,
    camera_table,
    self_weights,
    self_output,
    cross_gain,
    cross_query,
    cross_pair,
    cross_output,
    patch_weights,
    hidden_gain,
    widen_weights,
    narrow_weights,
    cotangent,
):
    batches, rows, width = tokens.shape
    cols = self_weights.shape[2]
    heads = cols // HEAD_DIM
    codes = camera_table.shape[0]
    patch_rows, patch_width = patches.shape[1:]
    n_rows, n_heads = lax.axis_size("rows"), lax.axis_size("heads")
    row_rank, head_rank = lax.axis_index("rows"), lax.axis_index("heads")
    groups = 1
    objects = batches // groups
    full_lengths = jnp.full((objects,), n_rows * rows, jnp.int32)
    count = objects * rows

    def own_columns(value):
        return lax.dynamic_slice_in_dim(value, head_rank * cols, cols, value.ndim - 1)

    table_flat = camera_table.reshape(codes, -1)
    cross_gain_f = cross_gain.astype(WIDE)
    hidden_gain_f = hidden_gain.astype(WIDE)

    qkv_rows = (
        self_weights.reshape(3, width, heads, HEAD_DIM).transpose(2, 0, 3, 1).reshape(3 * cols, width)
    )
    qkv_rows_back = self_weights.transpose(0, 2, 1).reshape(3 * cols, width)
    pair_rows = cross_pair.transpose(0, 2, 1).reshape(2 * cols, width)
    query_rows = cross_query.T

    local = jnp.stack([self_output, cross_output, query_rows])
    piece = cols // n_rows
    local = lax.dynamic_slice_in_dim(local, row_rank * piece, piece, 1)
    whole = lax.all_gather(jnp.stack(gather_heads(local)), "rows", axis=0)
    whole = whole.transpose(2, 1, 0, 3, 4).reshape(3, n_heads * cols, width)
    self_whole, cross_whole, query_whole = whole[0], whole[1], whole[2]

    def over_all_columns(value_t, weight):
        return mul(jnp.concatenate(gather_heads(value_t), axis=0), weight, TN)

    def by_object(weight, value):
        return jnp.stack(
            [mul(weight, value[i * rows : (i + 1) * rows], NT).astype(LOW) for i in range(objects)]
        )

    def column_terms(value, grads_t):
        return [
            mul(value, grads_t[i : i + cols], (((0,), (1,)), ((), ())))
            for i in range(0, grads_t.shape[0], cols)
        ]

    def one_group(group):
        part = slice(group * objects, (group + 1) * objects)
        inputs = tokens[part].reshape(count, width).astype(WIDE)
        patch_in = patches[part].reshape(objects * patch_rows, patch_width)
        lengths = patch_len[part]
        grad_low = cotangent[part].reshape(count, width)
        onehot = (cam_index[part].reshape(count)[:, None] == jnp.arange(codes)[None, :]).astype(LOW)
        shift_scale = mul(onehot, table_flat)
        gain_one = 1.0 + shift_scale[:, :width]
        unit_one, rate_one = normed(inputs)
        normed_one = (unit_one * gain_one + shift_scale[:, width:]).astype(LOW)
        qkv_t = by_object(qkv_rows, normed_one)
        by_kind = qkv_t.reshape(objects, heads, 3, HEAD_DIM, rows).transpose(2, 1, 3, 0, 4)
        by_kind = by_kind.reshape(3, cols, count)
        self_pair = lax.all_gather(by_kind[1:], "rows", axis=0)
        patch_mid = mul(patch_in, patch_weights).astype(LOW)
        own_pair = mul(pair_rows, patch_mid, NT).astype(LOW).reshape(2, cols, -1)
        pair_t = lax.all_gather(own_pair, "rows", axis=0)
        self_mixed_t, self_wide, self_log = cross_forward(by_kind[0], self_pair, full_lengths)
        after_self = inputs + over_all_columns(self_mixed_t, self_whole)
        unit_two, rate_two = normed(after_self)
        normed_two = (unit_two * cross_gain_f).astype(LOW)
        cross_q_t = mul(query_rows, normed_two, NT).astype(LOW)
        cross_mixed_t, cross_wide, cross_log = cross_forward(cross_q_t, pair_t, lengths)
        after_cross = after_self + over_all_columns(cross_mixed_t, cross_whole)
        unit_three, rate_three = normed(after_cross)
        normed_three = (unit_three * hidden_gain_f).astype(LOW)
        pre_act = mul(normed_three, widen_weights)
        activated, act_back = jax.vjp(gelu_tanh, pre_act)
        activated = activated.astype(LOW)
        grad_pre = act_back(mul(grad_low, narrow_weights, NT))[0].astype(LOW)
        grad_three = sum_heads(mul(grad_pre, widen_weights, NT)).astype(WIDE)
        yield "heads", {"hidden": mul(activated, narrow_weights)}
        yield "rows", {
            "narrow": mul(activated, grad_low, TN),
            "widen": mul(normed_three, grad_pre, TN),
        }
        hidden_gain_term = jnp.sum(own_columns(grad_three * unit_three), axis=0)
        grad_cross = grad_low.astype(WIDE) + normed_back(
            grad_three * hidden_gain_f, unit_three, rate_three
        )
        grad_cross_low = grad_cross.astype(LOW)
        cross_output_term = mul(cross_mixed_t, grad_cross_low)
        grad_mixed_t = mul(cross_output, grad_cross_low, NT).astype(LOW)
        grad_cq_t, grad_pair_t = cross_backward(
            cross_q_t, pair_t, lengths, grad_mixed_t, cross_wide, cross_log
        )
        grad_two = over_all_columns(grad_cq_t, query_whole)
        grad_pair_t = lax.psum_scatter(grad_pair_t, "rows", scatter_dimension=0, tiled=False)
        grad_pair_t = grad_pair_t.reshape(2 * cols, -1)
        query_term = mul(normed_two, grad_cq_t, (((0,), (1,)), ((), ())))
        cross_gain_term = jnp.sum(own_columns(grad_two * unit_two), axis=0)
        grad_self = grad_cross + normed_back(grad_two * cross_gain_f, unit_two, rate_two)
        grad_self_low = grad_self.astype(LOW)
        self_output_term = mul(self_mixed_t, grad_self_low)
        yield "heads", {"patch": mul(grad_pair_t, pair_rows, TN)}
        yield "rows", {
            "query": query_term,
            "pair": column_terms(patch_mid, grad_pair_t),
            "cross_output": cross_output_term,
            "self_output": self_output_term,
        }
        grad_self_mixed_t = mul(self_output, grad_self_low, NT).astype(LOW)
        grad_q_t, grad_kv_t = cross_backward(
            by_kind[0], self_pair, full_lengths, grad_self_mixed_t, self_wide, self_log
        )
        grad_kv_t = lax.psum_scatter(grad_kv_t, "rows", scatter_dimension=0, tiled=False)
        grad_qkv_t = jnp.concatenate([grad_q_t[None], grad_kv_t]).reshape(3 * cols, count)
        grad_qkv_t = yield "after", (grad_qkv_t, ["patch", "narrow", "widen"])
        grad_mid = yield "take", "patch"
        patch_term = mul(patch_in, own_columns(grad_mid), TN)
        patch_grad = mul(grad_mid, patch_weights, NT)
        grad_one = sum_heads(mul(grad_qkv_t, qkv_rows_back, TN))
        grad_one = yield "after", (grad_one, ["query", "pair", "cross_output", "self_output"])
        grad_one = grad_one.astype(WIDE)
        input_grad = grad_self + normed_back(grad_one * gain_one, unit_one, rate_one)
        own_grad = own_columns(grad_one)
        table_term = jnp.stack(
            [
                lax.dot_general(onehot.astype(WIDE), v, TN, precision=lax.Precision.HIGHEST)
                for v in (own_grad * own_columns(unit_one), own_grad)
            ],
            axis=1,
        )
        small = [patch_term, table_term.reshape(2 * codes, cols)]
        small += [hidden_gain_term[None], cross_gain_term[None], jnp.zeros((14, cols), WIDE)]
        yield "rows", {
            "self": column_terms(normed_one, grad_qkv_t),
            "small": jnp.concatenate(small, axis=0),
        }
        hidden_sum = yield "take", "hidden"
        result = (after_cross + hidden_sum.astype(WIDE)).astype(LOW)
        yield (
            "done",
            (
                result.reshape(objects, rows, width),
                input_grad.reshape(objects, rows, width),
                patch_grad.reshape(objects, patch_rows, patch_width),
            ),
        )

    steps = [one_group(group) for group in range(groups)]
    asked = [next(step) for step in steps]
    totals, ahead = {}, []
    while asked[0][0] != "done":
        kind, what = asked[0]
        answers = [None] * groups
        if kind == "take":
            answers = jnp.split(totals[what], groups)
        elif kind == "after":
            early = {name: totals[name] for name in what[1]}
            answers = [value for _, (value, _) in asked]
            answers[-1], early = lax.optimization_barrier((answers[-1], early))
            totals.update(early)
        else:
            terms = [value for _, value in asked]
            if kind == "heads":
                terms = jax.tree.map(lambda *parts: jnp.concatenate(parts, axis=0), *terms)
            else:
                for value in terms[1:]:
                    terms[0] = add_trees(terms[0], value)
                terms = terms[0]
            if kind == "rows":
                terms = jax.tree.map(lambda value: value.astype(LOW), terms)
            if kind == "heads":
                totals.update({name: sum_heads(value) for name, value in terms.items()})
            else:
                before = {name: totals[name] for name in ahead}
                terms, before = lax.optimization_barrier((terms, before))
                totals.update(before)
                totals.update(lax.psum(terms, kind))
                ahead = list(terms)
        asked = [step.send(value) for step, value in zip(steps, answers)]
    outputs, input_grads, patch_grads = (
        jnp.concatenate([value[i] for _, value in asked], axis=0) for i in range(3)
    )
    patch_total, table_total, gains = jnp.split(
        totals["small"], [patch_width, patch_width + 2 * codes]
    )
    gradients = (
        table_total.reshape(codes, 2, cols),
        jnp.stack(totals["self"]),
        totals["self_output"],
        gains[1],
        totals["query"],
        jnp.stack(totals["pair"]),
        totals["cross_output"],
        patch_total,
        gains[0],
        totals["widen"],
        totals["narrow"],
    )
    return (outputs, input_grads, patch_grads) + tuple(value.astype(WIDE) for value in gradients)


def solution(mesh):
    sizes = mesh.shape
    paired = sizes["heads"] == 4 and sizes["rows"] == 8
    heads = ("far", "near") if paired else "heads"
    if paired:
        names = (*heads, "rows")
        mesh = jax.sharding.Mesh(mesh.devices.reshape(2, 2, sizes["rows"]), names)
    in_specs = (
        P(None, "rows", None),
        P(None, "rows"),
        P(None, "rows", None),
        P(),
        P(),
        P(None, None, heads),
        P(heads, None),
        P(),
        P(None, heads),
        P(None, None, heads),
        P(heads, None),
        P(),
        P(),
        P(None, heads),
        P(heads, None),
        P(None, "rows", None),
    )
    out_specs = (
        P(None, "rows", None),
        P(None, "rows", None),
        P(None, "rows", None),
        P(None, None, heads),
        P(None, None, heads),
        P(heads, None),
        P(heads),
        P(None, heads),
        P(None, None, heads),
        P(heads, None),
        P(None, heads),
        P(heads),
        P(None, heads),
        P(heads, None),
    )
    return jax.shard_map(
        paired_device if paired else per_device,
        mesh=mesh,
        in_specs=in_specs,
        out_specs=out_specs,
        check_vma=False,
    )
```

```python
import jax
import jax.numpy as jnp
from jax import lax
from jax.experimental import pallas as pl
from jax.experimental.pallas import tpu as pltpu
from jax.sharding import PartitionSpec as P

HEAD_DIM = 64
EPSILON = 1e-05
SCALE = HEAD_DIM ** (-0.5)
LOW = jnp.bfloat16
WIDE = jnp.float32

NN = (((1,), (0,)), ((), ()))
NT = (((1,), (1,)), ((), ()))
TN = (((0,), (0,)), ((), ()))
T_LAST = (((0,), (1,)), ((), ()))


def mul(left, right, dims=NN):
    return lax.dot_general(left, right, dims, preferred_element_type=WIDE)


def load_values(values, block, values_t):
    rows = values_t.shape[1]
    at = slice(block * rows, (block + 1) * rows)
    values[at, :HEAD_DIM] = values_t.T
    values[at, HEAD_DIM:] = jnp.ones((rows, HEAD_DIM), values.dtype)


def attend_block(queries, keys_t, values):
    scores = mul(queries, keys_t)
    peak = jnp.max(scores, axis=1, keepdims=True)
    both = mul(jnp.exp(scores - peak).astype(LOW), values).T
    total = both[HEAD_DIM : HEAD_DIM + 1]
    return both[:HEAD_DIM] / total, peak.T + jnp.log(total)


def attend_block_back(scaled_q, grad_t, keys, keys_t, values, log_total, spread):
    probs = jnp.exp(mul(keys, scaled_q) - log_total)
    grad_scores = (probs * (mul(values, grad_t) - spread)).astype(LOW)
    return (
        (mul(keys_t, grad_scores) * SCALE).astype(LOW),
        mul(grad_scores, scaled_q.T),
        mul(probs.astype(LOW), grad_t.T),
    )


def estimate(rows, cols, passes):
    return pl.CostEstimate(
        flops=int(rows * cols * 1200 * passes), transcendentals=int(rows * cols), bytes_accessed=int(rows * 2048)
    )


VMEM_LIMIT = 48 << 20


def by_length(length, full, blocks, run):
    @pl.when(length * 4 > full)
    def _():
        run(blocks)

    @pl.when(length * 4 <= full)
    def _():
        run(blocks // 4)


def cross_forward(queries_t, pair_t, lengths):
    blocks, _, cols, all_patches = pair_t.shape
    objects = lengths.shape[0]
    heads = cols // HEAD_DIM
    rows, patch_rows = queries_t.shape[1] // objects, all_patches // objects

    def kernel(len_ref, q_ref, pair_ref, mixed_ref, wide_ref, log_ref, keys_t, values):
        queries = (q_ref[...] * LOW(SCALE)).T

        def run(live):
            for c in range(live):
                keys_t[:, c * patch_rows : (c + 1) * patch_rows] = pair_ref[c, 0]
                load_values(values, c, pair_ref[c, 1])
            size = live * patch_rows
            mixed, log_total = attend_block(queries, keys_t[:, :size], values[:size])
            mixed_ref[...] = mixed.astype(LOW)
            wide_ref[...] = mixed
            log_ref[...] = log_total

        by_length(len_ref[pl.program_id(0)], blocks * patch_rows, blocks, run)

    block = pl.BlockSpec((HEAD_DIM, rows), lambda b, j, lens: (j, b))
    return pl.pallas_call(
        kernel,
        grid_spec=pltpu.PrefetchScalarGridSpec(
            num_scalar_prefetch=1,
            grid=(objects, heads),
            in_specs=[
                block,
                pl.BlockSpec((blocks, 2, HEAD_DIM, patch_rows), lambda b, j, lens: (0, 0, j, b)),
            ],
            out_specs=[block, block, pl.BlockSpec((None, 1, rows), lambda b, j, lens: (j, 0, b))],
            scratch_shapes=[
                pltpu.VMEM((HEAD_DIM, blocks * patch_rows), LOW),
                pltpu.VMEM((blocks * patch_rows, 2 * HEAD_DIM), LOW),
            ],
        ),
        out_shape=[
            jax.ShapeDtypeStruct(queries_t.shape, LOW),
            jax.ShapeDtypeStruct(queries_t.shape, WIDE),
            jax.ShapeDtypeStruct((heads, 1, queries_t.shape[1]), WIDE),
        ],
        name="cross_forward",
        cost_estimate=estimate(objects * rows, blocks * patch_rows * heads, 1.4),
        compiler_params=pltpu.CompilerParams(vmem_limit_bytes=VMEM_LIMIT),
    )(lengths, queries_t, pair_t)


def cross_backward(queries_t, pair_t, lengths, grad_t_all, wide, log_total):
    blocks, _, cols, all_patches = pair_t.shape
    objects = lengths.shape[0]
    heads = cols // HEAD_DIM
    rows, patch_rows = queries_t.shape[1] // objects, all_patches // objects

    def kernel(len_ref, q_ref, pair_ref, g_ref, wide_ref, log_ref, out_q, out_pair, keys, keys_t, values):
        grad_t = g_ref[...]
        spread = jnp.sum(grad_t.astype(WIDE) * wide_ref[...], axis=0, keepdims=True)

        def run(live):
            for c in range(live):
                at = slice(c * patch_rows, (c + 1) * patch_rows)
                keys[at] = pair_ref[c, 0].T
                keys_t[:, at] = pair_ref[c, 0]
                values[at] = pair_ref[c, 1].T
            size = live * patch_rows
            out_q[...], grad_k, grad_v = attend_block_back(
                q_ref[...] * LOW(SCALE),
                grad_t,
                keys[:size],
                keys_t[:, :size],
                values[:size],
                log_ref[...],
                spread,
            )
            for c in range(live):
                at = slice(c * patch_rows, (c + 1) * patch_rows)
                out_pair[c, 0] = grad_k[at].T.astype(LOW)
                out_pair[c, 1] = grad_v[at].T.astype(LOW)
            for c in range(live, blocks):
                out_pair[c] = jnp.zeros_like(out_pair[c])

        by_length(len_ref[pl.program_id(0)], blocks * patch_rows, blocks, run)

    block = pl.BlockSpec((HEAD_DIM, rows), lambda b, j, lens: (j, b))
    pair_block = pl.BlockSpec((blocks, 2, HEAD_DIM, patch_rows), lambda b, j, lens: (0, 0, j, b))
    return pl.pallas_call(
        kernel,
        grid_spec=pltpu.PrefetchScalarGridSpec(
            num_scalar_prefetch=1,
            grid=(objects, heads),
            in_specs=[
                block,
                pair_block,
                block,
                block,
                pl.BlockSpec((None, 1, rows), lambda b, j, lens: (j, 0, b)),
            ],
            out_specs=[block, pair_block],
            scratch_shapes=[
                pltpu.VMEM((blocks * patch_rows, HEAD_DIM), LOW),
                pltpu.VMEM((HEAD_DIM, blocks * patch_rows), LOW),
                pltpu.VMEM((blocks * patch_rows, HEAD_DIM), LOW),
            ],
        ),
        out_shape=[
            jax.ShapeDtypeStruct(queries_t.shape, LOW),
            jax.ShapeDtypeStruct(pair_t.shape, LOW),
        ],
        name="cross_backward",
        cost_estimate=estimate(objects * rows, blocks * patch_rows * heads, 2.5),
        compiler_params=pltpu.CompilerParams(vmem_limit_bytes=VMEM_LIMIT),
    )(lengths, queries_t, pair_t, grad_t_all, wide, log_total)


def shift(value, step):
    size = lax.axis_size("heads")
    return lax.ppermute(value, "heads", [((i + step) % size, i) for i in range(size)])


def gather_heads(value):
    size = lax.axis_size("heads")
    if size != 4:
        return [value] + [shift(value, step) for step in range(1, size)]
    after, before = shift(value, 1), shift(value, -1)
    inner = lax.ppermute(after, "heads", [(1, 0), (2, 1)]) + lax.ppermute(before, "heads", [(1, 2), (2, 3)])
    return [value, after, inner, before]


def scatter_heads(partial):
    size, me = lax.axis_size("heads"), lax.axis_index("heads")

    def part(step):
        return lax.dynamic_index_in_dim(partial, (me + step) % size, 0, keepdims=False)

    if size != 4:
        total = part(0)
        for step in range(1, size):
            total = total + shift(part(step).astype(LOW), -step).astype(WIDE)
        return total
    far = part(2).astype(LOW)
    up = lax.ppermute(far, "heads", [(0, 1), (1, 2)]).astype(WIDE)
    down = lax.ppermute(far, "heads", [(2, 1), (3, 2)]).astype(WIDE)
    from_below = shift((part(1) + up).astype(LOW), -1)
    from_above = shift((part(3) + down).astype(LOW), 1)
    return part(0) + from_below.astype(WIDE) + from_above.astype(WIDE)


def in_order(parts):
    size, me = lax.axis_size("heads"), lax.axis_index("heads")
    out = jnp.zeros((size,) + parts[0].shape, parts[0].dtype)
    for step, value in enumerate(parts):
        out = lax.dynamic_update_index_in_dim(out, value, (me + step) % size, 0)
    return out.reshape((-1,) + parts[0].shape[1:])


def sum_heads(partial):
    size = lax.axis_size("heads")
    split = partial.reshape((size, -1) + partial.shape[1:])
    return in_order(gather_heads(scatter_heads(split).astype(LOW)))


def exchange_rows(value):
    return lax.all_to_all(value, "rows", 0, 0, tiled=True)


def normed(value):
    centred = value - jnp.mean(value, axis=-1, keepdims=True)
    rate = lax.rsqrt(jnp.mean(centred * centred, axis=-1, keepdims=True) + EPSILON)
    return centred * rate, rate


def normed_back(grad, unit, rate):
    return rate * (
        grad
        - jnp.mean(grad, axis=-1, keepdims=True)
        - unit * jnp.mean(grad * unit, axis=-1, keepdims=True)
    )


def gelu_tanh(pre_act):
    return jax.nn.gelu(pre_act, approximate=True)


def add_trees(former, latter):
    return jax.tree.map(jnp.add, former, latter)


def pair_forward(queries, pair, key_at, objects, length=None):
    blocks, _, width, count = queries.shape
    rows, pair_rows = count // objects, pair.shape[3] // objects
    lengths = jnp.full((objects,), blocks * pair_rows, jnp.int32) if length is None else length

    def kernel(len_ref, q_ref, k_ref, v_ref, mixed_ref, wide_ref, log_ref, keys_t, values):
        def run(live):
            @pl.when(pl.program_id(1) == 0)
            def _():
                for c in range(live):
                    keys_t[:, c * pair_rows : (c + 1) * pair_rows] = k_ref[c]
                    load_values(values, c, v_ref[c])

            size = live * pair_rows
            mixed, log_total = attend_block(
                (q_ref[...] * LOW(SCALE)).T, keys_t[:, :size], values[:size]
            )
            mixed_ref[...] = mixed.astype(LOW)
            wide_ref[...] = mixed
            log_ref[...] = log_total

        if length is None:
            run(blocks)
        else:
            by_length(len_ref[pl.program_id(0)], blocks * pair_rows, blocks, run)

    block = pl.BlockSpec((None, width, rows), lambda o, i, lens: (i, 0, o))
    return pl.pallas_call(
        kernel,
        grid_spec=pltpu.PrefetchScalarGridSpec(
            num_scalar_prefetch=1,
            grid=(objects, blocks),
            in_specs=[
                pl.BlockSpec((None, None, width, rows), lambda o, i, lens: (i, 0, 0, o)),
                pl.BlockSpec((blocks, None, width, pair_rows), lambda o, i, lens: (0, key_at, 0, o)),
                pl.BlockSpec((blocks, None, width, pair_rows), lambda o, i, lens: (0, key_at + 1, 0, o)),
            ],
            out_specs=[block, block, pl.BlockSpec((None, 1, rows), lambda o, i, lens: (i, 0, o))],
            scratch_shapes=[
                pltpu.VMEM((width, blocks * pair_rows), LOW),
                pltpu.VMEM((blocks * pair_rows, 2 * width), LOW),
            ],
        ),
        out_shape=[
            jax.ShapeDtypeStruct((blocks, width, count), LOW),
            jax.ShapeDtypeStruct((blocks, width, count), WIDE),
            jax.ShapeDtypeStruct((blocks, 1, count), WIDE),
        ],
        name="pair_forward",
        cost_estimate=estimate(objects * blocks * rows, blocks * pair_rows, 2 if length is None else 1.4),
        compiler_params=pltpu.CompilerParams(vmem_limit_bytes=VMEM_LIMIT),
    )(lengths, queries, pair, pair)


def pair_backward(queries, pair, key_at, objects, length, grad_mixed, wide, log_total):
    blocks, _, width, count = queries.shape
    rows = count // objects
    lengths = jnp.full((objects,), blocks * rows, jnp.int32) if length is None else length

    def kernel(len_ref, q_ref, k_ref, v_ref, g_ref, wide_ref, log_ref, out_ref, keys, keys_t, values, grad_k, grad_v):
        i = pl.program_id(1)

        def run(live):
            size = live * rows

            @pl.when(i == 0)
            def _():
                for c in range(live):
                    at = slice(c * rows, (c + 1) * rows)
                    keys[at] = k_ref[c].T
                    keys_t[:, at] = k_ref[c]
                    values[at] = v_ref[c].T

            grad_t = g_ref[...]
            spread = jnp.sum(grad_t.astype(WIDE) * wide_ref[...], axis=0, keepdims=True)
            out_ref[i, 0], term_k, term_v = attend_block_back(
                q_ref[...] * LOW(SCALE),
                grad_t,
                keys[:size],
                keys_t[:, :size],
                values[:size],
                log_ref[...],
                spread,
            )

            @pl.when(i == 0)
            def _():
                grad_k[:size] = term_k
                grad_v[:size] = term_v

            @pl.when(i > 0)
            def _():
                grad_k[:size] += term_k
                grad_v[:size] += term_v

            @pl.when(i == blocks - 1)
            def _():
                for c in range(live):
                    at = slice(c * rows, (c + 1) * rows)
                    out_ref[c, 1] = grad_k[at].T.astype(LOW)
                    out_ref[c, 2] = grad_v[at].T.astype(LOW)
                for c in range(live, blocks):
                    out_ref[c, 1:] = jnp.zeros_like(out_ref[c, 1:])

        if length is None:
            run(blocks)
        else:
            by_length(len_ref[pl.program_id(0)], blocks * rows, blocks, run)

    block = pl.BlockSpec((None, width, rows), lambda o, i, lens: (i, 0, o))
    return pl.pallas_call(
        kernel,
        grid_spec=pltpu.PrefetchScalarGridSpec(
            num_scalar_prefetch=1,
            grid=(objects, blocks),
            in_specs=[
                pl.BlockSpec((None, None, width, rows), lambda o, i, lens: (i, 0, 0, o)),
                pl.BlockSpec((blocks, None, width, rows), lambda o, i, lens: (0, key_at, 0, o)),
                pl.BlockSpec((blocks, None, width, rows), lambda o, i, lens: (0, key_at + 1, 0, o)),
                block,
                block,
                pl.BlockSpec((None, 1, rows), lambda o, i, lens: (i, 0, o)),
            ],
            out_specs=pl.BlockSpec((blocks, 3, width, rows), lambda o, i, lens: (0, 0, 0, o)),
            scratch_shapes=[
                pltpu.VMEM((blocks * rows, width), LOW),
                pltpu.VMEM((width, blocks * rows), LOW),
                pltpu.VMEM((blocks * rows, width), LOW),
                pltpu.VMEM((blocks * rows, width), WIDE),
                pltpu.VMEM((blocks * rows, width), WIDE),
            ],
        ),
        out_shape=jax.ShapeDtypeStruct((blocks, 3, width, count), LOW),
        name="pair_backward",
        cost_estimate=estimate(objects * blocks * rows, blocks * rows, 3 if length is None else 2),
        compiler_params=pltpu.CompilerParams(vmem_limit_bytes=VMEM_LIMIT),
    )(lengths, queries, pair, pair, grad_mixed, wide, log_total)


def swap(value, axis):
    return lax.ppermute(value, axis, [(0, 1), (1, 0)])


def sum_near(partial):
    low = partial.astype(LOW)
    return low.astype(WIDE) + swap(low, "near").astype(WIDE)


def tie(value, *others):
    return lax.optimization_barrier((value, *others))


def paired_device(
    tokens,
    cam_index,
    patches,
    patch_len,
    camera_table,
    self_weights,
    self_output,
    cross_gain,
    cross_query,
    cross_pair,
    cross_output,
    patch_weights,
    hidden_gain,
    widen_weights,
    narrow_weights,
    cotangent,
):
    objects = tokens.shape[0] // 2
    _, rows, width = tokens.shape
    cols = self_weights.shape[2]
    hidden = widen_weights.shape[1]
    heads = cols // HEAD_DIM
    codes = camera_table.shape[0]
    patch_width = patches.shape[2]
    count = objects * rows
    n_rows = lax.axis_size("rows")
    row_rank = lax.axis_index("rows")
    far, near = lax.axis_index("far"), lax.axis_index("near")

    def objects_of(value):
        return lax.dynamic_slice_in_dim(value, objects * far, objects, 0)

    def piece(value):
        size = value.shape[0] // n_rows
        return lax.dynamic_slice_in_dim(value, row_rank * size, size, 0)

    def join_rows(value):
        return lax.all_gather(value, "rows", axis=0, tiled=True)

    def both_columns(value):
        return [
            lax.dynamic_slice_in_dim(value, (2 * index + near) * cols, cols, value.ndim - 1)
            for index in range(2)
        ]

    def in_order(mine, away, axis=0):
        size = mine.shape[axis]
        shape = list(mine.shape)
        shape[axis] *= 2
        out = lax.dynamic_update_slice_in_dim(jnp.zeros(shape, mine.dtype), mine, far * size, axis)
        return lax.dynamic_update_slice_in_dim(out, away, (1 - far) * size, axis)

    def halves(value):
        value = value.reshape(objects, 2, rows // 2, -1)
        return [
            lax.dynamic_index_in_dim(value, index, 1, keepdims=False).reshape(count // 2, -1)
            for index in (near, 1 - near)
        ]

    def half_sum_near(partial):
        mine, away = halves(partial)
        return mine + swap(away.astype(LOW), "near").astype(WIDE)

    def over_heads(value):
        value = value.reshape(2, 2, objects, rows // 2, -1)
        value = jnp.where(far == 0, value, jnp.flip(value, 1))
        value = jnp.where(near == 0, value, jnp.flip(value, 0))
        return value.transpose(1, 2, 0, 3, 4).reshape(2 * objects, rows, -1)

    def to_pairs(value_t, slots):
        return value_t.reshape(n_rows, slots, HEAD_DIM, count)

    def times(weights, value):
        return mul(weights, value, NT).astype(LOW)

    def from_pairs(value):
        return value.reshape(-1, count)

    def over_all_columns(value_t, weight):
        return mul(jnp.concatenate([value_t, swap(value_t, "near")]), weight, TN)

    qkv_rows = self_weights.reshape(3, width, heads, HEAD_DIM).transpose(2, 0, 3, 1)
    qkv_rows = qkv_rows.reshape(3 * cols, width)
    pair_rows = cross_pair.reshape(2, width, heads, HEAD_DIM).transpose(2, 0, 3, 1)
    pair_rows = pair_rows.reshape(2 * cols, width)
    query_rows = cross_query.T

    qkv_away = join_rows(swap(piece(qkv_rows), "far"))

    table_flat = camera_table.reshape(codes, -1)
    cross_gain_f = cross_gain.astype(WIDE)
    hidden_gain_f = hidden_gain.astype(WIDE)

    inputs = objects_of(tokens).reshape(count, width).astype(WIDE)
    patch_in = objects_of(patches).reshape(count, patch_width)
    length = objects_of(patch_len)
    grad_low = objects_of(cotangent).reshape(count, width)
    codes_of = objects_of(cam_index).reshape(count)
    onehot = (codes_of[:, None] == jnp.arange(codes)[None, :]).astype(LOW)
    shift_scale = mul(onehot, table_flat)
    gain_one = 1.0 + shift_scale[:, :width]
    unit_one, rate_one = normed(inputs)
    normed_one = (unit_one * gain_one + shift_scale[:, width:]).astype(LOW)

    mine = [piece(v) for v in (self_output, query_rows, cross_output, pair_rows)]
    normed_one, *mine = tie(normed_one, *mine)
    mine = jnp.concatenate(mine, axis=0)
    across = swap(mine, "far")
    size = cols // n_rows
    pair_away = join_rows(across[3 * size :])
    two = [value[: 3 * size].reshape(3, 1, size, width) for value in (mine, across)]
    two = in_order(*two, axis=1)
    four = jnp.concatenate([two, swap(two, "near")], axis=1).reshape(12, size, width)
    whole = lax.all_gather(four, "rows", axis=1).reshape(3, 4 * cols, width)
    self_whole, query_whole, cross_whole = whole[0], whole[1], whole[2]

    qkv_both = in_order(qkv_rows, qkv_away)
    qkv = in_order(times(qkv_rows, normed_one), times(qkv_away, normed_one))
    qkv = exchange_rows(to_pairs(qkv, 3))
    patch_mid = mul(patch_in, patch_weights).astype(LOW)
    pair_both = in_order(pair_rows, pair_away)
    pair = to_pairs(times(pair_both, patch_mid), 2)

    mine = [piece(widen_weights.T), piece(narrow_weights)]
    qkv, *mine = tie(qkv, *mine)
    sent = lax.all_gather(jnp.stack(mine), ("far", "rows"), axis=1).reshape(2, 2 * hidden, width)
    widen_t, narrow = sent[0], sent[1]

    mixed, self_wide, self_log = pair_forward(qkv, qkv, 1, objects)
    mixed, pair = tie(exchange_rows(mixed), pair)
    pair = exchange_rows(pair)
    self_mixed_t = from_pairs(mixed)
    after_self = inputs + over_all_columns(self_mixed_t, self_whole)
    unit_two, rate_two = normed(after_self)
    normed_two = (unit_two * cross_gain_f).astype(LOW)
    cross_q, pair = tie(to_pairs(times(query_whole[: 2 * cols], normed_two), 1), pair)
    cross_q = exchange_rows(cross_q)
    mixed, cross_wide, cross_log = pair_forward(cross_q, pair, 0, objects, length)
    cross_mixed_t = from_pairs(exchange_rows(mixed))
    after_cross = after_self + over_all_columns(cross_mixed_t, cross_whole)
    unit_three, rate_three = normed(after_cross)
    normed_three = (unit_three * hidden_gain_f).astype(LOW)
    activated, act_back = jax.vjp(gelu_tanh, mul(normed_three, widen_t, NT))
    activated = activated.astype(LOW)
    grad_pre = act_back(mul(grad_low, narrow, NT))[0].astype(LOW)
    third, activated, grad_pre = tie(mul(grad_pre, widen_t).astype(LOW), activated, grad_pre)
    grad_three = third.astype(WIDE) + swap(third, "near").astype(WIDE)
    hidden_mine, hidden_away = halves(mul(activated, narrow))
    hidden_away, grad_three = tie(hidden_away.astype(LOW), grad_three)
    hidden_half = hidden_mine + swap(hidden_away, "near").astype(WIDE)
    result = (halves(after_cross)[0] + hidden_half).astype(LOW)

    def part_rows(both):
        return lax.psum_scatter(both, "rows", scatter_dimension=1, tiled=True)

    def own_and_away(value):
        return [lax.dynamic_index_in_dim(value, index, 0, keepdims=False) for index in (far, 1 - far)]

    def add_far(mine, away):
        return (mine.astype(WIDE) + away.astype(WIDE)).astype(LOW)

    def by_shard(left, right):
        return mul(left, right, NN).astype(LOW).reshape(2, -1, right.shape[1])

    hidden_terms = jnp.concatenate(
        [
            mul(value, against, TN).astype(LOW).reshape(2, hidden, width)
            for value, against in ((activated, grad_low), (grad_pre, normed_three))
        ],
        axis=1,
    )
    hidden_part = part_rows(hidden_terms)

    hidden_gain_term = jnp.sum(grad_three * unit_three, axis=0)
    grad_cross = grad_low.astype(WIDE) + normed_back(
        grad_three * hidden_gain_f, unit_three, rate_three
    )
    grad_cross_low = grad_cross.astype(LOW)
    grad_mixed = exchange_rows(to_pairs(times(cross_whole[: 2 * cols], grad_cross_low), 1)[:, 0])
    grad_mixed, result = tie(grad_mixed, result)
    result_two = jnp.stack([result, swap(result, "far")])
    grads = pair_backward(cross_q, pair, 0, objects, length, grad_mixed, cross_wide, cross_log)
    grads, result_two, hidden_part = tie(grads, result_two, hidden_part)
    hidden_own, hidden_away = own_and_away(hidden_part)
    grads, hidden_away = tie(exchange_rows(grads), swap(hidden_away, "far"))
    hidden_total = join_rows(add_far(hidden_own, hidden_away))
    grad_cq_t = from_pairs(grads[:, :1])
    grad_pair_t = from_pairs(grads[:, 1:])
    middle_terms = jnp.concatenate(
        [
            by_shard(cross_mixed_t, grad_cross_low),
            by_shard(grad_cq_t, normed_two),
            by_shard(grad_pair_t, patch_mid),
        ],
        axis=1,
    )
    grad_cq_away, middle_terms = tie(swap(grad_cq_t, "near"), middle_terms)
    middle_part = part_rows(middle_terms)
    grad_two = mul(jnp.concatenate([grad_cq_t, grad_cq_away]), query_whole, TN)
    grad_two, result_two = tie(grad_two, result_two)
    result_four = jnp.stack([result_two, swap(result_two, "near")])
    cross_gain_term = jnp.sum(grad_two * unit_two, axis=0)
    grad_self = grad_cross + normed_back(grad_two * cross_gain_f, unit_two, rate_two)
    grad_self_low = grad_self.astype(LOW)
    grad_mixed, grad_self_low, grad_mid = tie(
        to_pairs(times(self_whole[: 2 * cols], grad_self_low), 1)[:, 0],
        grad_self_low,
        mul(grad_pair_t, pair_both, TN).astype(LOW),
    )
    grad_mid_away = swap(grad_mid, "near")
    output_terms = by_shard(self_mixed_t, grad_self_low)
    grads = pair_backward(qkv, qkv, 1, objects, None, exchange_rows(grad_mixed), self_wide, self_log)
    grads, grad_mid_away, result_four = tie(grads, grad_mid_away, result_four)
    grad_mid = (grad_mid.astype(WIDE) + grad_mid_away.astype(WIDE)).astype(LOW)
    patch_half = mul(halves(grad_mid)[0], patch_weights, NT).astype(LOW)
    patch_two = jnp.stack([patch_half, swap(patch_half, "far")])
    patch_terms = jnp.stack([mul(value, patch_in, TN).astype(LOW) for value in both_columns(grad_mid)])
    patch_terms = jnp.pad(patch_terms, ((0, 0), (0, 0), (0, width - patch_width)))
    last_terms = jnp.pad(
        jnp.concatenate([output_terms, patch_terms], axis=1), ((0, 0), (3 * cols, 0), (0, 0))
    )
    hidden_gradients = [hidden_total[hidden:].T.astype(WIDE), hidden_total[:hidden].astype(WIDE)]
    grads, patch_two, last_terms, middle_part = tie(exchange_rows(grads), patch_two, last_terms, middle_part)
    grad_qkv_t = from_pairs(grads)
    last_terms = lax.dynamic_update_slice_in_dim(last_terms, by_shard(grad_qkv_t, normed_one), 0, 1)
    last_part = part_rows(last_terms)
    middle_own, middle_away = own_and_away(middle_part)
    first_mine, first_away = halves(mul(grad_qkv_t, qkv_both, TN))
    first_away, middle_away = tie(first_away.astype(LOW), middle_away)
    middle_total = join_rows(add_far(middle_own, swap(middle_away, "far")))
    grad_one = first_mine + swap(first_away, "near").astype(WIDE)
    gain_half, unit_half, rate_half, self_half = (
        halves(value)[0] for value in (gain_one, unit_one, rate_one, grad_self)
    )
    input_half = self_half + normed_back(grad_one * gain_half, unit_half, rate_half)
    input_half = input_half.astype(LOW)
    input_two = jnp.stack([input_half, swap(input_half, "far")])
    last_part, input_two, patch_two, hidden_gradients = tie(last_part, input_two, patch_two, hidden_gradients)
    input_four = jnp.stack([input_two, swap(input_two, "near")])
    patch_four = jnp.stack([patch_two, swap(patch_two, "near")])
    onehot_half = halves(onehot)[0].astype(WIDE)
    table_term = jnp.concatenate(
        [
            lax.dot_general(onehot_half, value, TN, precision=lax.Precision.HIGHEST)
            for value in (grad_one * unit_half, grad_one)
        ],
        axis=0,
    )
    small = [sum_near(table_term), hidden_gain_term[None], cross_gain_term[None], jnp.zeros((14, width), WIDE)]
    small = jnp.stack(both_columns(jnp.concatenate(small, axis=0).astype(LOW)))
    small = jnp.sum(lax.all_gather(small, "rows", axis=0).astype(WIDE), axis=0).astype(LOW)
    small_own, small_away = own_and_away(small)
    small_away, patch_four = tie(small_away, patch_four)
    small = small_own.astype(WIDE) + swap(small_away, "far").astype(WIDE)
    last_own, last_away = own_and_away(last_part)
    last_sum, input_four = tie(add_far(last_own, swap(last_away, "far")), input_four)
    last_total = join_rows(last_sum)
    input_grads = over_heads(input_four)
    outputs, patch_grads = over_heads(result_four), over_heads(patch_four)

    cross_output_total, query_total = middle_total[:cols], middle_total[cols : 2 * cols]
    pair_total = middle_total[2 * cols :].reshape(heads, 2, HEAD_DIM, width)
    self_total = last_total[: 3 * cols].reshape(heads, 3, HEAD_DIM, width)
    self_output_total = last_total[3 * cols : 4 * cols]
    patch_total = last_total[4 * cols :, :patch_width]
    gradients = (
        small[: 2 * codes].reshape(2, codes, cols).transpose(1, 0, 2),
        self_total.transpose(1, 3, 0, 2).reshape(3, width, cols),
        self_output_total,
        small[2 * codes + 1],
        query_total.T,
        pair_total.transpose(1, 3, 0, 2).reshape(2, width, cols),
        cross_output_total,
        patch_total.T,
        small[2 * codes],
        *hidden_gradients,
    )
    return (outputs, input_grads.astype(WIDE), patch_grads.astype(WIDE)) + tuple(
        value.astype(WIDE) for value in gradients
    )


def per_device(
    tokens,
    cam_index,
    patches,
    patch_len,
    camera_table,
    self_weights,
    self_output,
    cross_gain,
    cross_query,
    cross_pair,
    cross_output,
    patch_weights,
    hidden_gain,
    widen_weights,
    narrow_weights,
    cotangent,
):
    batches, rows, width = tokens.shape
    cols = self_weights.shape[2]
    heads = cols // HEAD_DIM
    codes = camera_table.shape[0]
    patch_rows, patch_width = patches.shape[1:]
    n_rows, n_heads = lax.axis_size("rows"), lax.axis_size("heads")
    row_rank, head_rank = lax.axis_index("rows"), lax.axis_index("heads")
    groups = 1
    objects = batches // groups
    full_lengths = jnp.full((objects,), n_rows * rows, jnp.int32)
    count = objects * rows

    def own_columns(value):
        return lax.dynamic_slice_in_dim(value, head_rank * cols, cols, value.ndim - 1)

    table_flat = camera_table.reshape(codes, -1)
    cross_gain_f = cross_gain.astype(WIDE)
    hidden_gain_f = hidden_gain.astype(WIDE)

    qkv_rows = (
        self_weights.reshape(3, width, heads, HEAD_DIM).transpose(2, 0, 3, 1).reshape(3 * cols, width)
    )
    qkv_rows_back = self_weights.transpose(0, 2, 1).reshape(3 * cols, width)
    pair_rows = cross_pair.transpose(0, 2, 1).reshape(2 * cols, width)
    query_rows = cross_query.T

    local = jnp.stack([self_output, cross_output, query_rows])
    piece = cols // n_rows
    local = lax.dynamic_slice_in_dim(local, row_rank * piece, piece, 1)
    whole = lax.all_gather(jnp.stack(gather_heads(local)), "rows", axis=0)
    whole = whole.transpose(2, 1, 0, 3, 4).reshape(3, n_heads * cols, width)
    self_whole, cross_whole, query_whole = whole[0], whole[1], whole[2]

    def over_all_columns(value_t, weight):
        return mul(jnp.concatenate(gather_heads(value_t), axis=0), weight, TN)

    def by_object(weight, value):
        return jnp.stack(
            [mul(weight, value[i * rows : (i + 1) * rows], NT).astype(LOW) for i in range(objects)]
        )

    def column_terms(value, grads_t):
        return [
            mul(value, grads_t[i : i + cols], (((0,), (1,)), ((), ())))
            for i in range(0, grads_t.shape[0], cols)
        ]

    def one_group(group):
        part = slice(group * objects, (group + 1) * objects)
        inputs = tokens[part].reshape(count, width).astype(WIDE)
        patch_in = patches[part].reshape(objects * patch_rows, patch_width)
        lengths = patch_len[part]
        grad_low = cotangent[part].reshape(count, width)
        onehot = (cam_index[part].reshape(count)[:, None] == jnp.arange(codes)[None, :]).astype(LOW)
        shift_scale = mul(onehot, table_flat)
        gain_one = 1.0 + shift_scale[:, :width]
        unit_one, rate_one = normed(inputs)
        normed_one = (unit_one * gain_one + shift_scale[:, width:]).astype(LOW)
        qkv_t = by_object(qkv_rows, normed_one)
        by_kind = qkv_t.reshape(objects, heads, 3, HEAD_DIM, rows).transpose(2, 1, 3, 0, 4)
        by_kind = by_kind.reshape(3, cols, count)
        self_pair = lax.all_gather(by_kind[1:], "rows", axis=0)
        patch_mid = mul(patch_in, patch_weights).astype(LOW)
        own_pair = mul(pair_rows, patch_mid, NT).astype(LOW).reshape(2, cols, -1)
        pair_t = lax.all_gather(own_pair, "rows", axis=0)
        self_mixed_t, self_wide, self_log = cross_forward(by_kind[0], self_pair, full_lengths)
        after_self = inputs + over_all_columns(self_mixed_t, self_whole)
        unit_two, rate_two = normed(after_self)
        normed_two = (unit_two * cross_gain_f).astype(LOW)
        cross_q_t = mul(query_rows, normed_two, NT).astype(LOW)
        cross_mixed_t, cross_wide, cross_log = cross_forward(cross_q_t, pair_t, lengths)
        after_cross = after_self + over_all_columns(cross_mixed_t, cross_whole)
        unit_three, rate_three = normed(after_cross)
        normed_three = (unit_three * hidden_gain_f).astype(LOW)
        pre_act = mul(normed_three, widen_weights)
        activated, act_back = jax.vjp(gelu_tanh, pre_act)
        activated = activated.astype(LOW)
        grad_pre = act_back(mul(grad_low, narrow_weights, NT))[0].astype(LOW)
        grad_three = sum_heads(mul(grad_pre, widen_weights, NT)).astype(WIDE)
        yield "heads", {"hidden": mul(activated, narrow_weights)}
        yield "rows", {
            "narrow": mul(activated, grad_low, TN),
            "widen": mul(normed_three, grad_pre, TN),
        }
        hidden_gain_term = jnp.sum(own_columns(grad_three * unit_three), axis=0)
        grad_cross = grad_low.astype(WIDE) + normed_back(
            grad_three * hidden_gain_f, unit_three, rate_three
        )
        grad_cross_low = grad_cross.astype(LOW)
        cross_output_term = mul(cross_mixed_t, grad_cross_low)
        grad_mixed_t = mul(cross_output, grad_cross_low, NT).astype(LOW)
        grad_cq_t, grad_pair_t = cross_backward(
            cross_q_t, pair_t, lengths, grad_mixed_t, cross_wide, cross_log
        )
        grad_two = over_all_columns(grad_cq_t, query_whole)
        grad_pair_t = lax.psum_scatter(grad_pair_t, "rows", scatter_dimension=0, tiled=False)
        grad_pair_t = grad_pair_t.reshape(2 * cols, -1)
        query_term = mul(normed_two, grad_cq_t, (((0,), (1,)), ((), ())))
        cross_gain_term = jnp.sum(own_columns(grad_two * unit_two), axis=0)
        grad_self = grad_cross + normed_back(grad_two * cross_gain_f, unit_two, rate_two)
        grad_self_low = grad_self.astype(LOW)
        self_output_term = mul(self_mixed_t, grad_self_low)
        yield "heads", {"patch": mul(grad_pair_t, pair_rows, TN)}
        yield "rows", {
            "query": query_term,
            "pair": column_terms(patch_mid, grad_pair_t),
            "cross_output": cross_output_term,
            "self_output": self_output_term,
        }
        grad_self_mixed_t = mul(self_output, grad_self_low, NT).astype(LOW)
        grad_q_t, grad_kv_t = cross_backward(
            by_kind[0], self_pair, full_lengths, grad_self_mixed_t, self_wide, self_log
        )
        grad_kv_t = lax.psum_scatter(grad_kv_t, "rows", scatter_dimension=0, tiled=False)
        grad_qkv_t = jnp.concatenate([grad_q_t[None], grad_kv_t]).reshape(3 * cols, count)
        grad_qkv_t = yield "after", (grad_qkv_t, ["patch", "narrow", "widen"])
        grad_mid = yield "take", "patch"
        patch_term = mul(patch_in, own_columns(grad_mid), TN)
        patch_grad = mul(grad_mid, patch_weights, NT)
        grad_one = sum_heads(mul(grad_qkv_t, qkv_rows_back, TN))
        grad_one = yield "after", (grad_one, ["query", "pair", "cross_output", "self_output"])
        grad_one = grad_one.astype(WIDE)
        input_grad = grad_self + normed_back(grad_one * gain_one, unit_one, rate_one)
        own_grad = own_columns(grad_one)
        table_term = jnp.stack(
            [
                lax.dot_general(onehot.astype(WIDE), v, TN, precision=lax.Precision.HIGHEST)
                for v in (own_grad * own_columns(unit_one), own_grad)
            ],
            axis=1,
        )
        small = [patch_term, table_term.reshape(2 * codes, cols)]
        small += [hidden_gain_term[None], cross_gain_term[None], jnp.zeros((14, cols), WIDE)]
        yield "rows", {
            "self": column_terms(normed_one, grad_qkv_t),
            "small": jnp.concatenate(small, axis=0),
        }
        hidden_sum = yield "take", "hidden"
        result = (after_cross + hidden_sum.astype(WIDE)).astype(LOW)
        yield (
            "done",
            (
                result.reshape(objects, rows, width),
                input_grad.reshape(objects, rows, width),
                patch_grad.reshape(objects, patch_rows, patch_width),
            ),
        )

    steps = [one_group(group) for group in range(groups)]
    asked = [next(step) for step in steps]
    totals, ahead = {}, []
    while asked[0][0] != "done":
        kind, what = asked[0]
        answers = [None] * groups
        if kind == "take":
            answers = jnp.split(totals[what], groups)
        elif kind == "after":
            early = {name: totals[name] for name in what[1]}
            answers = [value for _, (value, _) in asked]
            answers[-1], early = lax.optimization_barrier((answers[-1], early))
            totals.update(early)
        else:
            terms = [value for _, value in asked]
            if kind == "heads":
                terms = jax.tree.map(lambda *parts: jnp.concatenate(parts, axis=0), *terms)
            else:
                for value in terms[1:]:
                    terms[0] = add_trees(terms[0], value)
                terms = terms[0]
            if kind == "rows":
                terms = jax.tree.map(lambda value: value.astype(LOW), terms)
            if kind == "heads":
                totals.update({name: sum_heads(value) for name, value in terms.items()})
            else:
                before = {name: totals[name] for name in ahead}
                terms, before = lax.optimization_barrier((terms, before))
                totals.update(before)
                totals.update(lax.psum(terms, kind))
                ahead = list(terms)
        asked = [step.send(value) for step, value in zip(steps, answers)]
    outputs, input_grads, patch_grads = (
        jnp.concatenate([value[i] for _, value in asked], axis=0) for i in range(3)
    )
    patch_total, table_total, gains = jnp.split(
        totals["small"], [patch_width, patch_width + 2 * codes]
    )
    gradients = (
        table_total.reshape(codes, 2, cols),
        jnp.stack(totals["self"]),
        totals["self_output"],
        gains[1],
        totals["query"],
        jnp.stack(totals["pair"]),
        totals["cross_output"],
        patch_total,
        gains[0],
        totals["widen"],
        totals["narrow"],
    )
    return (outputs, input_grads, patch_grads) + tuple(value.astype(WIDE) for value in gradients)


def solution(mesh):
    sizes = mesh.shape
    paired = sizes["heads"] == 4 and sizes["rows"] == 8
    heads = ("far", "near") if paired else "heads"
    if paired:
        names = (*heads, "rows")
        mesh = jax.sharding.Mesh(mesh.devices.reshape(2, 2, sizes["rows"]), names)
    in_specs = (
        P(None, "rows", None),
        P(None, "rows"),
        P(None, "rows", None),
        P(),
        P(),
        P(None, None, heads),
        P(heads, None),
        P(),
        P(None, heads),
        P(None, None, heads),
        P(heads, None),
        P(),
        P(),
        P(None, heads),
        P(heads, None),
        P(None, "rows", None),
    )
    out_specs = (
        P(None, "rows", None),
        P(None, "rows", None),
        P(None, "rows", None),
        P(None, None, heads),
        P(None, None, heads),
        P(heads, None),
        P(heads),
        P(None, heads),
        P(None, None, heads),
        P(heads, None),
        P(None, heads),
        P(heads),
        P(None, heads),
        P(heads, None),
    )
    return jax.shard_map(
        paired_device if paired else per_device,
        mesh=mesh,
        in_specs=in_specs,
        out_specs=out_specs,
        check_vma=False,
    )
```

```python
import jax
import jax.numpy as jnp
from jax import lax
from jax.experimental import pallas as pl
from jax.experimental.pallas import tpu as pltpu
from jax.sharding import PartitionSpec as P

HEAD_DIM = 64
EPSILON = 1e-05
SCALE = HEAD_DIM ** (-0.5)
LOW = jnp.bfloat16
WIDE = jnp.float32

NN = (((1,), (0,)), ((), ()))
NT = (((1,), (1,)), ((), ()))
TN = (((0,), (0,)), ((), ()))
T_LAST = (((0,), (1,)), ((), ()))


def mul(left, right, dims=NN):
    return lax.dot_general(left, right, dims, preferred_element_type=WIDE)


def load_values(values, block, values_t):
    rows = values_t.shape[1]
    at = slice(block * rows, (block + 1) * rows)
    values[at, :HEAD_DIM] = values_t.T
    values[at, HEAD_DIM:] = jnp.ones((rows, HEAD_DIM), values.dtype)


def attend_block(queries, keys_t, values):
    scores = mul(queries, keys_t)
    peak = jnp.max(scores, axis=1, keepdims=True)
    both = mul(jnp.exp(scores - peak).astype(LOW), values).T
    total = both[HEAD_DIM : HEAD_DIM + 1]
    return both[:HEAD_DIM] / total, peak.T + jnp.log(total)


def attend_block_back(scaled_q, grad_t, keys, keys_t, values, log_total, spread):
    probs = jnp.exp(mul(keys, scaled_q) - log_total)
    grad_scores = (probs * (mul(values, grad_t) - spread)).astype(LOW)
    return (
        (mul(keys_t, grad_scores) * SCALE).astype(LOW),
        mul(grad_scores, scaled_q.T),
        mul(probs.astype(LOW), grad_t.T),
    )


def estimate(rows, cols, passes):
    return pl.CostEstimate(
        flops=int(rows * cols * 1200 * passes), transcendentals=int(rows * cols), bytes_accessed=int(rows * 2048)
    )


VMEM_LIMIT = 48 << 20


def by_length(length, full, blocks, run):
    @pl.when(length * 4 > full)
    def _():
        run(blocks)

    @pl.when(length * 4 <= full)
    def _():
        run(blocks // 4)


def cross_forward(queries_t, pair_t, lengths):
    blocks, _, cols, all_patches = pair_t.shape
    objects = lengths.shape[0]
    heads = cols // HEAD_DIM
    rows, patch_rows = queries_t.shape[1] // objects, all_patches // objects

    def kernel(len_ref, q_ref, pair_ref, mixed_ref, wide_ref, log_ref, keys_t, values):
        queries = (q_ref[...] * LOW(SCALE)).T

        def run(live):
            for c in range(live):
                keys_t[:, c * patch_rows : (c + 1) * patch_rows] = pair_ref[c, 0]
                load_values(values, c, pair_ref[c, 1])
            size = live * patch_rows
            mixed, log_total = attend_block(queries, keys_t[:, :size], values[:size])
            mixed_ref[...] = mixed.astype(LOW)
            wide_ref[...] = mixed
            log_ref[...] = log_total

        by_length(len_ref[pl.program_id(0)], blocks * patch_rows, blocks, run)

    block = pl.BlockSpec((HEAD_DIM, rows), lambda b, j, lens: (j, b))
    return pl.pallas_call(
        kernel,
        grid_spec=pltpu.PrefetchScalarGridSpec(
            num_scalar_prefetch=1,
            grid=(objects, heads),
            in_specs=[
                block,
                pl.BlockSpec((blocks, 2, HEAD_DIM, patch_rows), lambda b, j, lens: (0, 0, j, b)),
            ],
            out_specs=[block, block, pl.BlockSpec((None, 1, rows), lambda b, j, lens: (j, 0, b))],
            scratch_shapes=[
                pltpu.VMEM((HEAD_DIM, blocks * patch_rows), LOW),
                pltpu.VMEM((blocks * patch_rows, 2 * HEAD_DIM), LOW),
            ],
        ),
        out_shape=[
            jax.ShapeDtypeStruct(queries_t.shape, LOW),
            jax.ShapeDtypeStruct(queries_t.shape, WIDE),
            jax.ShapeDtypeStruct((heads, 1, queries_t.shape[1]), WIDE),
        ],
        name="cross_forward",
        cost_estimate=estimate(objects * rows, blocks * patch_rows * heads, 1.4),
        compiler_params=pltpu.CompilerParams(vmem_limit_bytes=VMEM_LIMIT),
    )(lengths, queries_t, pair_t)


def cross_backward(queries_t, pair_t, lengths, grad_t_all, wide, log_total):
    blocks, _, cols, all_patches = pair_t.shape
    objects = lengths.shape[0]
    heads = cols // HEAD_DIM
    rows, patch_rows = queries_t.shape[1] // objects, all_patches // objects

    def kernel(len_ref, q_ref, pair_ref, g_ref, wide_ref, log_ref, out_q, out_pair, keys, keys_t, values):
        grad_t = g_ref[...]
        spread = jnp.sum(grad_t.astype(WIDE) * wide_ref[...], axis=0, keepdims=True)

        def run(live):
            for c in range(live):
                at = slice(c * patch_rows, (c + 1) * patch_rows)
                keys[at] = pair_ref[c, 0].T
                keys_t[:, at] = pair_ref[c, 0]
                values[at] = pair_ref[c, 1].T
            size = live * patch_rows
            out_q[...], grad_k, grad_v = attend_block_back(
                q_ref[...] * LOW(SCALE),
                grad_t,
                keys[:size],
                keys_t[:, :size],
                values[:size],
                log_ref[...],
                spread,
            )
            for c in range(live):
                at = slice(c * patch_rows, (c + 1) * patch_rows)
                out_pair[c, 0] = grad_k[at].T.astype(LOW)
                out_pair[c, 1] = grad_v[at].T.astype(LOW)
            for c in range(live, blocks):
                out_pair[c] = jnp.zeros_like(out_pair[c])

        by_length(len_ref[pl.program_id(0)], blocks * patch_rows, blocks, run)

    block = pl.BlockSpec((HEAD_DIM, rows), lambda b, j, lens: (j, b))
    pair_block = pl.BlockSpec((blocks, 2, HEAD_DIM, patch_rows), lambda b, j, lens: (0, 0, j, b))
    return pl.pallas_call(
        kernel,
        grid_spec=pltpu.PrefetchScalarGridSpec(
            num_scalar_prefetch=1,
            grid=(objects, heads),
            in_specs=[
                block,
                pair_block,
                block,
                block,
                pl.BlockSpec((None, 1, rows), lambda b, j, lens: (j, 0, b)),
            ],
            out_specs=[block, pair_block],
            scratch_shapes=[
                pltpu.VMEM((blocks * patch_rows, HEAD_DIM), LOW),
                pltpu.VMEM((HEAD_DIM, blocks * patch_rows), LOW),
                pltpu.VMEM((blocks * patch_rows, HEAD_DIM), LOW),
            ],
        ),
        out_shape=[
            jax.ShapeDtypeStruct(queries_t.shape, LOW),
            jax.ShapeDtypeStruct(pair_t.shape, LOW),
        ],
        name="cross_backward",
        cost_estimate=estimate(objects * rows, blocks * patch_rows * heads, 2.5),
        compiler_params=pltpu.CompilerParams(vmem_limit_bytes=VMEM_LIMIT),
    )(lengths, queries_t, pair_t, grad_t_all, wide, log_total)


def shift(value, step):
    size = lax.axis_size("heads")
    return lax.ppermute(value, "heads", [((i + step) % size, i) for i in range(size)])


def gather_heads(value):
    size = lax.axis_size("heads")
    if size != 4:
        return [value] + [shift(value, step) for step in range(1, size)]
    after, before = shift(value, 1), shift(value, -1)
    inner = lax.ppermute(after, "heads", [(1, 0), (2, 1)]) + lax.ppermute(before, "heads", [(1, 2), (2, 3)])
    return [value, after, inner, before]


def scatter_heads(partial):
    size, me = lax.axis_size("heads"), lax.axis_index("heads")

    def part(step):
        return lax.dynamic_index_in_dim(partial, (me + step) % size, 0, keepdims=False)

    if size != 4:
        total = part(0)
        for step in range(1, size):
            total = total + shift(part(step).astype(LOW), -step).astype(WIDE)
        return total
    far = part(2).astype(LOW)
    up = lax.ppermute(far, "heads", [(0, 1), (1, 2)]).astype(WIDE)
    down = lax.ppermute(far, "heads", [(2, 1), (3, 2)]).astype(WIDE)
    from_below = shift((part(1) + up).astype(LOW), -1)
    from_above = shift((part(3) + down).astype(LOW), 1)
    return part(0) + from_below.astype(WIDE) + from_above.astype(WIDE)


def in_order(parts):
    size, me = lax.axis_size("heads"), lax.axis_index("heads")
    out = jnp.zeros((size,) + parts[0].shape, parts[0].dtype)
    for step, value in enumerate(parts):
        out = lax.dynamic_update_index_in_dim(out, value, (me + step) % size, 0)
    return out.reshape((-1,) + parts[0].shape[1:])


def sum_heads(partial):
    size = lax.axis_size("heads")
    split = partial.reshape((size, -1) + partial.shape[1:])
    return in_order(gather_heads(scatter_heads(split).astype(LOW)))


def exchange_rows(value):
    return lax.all_to_all(value, "rows", 0, 0, tiled=True)


def normed(value):
    centred = value - jnp.mean(value, axis=-1, keepdims=True)
    rate = lax.rsqrt(jnp.mean(centred * centred, axis=-1, keepdims=True) + EPSILON)
    return centred * rate, rate


def normed_back(grad, unit, rate):
    return rate * (
        grad
        - jnp.mean(grad, axis=-1, keepdims=True)
        - unit * jnp.mean(grad * unit, axis=-1, keepdims=True)
    )


def gelu_tanh(pre_act):
    return jax.nn.gelu(pre_act, approximate=True)


def add_trees(former, latter):
    return jax.tree.map(jnp.add, former, latter)


def pair_forward(queries, pair, key_at, length=None):
    blocks, objects, _, width, rows = queries.shape
    pair_rows = pair.shape[4]
    lengths = jnp.full((objects,), blocks * pair_rows, jnp.int32) if length is None else length

    def kernel(len_ref, q_ref, k_ref, v_ref, mixed_ref, wide_ref, log_ref, keys_t, values):
        def run(live):
            @pl.when(pl.program_id(1) == 0)
            def _():
                for c in range(live):
                    keys_t[:, c * pair_rows : (c + 1) * pair_rows] = k_ref[c]
                    load_values(values, c, v_ref[c])

            size = live * pair_rows
            mixed, log_total = attend_block(
                (q_ref[...] * LOW(SCALE)).T, keys_t[:, :size], values[:size]
            )
            mixed_ref[...] = mixed.astype(LOW)
            wide_ref[...] = mixed
            log_ref[...] = log_total

        if length is None:
            run(blocks)
        else:
            by_length(len_ref[pl.program_id(0)], blocks * pair_rows, blocks, run)

    block = pl.BlockSpec((None, None, width, rows), lambda o, i, lens: (i, o, 0, 0))
    return pl.pallas_call(
        kernel,
        grid_spec=pltpu.PrefetchScalarGridSpec(
            num_scalar_prefetch=1,
            grid=(objects, blocks),
            in_specs=[
                pl.BlockSpec((None, None, None, width, rows), lambda o, i, lens: (i, o, 0, 0, 0)),
                pl.BlockSpec((blocks, None, None, width, pair_rows), lambda o, i, lens: (0, o, key_at, 0, 0)),
                pl.BlockSpec((blocks, None, None, width, pair_rows), lambda o, i, lens: (0, o, key_at + 1, 0, 0)),
            ],
            out_specs=[block, block, pl.BlockSpec((None, None, 1, rows), lambda o, i, lens: (i, o, 0, 0))],
            scratch_shapes=[
                pltpu.VMEM((width, blocks * pair_rows), LOW),
                pltpu.VMEM((blocks * pair_rows, 2 * width), LOW),
            ],
        ),
        out_shape=[
            jax.ShapeDtypeStruct((blocks, objects, width, rows), LOW),
            jax.ShapeDtypeStruct((blocks, objects, width, rows), WIDE),
            jax.ShapeDtypeStruct((blocks, objects, 1, rows), WIDE),
        ],
        name="pair_forward",
        cost_estimate=estimate(objects * blocks * rows, blocks * pair_rows, 2 if length is None else 1.4),
        compiler_params=pltpu.CompilerParams(vmem_limit_bytes=VMEM_LIMIT),
    )(lengths, queries, pair, pair)


def pair_backward(queries, pair, key_at, length, grad_mixed, wide, log_total):
    blocks, objects, _, width, rows = queries.shape
    lengths = jnp.full((objects,), blocks * rows, jnp.int32) if length is None else length

    def kernel(len_ref, q_ref, k_ref, v_ref, g_ref, wide_ref, log_ref, out_ref, keys, keys_t, values, grad_k, grad_v):
        i = pl.program_id(1)

        def run(live):
            size = live * rows

            @pl.when(i == 0)
            def _():
                for c in range(live):
                    at = slice(c * rows, (c + 1) * rows)
                    keys[at] = k_ref[c].T
                    keys_t[:, at] = k_ref[c]
                    values[at] = v_ref[c].T

            grad_t = g_ref[...]
            spread = jnp.sum(grad_t.astype(WIDE) * wide_ref[...], axis=0, keepdims=True)
            out_ref[i, 0], term_k, term_v = attend_block_back(
                q_ref[...] * LOW(SCALE),
                grad_t,
                keys[:size],
                keys_t[:, :size],
                values[:size],
                log_ref[...],
                spread,
            )

            @pl.when(i == 0)
            def _():
                grad_k[:size] = term_k
                grad_v[:size] = term_v

            @pl.when(i > 0)
            def _():
                grad_k[:size] += term_k
                grad_v[:size] += term_v

            @pl.when(i == blocks - 1)
            def _():
                for c in range(live):
                    at = slice(c * rows, (c + 1) * rows)
                    out_ref[c, 1] = grad_k[at].T.astype(LOW)
                    out_ref[c, 2] = grad_v[at].T.astype(LOW)
                for c in range(live, blocks):
                    out_ref[c, 1:] = jnp.zeros_like(out_ref[c, 1:])

        if length is None:
            run(blocks)
        else:
            by_length(len_ref[pl.program_id(0)], blocks * rows, blocks, run)

    block = pl.BlockSpec((None, None, width, rows), lambda o, i, lens: (i, o, 0, 0))
    return pl.pallas_call(
        kernel,
        grid_spec=pltpu.PrefetchScalarGridSpec(
            num_scalar_prefetch=1,
            grid=(objects, blocks),
            in_specs=[
                pl.BlockSpec((None, None, None, width, rows), lambda o, i, lens: (i, o, 0, 0, 0)),
                pl.BlockSpec((blocks, None, None, width, rows), lambda o, i, lens: (0, o, key_at, 0, 0)),
                pl.BlockSpec((blocks, None, None, width, rows), lambda o, i, lens: (0, o, key_at + 1, 0, 0)),
                block,
                block,
                pl.BlockSpec((None, None, 1, rows), lambda o, i, lens: (i, o, 0, 0)),
            ],
            out_specs=pl.BlockSpec((blocks, None, 3, width, rows), lambda o, i, lens: (0, o, 0, 0, 0)),
            scratch_shapes=[
                pltpu.VMEM((blocks * rows, width), LOW),
                pltpu.VMEM((width, blocks * rows), LOW),
                pltpu.VMEM((blocks * rows, width), LOW),
                pltpu.VMEM((blocks * rows, width), WIDE),
                pltpu.VMEM((blocks * rows, width), WIDE),
            ],
        ),
        out_shape=jax.ShapeDtypeStruct((blocks, objects, 3, width, rows), LOW),
        name="pair_backward",
        cost_estimate=estimate(objects * blocks * rows, blocks * rows, 3 if length is None else 2),
        compiler_params=pltpu.CompilerParams(vmem_limit_bytes=VMEM_LIMIT),
    )(lengths, queries, pair, pair, grad_mixed, wide, log_total)


def swap(value, axis):
    return lax.ppermute(value, axis, [(0, 1), (1, 0)])


def sum_near(partial):
    low = partial.astype(LOW)
    return low.astype(WIDE) + swap(low, "near").astype(WIDE)


def tie(value, *others):
    return lax.optimization_barrier((value, *others))


def paired_device(
    tokens,
    cam_index,
    patches,
    patch_len,
    camera_table,
    self_weights,
    self_output,
    cross_gain,
    cross_query,
    cross_pair,
    cross_output,
    patch_weights,
    hidden_gain,
    widen_weights,
    narrow_weights,
    cotangent,
):
    objects = tokens.shape[0] // 2
    _, rows, width = tokens.shape
    cols = self_weights.shape[2]
    hidden = widen_weights.shape[1]
    heads = cols // HEAD_DIM
    codes = camera_table.shape[0]
    patch_width = patches.shape[2]
    count = objects * rows
    n_rows = lax.axis_size("rows")
    row_rank = lax.axis_index("rows")
    far, near = lax.axis_index("far"), lax.axis_index("near")

    def objects_of(value):
        return lax.dynamic_slice_in_dim(value, objects * far, objects, 0)

    def piece(value):
        size = value.shape[0] // n_rows
        return lax.dynamic_slice_in_dim(value, row_rank * size, size, 0)

    def join_rows(value):
        return lax.all_gather(value, "rows", axis=0, tiled=True)

    def both_columns(value):
        return [
            lax.dynamic_slice_in_dim(value, (2 * index + near) * cols, cols, value.ndim - 1)
            for index in range(2)
        ]

    def in_order(mine, away, axis=0):
        size = mine.shape[axis]
        shape = list(mine.shape)
        shape[axis] *= 2
        out = lax.dynamic_update_slice_in_dim(jnp.zeros(shape, mine.dtype), mine, far * size, axis)
        return lax.dynamic_update_slice_in_dim(out, away, (1 - far) * size, axis)

    def halves(value):
        value = value.reshape(objects, 2, rows // 2, -1)
        return [
            lax.dynamic_index_in_dim(value, index, 1, keepdims=False).reshape(count // 2, -1)
            for index in (near, 1 - near)
        ]

    def half_sum_near(partial):
        mine, away = halves(partial)
        return mine + swap(away.astype(LOW), "near").astype(WIDE)

    def over_heads(value):
        value = value.reshape(2, 2, objects, rows // 2, -1)
        value = jnp.where(far == 0, value, jnp.flip(value, 1))
        value = jnp.where(near == 0, value, jnp.flip(value, 0))
        return value.transpose(1, 2, 0, 3, 4).reshape(2 * objects, rows, -1)

    def to_pairs(weights, value, slots):
        parts = [
            mul(weights, value[i * rows : (i + 1) * rows], NT)
            .astype(LOW)
            .reshape(n_rows, slots, HEAD_DIM, rows)
            for i in range(objects)
        ]
        return jnp.stack(parts, axis=1)

    def from_pairs(value):
        return value.transpose(0, 2, 3, 1, 4).reshape(-1, count)

    def over_all_columns(value_t, weight):
        return mul(jnp.concatenate([value_t, swap(value_t, "near")]), weight, TN)

    qkv_rows = self_weights.reshape(3, width, heads, HEAD_DIM).transpose(2, 0, 3, 1)
    qkv_rows = qkv_rows.reshape(3 * cols, width)
    pair_rows = cross_pair.reshape(2, width, heads, HEAD_DIM).transpose(2, 0, 3, 1)
    pair_rows = pair_rows.reshape(2 * cols, width)
    query_rows = cross_query.T

    qkv_away = join_rows(swap(piece(qkv_rows), "far"))

    table_flat = camera_table.reshape(codes, -1)
    cross_gain_f = cross_gain.astype(WIDE)
    hidden_gain_f = hidden_gain.astype(WIDE)

    inputs = objects_of(tokens).reshape(count, width).astype(WIDE)
    patch_in = objects_of(patches).reshape(count, patch_width)
    length = objects_of(patch_len)
    grad_low = objects_of(cotangent).reshape(count, width)
    codes_of = objects_of(cam_index).reshape(count)
    onehot = (codes_of[:, None] == jnp.arange(codes)[None, :]).astype(LOW)
    shift_scale = mul(onehot, table_flat)
    gain_one = 1.0 + shift_scale[:, :width]
    unit_one, rate_one = normed(inputs)
    normed_one = (unit_one * gain_one + shift_scale[:, width:]).astype(LOW)

    mine = [piece(v) for v in (self_output, query_rows, cross_output, pair_rows)]
    normed_one, *mine = tie(normed_one, *mine)
    mine = jnp.concatenate(mine, axis=0)
    across = swap(mine, "far")
    size = cols // n_rows
    two = in_order(mine[None, : 3 * size], across[None, : 3 * size])
    four = jnp.concatenate([two, swap(two, "near")])
    sent = jnp.concatenate([four.reshape(-1, width), across[3 * size :]])
    sent = lax.all_gather(sent, "rows", axis=0)
    pair_away = sent[:, 12 * size :].reshape(2 * cols, width)
    whole = sent[:, : 12 * size].reshape(n_rows, 4, 3, size, width).transpose(2, 1, 0, 3, 4)
    self_whole, query_whole, cross_whole = whole.reshape(3, 4 * cols, width)

    qkv_both = in_order(qkv_rows, qkv_away)
    qkv = exchange_rows(to_pairs(qkv_both, normed_one, 3))
    patch_mid = mul(patch_in, patch_weights).astype(LOW)
    pair_both = in_order(pair_rows, pair_away)
    pair = to_pairs(pair_both, patch_mid, 2)

    mine = [piece(widen_weights), piece(narrow_weights)]
    qkv, *mine = tie(qkv, *mine)
    size = width // n_rows
    sent = lax.all_gather(jnp.concatenate(mine, axis=0), ("far", "rows"), axis=0)
    sent = sent.reshape(2, n_rows, 2, size, width)
    widen = sent[:, :, 0].reshape(2, width, hidden)
    widen = jnp.concatenate([widen[0], widen[1]], axis=1)
    narrow = sent[:, :, 1].reshape(2 * hidden, width)

    mixed, self_wide, self_log = pair_forward(qkv, qkv, 1)
    mixed, pair = tie(exchange_rows(mixed), pair)
    pair = exchange_rows(pair)
    self_mixed_t = from_pairs(mixed[:, :, None])
    after_self = inputs + over_all_columns(self_mixed_t, self_whole)
    unit_two, rate_two = normed(after_self)
    normed_two = (unit_two * cross_gain_f).astype(LOW)
    cross_q, pair = tie(to_pairs(query_whole[: 2 * cols], normed_two, 1), pair)
    cross_q = exchange_rows(cross_q)
    mixed, cross_wide, cross_log = pair_forward(cross_q, pair, 0, length)
    cross_mixed_t = from_pairs(exchange_rows(mixed)[:, :, None])
    after_cross = after_self + over_all_columns(cross_mixed_t, cross_whole)
    unit_three, rate_three = normed(after_cross)
    normed_three = (unit_three * hidden_gain_f).astype(LOW)
    activated, act_back = jax.vjp(gelu_tanh, mul(normed_three, widen))
    activated = activated.astype(LOW)
    grad_pre = act_back(mul(grad_low, narrow, NT))[0].astype(LOW)
    third, activated, grad_pre = tie(mul(grad_pre, widen, NT).astype(LOW), activated, grad_pre)
    grad_three = third.astype(WIDE) + swap(third, "near").astype(WIDE)
    hidden_mine, hidden_away = halves(mul(activated, narrow))
    hidden_away, grad_three = tie(hidden_away.astype(LOW), grad_three)
    hidden_half = hidden_mine + swap(hidden_away, "near").astype(WIDE)
    result = (halves(after_cross)[0] + hidden_half).astype(LOW)

    def part_rows(both):
        return lax.psum_scatter(both, "rows", scatter_dimension=1, tiled=True)

    def own_and_away(value):
        return [lax.dynamic_index_in_dim(value, index, 0, keepdims=False) for index in (far, 1 - far)]

    def add_far(mine, away):
        return (mine.astype(WIDE) + away.astype(WIDE)).astype(LOW)

    def by_shard(left, right):
        return mul(left, right, NN).astype(LOW).reshape(2, -1, right.shape[1])

    hidden_terms = jnp.concatenate(
        [
            mul(value, against, TN).astype(LOW).reshape(2, hidden, width)
            for value, against in ((activated, grad_low), (grad_pre, normed_three))
        ],
        axis=1,
    )
    hidden_part = part_rows(hidden_terms)

    hidden_gain_term = jnp.sum(grad_three * unit_three, axis=0)
    grad_cross = grad_low.astype(WIDE) + normed_back(
        grad_three * hidden_gain_f, unit_three, rate_three
    )
    grad_cross_low = grad_cross.astype(LOW)
    grad_mixed = exchange_rows(to_pairs(cross_whole[: 2 * cols], grad_cross_low, 1)[:, :, 0])
    grad_mixed, result = tie(grad_mixed, result)
    result_two = jnp.stack([result, swap(result, "far")])
    grads = pair_backward(cross_q, pair, 0, length, grad_mixed, cross_wide, cross_log)
    grads, result_two, hidden_part = tie(grads, result_two, hidden_part)
    hidden_own, hidden_away = own_and_away(hidden_part)
    grads, hidden_away = tie(exchange_rows(grads), swap(hidden_away, "far"))
    hidden_total = join_rows(add_far(hidden_own, hidden_away))
    grad_cq_t = from_pairs(grads[:, :, :1])
    grad_pair_t = from_pairs(grads[:, :, 1:])
    middle_terms = jnp.concatenate(
        [
            by_shard(cross_mixed_t, grad_cross_low),
            by_shard(grad_cq_t, normed_two),
            by_shard(grad_pair_t, patch_mid),
        ],
        axis=1,
    )
    grad_cq_away, middle_terms = tie(swap(grad_cq_t, "near"), middle_terms)
    middle_part = part_rows(middle_terms)
    grad_two = mul(jnp.concatenate([grad_cq_t, grad_cq_away]), query_whole, TN)
    grad_two, result_two = tie(grad_two, result_two)
    result_four = jnp.stack([result_two, swap(result_two, "near")])
    cross_gain_term = jnp.sum(grad_two * unit_two, axis=0)
    grad_self = grad_cross + normed_back(grad_two * cross_gain_f, unit_two, rate_two)
    grad_self_low = grad_self.astype(LOW)
    grad_mixed, grad_self_low, grad_mid = tie(
        to_pairs(self_whole[: 2 * cols], grad_self_low, 1)[:, :, 0],
        grad_self_low,
        mul(grad_pair_t, pair_both, TN).astype(LOW),
    )
    grad_mid_away = swap(grad_mid, "near")
    output_terms = by_shard(self_mixed_t, grad_self_low)
    grads = pair_backward(qkv, qkv, 1, None, exchange_rows(grad_mixed), self_wide, self_log)
    grads, grad_mid_away, result_four = tie(grads, grad_mid_away, result_four)
    grad_mid = (grad_mid.astype(WIDE) + grad_mid_away.astype(WIDE)).astype(LOW)
    patch_half = mul(halves(grad_mid)[0], patch_weights, NT).astype(LOW)
    patch_two = jnp.stack([patch_half, swap(patch_half, "far")])
    patch_terms = jnp.stack([mul(value, patch_in, TN).astype(LOW) for value in both_columns(grad_mid)])
    patch_terms = jnp.pad(patch_terms, ((0, 0), (0, 0), (0, width - patch_width)))
    last_terms = jnp.pad(
        jnp.concatenate([output_terms, patch_terms], axis=1), ((0, 0), (3 * cols, 0), (0, 0))
    )
    grads, patch_two, last_terms, hidden_total, middle_part = tie(
        exchange_rows(grads), patch_two, last_terms, hidden_total, middle_part
    )
    grad_qkv_t = from_pairs(grads)
    last_terms = lax.dynamic_update_slice_in_dim(last_terms, by_shard(grad_qkv_t, normed_one), 0, 1)
    last_part = part_rows(last_terms)
    middle_own, middle_away = own_and_away(middle_part)
    first_mine, first_away = halves(mul(grad_qkv_t, qkv_both, TN))
    first_away, middle_away = tie(first_away.astype(LOW), middle_away)
    middle_total = join_rows(add_far(middle_own, swap(middle_away, "far")))
    grad_one = first_mine + swap(first_away, "near").astype(WIDE)
    gain_half, unit_half, rate_half, self_half = (
        halves(value)[0] for value in (gain_one, unit_one, rate_one, grad_self)
    )
    input_half = self_half + normed_back(grad_one * gain_half, unit_half, rate_half)
    input_half = input_half.astype(LOW)
    input_two = jnp.stack([input_half, swap(input_half, "far")])
    onehot_half = halves(onehot)[0].astype(WIDE)
    table_term = jnp.concatenate(
        [
            lax.dot_general(onehot_half, value, TN, precision=lax.Precision.HIGHEST)
            for value in (grad_one * unit_half, grad_one)
        ],
        axis=0,
    )
    small = [sum_near(table_term), hidden_gain_term[None], cross_gain_term[None], jnp.zeros((14, width), WIDE)]
    small = jnp.stack(both_columns(jnp.concatenate(small, axis=0).astype(LOW)))
    small = jnp.sum(lax.all_gather(small, "rows", axis=0).astype(WIDE), axis=0).astype(LOW)
    small_own, small_away = own_and_away(small)
    small = small_own.astype(WIDE) + swap(small_away, "far").astype(WIDE)
    last_part, input_two, patch_two, small = tie(last_part, input_two, patch_two, small)
    input_four = jnp.stack([input_two, swap(input_two, "near")])
    patch_four = jnp.stack([patch_two, swap(patch_two, "near")])
    outputs = over_heads(result_four)
    hidden_gradients = [hidden_total[hidden:].T.astype(WIDE), hidden_total[:hidden].astype(WIDE)]
    last_own, last_away = own_and_away(last_part)
    last_sum, input_four, outputs, hidden_gradients = tie(
        add_far(last_own, swap(last_away, "far")), input_four, outputs, hidden_gradients
    )
    last_total = join_rows(last_sum)
    middle_total, patch_four = tie(middle_total, patch_four)
    input_grads, patch_grads = over_heads(input_four), over_heads(patch_four)

    cross_output_total, query_total = middle_total[:cols], middle_total[cols : 2 * cols]
    pair_total = middle_total[2 * cols :].reshape(heads, 2, HEAD_DIM, width)
    self_total = last_total[: 3 * cols].reshape(heads, 3, HEAD_DIM, width)
    self_output_total = last_total[3 * cols : 4 * cols]
    patch_total = last_total[4 * cols :, :patch_width]
    gradients = (
        small[: 2 * codes].reshape(2, codes, cols).transpose(1, 0, 2),
        self_total.transpose(1, 3, 0, 2).reshape(3, width, cols),
        self_output_total,
        small[2 * codes + 1],
        query_total.T,
        pair_total.transpose(1, 3, 0, 2).reshape(2, width, cols),
        cross_output_total,
        patch_total.T,
        small[2 * codes],
        *hidden_gradients,
    )
    return (outputs, input_grads.astype(WIDE), patch_grads.astype(WIDE)) + tuple(
        value.astype(WIDE) for value in gradients
    )


def per_device(
    tokens,
    cam_index,
    patches,
    patch_len,
    camera_table,
    self_weights,
    self_output,
    cross_gain,
    cross_query,
    cross_pair,
    cross_output,
    patch_weights,
    hidden_gain,
    widen_weights,
    narrow_weights,
    cotangent,
):
    batches, rows, width = tokens.shape
    cols = self_weights.shape[2]
    heads = cols // HEAD_DIM
    codes = camera_table.shape[0]
    patch_rows, patch_width = patches.shape[1:]
    n_rows, n_heads = lax.axis_size("rows"), lax.axis_size("heads")
    row_rank, head_rank = lax.axis_index("rows"), lax.axis_index("heads")
    groups = 1
    objects = batches // groups
    full_lengths = jnp.full((objects,), n_rows * rows, jnp.int32)
    count = objects * rows

    def own_columns(value):
        return lax.dynamic_slice_in_dim(value, head_rank * cols, cols, value.ndim - 1)

    table_flat = camera_table.reshape(codes, -1)
    cross_gain_f = cross_gain.astype(WIDE)
    hidden_gain_f = hidden_gain.astype(WIDE)

    qkv_rows = (
        self_weights.reshape(3, width, heads, HEAD_DIM).transpose(2, 0, 3, 1).reshape(3 * cols, width)
    )
    qkv_rows_back = self_weights.transpose(0, 2, 1).reshape(3 * cols, width)
    pair_rows = cross_pair.transpose(0, 2, 1).reshape(2 * cols, width)
    query_rows = cross_query.T

    local = jnp.stack([self_output, cross_output, query_rows])
    piece = cols // n_rows
    local = lax.dynamic_slice_in_dim(local, row_rank * piece, piece, 1)
    whole = lax.all_gather(jnp.stack(gather_heads(local)), "rows", axis=0)
    whole = whole.transpose(2, 1, 0, 3, 4).reshape(3, n_heads * cols, width)
    self_whole, cross_whole, query_whole = whole[0], whole[1], whole[2]

    def over_all_columns(value_t, weight):
        return mul(jnp.concatenate(gather_heads(value_t), axis=0), weight, TN)

    def by_object(weight, value):
        return jnp.stack(
            [mul(weight, value[i * rows : (i + 1) * rows], NT).astype(LOW) for i in range(objects)]
        )

    def column_terms(value, grads_t):
        return [
            mul(value, grads_t[i : i + cols], (((0,), (1,)), ((), ())))
            for i in range(0, grads_t.shape[0], cols)
        ]

    def one_group(group):
        part = slice(group * objects, (group + 1) * objects)
        inputs = tokens[part].reshape(count, width).astype(WIDE)
        patch_in = patches[part].reshape(objects * patch_rows, patch_width)
        lengths = patch_len[part]
        grad_low = cotangent[part].reshape(count, width)
        onehot = (cam_index[part].reshape(count)[:, None] == jnp.arange(codes)[None, :]).astype(LOW)
        shift_scale = mul(onehot, table_flat)
        gain_one = 1.0 + shift_scale[:, :width]
        unit_one, rate_one = normed(inputs)
        normed_one = (unit_one * gain_one + shift_scale[:, width:]).astype(LOW)
        qkv_t = by_object(qkv_rows, normed_one)
        by_kind = qkv_t.reshape(objects, heads, 3, HEAD_DIM, rows).transpose(2, 1, 3, 0, 4)
        by_kind = by_kind.reshape(3, cols, count)
        self_pair = lax.all_gather(by_kind[1:], "rows", axis=0)
        patch_mid = mul(patch_in, patch_weights).astype(LOW)
        own_pair = mul(pair_rows, patch_mid, NT).astype(LOW).reshape(2, cols, -1)
        pair_t = lax.all_gather(own_pair, "rows", axis=0)
        self_mixed_t, self_wide, self_log = cross_forward(by_kind[0], self_pair, full_lengths)
        after_self = inputs + over_all_columns(self_mixed_t, self_whole)
        unit_two, rate_two = normed(after_self)
        normed_two = (unit_two * cross_gain_f).astype(LOW)
        cross_q_t = mul(query_rows, normed_two, NT).astype(LOW)
        cross_mixed_t, cross_wide, cross_log = cross_forward(cross_q_t, pair_t, lengths)
        after_cross = after_self + over_all_columns(cross_mixed_t, cross_whole)
        unit_three, rate_three = normed(after_cross)
        normed_three = (unit_three * hidden_gain_f).astype(LOW)
        pre_act = mul(normed_three, widen_weights)
        activated, act_back = jax.vjp(gelu_tanh, pre_act)
        activated = activated.astype(LOW)
        grad_pre = act_back(mul(grad_low, narrow_weights, NT))[0].astype(LOW)
        grad_three = sum_heads(mul(grad_pre, widen_weights, NT)).astype(WIDE)
        yield "heads", {"hidden": mul(activated, narrow_weights)}
        yield "rows", {
            "narrow": mul(activated, grad_low, TN),
            "widen": mul(normed_three, grad_pre, TN),
        }
        hidden_gain_term = jnp.sum(own_columns(grad_three * unit_three), axis=0)
        grad_cross = grad_low.astype(WIDE) + normed_back(
            grad_three * hidden_gain_f, unit_three, rate_three
        )
        grad_cross_low = grad_cross.astype(LOW)
        cross_output_term = mul(cross_mixed_t, grad_cross_low)
        grad_mixed_t = mul(cross_output, grad_cross_low, NT).astype(LOW)
        grad_cq_t, grad_pair_t = cross_backward(
            cross_q_t, pair_t, lengths, grad_mixed_t, cross_wide, cross_log
        )
        grad_two = over_all_columns(grad_cq_t, query_whole)
        grad_pair_t = lax.psum_scatter(grad_pair_t, "rows", scatter_dimension=0, tiled=False)
        grad_pair_t = grad_pair_t.reshape(2 * cols, -1)
        query_term = mul(normed_two, grad_cq_t, (((0,), (1,)), ((), ())))
        cross_gain_term = jnp.sum(own_columns(grad_two * unit_two), axis=0)
        grad_self = grad_cross + normed_back(grad_two * cross_gain_f, unit_two, rate_two)
        grad_self_low = grad_self.astype(LOW)
        self_output_term = mul(self_mixed_t, grad_self_low)
        yield "heads", {"patch": mul(grad_pair_t, pair_rows, TN)}
        yield "rows", {
            "query": query_term,
            "pair": column_terms(patch_mid, grad_pair_t),
            "cross_output": cross_output_term,
            "self_output": self_output_term,
        }
        grad_self_mixed_t = mul(self_output, grad_self_low, NT).astype(LOW)
        grad_q_t, grad_kv_t = cross_backward(
            by_kind[0], self_pair, full_lengths, grad_self_mixed_t, self_wide, self_log
        )
        grad_kv_t = lax.psum_scatter(grad_kv_t, "rows", scatter_dimension=0, tiled=False)
        grad_qkv_t = jnp.concatenate([grad_q_t[None], grad_kv_t]).reshape(3 * cols, count)
        grad_qkv_t = yield "after", (grad_qkv_t, ["patch", "narrow", "widen"])
        grad_mid = yield "take", "patch"
        patch_term = mul(patch_in, own_columns(grad_mid), TN)
        patch_grad = mul(grad_mid, patch_weights, NT)
        grad_one = sum_heads(mul(grad_qkv_t, qkv_rows_back, TN))
        grad_one = yield "after", (grad_one, ["query", "pair", "cross_output", "self_output"])
        grad_one = grad_one.astype(WIDE)
        input_grad = grad_self + normed_back(grad_one * gain_one, unit_one, rate_one)
        own_grad = own_columns(grad_one)
        table_term = jnp.stack(
            [
                lax.dot_general(onehot.astype(WIDE), v, TN, precision=lax.Precision.HIGHEST)
                for v in (own_grad * own_columns(unit_one), own_grad)
            ],
            axis=1,
        )
        small = [patch_term, table_term.reshape(2 * codes, cols)]
        small += [hidden_gain_term[None], cross_gain_term[None], jnp.zeros((14, cols), WIDE)]
        yield "rows", {
            "self": column_terms(normed_one, grad_qkv_t),
            "small": jnp.concatenate(small, axis=0),
        }
        hidden_sum = yield "take", "hidden"
        result = (after_cross + hidden_sum.astype(WIDE)).astype(LOW)
        yield (
            "done",
            (
                result.reshape(objects, rows, width),
                input_grad.reshape(objects, rows, width),
                patch_grad.reshape(objects, patch_rows, patch_width),
            ),
        )

    steps = [one_group(group) for group in range(groups)]
    asked = [next(step) for step in steps]
    totals, ahead = {}, []
    while asked[0][0] != "done":
        kind, what = asked[0]
        answers = [None] * groups
        if kind == "take":
            answers = jnp.split(totals[what], groups)
        elif kind == "after":
            early = {name: totals[name] for name in what[1]}
            answers = [value for _, (value, _) in asked]
            answers[-1], early = lax.optimization_barrier((answers[-1], early))
            totals.update(early)
        else:
            terms = [value for _, value in asked]
            if kind == "heads":
                terms = jax.tree.map(lambda *parts: jnp.concatenate(parts, axis=0), *terms)
            else:
                for value in terms[1:]:
                    terms[0] = add_trees(terms[0], value)
                terms = terms[0]
            if kind == "rows":
                terms = jax.tree.map(lambda value: value.astype(LOW), terms)
            if kind == "heads":
                totals.update({name: sum_heads(value) for name, value in terms.items()})
            else:
                before = {name: totals[name] for name in ahead}
                terms, before = lax.optimization_barrier((terms, before))
                totals.update(before)
                totals.update(lax.psum(terms, kind))
                ahead = list(terms)
        asked = [step.send(value) for step, value in zip(steps, answers)]
    outputs, input_grads, patch_grads = (
        jnp.concatenate([value[i] for _, value in asked], axis=0) for i in range(3)
    )
    patch_total, table_total, gains = jnp.split(
        totals["small"], [patch_width, patch_width + 2 * codes]
    )
    gradients = (
        table_total.reshape(codes, 2, cols),
        jnp.stack(totals["self"]),
        totals["self_output"],
        gains[1],
        totals["query"],
        jnp.stack(totals["pair"]),
        totals["cross_output"],
        patch_total,
        gains[0],
        totals["widen"],
        totals["narrow"],
    )
    return (outputs, input_grads, patch_grads) + tuple(value.astype(WIDE) for value in gradients)


def solution(mesh):
    sizes = mesh.shape
    paired = sizes["heads"] == 4 and sizes["rows"] == 8
    heads = ("far", "near") if paired else "heads"
    if paired:
        names = (*heads, "rows")
        mesh = jax.sharding.Mesh(mesh.devices.reshape(2, 2, sizes["rows"]), names)
    in_specs = (
        P(None, "rows", None),
        P(None, "rows"),
        P(None, "rows", None),
        P(),
        P(),
        P(None, None, heads),
        P(heads, None),
        P(),
        P(None, heads),
        P(None, None, heads),
        P(heads, None),
        P(),
        P(),
        P(None, heads),
        P(heads, None),
        P(None, "rows", None),
    )
    out_specs = (
        P(None, "rows", None),
        P(None, "rows", None),
        P(None, "rows", None),
        P(None, None, heads),
        P(None, None, heads),
        P(heads, None),
        P(heads),
        P(None, heads),
        P(None, None, heads),
        P(heads, None),
        P(None, heads),
        P(heads),
        P(None, heads),
        P(heads, None),
    )
    return jax.shard_map(
        paired_device if paired else per_device,
        mesh=mesh,
        in_specs=in_specs,
        out_specs=out_specs,
        check_vma=False,
    )
```

```python
import jax
import jax.numpy as jnp
from jax import lax
from jax.experimental import pallas as pl
from jax.experimental.pallas import tpu as pltpu
from jax.sharding import PartitionSpec as P

HEAD_DIM = 64
EPSILON = 1e-05
SCALE = HEAD_DIM ** (-0.5)
LOW = jnp.bfloat16
WIDE = jnp.float32

NN = (((1,), (0,)), ((), ()))
NT = (((1,), (1,)), ((), ()))
TN = (((0,), (0,)), ((), ()))
T_LAST = (((0,), (1,)), ((), ()))


def mul(left, right, dims=NN):
    return lax.dot_general(left, right, dims, preferred_element_type=WIDE)


def load_values(values, block, values_t):
    rows = values_t.shape[1]
    at = slice(block * rows, (block + 1) * rows)
    values[at, :HEAD_DIM] = values_t.T
    values[at, HEAD_DIM:] = jnp.ones((rows, HEAD_DIM), values.dtype)


def attend_block(queries, keys_t, values):
    scores = mul(queries, keys_t)
    peak = jnp.max(scores, axis=1, keepdims=True)
    both = mul(jnp.exp(scores - peak).astype(LOW), values).T
    total = both[HEAD_DIM : HEAD_DIM + 1]
    return both[:HEAD_DIM] / total, peak.T + jnp.log(total)


def attend_block_back(scaled_q, grad_t, keys, keys_t, values, log_total, spread):
    probs = jnp.exp(mul(keys, scaled_q) - log_total)
    grad_scores = (probs * (mul(values, grad_t) - spread)).astype(LOW)
    return (
        (mul(keys_t, grad_scores) * SCALE).astype(LOW),
        mul(grad_scores, scaled_q.T),
        mul(probs.astype(LOW), grad_t.T),
    )


def estimate(rows, cols, passes):
    return pl.CostEstimate(
        flops=int(rows * cols * 1200 * passes), transcendentals=int(rows * cols), bytes_accessed=int(rows * 2048)
    )


VMEM_LIMIT = 48 << 20


def by_length(length, full, blocks, run):
    @pl.when(length * 4 > full)
    def _():
        run(blocks)

    @pl.when(length * 4 <= full)
    def _():
        run(blocks // 4)


def cross_forward(queries_t, pair_t, lengths):
    blocks, _, cols, all_patches = pair_t.shape
    objects = lengths.shape[0]
    heads = cols // HEAD_DIM
    rows, patch_rows = queries_t.shape[1] // objects, all_patches // objects

    def kernel(len_ref, q_ref, pair_ref, mixed_ref, wide_ref, log_ref, keys_t, values):
        queries = (q_ref[...] * LOW(SCALE)).T

        def run(live):
            for c in range(live):
                keys_t[:, c * patch_rows : (c + 1) * patch_rows] = pair_ref[c, 0]
                load_values(values, c, pair_ref[c, 1])
            size = live * patch_rows
            mixed, log_total = attend_block(queries, keys_t[:, :size], values[:size])
            mixed_ref[...] = mixed.astype(LOW)
            wide_ref[...] = mixed
            log_ref[...] = log_total

        by_length(len_ref[pl.program_id(0)], blocks * patch_rows, blocks, run)

    block = pl.BlockSpec((HEAD_DIM, rows), lambda b, j, lens: (j, b))
    return pl.pallas_call(
        kernel,
        grid_spec=pltpu.PrefetchScalarGridSpec(
            num_scalar_prefetch=1,
            grid=(objects, heads),
            in_specs=[
                block,
                pl.BlockSpec((blocks, 2, HEAD_DIM, patch_rows), lambda b, j, lens: (0, 0, j, b)),
            ],
            out_specs=[block, block, pl.BlockSpec((None, 1, rows), lambda b, j, lens: (j, 0, b))],
            scratch_shapes=[
                pltpu.VMEM((HEAD_DIM, blocks * patch_rows), LOW),
                pltpu.VMEM((blocks * patch_rows, 2 * HEAD_DIM), LOW),
            ],
        ),
        out_shape=[
            jax.ShapeDtypeStruct(queries_t.shape, LOW),
            jax.ShapeDtypeStruct(queries_t.shape, WIDE),
            jax.ShapeDtypeStruct((heads, 1, queries_t.shape[1]), WIDE),
        ],
        name="cross_forward",
        cost_estimate=estimate(objects * rows, blocks * patch_rows * heads, 1.4),
        compiler_params=pltpu.CompilerParams(vmem_limit_bytes=VMEM_LIMIT),
    )(lengths, queries_t, pair_t)


def cross_backward(queries_t, pair_t, lengths, grad_t_all, wide, log_total):
    blocks, _, cols, all_patches = pair_t.shape
    objects = lengths.shape[0]
    heads = cols // HEAD_DIM
    rows, patch_rows = queries_t.shape[1] // objects, all_patches // objects

    def kernel(len_ref, q_ref, pair_ref, g_ref, wide_ref, log_ref, out_q, out_pair, keys, keys_t, values):
        grad_t = g_ref[...]
        spread = jnp.sum(grad_t.astype(WIDE) * wide_ref[...], axis=0, keepdims=True)

        def run(live):
            for c in range(live):
                at = slice(c * patch_rows, (c + 1) * patch_rows)
                keys[at] = pair_ref[c, 0].T
                keys_t[:, at] = pair_ref[c, 0]
                values[at] = pair_ref[c, 1].T
            size = live * patch_rows
            out_q[...], grad_k, grad_v = attend_block_back(
                q_ref[...] * LOW(SCALE),
                grad_t,
                keys[:size],
                keys_t[:, :size],
                values[:size],
                log_ref[...],
                spread,
            )
            for c in range(live):
                at = slice(c * patch_rows, (c + 1) * patch_rows)
                out_pair[c, 0] = grad_k[at].T.astype(LOW)
                out_pair[c, 1] = grad_v[at].T.astype(LOW)
            for c in range(live, blocks):
                out_pair[c] = jnp.zeros_like(out_pair[c])

        by_length(len_ref[pl.program_id(0)], blocks * patch_rows, blocks, run)

    block = pl.BlockSpec((HEAD_DIM, rows), lambda b, j, lens: (j, b))
    pair_block = pl.BlockSpec((blocks, 2, HEAD_DIM, patch_rows), lambda b, j, lens: (0, 0, j, b))
    return pl.pallas_call(
        kernel,
        grid_spec=pltpu.PrefetchScalarGridSpec(
            num_scalar_prefetch=1,
            grid=(objects, heads),
            in_specs=[
                block,
                pair_block,
                block,
                block,
                pl.BlockSpec((None, 1, rows), lambda b, j, lens: (j, 0, b)),
            ],
            out_specs=[block, pair_block],
            scratch_shapes=[
                pltpu.VMEM((blocks * patch_rows, HEAD_DIM), LOW),
                pltpu.VMEM((HEAD_DIM, blocks * patch_rows), LOW),
                pltpu.VMEM((blocks * patch_rows, HEAD_DIM), LOW),
            ],
        ),
        out_shape=[
            jax.ShapeDtypeStruct(queries_t.shape, LOW),
            jax.ShapeDtypeStruct(pair_t.shape, LOW),
        ],
        name="cross_backward",
        cost_estimate=estimate(objects * rows, blocks * patch_rows * heads, 2.5),
        compiler_params=pltpu.CompilerParams(vmem_limit_bytes=VMEM_LIMIT),
    )(lengths, queries_t, pair_t, grad_t_all, wide, log_total)


def shift(value, step):
    size = lax.axis_size("heads")
    return lax.ppermute(value, "heads", [((i + step) % size, i) for i in range(size)])


def gather_heads(value):
    size = lax.axis_size("heads")
    if size != 4:
        return [value] + [shift(value, step) for step in range(1, size)]
    after, before = shift(value, 1), shift(value, -1)
    inner = lax.ppermute(after, "heads", [(1, 0), (2, 1)]) + lax.ppermute(before, "heads", [(1, 2), (2, 3)])
    return [value, after, inner, before]


def scatter_heads(partial):
    size, me = lax.axis_size("heads"), lax.axis_index("heads")

    def part(step):
        return lax.dynamic_index_in_dim(partial, (me + step) % size, 0, keepdims=False)

    if size != 4:
        total = part(0)
        for step in range(1, size):
            total = total + shift(part(step).astype(LOW), -step).astype(WIDE)
        return total
    far = part(2).astype(LOW)
    up = lax.ppermute(far, "heads", [(0, 1), (1, 2)]).astype(WIDE)
    down = lax.ppermute(far, "heads", [(2, 1), (3, 2)]).astype(WIDE)
    from_below = shift((part(1) + up).astype(LOW), -1)
    from_above = shift((part(3) + down).astype(LOW), 1)
    return part(0) + from_below.astype(WIDE) + from_above.astype(WIDE)


def in_order(parts):
    size, me = lax.axis_size("heads"), lax.axis_index("heads")
    out = jnp.zeros((size,) + parts[0].shape, parts[0].dtype)
    for step, value in enumerate(parts):
        out = lax.dynamic_update_index_in_dim(out, value, (me + step) % size, 0)
    return out.reshape((-1,) + parts[0].shape[1:])


def sum_heads(partial):
    size = lax.axis_size("heads")
    split = partial.reshape((size, -1) + partial.shape[1:])
    return in_order(gather_heads(scatter_heads(split).astype(LOW)))


def exchange_rows(value):
    return lax.all_to_all(value, "rows", 0, 0, tiled=True)


def normed(value):
    centred = value - jnp.mean(value, axis=-1, keepdims=True)
    rate = lax.rsqrt(jnp.mean(centred * centred, axis=-1, keepdims=True) + EPSILON)
    return centred * rate, rate


def normed_back(grad, unit, rate):
    return rate * (
        grad
        - jnp.mean(grad, axis=-1, keepdims=True)
        - unit * jnp.mean(grad * unit, axis=-1, keepdims=True)
    )


def gelu_tanh(pre_act):
    return jax.nn.gelu(pre_act, approximate=True)


def add_trees(former, latter):
    return jax.tree.map(jnp.add, former, latter)


def pair_forward(queries, pair, key_at, length=None):
    blocks, objects, _, width, rows = queries.shape
    pair_rows = pair.shape[4]
    lengths = jnp.full((objects,), blocks * pair_rows, jnp.int32) if length is None else length

    def kernel(len_ref, q_ref, k_ref, v_ref, mixed_ref, wide_ref, log_ref, keys_t, values):
        def run(live):
            @pl.when(pl.program_id(1) == 0)
            def _():
                for c in range(live):
                    keys_t[:, c * pair_rows : (c + 1) * pair_rows] = k_ref[c]
                    load_values(values, c, v_ref[c])

            size = live * pair_rows
            mixed, log_total = attend_block(
                (q_ref[...] * LOW(SCALE)).T, keys_t[:, :size], values[:size]
            )
            mixed_ref[...] = mixed.astype(LOW)
            wide_ref[...] = mixed
            log_ref[...] = log_total

        if length is None:
            run(blocks)
        else:
            by_length(len_ref[pl.program_id(0)], blocks * pair_rows, blocks, run)

    block = pl.BlockSpec((None, None, width, rows), lambda o, i, lens: (i, o, 0, 0))
    return pl.pallas_call(
        kernel,
        grid_spec=pltpu.PrefetchScalarGridSpec(
            num_scalar_prefetch=1,
            grid=(objects, blocks),
            in_specs=[
                pl.BlockSpec((None, None, None, width, rows), lambda o, i, lens: (i, o, 0, 0, 0)),
                pl.BlockSpec((blocks, None, None, width, pair_rows), lambda o, i, lens: (0, o, key_at, 0, 0)),
                pl.BlockSpec((blocks, None, None, width, pair_rows), lambda o, i, lens: (0, o, key_at + 1, 0, 0)),
            ],
            out_specs=[block, block, pl.BlockSpec((None, None, 1, rows), lambda o, i, lens: (i, o, 0, 0))],
            scratch_shapes=[
                pltpu.VMEM((width, blocks * pair_rows), LOW),
                pltpu.VMEM((blocks * pair_rows, 2 * width), LOW),
            ],
        ),
        out_shape=[
            jax.ShapeDtypeStruct((blocks, objects, width, rows), LOW),
            jax.ShapeDtypeStruct((blocks, objects, width, rows), WIDE),
            jax.ShapeDtypeStruct((blocks, objects, 1, rows), WIDE),
        ],
        name="pair_forward",
        cost_estimate=estimate(objects * blocks * rows, blocks * pair_rows, 2 if length is None else 1.4),
        compiler_params=pltpu.CompilerParams(vmem_limit_bytes=VMEM_LIMIT),
    )(lengths, queries, pair, pair)


def pair_backward(queries, pair, key_at, length, grad_mixed, wide, log_total):
    blocks, objects, _, width, rows = queries.shape
    lengths = jnp.full((objects,), blocks * rows, jnp.int32) if length is None else length

    def kernel(len_ref, q_ref, k_ref, v_ref, g_ref, wide_ref, log_ref, out_ref, keys, keys_t, values, grad_k, grad_v):
        i = pl.program_id(1)

        def run(live):
            size = live * rows

            @pl.when(i == 0)
            def _():
                for c in range(live):
                    at = slice(c * rows, (c + 1) * rows)
                    keys[at] = k_ref[c].T
                    keys_t[:, at] = k_ref[c]
                    values[at] = v_ref[c].T

            grad_t = g_ref[...]
            spread = jnp.sum(grad_t.astype(WIDE) * wide_ref[...], axis=0, keepdims=True)
            out_ref[i, 0], term_k, term_v = attend_block_back(
                q_ref[...] * LOW(SCALE),
                grad_t,
                keys[:size],
                keys_t[:, :size],
                values[:size],
                log_ref[...],
                spread,
            )

            @pl.when(i == 0)
            def _():
                grad_k[:size] = term_k
                grad_v[:size] = term_v

            @pl.when(i > 0)
            def _():
                grad_k[:size] += term_k
                grad_v[:size] += term_v

            @pl.when(i == blocks - 1)
            def _():
                for c in range(live):
                    at = slice(c * rows, (c + 1) * rows)
                    out_ref[c, 1] = grad_k[at].T.astype(LOW)
                    out_ref[c, 2] = grad_v[at].T.astype(LOW)
                for c in range(live, blocks):
                    out_ref[c, 1:] = jnp.zeros_like(out_ref[c, 1:])

        if length is None:
            run(blocks)
        else:
            by_length(len_ref[pl.program_id(0)], blocks * rows, blocks, run)

    block = pl.BlockSpec((None, None, width, rows), lambda o, i, lens: (i, o, 0, 0))
    return pl.pallas_call(
        kernel,
        grid_spec=pltpu.PrefetchScalarGridSpec(
            num_scalar_prefetch=1,
            grid=(objects, blocks),
            in_specs=[
                pl.BlockSpec((None, None, None, width, rows), lambda o, i, lens: (i, o, 0, 0, 0)),
                pl.BlockSpec((blocks, None, None, width, rows), lambda o, i, lens: (0, o, key_at, 0, 0)),
                pl.BlockSpec((blocks, None, None, width, rows), lambda o, i, lens: (0, o, key_at + 1, 0, 0)),
                block,
                block,
                pl.BlockSpec((None, None, 1, rows), lambda o, i, lens: (i, o, 0, 0)),
            ],
            out_specs=pl.BlockSpec((blocks, None, 3, width, rows), lambda o, i, lens: (0, o, 0, 0, 0)),
            scratch_shapes=[
                pltpu.VMEM((blocks * rows, width), LOW),
                pltpu.VMEM((width, blocks * rows), LOW),
                pltpu.VMEM((blocks * rows, width), LOW),
                pltpu.VMEM((blocks * rows, width), WIDE),
                pltpu.VMEM((blocks * rows, width), WIDE),
            ],
        ),
        out_shape=jax.ShapeDtypeStruct((blocks, objects, 3, width, rows), LOW),
        name="pair_backward",
        cost_estimate=estimate(objects * blocks * rows, blocks * rows, 3 if length is None else 2),
        compiler_params=pltpu.CompilerParams(vmem_limit_bytes=VMEM_LIMIT),
    )(lengths, queries, pair, pair, grad_mixed, wide, log_total)


def swap(value, axis):
    return lax.ppermute(value, axis, [(0, 1), (1, 0)])


def sum_near(partial):
    low = partial.astype(LOW)
    return low.astype(WIDE) + swap(low, "near").astype(WIDE)


def tie(value, *others):
    return lax.optimization_barrier((value, *others))


def paired_device(
    tokens,
    cam_index,
    patches,
    patch_len,
    camera_table,
    self_weights,
    self_output,
    cross_gain,
    cross_query,
    cross_pair,
    cross_output,
    patch_weights,
    hidden_gain,
    widen_weights,
    narrow_weights,
    cotangent,
):
    objects = tokens.shape[0] // 2
    _, rows, width = tokens.shape
    cols = self_weights.shape[2]
    hidden = widen_weights.shape[1]
    heads = cols // HEAD_DIM
    codes = camera_table.shape[0]
    patch_width = patches.shape[2]
    count = objects * rows
    n_rows = lax.axis_size("rows")
    row_rank = lax.axis_index("rows")
    far, near = lax.axis_index("far"), lax.axis_index("near")

    def objects_of(value):
        return lax.dynamic_slice_in_dim(value, objects * far, objects, 0)

    def piece(value):
        size = value.shape[0] // n_rows
        return lax.dynamic_slice_in_dim(value, row_rank * size, size, 0)

    def join_rows(value):
        return lax.all_gather(value, "rows", axis=0, tiled=True)

    def both_columns(value):
        return [
            lax.dynamic_slice_in_dim(value, (2 * index + near) * cols, cols, value.ndim - 1)
            for index in range(2)
        ]

    def in_order(mine, away, axis=0):
        size = mine.shape[axis]
        shape = list(mine.shape)
        shape[axis] *= 2
        out = lax.dynamic_update_slice_in_dim(jnp.zeros(shape, mine.dtype), mine, far * size, axis)
        return lax.dynamic_update_slice_in_dim(out, away, (1 - far) * size, axis)

    def halves(value):
        value = value.reshape(objects, 2, rows // 2, -1)
        return [
            lax.dynamic_index_in_dim(value, index, 1, keepdims=False).reshape(count // 2, -1)
            for index in (near, 1 - near)
        ]

    def half_sum_near(partial):
        mine, away = halves(partial)
        return mine + swap(away.astype(LOW), "near").astype(WIDE)

    def over_heads(value):
        value = value.reshape(2, 2, objects, rows // 2, -1)
        value = jnp.where(far == 0, value, jnp.flip(value, 1))
        value = jnp.where(near == 0, value, jnp.flip(value, 0))
        return value.transpose(1, 2, 0, 3, 4).reshape(2 * objects, rows, -1)

    def to_pairs(weights, value, slots):
        parts = [
            mul(weights, value[i * rows : (i + 1) * rows], NT)
            .astype(LOW)
            .reshape(n_rows, slots, HEAD_DIM, rows)
            for i in range(objects)
        ]
        return jnp.stack(parts, axis=1)

    def from_pairs(value):
        return value.transpose(0, 2, 3, 1, 4).reshape(-1, count)

    def over_all_columns(value_t, weight):
        return mul(jnp.concatenate([value_t, swap(value_t, "near")]), weight, TN)

    qkv_rows = self_weights.reshape(3, width, heads, HEAD_DIM).transpose(2, 0, 3, 1)
    qkv_rows = qkv_rows.reshape(3 * cols, width)
    pair_rows = cross_pair.reshape(2, width, heads, HEAD_DIM).transpose(2, 0, 3, 1)
    pair_rows = pair_rows.reshape(2 * cols, width)
    query_rows = cross_query.T

    qkv_away = join_rows(swap(piece(qkv_rows), "far"))

    table_flat = camera_table.reshape(codes, -1)
    cross_gain_f = cross_gain.astype(WIDE)
    hidden_gain_f = hidden_gain.astype(WIDE)

    inputs = objects_of(tokens).reshape(count, width).astype(WIDE)
    patch_in = objects_of(patches).reshape(count, patch_width)
    length = objects_of(patch_len)
    grad_low = objects_of(cotangent).reshape(count, width)
    codes_of = objects_of(cam_index).reshape(count)
    onehot = (codes_of[:, None] == jnp.arange(codes)[None, :]).astype(LOW)
    shift_scale = mul(onehot, table_flat)
    gain_one = 1.0 + shift_scale[:, :width]
    unit_one, rate_one = normed(inputs)
    normed_one = (unit_one * gain_one + shift_scale[:, width:]).astype(LOW)

    mine = [piece(v) for v in (self_output, query_rows, cross_output, pair_rows)]
    normed_one, *mine = tie(normed_one, *mine)
    mine = jnp.concatenate(mine, axis=0)
    across = swap(mine, "far")
    size = cols // n_rows
    two = in_order(mine[None, : 3 * size], across[None, : 3 * size])
    four = jnp.concatenate([two, swap(two, "near")])
    sent = jnp.concatenate([four.reshape(-1, width), across[3 * size :]])
    sent = lax.all_gather(sent, "rows", axis=0)
    pair_away = sent[:, 12 * size :].reshape(2 * cols, width)
    whole = sent[:, : 12 * size].reshape(n_rows, 4, 3, size, width).transpose(2, 1, 0, 3, 4)
    self_whole, query_whole, cross_whole = whole.reshape(3, 4 * cols, width)

    qkv_both = in_order(qkv_rows, qkv_away)
    qkv = exchange_rows(to_pairs(qkv_both, normed_one, 3))
    patch_mid = mul(patch_in, patch_weights).astype(LOW)
    pair_both = in_order(pair_rows, pair_away)
    pair = to_pairs(pair_both, patch_mid, 2)

    mine = [piece(widen_weights), piece(narrow_weights)]
    qkv, *mine = tie(qkv, *mine)
    size = width // n_rows
    sent = lax.all_gather(jnp.concatenate(mine, axis=0), ("far", "rows"), axis=0)
    sent = sent.reshape(2, n_rows, 2, size, width)
    widen = sent[:, :, 0].reshape(2, width, hidden)
    widen = jnp.concatenate([widen[0], widen[1]], axis=1)
    narrow = sent[:, :, 1].reshape(2 * hidden, width)

    mixed, self_wide, self_log = pair_forward(qkv, qkv, 1)
    mixed, pair = tie(exchange_rows(mixed), pair)
    pair = exchange_rows(pair)
    self_mixed_t = from_pairs(mixed[:, :, None])
    after_self = inputs + over_all_columns(self_mixed_t, self_whole)
    unit_two, rate_two = normed(after_self)
    normed_two = (unit_two * cross_gain_f).astype(LOW)
    cross_q, pair = tie(to_pairs(query_whole[: 2 * cols], normed_two, 1), pair)
    cross_q = exchange_rows(cross_q)
    mixed, cross_wide, cross_log = pair_forward(cross_q, pair, 0, length)
    cross_mixed_t = from_pairs(exchange_rows(mixed)[:, :, None])
    after_cross = after_self + over_all_columns(cross_mixed_t, cross_whole)
    unit_three, rate_three = normed(after_cross)
    normed_three = (unit_three * hidden_gain_f).astype(LOW)
    activated, act_back = jax.vjp(gelu_tanh, mul(normed_three, widen))
    activated = activated.astype(LOW)
    grad_pre = act_back(mul(grad_low, narrow, NT))[0].astype(LOW)
    third, activated, grad_pre = tie(mul(grad_pre, widen, NT).astype(LOW), activated, grad_pre)
    grad_three = third.astype(WIDE) + swap(third, "near").astype(WIDE)
    hidden_mine, hidden_away = halves(mul(activated, narrow))
    hidden_away, grad_three = tie(hidden_away.astype(LOW), grad_three)
    hidden_half = hidden_mine + swap(hidden_away, "near").astype(WIDE)
    result = (halves(after_cross)[0] + hidden_half).astype(LOW)

    def part_rows(both):
        return lax.psum_scatter(both, "rows", scatter_dimension=1, tiled=True)

    def own_and_away(value):
        return [lax.dynamic_index_in_dim(value, index, 0, keepdims=False) for index in (far, 1 - far)]

    def add_far(mine, away):
        return (mine.astype(WIDE) + away.astype(WIDE)).astype(LOW)

    def by_shard(left, right):
        return mul(left, right, NN).astype(LOW).reshape(2, -1, right.shape[1])

    hidden_terms = jnp.concatenate(
        [
            mul(value, against, TN).astype(LOW).reshape(2, hidden, width)
            for value, against in ((activated, grad_low), (grad_pre, normed_three))
        ],
        axis=1,
    )
    hidden_part = part_rows(hidden_terms)

    hidden_gain_term = jnp.sum(grad_three * unit_three, axis=0)
    grad_cross = grad_low.astype(WIDE) + normed_back(
        grad_three * hidden_gain_f, unit_three, rate_three
    )
    grad_cross_low = grad_cross.astype(LOW)
    grad_mixed = exchange_rows(to_pairs(cross_whole[: 2 * cols], grad_cross_low, 1)[:, :, 0])
    grad_mixed, result = tie(grad_mixed, result)
    result_two = jnp.stack([result, swap(result, "far")])
    grads = pair_backward(cross_q, pair, 0, length, grad_mixed, cross_wide, cross_log)
    grads, result_two, hidden_part = tie(grads, result_two, hidden_part)
    hidden_own, hidden_away = own_and_away(hidden_part)
    grads, hidden_away = tie(exchange_rows(grads), swap(hidden_away, "far"))
    hidden_total = join_rows(add_far(hidden_own, hidden_away))
    grad_cq_t = from_pairs(grads[:, :, :1])
    grad_pair_t = from_pairs(grads[:, :, 1:])
    middle_terms = jnp.concatenate(
        [
            by_shard(cross_mixed_t, grad_cross_low),
            by_shard(grad_cq_t, normed_two),
            by_shard(grad_pair_t, patch_mid),
        ],
        axis=1,
    )
    grad_cq_away, middle_terms = tie(swap(grad_cq_t, "near"), middle_terms)
    middle_part = part_rows(middle_terms)
    grad_two = mul(jnp.concatenate([grad_cq_t, grad_cq_away]), query_whole, TN)
    grad_two, result_two = tie(grad_two, result_two)
    result_four = jnp.stack([result_two, swap(result_two, "near")])
    cross_gain_term = jnp.sum(grad_two * unit_two, axis=0)
    grad_self = grad_cross + normed_back(grad_two * cross_gain_f, unit_two, rate_two)
    grad_self_low = grad_self.astype(LOW)
    grad_mixed, grad_self_low, grad_mid = tie(
        to_pairs(self_whole[: 2 * cols], grad_self_low, 1)[:, :, 0],
        grad_self_low,
        mul(grad_pair_t, pair_both, TN).astype(LOW),
    )
    grad_mid_away = swap(grad_mid, "near")
    output_terms = by_shard(self_mixed_t, grad_self_low)
    grads = pair_backward(qkv, qkv, 1, None, exchange_rows(grad_mixed), self_wide, self_log)
    grads, grad_mid_away, result_four, hidden_total = tie(grads, grad_mid_away, result_four, hidden_total)
    grad_mid = (grad_mid.astype(WIDE) + grad_mid_away.astype(WIDE)).astype(LOW)
    patch_half = mul(halves(grad_mid)[0], patch_weights, NT).astype(LOW)
    patch_two = jnp.stack([patch_half, swap(patch_half, "far")])
    patch_terms = jnp.stack([mul(value, patch_in, TN).astype(LOW) for value in both_columns(grad_mid)])
    patch_terms = jnp.pad(patch_terms, ((0, 0), (0, 0), (0, width - patch_width)))
    last_terms = jnp.pad(
        jnp.concatenate([output_terms, patch_terms], axis=1), ((0, 0), (3 * cols, 0), (0, 0))
    )
    grads, patch_two, last_terms, middle_part = tie(exchange_rows(grads), patch_two, last_terms, middle_part)
    grad_qkv_t = from_pairs(grads)
    last_terms = lax.dynamic_update_slice_in_dim(last_terms, by_shard(grad_qkv_t, normed_one), 0, 1)
    last_part = part_rows(last_terms)
    middle_own, middle_away = own_and_away(middle_part)
    first_mine, first_away = halves(mul(grad_qkv_t, qkv_both, TN))
    first_away, middle_away = tie(first_away.astype(LOW), middle_away)
    middle_total = join_rows(add_far(middle_own, swap(middle_away, "far")))
    grad_one = first_mine + swap(first_away, "near").astype(WIDE)
    gain_half, unit_half, rate_half, self_half = (
        halves(value)[0] for value in (gain_one, unit_one, rate_one, grad_self)
    )
    input_half = self_half + normed_back(grad_one * gain_half, unit_half, rate_half)
    input_half = input_half.astype(LOW)
    input_two = jnp.stack([input_half, swap(input_half, "far")])
    onehot_half = halves(onehot)[0].astype(WIDE)
    table_term = jnp.concatenate(
        [
            lax.dot_general(onehot_half, value, TN, precision=lax.Precision.HIGHEST)
            for value in (grad_one * unit_half, grad_one)
        ],
        axis=0,
    )
    small = [sum_near(table_term), hidden_gain_term[None], cross_gain_term[None], jnp.zeros((14, width), WIDE)]
    small = jnp.stack(both_columns(jnp.concatenate(small, axis=0).astype(LOW)))
    small = jnp.sum(lax.all_gather(small, "rows", axis=0).astype(WIDE), axis=0).astype(LOW)
    small_own, small_away = own_and_away(small)
    small = small_own.astype(WIDE) + swap(small_away, "far").astype(WIDE)
    last_part, input_two, patch_two, small = tie(last_part, input_two, patch_two, small)
    input_four = jnp.stack([input_two, swap(input_two, "near")])
    patch_four = jnp.stack([patch_two, swap(patch_two, "near")])
    outputs = over_heads(result_four)
    hidden_gradients = [hidden_total[hidden:].T.astype(WIDE), hidden_total[:hidden].astype(WIDE)]
    last_own, last_away = own_and_away(last_part)
    last_sum, input_four, outputs, hidden_gradients = tie(
        add_far(last_own, swap(last_away, "far")), input_four, outputs, hidden_gradients
    )
    last_total = join_rows(last_sum)
    input_four, patch_four = tie(input_four, patch_four)
    input_grads, patch_grads = over_heads(input_four), over_heads(patch_four)

    cross_output_total, query_total = middle_total[:cols], middle_total[cols : 2 * cols]
    pair_total = middle_total[2 * cols :].reshape(heads, 2, HEAD_DIM, width)
    self_total = last_total[: 3 * cols].reshape(heads, 3, HEAD_DIM, width)
    self_output_total = last_total[3 * cols : 4 * cols]
    patch_total = last_total[4 * cols :, :patch_width]
    gradients = (
        small[: 2 * codes].reshape(2, codes, cols).transpose(1, 0, 2),
        self_total.transpose(1, 3, 0, 2).reshape(3, width, cols),
        self_output_total,
        small[2 * codes + 1],
        query_total.T,
        pair_total.transpose(1, 3, 0, 2).reshape(2, width, cols),
        cross_output_total,
        patch_total.T,
        small[2 * codes],
        *hidden_gradients,
    )
    return (outputs, input_grads.astype(WIDE), patch_grads.astype(WIDE)) + tuple(
        value.astype(WIDE) for value in gradients
    )


def per_device(
    tokens,
    cam_index,
    patches,
    patch_len,
    camera_table,
    self_weights,
    self_output,
    cross_gain,
    cross_query,
    cross_pair,
    cross_output,
    patch_weights,
    hidden_gain,
    widen_weights,
    narrow_weights,
    cotangent,
):
    batches, rows, width = tokens.shape
    cols = self_weights.shape[2]
    heads = cols // HEAD_DIM
    codes = camera_table.shape[0]
    patch_rows, patch_width = patches.shape[1:]
    n_rows, n_heads = lax.axis_size("rows"), lax.axis_size("heads")
    row_rank, head_rank = lax.axis_index("rows"), lax.axis_index("heads")
    groups = 1
    objects = batches // groups
    full_lengths = jnp.full((objects,), n_rows * rows, jnp.int32)
    count = objects * rows

    def own_columns(value):
        return lax.dynamic_slice_in_dim(value, head_rank * cols, cols, value.ndim - 1)

    table_flat = camera_table.reshape(codes, -1)
    cross_gain_f = cross_gain.astype(WIDE)
    hidden_gain_f = hidden_gain.astype(WIDE)

    qkv_rows = (
        self_weights.reshape(3, width, heads, HEAD_DIM).transpose(2, 0, 3, 1).reshape(3 * cols, width)
    )
    qkv_rows_back = self_weights.transpose(0, 2, 1).reshape(3 * cols, width)
    pair_rows = cross_pair.transpose(0, 2, 1).reshape(2 * cols, width)
    query_rows = cross_query.T

    local = jnp.stack([self_output, cross_output, query_rows])
    piece = cols // n_rows
    local = lax.dynamic_slice_in_dim(local, row_rank * piece, piece, 1)
    whole = lax.all_gather(jnp.stack(gather_heads(local)), "rows", axis=0)
    whole = whole.transpose(2, 1, 0, 3, 4).reshape(3, n_heads * cols, width)
    self_whole, cross_whole, query_whole = whole[0], whole[1], whole[2]

    def over_all_columns(value_t, weight):
        return mul(jnp.concatenate(gather_heads(value_t), axis=0), weight, TN)

    def by_object(weight, value):
        return jnp.stack(
            [mul(weight, value[i * rows : (i + 1) * rows], NT).astype(LOW) for i in range(objects)]
        )

    def column_terms(value, grads_t):
        return [
            mul(value, grads_t[i : i + cols], (((0,), (1,)), ((), ())))
            for i in range(0, grads_t.shape[0], cols)
        ]

    def one_group(group):
        part = slice(group * objects, (group + 1) * objects)
        inputs = tokens[part].reshape(count, width).astype(WIDE)
        patch_in = patches[part].reshape(objects * patch_rows, patch_width)
        lengths = patch_len[part]
        grad_low = cotangent[part].reshape(count, width)
        onehot = (cam_index[part].reshape(count)[:, None] == jnp.arange(codes)[None, :]).astype(LOW)
        shift_scale = mul(onehot, table_flat)
        gain_one = 1.0 + shift_scale[:, :width]
        unit_one, rate_one = normed(inputs)
        normed_one = (unit_one * gain_one + shift_scale[:, width:]).astype(LOW)
        qkv_t = by_object(qkv_rows, normed_one)
        by_kind = qkv_t.reshape(objects, heads, 3, HEAD_DIM, rows).transpose(2, 1, 3, 0, 4)
        by_kind = by_kind.reshape(3, cols, count)
        self_pair = lax.all_gather(by_kind[1:], "rows", axis=0)
        patch_mid = mul(patch_in, patch_weights).astype(LOW)
        own_pair = mul(pair_rows, patch_mid, NT).astype(LOW).reshape(2, cols, -1)
        pair_t = lax.all_gather(own_pair, "rows", axis=0)
        self_mixed_t, self_wide, self_log = cross_forward(by_kind[0], self_pair, full_lengths)
        after_self = inputs + over_all_columns(self_mixed_t, self_whole)
        unit_two, rate_two = normed(after_self)
        normed_two = (unit_two * cross_gain_f).astype(LOW)
        cross_q_t = mul(query_rows, normed_two, NT).astype(LOW)
        cross_mixed_t, cross_wide, cross_log = cross_forward(cross_q_t, pair_t, lengths)
        after_cross = after_self + over_all_columns(cross_mixed_t, cross_whole)
        unit_three, rate_three = normed(after_cross)
        normed_three = (unit_three * hidden_gain_f).astype(LOW)
        pre_act = mul(normed_three, widen_weights)
        activated, act_back = jax.vjp(gelu_tanh, pre_act)
        activated = activated.astype(LOW)
        grad_pre = act_back(mul(grad_low, narrow_weights, NT))[0].astype(LOW)
        grad_three = sum_heads(mul(grad_pre, widen_weights, NT)).astype(WIDE)
        yield "heads", {"hidden": mul(activated, narrow_weights)}
        yield "rows", {
            "narrow": mul(activated, grad_low, TN),
            "widen": mul(normed_three, grad_pre, TN),
        }
        hidden_gain_term = jnp.sum(own_columns(grad_three * unit_three), axis=0)
        grad_cross = grad_low.astype(WIDE) + normed_back(
            grad_three * hidden_gain_f, unit_three, rate_three
        )
        grad_cross_low = grad_cross.astype(LOW)
        cross_output_term = mul(cross_mixed_t, grad_cross_low)
        grad_mixed_t = mul(cross_output, grad_cross_low, NT).astype(LOW)
        grad_cq_t, grad_pair_t = cross_backward(
            cross_q_t, pair_t, lengths, grad_mixed_t, cross_wide, cross_log
        )
        grad_two = over_all_columns(grad_cq_t, query_whole)
        grad_pair_t = lax.psum_scatter(grad_pair_t, "rows", scatter_dimension=0, tiled=False)
        grad_pair_t = grad_pair_t.reshape(2 * cols, -1)
        query_term = mul(normed_two, grad_cq_t, (((0,), (1,)), ((), ())))
        cross_gain_term = jnp.sum(own_columns(grad_two * unit_two), axis=0)
        grad_self = grad_cross + normed_back(grad_two * cross_gain_f, unit_two, rate_two)
        grad_self_low = grad_self.astype(LOW)
        self_output_term = mul(self_mixed_t, grad_self_low)
        yield "heads", {"patch": mul(grad_pair_t, pair_rows, TN)}
        yield "rows", {
            "query": query_term,
            "pair": column_terms(patch_mid, grad_pair_t),
            "cross_output": cross_output_term,
            "self_output": self_output_term,
        }
        grad_self_mixed_t = mul(self_output, grad_self_low, NT).astype(LOW)
        grad_q_t, grad_kv_t = cross_backward(
            by_kind[0], self_pair, full_lengths, grad_self_mixed_t, self_wide, self_log
        )
        grad_kv_t = lax.psum_scatter(grad_kv_t, "rows", scatter_dimension=0, tiled=False)
        grad_qkv_t = jnp.concatenate([grad_q_t[None], grad_kv_t]).reshape(3 * cols, count)
        grad_qkv_t = yield "after", (grad_qkv_t, ["patch", "narrow", "widen"])
        grad_mid = yield "take", "patch"
        patch_term = mul(patch_in, own_columns(grad_mid), TN)
        patch_grad = mul(grad_mid, patch_weights, NT)
        grad_one = sum_heads(mul(grad_qkv_t, qkv_rows_back, TN))
        grad_one = yield "after", (grad_one, ["query", "pair", "cross_output", "self_output"])
        grad_one = grad_one.astype(WIDE)
        input_grad = grad_self + normed_back(grad_one * gain_one, unit_one, rate_one)
        own_grad = own_columns(grad_one)
        table_term = jnp.stack(
            [
                lax.dot_general(onehot.astype(WIDE), v, TN, precision=lax.Precision.HIGHEST)
                for v in (own_grad * own_columns(unit_one), own_grad)
            ],
            axis=1,
        )
        small = [patch_term, table_term.reshape(2 * codes, cols)]
        small += [hidden_gain_term[None], cross_gain_term[None], jnp.zeros((14, cols), WIDE)]
        yield "rows", {
            "self": column_terms(normed_one, grad_qkv_t),
            "small": jnp.concatenate(small, axis=0),
        }
        hidden_sum = yield "take", "hidden"
        result = (after_cross + hidden_sum.astype(WIDE)).astype(LOW)
        yield (
            "done",
            (
                result.reshape(objects, rows, width),
                input_grad.reshape(objects, rows, width),
                patch_grad.reshape(objects, patch_rows, patch_width),
            ),
        )

    steps = [one_group(group) for group in range(groups)]
    asked = [next(step) for step in steps]
    totals, ahead = {}, []
    while asked[0][0] != "done":
        kind, what = asked[0]
        answers = [None] * groups
        if kind == "take":
            answers = jnp.split(totals[what], groups)
        elif kind == "after":
            early = {name: totals[name] for name in what[1]}
            answers = [value for _, (value, _) in asked]
            answers[-1], early = lax.optimization_barrier((answers[-1], early))
            totals.update(early)
        else:
            terms = [value for _, value in asked]
            if kind == "heads":
                terms = jax.tree.map(lambda *parts: jnp.concatenate(parts, axis=0), *terms)
            else:
                for value in terms[1:]:
                    terms[0] = add_trees(terms[0], value)
                terms = terms[0]
            if kind == "rows":
                terms = jax.tree.map(lambda value: value.astype(LOW), terms)
            if kind == "heads":
                totals.update({name: sum_heads(value) for name, value in terms.items()})
            else:
                before = {name: totals[name] for name in ahead}
                terms, before = lax.optimization_barrier((terms, before))
                totals.update(before)
                totals.update(lax.psum(terms, kind))
                ahead = list(terms)
        asked = [step.send(value) for step, value in zip(steps, answers)]
    outputs, input_grads, patch_grads = (
        jnp.concatenate([value[i] for _, value in asked], axis=0) for i in range(3)
    )
    patch_total, table_total, gains = jnp.split(
        totals["small"], [patch_width, patch_width + 2 * codes]
    )
    gradients = (
        table_total.reshape(codes, 2, cols),
        jnp.stack(totals["self"]),
        totals["self_output"],
        gains[1],
        totals["query"],
        jnp.stack(totals["pair"]),
        totals["cross_output"],
        patch_total,
        gains[0],
        totals["widen"],
        totals["narrow"],
    )
    return (outputs, input_grads, patch_grads) + tuple(value.astype(WIDE) for value in gradients)


def solution(mesh):
    sizes = mesh.shape
    paired = sizes["heads"] == 4 and sizes["rows"] == 8
    heads = ("far", "near") if paired else "heads"
    if paired:
        names = (*heads, "rows")
        mesh = jax.sharding.Mesh(mesh.devices.reshape(2, 2, sizes["rows"]), names)
    in_specs = (
        P(None, "rows", None),
        P(None, "rows"),
        P(None, "rows", None),
        P(),
        P(),
        P(None, None, heads),
        P(heads, None),
        P(),
        P(None, heads),
        P(None, None, heads),
        P(heads, None),
        P(),
        P(),
        P(None, heads),
        P(heads, None),
        P(None, "rows", None),
    )
    out_specs = (
        P(None, "rows", None),
        P(None, "rows", None),
        P(None, "rows", None),
        P(None, None, heads),
        P(None, None, heads),
        P(heads, None),
        P(heads),
        P(None, heads),
        P(None, None, heads),
        P(heads, None),
        P(None, heads),
        P(heads),
        P(None, heads),
        P(heads, None),
    )
    return jax.shard_map(
        paired_device if paired else per_device,
        mesh=mesh,
        in_specs=in_specs,
        out_specs=out_specs,
        check_vma=False,
    )
```

```python
import jax
import jax.numpy as jnp
from jax import lax
from jax.experimental import pallas as pl
from jax.experimental.pallas import tpu as pltpu
from jax.sharding import PartitionSpec as P

HEAD_DIM = 64
EPSILON = 1e-05
SCALE = HEAD_DIM ** (-0.5)
LOW = jnp.bfloat16
WIDE = jnp.float32

NN = (((1,), (0,)), ((), ()))
NT = (((1,), (1,)), ((), ()))
TN = (((0,), (0,)), ((), ()))
T_LAST = (((0,), (1,)), ((), ()))


def mul(left, right, dims=NN):
    return lax.dot_general(left, right, dims, preferred_element_type=WIDE)


def load_values(values, block, values_t):
    rows = values_t.shape[1]
    at = slice(block * rows, (block + 1) * rows)
    values[at, :HEAD_DIM] = values_t.T
    values[at, HEAD_DIM:] = jnp.ones((rows, HEAD_DIM), values.dtype)


def attend_block(queries, keys_t, values):
    scores = mul(queries, keys_t)
    peak = jnp.max(scores, axis=1, keepdims=True)
    both = mul(jnp.exp(scores - peak).astype(LOW), values).T
    total = both[HEAD_DIM : HEAD_DIM + 1]
    return both[:HEAD_DIM] / total, peak.T + jnp.log(total)


def attend_block_back(scaled_q, grad_t, keys, keys_t, values, log_total, spread):
    probs = jnp.exp(mul(keys, scaled_q) - log_total)
    grad_scores = (probs * (mul(values, grad_t) - spread)).astype(LOW)
    return (
        (mul(keys_t, grad_scores) * SCALE).astype(LOW),
        mul(grad_scores, scaled_q.T),
        mul(probs.astype(LOW), grad_t.T),
    )


def estimate(rows, cols, passes):
    return pl.CostEstimate(
        flops=int(rows * cols * 1200 * passes), transcendentals=int(rows * cols), bytes_accessed=int(rows * 2048)
    )


VMEM_LIMIT = 48 << 20


def by_length(length, full, blocks, run):
    @pl.when(length * 4 > full)
    def _():
        run(blocks)

    @pl.when(length * 4 <= full)
    def _():
        run(blocks // 4)


def cross_forward(queries_t, pair_t, lengths):
    blocks, _, cols, all_patches = pair_t.shape
    objects = lengths.shape[0]
    heads = cols // HEAD_DIM
    rows, patch_rows = queries_t.shape[1] // objects, all_patches // objects

    def kernel(len_ref, q_ref, pair_ref, mixed_ref, wide_ref, log_ref, keys_t, values):
        queries = (q_ref[...] * LOW(SCALE)).T

        def run(live):
            for c in range(live):
                keys_t[:, c * patch_rows : (c + 1) * patch_rows] = pair_ref[c, 0]
                load_values(values, c, pair_ref[c, 1])
            size = live * patch_rows
            mixed, log_total = attend_block(queries, keys_t[:, :size], values[:size])
            mixed_ref[...] = mixed.astype(LOW)
            wide_ref[...] = mixed
            log_ref[...] = log_total

        by_length(len_ref[pl.program_id(0)], blocks * patch_rows, blocks, run)

    block = pl.BlockSpec((HEAD_DIM, rows), lambda b, j, lens: (j, b))
    return pl.pallas_call(
        kernel,
        grid_spec=pltpu.PrefetchScalarGridSpec(
            num_scalar_prefetch=1,
            grid=(objects, heads),
            in_specs=[
                block,
                pl.BlockSpec((blocks, 2, HEAD_DIM, patch_rows), lambda b, j, lens: (0, 0, j, b)),
            ],
            out_specs=[block, block, pl.BlockSpec((None, 1, rows), lambda b, j, lens: (j, 0, b))],
            scratch_shapes=[
                pltpu.VMEM((HEAD_DIM, blocks * patch_rows), LOW),
                pltpu.VMEM((blocks * patch_rows, 2 * HEAD_DIM), LOW),
            ],
        ),
        out_shape=[
            jax.ShapeDtypeStruct(queries_t.shape, LOW),
            jax.ShapeDtypeStruct(queries_t.shape, WIDE),
            jax.ShapeDtypeStruct((heads, 1, queries_t.shape[1]), WIDE),
        ],
        name="cross_forward",
        cost_estimate=estimate(objects * rows, blocks * patch_rows * heads, 1.4),
        compiler_params=pltpu.CompilerParams(vmem_limit_bytes=VMEM_LIMIT),
    )(lengths, queries_t, pair_t)


def cross_backward(queries_t, pair_t, lengths, grad_t_all, wide, log_total):
    blocks, _, cols, all_patches = pair_t.shape
    objects = lengths.shape[0]
    heads = cols // HEAD_DIM
    rows, patch_rows = queries_t.shape[1] // objects, all_patches // objects

    def kernel(len_ref, q_ref, pair_ref, g_ref, wide_ref, log_ref, out_q, out_pair, keys, keys_t, values):
        grad_t = g_ref[...]
        spread = jnp.sum(grad_t.astype(WIDE) * wide_ref[...], axis=0, keepdims=True)

        def run(live):
            for c in range(live):
                at = slice(c * patch_rows, (c + 1) * patch_rows)
                keys[at] = pair_ref[c, 0].T
                keys_t[:, at] = pair_ref[c, 0]
                values[at] = pair_ref[c, 1].T
            size = live * patch_rows
            out_q[...], grad_k, grad_v = attend_block_back(
                q_ref[...] * LOW(SCALE),
                grad_t,
                keys[:size],
                keys_t[:, :size],
                values[:size],
                log_ref[...],
                spread,
            )
            for c in range(live):
                at = slice(c * patch_rows, (c + 1) * patch_rows)
                out_pair[c, 0] = grad_k[at].T.astype(LOW)
                out_pair[c, 1] = grad_v[at].T.astype(LOW)
            for c in range(live, blocks):
                out_pair[c] = jnp.zeros_like(out_pair[c])

        by_length(len_ref[pl.program_id(0)], blocks * patch_rows, blocks, run)

    block = pl.BlockSpec((HEAD_DIM, rows), lambda b, j, lens: (j, b))
    pair_block = pl.BlockSpec((blocks, 2, HEAD_DIM, patch_rows), lambda b, j, lens: (0, 0, j, b))
    return pl.pallas_call(
        kernel,
        grid_spec=pltpu.PrefetchScalarGridSpec(
            num_scalar_prefetch=1,
            grid=(objects, heads),
            in_specs=[
                block,
                pair_block,
                block,
                block,
                pl.BlockSpec((None, 1, rows), lambda b, j, lens: (j, 0, b)),
            ],
            out_specs=[block, pair_block],
            scratch_shapes=[
                pltpu.VMEM((blocks * patch_rows, HEAD_DIM), LOW),
                pltpu.VMEM((HEAD_DIM, blocks * patch_rows), LOW),
                pltpu.VMEM((blocks * patch_rows, HEAD_DIM), LOW),
            ],
        ),
        out_shape=[
            jax.ShapeDtypeStruct(queries_t.shape, LOW),
            jax.ShapeDtypeStruct(pair_t.shape, LOW),
        ],
        name="cross_backward",
        cost_estimate=estimate(objects * rows, blocks * patch_rows * heads, 2.5),
        compiler_params=pltpu.CompilerParams(vmem_limit_bytes=VMEM_LIMIT),
    )(lengths, queries_t, pair_t, grad_t_all, wide, log_total)


def shift(value, step):
    size = lax.axis_size("heads")
    return lax.ppermute(value, "heads", [((i + step) % size, i) for i in range(size)])


def gather_heads(value):
    size = lax.axis_size("heads")
    if size != 4:
        return [value] + [shift(value, step) for step in range(1, size)]
    after, before = shift(value, 1), shift(value, -1)
    inner = lax.ppermute(after, "heads", [(1, 0), (2, 1)]) + lax.ppermute(before, "heads", [(1, 2), (2, 3)])
    return [value, after, inner, before]


def scatter_heads(partial):
    size, me = lax.axis_size("heads"), lax.axis_index("heads")

    def part(step):
        return lax.dynamic_index_in_dim(partial, (me + step) % size, 0, keepdims=False)

    if size != 4:
        total = part(0)
        for step in range(1, size):
            total = total + shift(part(step).astype(LOW), -step).astype(WIDE)
        return total
    far = part(2).astype(LOW)
    up = lax.ppermute(far, "heads", [(0, 1), (1, 2)]).astype(WIDE)
    down = lax.ppermute(far, "heads", [(2, 1), (3, 2)]).astype(WIDE)
    from_below = shift((part(1) + up).astype(LOW), -1)
    from_above = shift((part(3) + down).astype(LOW), 1)
    return part(0) + from_below.astype(WIDE) + from_above.astype(WIDE)


def in_order(parts):
    size, me = lax.axis_size("heads"), lax.axis_index("heads")
    out = jnp.zeros((size,) + parts[0].shape, parts[0].dtype)
    for step, value in enumerate(parts):
        out = lax.dynamic_update_index_in_dim(out, value, (me + step) % size, 0)
    return out.reshape((-1,) + parts[0].shape[1:])


def sum_heads(partial):
    size = lax.axis_size("heads")
    split = partial.reshape((size, -1) + partial.shape[1:])
    return in_order(gather_heads(scatter_heads(split).astype(LOW)))


def exchange_rows(value):
    return lax.all_to_all(value, "rows", 0, 0, tiled=True)


def normed(value):
    centred = value - jnp.mean(value, axis=-1, keepdims=True)
    rate = lax.rsqrt(jnp.mean(centred * centred, axis=-1, keepdims=True) + EPSILON)
    return centred * rate, rate


def normed_back(grad, unit, rate):
    return rate * (
        grad
        - jnp.mean(grad, axis=-1, keepdims=True)
        - unit * jnp.mean(grad * unit, axis=-1, keepdims=True)
    )


def gelu_tanh(pre_act):
    return jax.nn.gelu(pre_act, approximate=True)


def add_trees(former, latter):
    return jax.tree.map(jnp.add, former, latter)


def pair_forward(queries, pair, key_at, length=None):
    blocks, objects, _, width, rows = queries.shape
    pair_rows = pair.shape[4]
    lengths = jnp.full((objects,), blocks * pair_rows, jnp.int32) if length is None else length

    def kernel(len_ref, q_ref, k_ref, v_ref, mixed_ref, wide_ref, log_ref, keys_t, values):
        def run(live):
            @pl.when(pl.program_id(1) == 0)
            def _():
                for c in range(live):
                    keys_t[:, c * pair_rows : (c + 1) * pair_rows] = k_ref[c]
                    load_values(values, c, v_ref[c])

            size = live * pair_rows
            mixed, log_total = attend_block(
                (q_ref[...] * LOW(SCALE)).T, keys_t[:, :size], values[:size]
            )
            mixed_ref[...] = mixed.astype(LOW)
            wide_ref[...] = mixed
            log_ref[...] = log_total

        if length is None:
            run(blocks)
        else:
            by_length(len_ref[pl.program_id(0)], blocks * pair_rows, blocks, run)

    block = pl.BlockSpec((None, None, width, rows), lambda o, i, lens: (i, o, 0, 0))
    return pl.pallas_call(
        kernel,
        grid_spec=pltpu.PrefetchScalarGridSpec(
            num_scalar_prefetch=1,
            grid=(objects, blocks),
            in_specs=[
                pl.BlockSpec((None, None, None, width, rows), lambda o, i, lens: (i, o, 0, 0, 0)),
                pl.BlockSpec((blocks, None, None, width, pair_rows), lambda o, i, lens: (0, o, key_at, 0, 0)),
                pl.BlockSpec((blocks, None, None, width, pair_rows), lambda o, i, lens: (0, o, key_at + 1, 0, 0)),
            ],
            out_specs=[block, block, pl.BlockSpec((None, None, 1, rows), lambda o, i, lens: (i, o, 0, 0))],
            scratch_shapes=[
                pltpu.VMEM((width, blocks * pair_rows), LOW),
                pltpu.VMEM((blocks * pair_rows, 2 * width), LOW),
            ],
        ),
        out_shape=[
            jax.ShapeDtypeStruct((blocks, objects, width, rows), LOW),
            jax.ShapeDtypeStruct((blocks, objects, width, rows), WIDE),
            jax.ShapeDtypeStruct((blocks, objects, 1, rows), WIDE),
        ],
        name="pair_forward",
        cost_estimate=estimate(objects * blocks * rows, blocks * pair_rows, 2 if length is None else 1.4),
        compiler_params=pltpu.CompilerParams(vmem_limit_bytes=VMEM_LIMIT),
    )(lengths, queries, pair, pair)


def pair_backward(queries, pair, key_at, length, grad_mixed, wide, log_total):
    blocks, objects, _, width, rows = queries.shape
    lengths = jnp.full((objects,), blocks * rows, jnp.int32) if length is None else length

    def kernel(len_ref, q_ref, k_ref, v_ref, g_ref, wide_ref, log_ref, out_ref, keys, keys_t, values, grad_k, grad_v):
        i = pl.program_id(1)

        def run(live):
            size = live * rows

            @pl.when(i == 0)
            def _():
                for c in range(live):
                    at = slice(c * rows, (c + 1) * rows)
                    keys[at] = k_ref[c].T
                    keys_t[:, at] = k_ref[c]
                    values[at] = v_ref[c].T

            grad_t = g_ref[...]
            spread = jnp.sum(grad_t.astype(WIDE) * wide_ref[...], axis=0, keepdims=True)
            out_ref[i, 0], term_k, term_v = attend_block_back(
                q_ref[...] * LOW(SCALE),
                grad_t,
                keys[:size],
                keys_t[:, :size],
                values[:size],
                log_ref[...],
                spread,
            )

            @pl.when(i == 0)
            def _():
                grad_k[:size] = term_k
                grad_v[:size] = term_v

            @pl.when(i > 0)
            def _():
                grad_k[:size] += term_k
                grad_v[:size] += term_v

            @pl.when(i == blocks - 1)
            def _():
                for c in range(live):
                    at = slice(c * rows, (c + 1) * rows)
                    out_ref[c, 1] = grad_k[at].T.astype(LOW)
                    out_ref[c, 2] = grad_v[at].T.astype(LOW)
                for c in range(live, blocks):
                    out_ref[c, 1:] = jnp.zeros_like(out_ref[c, 1:])

        if length is None:
            run(blocks)
        else:
            by_length(len_ref[pl.program_id(0)], blocks * rows, blocks, run)

    block = pl.BlockSpec((None, None, width, rows), lambda o, i, lens: (i, o, 0, 0))
    return pl.pallas_call(
        kernel,
        grid_spec=pltpu.PrefetchScalarGridSpec(
            num_scalar_prefetch=1,
            grid=(objects, blocks),
            in_specs=[
                pl.BlockSpec((None, None, None, width, rows), lambda o, i, lens: (i, o, 0, 0, 0)),
                pl.BlockSpec((blocks, None, None, width, rows), lambda o, i, lens: (0, o, key_at, 0, 0)),
                pl.BlockSpec((blocks, None, None, width, rows), lambda o, i, lens: (0, o, key_at + 1, 0, 0)),
                block,
                block,
                pl.BlockSpec((None, None, 1, rows), lambda o, i, lens: (i, o, 0, 0)),
            ],
            out_specs=pl.BlockSpec((blocks, None, 3, width, rows), lambda o, i, lens: (0, o, 0, 0, 0)),
            scratch_shapes=[
                pltpu.VMEM((blocks * rows, width), LOW),
                pltpu.VMEM((width, blocks * rows), LOW),
                pltpu.VMEM((blocks * rows, width), LOW),
                pltpu.VMEM((blocks * rows, width), WIDE),
                pltpu.VMEM((blocks * rows, width), WIDE),
            ],
        ),
        out_shape=jax.ShapeDtypeStruct((blocks, objects, 3, width, rows), LOW),
        name="pair_backward",
        cost_estimate=estimate(objects * blocks * rows, blocks * rows, 3 if length is None else 2),
        compiler_params=pltpu.CompilerParams(vmem_limit_bytes=VMEM_LIMIT),
    )(lengths, queries, pair, pair, grad_mixed, wide, log_total)


def swap(value, axis):
    return lax.ppermute(value, axis, [(0, 1), (1, 0)])


def sum_near(partial):
    low = partial.astype(LOW)
    return low.astype(WIDE) + swap(low, "near").astype(WIDE)


def tie(value, *others):
    return lax.optimization_barrier((value, *others))


def paired_device(
    tokens,
    cam_index,
    patches,
    patch_len,
    camera_table,
    self_weights,
    self_output,
    cross_gain,
    cross_query,
    cross_pair,
    cross_output,
    patch_weights,
    hidden_gain,
    widen_weights,
    narrow_weights,
    cotangent,
):
    objects = tokens.shape[0] // 2
    _, rows, width = tokens.shape
    cols = self_weights.shape[2]
    hidden = widen_weights.shape[1]
    heads = cols // HEAD_DIM
    codes = camera_table.shape[0]
    patch_width = patches.shape[2]
    count = objects * rows
    n_rows = lax.axis_size("rows")
    row_rank = lax.axis_index("rows")
    far, near = lax.axis_index("far"), lax.axis_index("near")

    def objects_of(value):
        return lax.dynamic_slice_in_dim(value, objects * far, objects, 0)

    def piece(value):
        size = value.shape[0] // n_rows
        return lax.dynamic_slice_in_dim(value, row_rank * size, size, 0)

    def join_rows(value):
        return lax.all_gather(value, "rows", axis=0, tiled=True)

    def both_columns(value):
        return [
            lax.dynamic_slice_in_dim(value, (2 * index + near) * cols, cols, value.ndim - 1)
            for index in range(2)
        ]

    def in_order(mine, away, axis=0):
        size = mine.shape[axis]
        shape = list(mine.shape)
        shape[axis] *= 2
        out = lax.dynamic_update_slice_in_dim(jnp.zeros(shape, mine.dtype), mine, far * size, axis)
        return lax.dynamic_update_slice_in_dim(out, away, (1 - far) * size, axis)

    def halves(value):
        value = value.reshape(objects, 2, rows // 2, -1)
        return [
            lax.dynamic_index_in_dim(value, index, 1, keepdims=False).reshape(count // 2, -1)
            for index in (near, 1 - near)
        ]

    def half_sum_near(partial):
        mine, away = halves(partial)
        return mine + swap(away.astype(LOW), "near").astype(WIDE)

    def over_heads(value):
        value = value.reshape(2, 2, objects, rows // 2, -1)
        value = jnp.where(far == 0, value, jnp.flip(value, 1))
        value = jnp.where(near == 0, value, jnp.flip(value, 0))
        return value.transpose(1, 2, 0, 3, 4).reshape(2 * objects, rows, -1)

    def to_pairs(weights, value, slots):
        parts = [
            mul(weights, value[i * rows : (i + 1) * rows], NT)
            .astype(LOW)
            .reshape(n_rows, slots, HEAD_DIM, rows)
            for i in range(objects)
        ]
        return jnp.stack(parts, axis=1)

    def from_pairs(value):
        return value.transpose(0, 2, 3, 1, 4).reshape(-1, count)

    def over_all_columns(value_t, weight):
        return mul(jnp.concatenate([value_t, swap(value_t, "near")]), weight, TN)

    qkv_rows = self_weights.reshape(3, width, heads, HEAD_DIM).transpose(2, 0, 3, 1)
    qkv_rows = qkv_rows.reshape(3 * cols, width)
    pair_rows = cross_pair.reshape(2, width, heads, HEAD_DIM).transpose(2, 0, 3, 1)
    pair_rows = pair_rows.reshape(2 * cols, width)
    query_rows = cross_query.T

    qkv_away = join_rows(swap(piece(qkv_rows), "far"))

    table_flat = camera_table.reshape(codes, -1)
    cross_gain_f = cross_gain.astype(WIDE)
    hidden_gain_f = hidden_gain.astype(WIDE)

    inputs = objects_of(tokens).reshape(count, width).astype(WIDE)
    patch_in = objects_of(patches).reshape(count, patch_width)
    length = objects_of(patch_len)
    grad_low = objects_of(cotangent).reshape(count, width)
    codes_of = objects_of(cam_index).reshape(count)
    onehot = (codes_of[:, None] == jnp.arange(codes)[None, :]).astype(LOW)
    shift_scale = mul(onehot, table_flat)
    gain_one = 1.0 + shift_scale[:, :width]
    unit_one, rate_one = normed(inputs)
    normed_one = (unit_one * gain_one + shift_scale[:, width:]).astype(LOW)

    mine = [piece(v) for v in (self_output, query_rows, cross_output, pair_rows)]
    normed_one, *mine = tie(normed_one, *mine)
    mine = jnp.concatenate(mine, axis=0)
    across = swap(mine, "far")
    size = cols // n_rows
    two = in_order(mine[None, : 3 * size], across[None, : 3 * size])
    four = jnp.concatenate([two, swap(two, "near")])
    sent = jnp.concatenate([four.reshape(-1, width), across[3 * size :]])
    sent = lax.all_gather(sent, "rows", axis=0)
    pair_away = sent[:, 12 * size :].reshape(2 * cols, width)
    whole = sent[:, : 12 * size].reshape(n_rows, 4, 3, size, width).transpose(2, 1, 0, 3, 4)
    self_whole, query_whole, cross_whole = whole.reshape(3, 4 * cols, width)

    qkv_both = in_order(qkv_rows, qkv_away)
    qkv = exchange_rows(to_pairs(qkv_both, normed_one, 3))
    patch_mid = mul(patch_in, patch_weights).astype(LOW)
    pair_both = in_order(pair_rows, pair_away)
    pair = to_pairs(pair_both, patch_mid, 2)

    mine = [piece(widen_weights), piece(narrow_weights)]
    qkv, *mine = tie(qkv, *mine)
    size = width // n_rows
    sent = lax.all_gather(jnp.concatenate(mine, axis=0), ("far", "rows"), axis=0)
    sent = sent.reshape(2, n_rows, 2, size, width)
    widen = sent[:, :, 0].reshape(2, width, hidden)
    widen = jnp.concatenate([widen[0], widen[1]], axis=1)
    narrow = sent[:, :, 1].reshape(2 * hidden, width)

    mixed, self_wide, self_log = pair_forward(qkv, qkv, 1)
    mixed, pair = tie(exchange_rows(mixed), pair)
    pair = exchange_rows(pair)
    self_mixed_t = from_pairs(mixed[:, :, None])
    after_self = inputs + over_all_columns(self_mixed_t, self_whole)
    unit_two, rate_two = normed(after_self)
    normed_two = (unit_two * cross_gain_f).astype(LOW)
    cross_q, pair = tie(to_pairs(query_whole[: 2 * cols], normed_two, 1), pair)
    cross_q = exchange_rows(cross_q)
    mixed, cross_wide, cross_log = pair_forward(cross_q, pair, 0, length)
    cross_mixed_t = from_pairs(exchange_rows(mixed)[:, :, None])
    after_cross = after_self + over_all_columns(cross_mixed_t, cross_whole)
    unit_three, rate_three = normed(after_cross)
    normed_three = (unit_three * hidden_gain_f).astype(LOW)
    activated, act_back = jax.vjp(gelu_tanh, mul(normed_three, widen))
    activated = activated.astype(LOW)
    grad_pre = act_back(mul(grad_low, narrow, NT))[0].astype(LOW)
    third, activated, grad_pre = tie(mul(grad_pre, widen, NT).astype(LOW), activated, grad_pre)
    grad_three = third.astype(WIDE) + swap(third, "near").astype(WIDE)
    hidden_mine, hidden_away = halves(mul(activated, narrow))
    hidden_away, grad_three = tie(hidden_away.astype(LOW), grad_three)
    hidden_half = hidden_mine + swap(hidden_away, "near").astype(WIDE)
    result = (halves(after_cross)[0] + hidden_half).astype(LOW)

    def part_rows(both):
        return lax.psum_scatter(both, "rows", scatter_dimension=1, tiled=True)

    def own_and_away(value):
        return [lax.dynamic_index_in_dim(value, index, 0, keepdims=False) for index in (far, 1 - far)]

    def add_far(mine, away):
        return (mine.astype(WIDE) + away.astype(WIDE)).astype(LOW)

    def by_shard(left, right):
        return mul(left, right, NN).astype(LOW).reshape(2, -1, right.shape[1])

    hidden_terms = jnp.concatenate(
        [
            mul(activated, grad_low, TN).astype(LOW).reshape(2, hidden, width),
            jnp.stack(
                [mul(normed_three, value, TN).astype(LOW) for value in jnp.split(grad_pre, 2, axis=1)]
            ),
        ],
        axis=1,
    )
    hidden_part = part_rows(hidden_terms)

    hidden_gain_term = jnp.sum(grad_three * unit_three, axis=0)
    grad_cross = grad_low.astype(WIDE) + normed_back(
        grad_three * hidden_gain_f, unit_three, rate_three
    )
    grad_cross_low = grad_cross.astype(LOW)
    grad_mixed = exchange_rows(to_pairs(cross_whole[: 2 * cols], grad_cross_low, 1)[:, :, 0])
    grad_mixed, result = tie(grad_mixed, result)
    result_two = jnp.stack([result, swap(result, "far")])
    grads = pair_backward(cross_q, pair, 0, length, grad_mixed, cross_wide, cross_log)
    grads, result_two, hidden_part = tie(grads, result_two, hidden_part)
    hidden_own, hidden_away = own_and_away(hidden_part)
    grads, hidden_away = tie(exchange_rows(grads), swap(hidden_away, "far"))
    hidden_total = join_rows(add_far(hidden_own, hidden_away))
    grad_cq_t = from_pairs(grads[:, :, :1])
    grad_pair_t = from_pairs(grads[:, :, 1:])
    middle_terms = jnp.concatenate(
        [
            by_shard(cross_mixed_t, grad_cross_low),
            by_shard(grad_cq_t, normed_two),
            by_shard(grad_pair_t, patch_mid),
        ],
        axis=1,
    )
    grad_cq_away, middle_terms = tie(swap(grad_cq_t, "near"), middle_terms)
    middle_part = part_rows(middle_terms)
    grad_two = mul(jnp.concatenate([grad_cq_t, grad_cq_away]), query_whole, TN)
    grad_two, result_two = tie(grad_two, result_two)
    result_four = jnp.stack([result_two, swap(result_two, "near")])
    cross_gain_term = jnp.sum(grad_two * unit_two, axis=0)
    grad_self = grad_cross + normed_back(grad_two * cross_gain_f, unit_two, rate_two)
    grad_self_low = grad_self.astype(LOW)
    grad_mixed, grad_self_low, grad_mid = tie(
        to_pairs(self_whole[: 2 * cols], grad_self_low, 1)[:, :, 0],
        grad_self_low,
        mul(grad_pair_t, pair_both, TN).astype(LOW),
    )
    grad_mid_away = swap(grad_mid, "near")
    output_terms = by_shard(self_mixed_t, grad_self_low)
    grads = pair_backward(qkv, qkv, 1, None, exchange_rows(grad_mixed), self_wide, self_log)
    grads, grad_mid_away, result_four, hidden_total = tie(grads, grad_mid_away, result_four, hidden_total)
    grad_mid = (grad_mid.astype(WIDE) + grad_mid_away.astype(WIDE)).astype(LOW)
    patch_half = mul(halves(grad_mid)[0], patch_weights, NT).astype(LOW)
    patch_two = jnp.stack([patch_half, swap(patch_half, "far")])
    patch_terms = jnp.stack([mul(value, patch_in, TN).astype(LOW) for value in both_columns(grad_mid)])
    patch_terms = jnp.pad(patch_terms, ((0, 0), (0, 0), (0, width - patch_width)))
    last_terms = jnp.pad(
        jnp.concatenate([output_terms, patch_terms], axis=1), ((0, 0), (3 * cols, 0), (0, 0))
    )
    grads, patch_two, last_terms, middle_part = tie(exchange_rows(grads), patch_two, last_terms, middle_part)
    grad_qkv_t = from_pairs(grads)
    last_terms = lax.dynamic_update_slice_in_dim(last_terms, by_shard(grad_qkv_t, normed_one), 0, 1)
    last_part = part_rows(last_terms)
    middle_own, middle_away = own_and_away(middle_part)
    first_mine, first_away = halves(mul(grad_qkv_t, qkv_both, TN))
    first_away, middle_away = tie(first_away.astype(LOW), middle_away)
    middle_total = join_rows(add_far(middle_own, swap(middle_away, "far")))
    grad_one = first_mine + swap(first_away, "near").astype(WIDE)
    gain_half, unit_half, rate_half, self_half = (
        halves(value)[0] for value in (gain_one, unit_one, rate_one, grad_self)
    )
    input_half = self_half + normed_back(grad_one * gain_half, unit_half, rate_half)
    input_half = input_half.astype(LOW)
    input_two = jnp.stack([input_half, swap(input_half, "far")])
    onehot_half = halves(onehot)[0].astype(WIDE)
    table_term = jnp.concatenate(
        [
            lax.dot_general(onehot_half, value, TN, precision=lax.Precision.HIGHEST)
            for value in (grad_one * unit_half, grad_one)
        ],
        axis=0,
    )
    small = [sum_near(table_term), hidden_gain_term[None], cross_gain_term[None], jnp.zeros((14, width), WIDE)]
    small = jnp.stack(both_columns(jnp.concatenate(small, axis=0).astype(LOW)))
    small = jnp.sum(lax.all_gather(small, "rows", axis=0).astype(WIDE), axis=0).astype(LOW)
    small_own, small_away = own_and_away(small)
    small = small_own.astype(WIDE) + swap(small_away, "far").astype(WIDE)
    last_part, input_two, patch_two, small = tie(last_part, input_two, patch_two, small)
    input_four = jnp.stack([input_two, swap(input_two, "near")])
    patch_four = jnp.stack([patch_two, swap(patch_two, "near")])
    outputs = over_heads(result_four)
    hidden_gradients = [hidden_total[hidden:].astype(WIDE), hidden_total[:hidden].astype(WIDE)]
    last_own, last_away = own_and_away(last_part)
    last_sum, input_four = tie(add_far(last_own, swap(last_away, "far")), input_four)
    last_total = join_rows(last_sum)
    middle_total, outputs, hidden_gradients = tie(middle_total, outputs, hidden_gradients)
    input_four, patch_four = tie(input_four, patch_four)
    input_grads, patch_grads = over_heads(input_four), over_heads(patch_four)

    cross_output_total, query_total = middle_total[:cols], middle_total[cols : 2 * cols]
    pair_total = middle_total[2 * cols :].reshape(heads, 2, HEAD_DIM, width)
    self_total = last_total[: 3 * cols].reshape(heads, 3, HEAD_DIM, width)
    self_output_total = last_total[3 * cols : 4 * cols]
    patch_total = last_total[4 * cols :, :patch_width]
    gradients = (
        small[: 2 * codes].reshape(2, codes, cols).transpose(1, 0, 2),
        self_total.transpose(1, 3, 0, 2).reshape(3, width, cols),
        self_output_total,
        small[2 * codes + 1],
        query_total.T,
        pair_total.transpose(1, 3, 0, 2).reshape(2, width, cols),
        cross_output_total,
        patch_total.T,
        small[2 * codes],
        *hidden_gradients,
    )
    return (outputs, input_grads.astype(WIDE), patch_grads.astype(WIDE)) + tuple(
        value.astype(WIDE) for value in gradients
    )


def per_device(
    tokens,
    cam_index,
    patches,
    patch_len,
    camera_table,
    self_weights,
    self_output,
    cross_gain,
    cross_query,
    cross_pair,
    cross_output,
    patch_weights,
    hidden_gain,
    widen_weights,
    narrow_weights,
    cotangent,
):
    batches, rows, width = tokens.shape
    cols = self_weights.shape[2]
    heads = cols // HEAD_DIM
    codes = camera_table.shape[0]
    patch_rows, patch_width = patches.shape[1:]
    n_rows, n_heads = lax.axis_size("rows"), lax.axis_size("heads")
    row_rank, head_rank = lax.axis_index("rows"), lax.axis_index("heads")
    groups = 1
    objects = batches // groups
    full_lengths = jnp.full((objects,), n_rows * rows, jnp.int32)
    count = objects * rows

    def own_columns(value):
        return lax.dynamic_slice_in_dim(value, head_rank * cols, cols, value.ndim - 1)

    table_flat = camera_table.reshape(codes, -1)
    cross_gain_f = cross_gain.astype(WIDE)
    hidden_gain_f = hidden_gain.astype(WIDE)

    qkv_rows = (
        self_weights.reshape(3, width, heads, HEAD_DIM).transpose(2, 0, 3, 1).reshape(3 * cols, width)
    )
    qkv_rows_back = self_weights.transpose(0, 2, 1).reshape(3 * cols, width)
    pair_rows = cross_pair.transpose(0, 2, 1).reshape(2 * cols, width)
    query_rows = cross_query.T

    local = jnp.stack([self_output, cross_output, query_rows])
    piece = cols // n_rows
    local = lax.dynamic_slice_in_dim(local, row_rank * piece, piece, 1)
    whole = lax.all_gather(jnp.stack(gather_heads(local)), "rows", axis=0)
    whole = whole.transpose(2, 1, 0, 3, 4).reshape(3, n_heads * cols, width)
    self_whole, cross_whole, query_whole = whole[0], whole[1], whole[2]

    def over_all_columns(value_t, weight):
        return mul(jnp.concatenate(gather_heads(value_t), axis=0), weight, TN)

    def by_object(weight, value):
        return jnp.stack(
            [mul(weight, value[i * rows : (i + 1) * rows], NT).astype(LOW) for i in range(objects)]
        )

    def column_terms(value, grads_t):
        return [
            mul(value, grads_t[i : i + cols], (((0,), (1,)), ((), ())))
            for i in range(0, grads_t.shape[0], cols)
        ]

    def one_group(group):
        part = slice(group * objects, (group + 1) * objects)
        inputs = tokens[part].reshape(count, width).astype(WIDE)
        patch_in = patches[part].reshape(objects * patch_rows, patch_width)
        lengths = patch_len[part]
        grad_low = cotangent[part].reshape(count, width)
        onehot = (cam_index[part].reshape(count)[:, None] == jnp.arange(codes)[None, :]).astype(LOW)
        shift_scale = mul(onehot, table_flat)
        gain_one = 1.0 + shift_scale[:, :width]
        unit_one, rate_one = normed(inputs)
        normed_one = (unit_one * gain_one + shift_scale[:, width:]).astype(LOW)
        qkv_t = by_object(qkv_rows, normed_one)
        by_kind = qkv_t.reshape(objects, heads, 3, HEAD_DIM, rows).transpose(2, 1, 3, 0, 4)
        by_kind = by_kind.reshape(3, cols, count)
        self_pair = lax.all_gather(by_kind[1:], "rows", axis=0)
        patch_mid = mul(patch_in, patch_weights).astype(LOW)
        own_pair = mul(pair_rows, patch_mid, NT).astype(LOW).reshape(2, cols, -1)
        pair_t = lax.all_gather(own_pair, "rows", axis=0)
        self_mixed_t, self_wide, self_log = cross_forward(by_kind[0], self_pair, full_lengths)
        after_self = inputs + over_all_columns(self_mixed_t, self_whole)
        unit_two, rate_two = normed(after_self)
        normed_two = (unit_two * cross_gain_f).astype(LOW)
        cross_q_t = mul(query_rows, normed_two, NT).astype(LOW)
        cross_mixed_t, cross_wide, cross_log = cross_forward(cross_q_t, pair_t, lengths)
        after_cross = after_self + over_all_columns(cross_mixed_t, cross_whole)
        unit_three, rate_three = normed(after_cross)
        normed_three = (unit_three * hidden_gain_f).astype(LOW)
        pre_act = mul(normed_three, widen_weights)
        activated, act_back = jax.vjp(gelu_tanh, pre_act)
        activated = activated.astype(LOW)
        grad_pre = act_back(mul(grad_low, narrow_weights, NT))[0].astype(LOW)
        grad_three = sum_heads(mul(grad_pre, widen_weights, NT)).astype(WIDE)
        yield "heads", {"hidden": mul(activated, narrow_weights)}
        yield "rows", {
            "narrow": mul(activated, grad_low, TN),
            "widen": mul(normed_three, grad_pre, TN),
        }
        hidden_gain_term = jnp.sum(own_columns(grad_three * unit_three), axis=0)
        grad_cross = grad_low.astype(WIDE) + normed_back(
            grad_three * hidden_gain_f, unit_three, rate_three
        )
        grad_cross_low = grad_cross.astype(LOW)
        cross_output_term = mul(cross_mixed_t, grad_cross_low)
        grad_mixed_t = mul(cross_output, grad_cross_low, NT).astype(LOW)
        grad_cq_t, grad_pair_t = cross_backward(
            cross_q_t, pair_t, lengths, grad_mixed_t, cross_wide, cross_log
        )
        grad_two = over_all_columns(grad_cq_t, query_whole)
        grad_pair_t = lax.psum_scatter(grad_pair_t, "rows", scatter_dimension=0, tiled=False)
        grad_pair_t = grad_pair_t.reshape(2 * cols, -1)
        query_term = mul(normed_two, grad_cq_t, (((0,), (1,)), ((), ())))
        cross_gain_term = jnp.sum(own_columns(grad_two * unit_two), axis=0)
        grad_self = grad_cross + normed_back(grad_two * cross_gain_f, unit_two, rate_two)
        grad_self_low = grad_self.astype(LOW)
        self_output_term = mul(self_mixed_t, grad_self_low)
        yield "heads", {"patch": mul(grad_pair_t, pair_rows, TN)}
        yield "rows", {
            "query": query_term,
            "pair": column_terms(patch_mid, grad_pair_t),
            "cross_output": cross_output_term,
            "self_output": self_output_term,
        }
        grad_self_mixed_t = mul(self_output, grad_self_low, NT).astype(LOW)
        grad_q_t, grad_kv_t = cross_backward(
            by_kind[0], self_pair, full_lengths, grad_self_mixed_t, self_wide, self_log
        )
        grad_kv_t = lax.psum_scatter(grad_kv_t, "rows", scatter_dimension=0, tiled=False)
        grad_qkv_t = jnp.concatenate([grad_q_t[None], grad_kv_t]).reshape(3 * cols, count)
        grad_qkv_t = yield "after", (grad_qkv_t, ["patch", "narrow", "widen"])
        grad_mid = yield "take", "patch"
        patch_term = mul(patch_in, own_columns(grad_mid), TN)
        patch_grad = mul(grad_mid, patch_weights, NT)
        grad_one = sum_heads(mul(grad_qkv_t, qkv_rows_back, TN))
        grad_one = yield "after", (grad_one, ["query", "pair", "cross_output", "self_output"])
        grad_one = grad_one.astype(WIDE)
        input_grad = grad_self + normed_back(grad_one * gain_one, unit_one, rate_one)
        own_grad = own_columns(grad_one)
        table_term = jnp.stack(
            [
                lax.dot_general(onehot.astype(WIDE), v, TN, precision=lax.Precision.HIGHEST)
                for v in (own_grad * own_columns(unit_one), own_grad)
            ],
            axis=1,
        )
        small = [patch_term, table_term.reshape(2 * codes, cols)]
        small += [hidden_gain_term[None], cross_gain_term[None], jnp.zeros((14, cols), WIDE)]
        yield "rows", {
            "self": column_terms(normed_one, grad_qkv_t),
            "small": jnp.concatenate(small, axis=0),
        }
        hidden_sum = yield "take", "hidden"
        result = (after_cross + hidden_sum.astype(WIDE)).astype(LOW)
        yield (
            "done",
            (
                result.reshape(objects, rows, width),
                input_grad.reshape(objects, rows, width),
                patch_grad.reshape(objects, patch_rows, patch_width),
            ),
        )

    steps = [one_group(group) for group in range(groups)]
    asked = [next(step) for step in steps]
    totals, ahead = {}, []
    while asked[0][0] != "done":
        kind, what = asked[0]
        answers = [None] * groups
        if kind == "take":
            answers = jnp.split(totals[what], groups)
        elif kind == "after":
            early = {name: totals[name] for name in what[1]}
            answers = [value for _, (value, _) in asked]
            answers[-1], early = lax.optimization_barrier((answers[-1], early))
            totals.update(early)
        else:
            terms = [value for _, value in asked]
            if kind == "heads":
                terms = jax.tree.map(lambda *parts: jnp.concatenate(parts, axis=0), *terms)
            else:
                for value in terms[1:]:
                    terms[0] = add_trees(terms[0], value)
                terms = terms[0]
            if kind == "rows":
                terms = jax.tree.map(lambda value: value.astype(LOW), terms)
            if kind == "heads":
                totals.update({name: sum_heads(value) for name, value in terms.items()})
            else:
                before = {name: totals[name] for name in ahead}
                terms, before = lax.optimization_barrier((terms, before))
                totals.update(before)
                totals.update(lax.psum(terms, kind))
                ahead = list(terms)
        asked = [step.send(value) for step, value in zip(steps, answers)]
    outputs, input_grads, patch_grads = (
        jnp.concatenate([value[i] for _, value in asked], axis=0) for i in range(3)
    )
    patch_total, table_total, gains = jnp.split(
        totals["small"], [patch_width, patch_width + 2 * codes]
    )
    gradients = (
        table_total.reshape(codes, 2, cols),
        jnp.stack(totals["self"]),
        totals["self_output"],
        gains[1],
        totals["query"],
        jnp.stack(totals["pair"]),
        totals["cross_output"],
        patch_total,
        gains[0],
        totals["widen"],
        totals["narrow"],
    )
    return (outputs, input_grads, patch_grads) + tuple(value.astype(WIDE) for value in gradients)


def solution(mesh):
    sizes = mesh.shape
    paired = sizes["heads"] == 4 and sizes["rows"] == 8
    heads = ("far", "near") if paired else "heads"
    if paired:
        names = (*heads, "rows")
        mesh = jax.sharding.Mesh(mesh.devices.reshape(2, 2, sizes["rows"]), names)
    in_specs = (
        P(None, "rows", None),
        P(None, "rows"),
        P(None, "rows", None),
        P(),
        P(),
        P(None, None, heads),
        P(heads, None),
        P(),
        P(None, heads),
        P(None, None, heads),
        P(heads, None),
        P(),
        P(),
        P(None, heads),
        P(heads, None),
        P(None, "rows", None),
    )
    out_specs = (
        P(None, "rows", None),
        P(None, "rows", None),
        P(None, "rows", None),
        P(None, None, heads),
        P(None, None, heads),
        P(heads, None),
        P(heads),
        P(None, heads),
        P(None, None, heads),
        P(heads, None),
        P(None, heads),
        P(heads),
        P(None, heads),
        P(heads, None),
    )
    return jax.shard_map(
        paired_device if paired else per_device,
        mesh=mesh,
        in_specs=in_specs,
        out_specs=out_specs,
        check_vma=False,
    )
```

```python
import jax
import jax.numpy as jnp
from jax import lax
from jax.experimental import pallas as pl
from jax.experimental.pallas import tpu as pltpu
from jax.sharding import PartitionSpec as P

HEAD_DIM = 64
EPSILON = 1e-05
SCALE = HEAD_DIM ** (-0.5)
LOW = jnp.bfloat16
WIDE = jnp.float32

NN = (((1,), (0,)), ((), ()))
NT = (((1,), (1,)), ((), ()))
TN = (((0,), (0,)), ((), ()))
T_LAST = (((0,), (1,)), ((), ()))


def mul(left, right, dims=NN):
    return lax.dot_general(left, right, dims, preferred_element_type=WIDE)


def load_values(values, block, values_t):
    rows = values_t.shape[1]
    at = slice(block * rows, (block + 1) * rows)
    values[at, :HEAD_DIM] = values_t.T
    values[at, HEAD_DIM:] = jnp.ones((rows, HEAD_DIM), values.dtype)


def attend_block(queries, keys_t, values):
    scores = mul(queries, keys_t)
    peak = jnp.max(scores, axis=1, keepdims=True)
    both = mul(jnp.exp(scores - peak).astype(LOW), values).T
    total = both[HEAD_DIM : HEAD_DIM + 1]
    return both[:HEAD_DIM] / total, peak.T + jnp.log(total)


def attend_block_back(scaled_q, grad_t, keys, keys_t, values, log_total, spread):
    probs = jnp.exp(mul(keys, scaled_q) - log_total)
    grad_scores = (probs * (mul(values, grad_t) - spread)).astype(LOW)
    return (
        (mul(keys_t, grad_scores) * SCALE).astype(LOW),
        mul(grad_scores, scaled_q.T),
        mul(probs.astype(LOW), grad_t.T),
    )


def estimate(rows, cols, passes):
    return pl.CostEstimate(
        flops=int(rows * cols * 1200 * passes), transcendentals=int(rows * cols), bytes_accessed=int(rows * 2048)
    )


VMEM_LIMIT = 48 << 20


def by_length(length, full, blocks, run):
    @pl.when(length * 4 > full)
    def _():
        run(blocks)

    @pl.when(length * 4 <= full)
    def _():
        run(blocks // 4)


def cross_forward(queries_t, pair_t, lengths):
    blocks, _, cols, all_patches = pair_t.shape
    objects = lengths.shape[0]
    heads = cols // HEAD_DIM
    rows, patch_rows = queries_t.shape[1] // objects, all_patches // objects

    def kernel(len_ref, q_ref, pair_ref, mixed_ref, wide_ref, log_ref, keys_t, values):
        queries = (q_ref[...] * LOW(SCALE)).T

        def run(live):
            for c in range(live):
                keys_t[:, c * patch_rows : (c + 1) * patch_rows] = pair_ref[c, 0]
                load_values(values, c, pair_ref[c, 1])
            size = live * patch_rows
            mixed, log_total = attend_block(queries, keys_t[:, :size], values[:size])
            mixed_ref[...] = mixed.astype(LOW)
            wide_ref[...] = mixed
            log_ref[...] = log_total

        by_length(len_ref[pl.program_id(0)], blocks * patch_rows, blocks, run)

    block = pl.BlockSpec((HEAD_DIM, rows), lambda b, j, lens: (j, b))
    return pl.pallas_call(
        kernel,
        grid_spec=pltpu.PrefetchScalarGridSpec(
            num_scalar_prefetch=1,
            grid=(objects, heads),
            in_specs=[
                block,
                pl.BlockSpec((blocks, 2, HEAD_DIM, patch_rows), lambda b, j, lens: (0, 0, j, b)),
            ],
            out_specs=[block, block, pl.BlockSpec((None, 1, rows), lambda b, j, lens: (j, 0, b))],
            scratch_shapes=[
                pltpu.VMEM((HEAD_DIM, blocks * patch_rows), LOW),
                pltpu.VMEM((blocks * patch_rows, 2 * HEAD_DIM), LOW),
            ],
        ),
        out_shape=[
            jax.ShapeDtypeStruct(queries_t.shape, LOW),
            jax.ShapeDtypeStruct(queries_t.shape, WIDE),
            jax.ShapeDtypeStruct((heads, 1, queries_t.shape[1]), WIDE),
        ],
        name="cross_forward",
        cost_estimate=estimate(objects * rows, blocks * patch_rows * heads, 1.4),
        compiler_params=pltpu.CompilerParams(vmem_limit_bytes=VMEM_LIMIT),
    )(lengths, queries_t, pair_t)


def cross_backward(queries_t, pair_t, lengths, grad_t_all, wide, log_total):
    blocks, _, cols, all_patches = pair_t.shape
    objects = lengths.shape[0]
    heads = cols // HEAD_DIM
    rows, patch_rows = queries_t.shape[1] // objects, all_patches // objects

    def kernel(len_ref, q_ref, pair_ref, g_ref, wide_ref, log_ref, out_q, out_pair, keys, keys_t, values):
        grad_t = g_ref[...]
        spread = jnp.sum(grad_t.astype(WIDE) * wide_ref[...], axis=0, keepdims=True)

        def run(live):
            for c in range(live):
                at = slice(c * patch_rows, (c + 1) * patch_rows)
                keys[at] = pair_ref[c, 0].T
                keys_t[:, at] = pair_ref[c, 0]
                values[at] = pair_ref[c, 1].T
            size = live * patch_rows
            out_q[...], grad_k, grad_v = attend_block_back(
                q_ref[...] * LOW(SCALE),
                grad_t,
                keys[:size],
                keys_t[:, :size],
                values[:size],
                log_ref[...],
                spread,
            )
            for c in range(live):
                at = slice(c * patch_rows, (c + 1) * patch_rows)
                out_pair[c, 0] = grad_k[at].T.astype(LOW)
                out_pair[c, 1] = grad_v[at].T.astype(LOW)
            for c in range(live, blocks):
                out_pair[c] = jnp.zeros_like(out_pair[c])

        by_length(len_ref[pl.program_id(0)], blocks * patch_rows, blocks, run)

    block = pl.BlockSpec((HEAD_DIM, rows), lambda b, j, lens: (j, b))
    pair_block = pl.BlockSpec((blocks, 2, HEAD_DIM, patch_rows), lambda b, j, lens: (0, 0, j, b))
    return pl.pallas_call(
        kernel,
        grid_spec=pltpu.PrefetchScalarGridSpec(
            num_scalar_prefetch=1,
            grid=(objects, heads),
            in_specs=[
                block,
                pair_block,
                block,
                block,
                pl.BlockSpec((None, 1, rows), lambda b, j, lens: (j, 0, b)),
            ],
            out_specs=[block, pair_block],
            scratch_shapes=[
                pltpu.VMEM((blocks * patch_rows, HEAD_DIM), LOW),
                pltpu.VMEM((HEAD_DIM, blocks * patch_rows), LOW),
                pltpu.VMEM((blocks * patch_rows, HEAD_DIM), LOW),
            ],
        ),
        out_shape=[
            jax.ShapeDtypeStruct(queries_t.shape, LOW),
            jax.ShapeDtypeStruct(pair_t.shape, LOW),
        ],
        name="cross_backward",
        cost_estimate=estimate(objects * rows, blocks * patch_rows * heads, 2.5),
        compiler_params=pltpu.CompilerParams(vmem_limit_bytes=VMEM_LIMIT),
    )(lengths, queries_t, pair_t, grad_t_all, wide, log_total)


def shift(value, step):
    size = lax.axis_size("heads")
    return lax.ppermute(value, "heads", [((i + step) % size, i) for i in range(size)])


def gather_heads(value):
    size = lax.axis_size("heads")
    if size != 4:
        return [value] + [shift(value, step) for step in range(1, size)]
    after, before = shift(value, 1), shift(value, -1)
    inner = lax.ppermute(after, "heads", [(1, 0), (2, 1)]) + lax.ppermute(before, "heads", [(1, 2), (2, 3)])
    return [value, after, inner, before]


def scatter_heads(partial):
    size, me = lax.axis_size("heads"), lax.axis_index("heads")

    def part(step):
        return lax.dynamic_index_in_dim(partial, (me + step) % size, 0, keepdims=False)

    if size != 4:
        total = part(0)
        for step in range(1, size):
            total = total + shift(part(step).astype(LOW), -step).astype(WIDE)
        return total
    far = part(2).astype(LOW)
    up = lax.ppermute(far, "heads", [(0, 1), (1, 2)]).astype(WIDE)
    down = lax.ppermute(far, "heads", [(2, 1), (3, 2)]).astype(WIDE)
    from_below = shift((part(1) + up).astype(LOW), -1)
    from_above = shift((part(3) + down).astype(LOW), 1)
    return part(0) + from_below.astype(WIDE) + from_above.astype(WIDE)


def in_order(parts):
    size, me = lax.axis_size("heads"), lax.axis_index("heads")
    out = jnp.zeros((size,) + parts[0].shape, parts[0].dtype)
    for step, value in enumerate(parts):
        out = lax.dynamic_update_index_in_dim(out, value, (me + step) % size, 0)
    return out.reshape((-1,) + parts[0].shape[1:])


def sum_heads(partial):
    size = lax.axis_size("heads")
    split = partial.reshape((size, -1) + partial.shape[1:])
    return in_order(gather_heads(scatter_heads(split).astype(LOW)))


def exchange_rows(value):
    return lax.all_to_all(value, "rows", 0, 0, tiled=True)


def normed(value):
    centred = value - jnp.mean(value, axis=-1, keepdims=True)
    rate = lax.rsqrt(jnp.mean(centred * centred, axis=-1, keepdims=True) + EPSILON)
    return centred * rate, rate


def normed_back(grad, unit, rate):
    return rate * (
        grad
        - jnp.mean(grad, axis=-1, keepdims=True)
        - unit * jnp.mean(grad * unit, axis=-1, keepdims=True)
    )


def gelu_tanh(pre_act):
    return jax.nn.gelu(pre_act, approximate=True)


def add_trees(former, latter):
    return jax.tree.map(jnp.add, former, latter)


def pair_forward(queries, pair, key_at, length=None):
    blocks, objects, _, width, rows = queries.shape
    pair_rows = pair.shape[4]
    lengths = jnp.full((objects,), blocks * pair_rows, jnp.int32) if length is None else length

    def kernel(len_ref, q_ref, k_ref, v_ref, mixed_ref, wide_ref, log_ref, keys_t, values):
        def run(live):
            @pl.when(pl.program_id(1) == 0)
            def _():
                for c in range(live):
                    keys_t[:, c * pair_rows : (c + 1) * pair_rows] = k_ref[c]
                    load_values(values, c, v_ref[c])

            size = live * pair_rows
            mixed, log_total = attend_block(
                (q_ref[...] * LOW(SCALE)).T, keys_t[:, :size], values[:size]
            )
            mixed_ref[...] = mixed.astype(LOW)
            wide_ref[...] = mixed
            log_ref[...] = log_total

        if length is None:
            run(blocks)
        else:
            by_length(len_ref[pl.program_id(0)], blocks * pair_rows, blocks, run)

    block = pl.BlockSpec((None, None, width, rows), lambda o, i, lens: (i, o, 0, 0))
    return pl.pallas_call(
        kernel,
        grid_spec=pltpu.PrefetchScalarGridSpec(
            num_scalar_prefetch=1,
            grid=(objects, blocks),
            in_specs=[
                pl.BlockSpec((None, None, None, width, rows), lambda o, i, lens: (i, o, 0, 0, 0)),
                pl.BlockSpec((blocks, None, None, width, pair_rows), lambda o, i, lens: (0, o, key_at, 0, 0)),
                pl.BlockSpec((blocks, None, None, width, pair_rows), lambda o, i, lens: (0, o, key_at + 1, 0, 0)),
            ],
            out_specs=[block, block, pl.BlockSpec((None, None, 1, rows), lambda o, i, lens: (i, o, 0, 0))],
            scratch_shapes=[
                pltpu.VMEM((width, blocks * pair_rows), LOW),
                pltpu.VMEM((blocks * pair_rows, 2 * width), LOW),
            ],
        ),
        out_shape=[
            jax.ShapeDtypeStruct((blocks, objects, width, rows), LOW),
            jax.ShapeDtypeStruct((blocks, objects, width, rows), WIDE),
            jax.ShapeDtypeStruct((blocks, objects, 1, rows), WIDE),
        ],
        name="pair_forward",
        cost_estimate=estimate(objects * blocks * rows, blocks * pair_rows, 2 if length is None else 1.4),
        compiler_params=pltpu.CompilerParams(vmem_limit_bytes=VMEM_LIMIT),
    )(lengths, queries, pair, pair)


def pair_backward(queries, pair, key_at, length, grad_mixed, wide, log_total):
    blocks, objects, _, width, rows = queries.shape
    lengths = jnp.full((objects,), blocks * rows, jnp.int32) if length is None else length

    def kernel(len_ref, q_ref, k_ref, v_ref, g_ref, wide_ref, log_ref, out_ref, keys, keys_t, values, grad_k, grad_v):
        i = pl.program_id(1)

        def run(live):
            size = live * rows

            @pl.when(i == 0)
            def _():
                for c in range(live):
                    at = slice(c * rows, (c + 1) * rows)
                    keys[at] = k_ref[c].T
                    keys_t[:, at] = k_ref[c]
                    values[at] = v_ref[c].T

            grad_t = g_ref[...]
            spread = jnp.sum(grad_t.astype(WIDE) * wide_ref[...], axis=0, keepdims=True)
            out_ref[i, 0], term_k, term_v = attend_block_back(
                q_ref[...] * LOW(SCALE),
                grad_t,
                keys[:size],
                keys_t[:, :size],
                values[:size],
                log_ref[...],
                spread,
            )

            @pl.when(i == 0)
            def _():
                grad_k[:size] = term_k
                grad_v[:size] = term_v

            @pl.when(i > 0)
            def _():
                grad_k[:size] += term_k
                grad_v[:size] += term_v

            @pl.when(i == blocks - 1)
            def _():
                for c in range(live):
                    at = slice(c * rows, (c + 1) * rows)
                    out_ref[c, 1] = grad_k[at].T.astype(LOW)
                    out_ref[c, 2] = grad_v[at].T.astype(LOW)
                for c in range(live, blocks):
                    out_ref[c, 1:] = jnp.zeros_like(out_ref[c, 1:])

        if length is None:
            run(blocks)
        else:
            by_length(len_ref[pl.program_id(0)], blocks * rows, blocks, run)

    block = pl.BlockSpec((None, None, width, rows), lambda o, i, lens: (i, o, 0, 0))
    return pl.pallas_call(
        kernel,
        grid_spec=pltpu.PrefetchScalarGridSpec(
            num_scalar_prefetch=1,
            grid=(objects, blocks),
            in_specs=[
                pl.BlockSpec((None, None, None, width, rows), lambda o, i, lens: (i, o, 0, 0, 0)),
                pl.BlockSpec((blocks, None, None, width, rows), lambda o, i, lens: (0, o, key_at, 0, 0)),
                pl.BlockSpec((blocks, None, None, width, rows), lambda o, i, lens: (0, o, key_at + 1, 0, 0)),
                block,
                block,
                pl.BlockSpec((None, None, 1, rows), lambda o, i, lens: (i, o, 0, 0)),
            ],
            out_specs=pl.BlockSpec((blocks, None, 3, width, rows), lambda o, i, lens: (0, o, 0, 0, 0)),
            scratch_shapes=[
                pltpu.VMEM((blocks * rows, width), LOW),
                pltpu.VMEM((width, blocks * rows), LOW),
                pltpu.VMEM((blocks * rows, width), LOW),
                pltpu.VMEM((blocks * rows, width), WIDE),
                pltpu.VMEM((blocks * rows, width), WIDE),
            ],
        ),
        out_shape=jax.ShapeDtypeStruct((blocks, objects, 3, width, rows), LOW),
        name="pair_backward",
        cost_estimate=estimate(objects * blocks * rows, blocks * rows, 3 if length is None else 2),
        compiler_params=pltpu.CompilerParams(vmem_limit_bytes=VMEM_LIMIT),
    )(lengths, queries, pair, pair, grad_mixed, wide, log_total)


def swap(value, axis):
    return lax.ppermute(value, axis, [(0, 1), (1, 0)])


def sum_near(partial):
    low = partial.astype(LOW)
    return low.astype(WIDE) + swap(low, "near").astype(WIDE)


def tie(value, *others):
    return lax.optimization_barrier((value, *others))


def paired_device(
    tokens,
    cam_index,
    patches,
    patch_len,
    camera_table,
    self_weights,
    self_output,
    cross_gain,
    cross_query,
    cross_pair,
    cross_output,
    patch_weights,
    hidden_gain,
    widen_weights,
    narrow_weights,
    cotangent,
):
    objects = tokens.shape[0] // 2
    _, rows, width = tokens.shape
    cols = self_weights.shape[2]
    hidden = widen_weights.shape[1]
    heads = cols // HEAD_DIM
    codes = camera_table.shape[0]
    patch_width = patches.shape[2]
    count = objects * rows
    n_rows = lax.axis_size("rows")
    row_rank = lax.axis_index("rows")
    far, near = lax.axis_index("far"), lax.axis_index("near")

    def objects_of(value):
        return lax.dynamic_slice_in_dim(value, objects * far, objects, 0)

    def piece(value):
        size = value.shape[0] // n_rows
        return lax.dynamic_slice_in_dim(value, row_rank * size, size, 0)

    def join_rows(value):
        return lax.all_gather(value, "rows", axis=0, tiled=True)

    def both_columns(value):
        return [
            lax.dynamic_slice_in_dim(value, (2 * index + near) * cols, cols, value.ndim - 1)
            for index in range(2)
        ]

    def in_order(mine, away, axis=0):
        size = mine.shape[axis]
        shape = list(mine.shape)
        shape[axis] *= 2
        out = lax.dynamic_update_slice_in_dim(jnp.zeros(shape, mine.dtype), mine, far * size, axis)
        return lax.dynamic_update_slice_in_dim(out, away, (1 - far) * size, axis)

    def halves(value):
        value = value.reshape(objects, 2, rows // 2, -1)
        return [
            lax.dynamic_index_in_dim(value, index, 1, keepdims=False).reshape(count // 2, -1)
            for index in (near, 1 - near)
        ]

    def half_sum_near(partial):
        mine, away = halves(partial)
        return mine + swap(away.astype(LOW), "near").astype(WIDE)

    def over_heads(value):
        value = value.reshape(2, 2, objects, rows // 2, -1)
        value = jnp.where(far == 0, value, jnp.flip(value, 1))
        value = jnp.where(near == 0, value, jnp.flip(value, 0))
        return value.transpose(1, 2, 0, 3, 4).reshape(2 * objects, rows, -1)

    def to_pairs(weights, value, slots):
        parts = [
            mul(weights, value[i * rows : (i + 1) * rows], NT)
            .astype(LOW)
            .reshape(n_rows, slots, HEAD_DIM, rows)
            for i in range(objects)
        ]
        return jnp.stack(parts, axis=1)

    def from_pairs(value):
        return value.transpose(0, 2, 3, 1, 4).reshape(-1, count)

    def over_all_columns(value_t, weight):
        return mul(jnp.concatenate([value_t, swap(value_t, "near")]), weight, TN)

    qkv_rows = self_weights.reshape(3, width, heads, HEAD_DIM).transpose(2, 0, 3, 1)
    qkv_rows = qkv_rows.reshape(3 * cols, width)
    pair_rows = cross_pair.reshape(2, width, heads, HEAD_DIM).transpose(2, 0, 3, 1)
    pair_rows = pair_rows.reshape(2 * cols, width)
    query_rows = cross_query.T

    qkv_away = join_rows(swap(piece(qkv_rows), "far"))

    table_flat = camera_table.reshape(codes, -1)
    cross_gain_f = cross_gain.astype(WIDE)
    hidden_gain_f = hidden_gain.astype(WIDE)

    inputs = objects_of(tokens).reshape(count, width).astype(WIDE)
    patch_in = objects_of(patches).reshape(count, patch_width)
    length = objects_of(patch_len)
    grad_low = objects_of(cotangent).reshape(count, width)
    codes_of = objects_of(cam_index).reshape(count)
    onehot = (codes_of[:, None] == jnp.arange(codes)[None, :]).astype(LOW)
    shift_scale = mul(onehot, table_flat)
    gain_one = 1.0 + shift_scale[:, :width]
    unit_one, rate_one = normed(inputs)
    normed_one = (unit_one * gain_one + shift_scale[:, width:]).astype(LOW)

    mine = [piece(v) for v in (self_output, query_rows, cross_output, pair_rows)]
    normed_one, *mine = tie(normed_one, *mine)
    mine = jnp.concatenate(mine, axis=0)
    across = swap(mine, "far")
    size = cols // n_rows
    two = in_order(mine[None, : 3 * size], across[None, : 3 * size])
    four = jnp.concatenate([two, swap(two, "near")])
    sent = jnp.concatenate([four.reshape(-1, width), across[3 * size :]])
    sent = lax.all_gather(sent, "rows", axis=0)
    pair_away = sent[:, 12 * size :].reshape(2 * cols, width)
    whole = sent[:, : 12 * size].reshape(n_rows, 4, 3, size, width).transpose(2, 1, 0, 3, 4)
    self_whole, query_whole, cross_whole = whole.reshape(3, 4 * cols, width)

    qkv_both = in_order(qkv_rows, qkv_away)
    qkv = exchange_rows(to_pairs(qkv_both, normed_one, 3))
    patch_mid = mul(patch_in, patch_weights).astype(LOW)
    pair_both = in_order(pair_rows, pair_away)
    pair = to_pairs(pair_both, patch_mid, 2)

    mine = [piece(widen_weights), piece(narrow_weights)]
    qkv, *mine = tie(qkv, *mine)
    size = width // n_rows
    sent = lax.all_gather(jnp.concatenate(mine, axis=0), ("far", "rows"), axis=0)
    sent = sent.reshape(2, n_rows, 2, size, width)
    widen = sent[:, :, 0].reshape(2, width, hidden)
    widen = jnp.concatenate([widen[0], widen[1]], axis=1)
    narrow = sent[:, :, 1].reshape(2 * hidden, width)

    mixed, self_wide, self_log = pair_forward(qkv, qkv, 1)
    mixed, pair = tie(exchange_rows(mixed), pair)
    pair = exchange_rows(pair)
    self_mixed_t = from_pairs(mixed[:, :, None])
    after_self = inputs + over_all_columns(self_mixed_t, self_whole)
    unit_two, rate_two = normed(after_self)
    normed_two = (unit_two * cross_gain_f).astype(LOW)
    cross_q, pair = tie(to_pairs(query_whole[: 2 * cols], normed_two, 1), pair)
    cross_q = exchange_rows(cross_q)
    mixed, cross_wide, cross_log = pair_forward(cross_q, pair, 0, length)
    cross_mixed_t = from_pairs(exchange_rows(mixed)[:, :, None])
    after_cross = after_self + over_all_columns(cross_mixed_t, cross_whole)
    unit_three, rate_three = normed(after_cross)
    normed_three = (unit_three * hidden_gain_f).astype(LOW)
    activated, act_back = jax.vjp(gelu_tanh, mul(normed_three, widen))
    activated = activated.astype(LOW)
    grad_pre = act_back(mul(grad_low, narrow, NT))[0].astype(LOW)
    third, activated, grad_pre = tie(mul(grad_pre, widen, NT).astype(LOW), activated, grad_pre)
    grad_three = third.astype(WIDE) + swap(third, "near").astype(WIDE)
    hidden_mine, hidden_away = halves(mul(activated, narrow))
    hidden_away, grad_three = tie(hidden_away.astype(LOW), grad_three)
    hidden_half = hidden_mine + swap(hidden_away, "near").astype(WIDE)
    result = (halves(after_cross)[0] + hidden_half).astype(LOW)

    def part_rows(both):
        return lax.psum_scatter(both, "rows", scatter_dimension=1, tiled=True)

    def own_and_away(value):
        return [lax.dynamic_index_in_dim(value, index, 0, keepdims=False) for index in (far, 1 - far)]

    def add_far(mine, away):
        return (mine.astype(WIDE) + away.astype(WIDE)).astype(LOW)

    def by_shard(left, right):
        return mul(left, right, NN).astype(LOW).reshape(2, -1, right.shape[1])

    hidden_terms = jnp.concatenate(
        [
            mul(activated, grad_low, TN).astype(LOW).reshape(2, hidden, width),
            jnp.stack(
                [mul(normed_three, value, TN).astype(LOW) for value in jnp.split(grad_pre, 2, axis=1)]
            ),
        ],
        axis=1,
    )
    hidden_part = part_rows(hidden_terms)

    hidden_gain_term = jnp.sum(grad_three * unit_three, axis=0)
    grad_cross = grad_low.astype(WIDE) + normed_back(
        grad_three * hidden_gain_f, unit_three, rate_three
    )
    grad_cross_low = grad_cross.astype(LOW)
    grad_mixed = exchange_rows(to_pairs(cross_whole[: 2 * cols], grad_cross_low, 1)[:, :, 0])
    grad_mixed, result = tie(grad_mixed, result)
    result_two = jnp.stack([result, swap(result, "far")])
    grads = pair_backward(cross_q, pair, 0, length, grad_mixed, cross_wide, cross_log)
    grads, result_two, hidden_part = tie(grads, result_two, hidden_part)
    hidden_own, hidden_away = own_and_away(hidden_part)
    grads, hidden_away = tie(exchange_rows(grads), swap(hidden_away, "far"))
    hidden_total = join_rows(add_far(hidden_own, hidden_away))
    grad_cq_t = from_pairs(grads[:, :, :1])
    grad_pair_t = from_pairs(grads[:, :, 1:])
    middle_terms = jnp.concatenate(
        [
            by_shard(cross_mixed_t, grad_cross_low),
            by_shard(grad_cq_t, normed_two),
            by_shard(grad_pair_t, patch_mid),
        ],
        axis=1,
    )
    grad_cq_away, middle_terms = tie(swap(grad_cq_t, "near"), middle_terms)
    middle_part = part_rows(middle_terms)
    grad_two = mul(jnp.concatenate([grad_cq_t, grad_cq_away]), query_whole, TN)
    grad_two, result_two = tie(grad_two, result_two)
    result_four = jnp.stack([result_two, swap(result_two, "near")])
    cross_gain_term = jnp.sum(grad_two * unit_two, axis=0)
    grad_self = grad_cross + normed_back(grad_two * cross_gain_f, unit_two, rate_two)
    grad_self_low = grad_self.astype(LOW)
    grad_mixed, grad_self_low, grad_mid = tie(
        to_pairs(self_whole[: 2 * cols], grad_self_low, 1)[:, :, 0],
        grad_self_low,
        mul(grad_pair_t, pair_both, TN).astype(LOW),
    )
    grad_mid_away = swap(grad_mid, "near")
    output_terms = by_shard(self_mixed_t, grad_self_low)
    grads = pair_backward(qkv, qkv, 1, None, exchange_rows(grad_mixed), self_wide, self_log)
    grads, grad_mid_away, result_four, hidden_total = tie(grads, grad_mid_away, result_four, hidden_total)
    grad_mid = (grad_mid.astype(WIDE) + grad_mid_away.astype(WIDE)).astype(LOW)
    patch_half = mul(halves(grad_mid)[0], patch_weights, NT).astype(LOW)
    patch_two = jnp.stack([patch_half, swap(patch_half, "far")])
    patch_terms = jnp.stack([mul(value, patch_in, TN).astype(LOW) for value in both_columns(grad_mid)])
    patch_terms = jnp.pad(patch_terms, ((0, 0), (0, 0), (0, width - patch_width)))
    last_terms = jnp.pad(
        jnp.concatenate([output_terms, patch_terms], axis=1), ((0, 0), (3 * cols, 0), (0, 0))
    )
    grads, patch_two, last_terms, middle_part = tie(exchange_rows(grads), patch_two, last_terms, middle_part)
    grad_qkv_t = from_pairs(grads)
    last_terms = lax.dynamic_update_slice_in_dim(last_terms, by_shard(grad_qkv_t, normed_one), 0, 1)
    last_part = part_rows(last_terms)
    middle_own, middle_away = own_and_away(middle_part)
    first_mine, first_away = halves(mul(grad_qkv_t, qkv_both, TN))
    first_away, middle_away = tie(first_away.astype(LOW), middle_away)
    middle_total = join_rows(add_far(middle_own, swap(middle_away, "far")))
    grad_one = first_mine + swap(first_away, "near").astype(WIDE)
    gain_half, unit_half, rate_half, self_half = (
        halves(value)[0] for value in (gain_one, unit_one, rate_one, grad_self)
    )
    input_half = self_half + normed_back(grad_one * gain_half, unit_half, rate_half)
    input_half = input_half.astype(LOW)
    input_two = jnp.stack([input_half, swap(input_half, "far")])
    onehot_half = halves(onehot)[0].astype(WIDE)
    table_term = jnp.concatenate(
        [
            lax.dot_general(onehot_half, value, TN, precision=lax.Precision.HIGHEST)
            for value in (grad_one * unit_half, grad_one)
        ],
        axis=0,
    )
    small = [sum_near(table_term), hidden_gain_term[None], cross_gain_term[None], jnp.zeros((14, width), WIDE)]
    small = jnp.stack(both_columns(jnp.concatenate(small, axis=0).astype(LOW)))
    small = jnp.sum(lax.all_gather(small, "rows", axis=0).astype(WIDE), axis=0).astype(LOW)
    last_part, input_two, patch_two, small = tie(last_part, input_two, patch_two, small)
    input_four = jnp.stack([input_two, swap(input_two, "near")])
    patch_four = jnp.stack([patch_two, swap(patch_two, "near")])
    outputs = over_heads(result_four)
    hidden_gradients = [hidden_total[hidden:].astype(WIDE), hidden_total[:hidden].astype(WIDE)]
    last_own, last_away = own_and_away(last_part)
    last_sum, input_four = tie(add_far(last_own, swap(last_away, "far")), input_four)
    last_total = join_rows(last_sum)
    middle_total, outputs, hidden_gradients = tie(middle_total, outputs, hidden_gradients)
    small_own, small_away = own_and_away(small)
    small = small_own.astype(WIDE) + swap(small_away, "far").astype(WIDE)
    input_four, patch_four = tie(input_four, patch_four)
    input_grads, patch_grads = over_heads(input_four), over_heads(patch_four)

    cross_output_total, query_total = middle_total[:cols], middle_total[cols : 2 * cols]
    pair_total = middle_total[2 * cols :].reshape(heads, 2, HEAD_DIM, width)
    self_total = last_total[: 3 * cols].reshape(heads, 3, HEAD_DIM, width)
    self_output_total = last_total[3 * cols : 4 * cols]
    patch_total = last_total[4 * cols :, :patch_width]
    gradients = (
        small[: 2 * codes].reshape(2, codes, cols).transpose(1, 0, 2),
        self_total.transpose(1, 3, 0, 2).reshape(3, width, cols),
        self_output_total,
        small[2 * codes + 1],
        query_total.T,
        pair_total.transpose(1, 3, 0, 2).reshape(2, width, cols),
        cross_output_total,
        patch_total.T,
        small[2 * codes],
        *hidden_gradients,
    )
    return (outputs, input_grads.astype(WIDE), patch_grads.astype(WIDE)) + tuple(
        value.astype(WIDE) for value in gradients
    )


def per_device(
    tokens,
    cam_index,
    patches,
    patch_len,
    camera_table,
    self_weights,
    self_output,
    cross_gain,
    cross_query,
    cross_pair,
    cross_output,
    patch_weights,
    hidden_gain,
    widen_weights,
    narrow_weights,
    cotangent,
):
    batches, rows, width = tokens.shape
    cols = self_weights.shape[2]
    heads = cols // HEAD_DIM
    codes = camera_table.shape[0]
    patch_rows, patch_width = patches.shape[1:]
    n_rows, n_heads = lax.axis_size("rows"), lax.axis_size("heads")
    row_rank, head_rank = lax.axis_index("rows"), lax.axis_index("heads")
    groups = 1
    objects = batches // groups
    full_lengths = jnp.full((objects,), n_rows * rows, jnp.int32)
    count = objects * rows

    def own_columns(value):
        return lax.dynamic_slice_in_dim(value, head_rank * cols, cols, value.ndim - 1)

    table_flat = camera_table.reshape(codes, -1)
    cross_gain_f = cross_gain.astype(WIDE)
    hidden_gain_f = hidden_gain.astype(WIDE)

    qkv_rows = (
        self_weights.reshape(3, width, heads, HEAD_DIM).transpose(2, 0, 3, 1).reshape(3 * cols, width)
    )
    qkv_rows_back = self_weights.transpose(0, 2, 1).reshape(3 * cols, width)
    pair_rows = cross_pair.transpose(0, 2, 1).reshape(2 * cols, width)
    query_rows = cross_query.T

    local = jnp.stack([self_output, cross_output, query_rows])
    piece = cols // n_rows
    local = lax.dynamic_slice_in_dim(local, row_rank * piece, piece, 1)
    whole = lax.all_gather(jnp.stack(gather_heads(local)), "rows", axis=0)
    whole = whole.transpose(2, 1, 0, 3, 4).reshape(3, n_heads * cols, width)
    self_whole, cross_whole, query_whole = whole[0], whole[1], whole[2]

    def over_all_columns(value_t, weight):
        return mul(jnp.concatenate(gather_heads(value_t), axis=0), weight, TN)

    def by_object(weight, value):
        return jnp.stack(
            [mul(weight, value[i * rows : (i + 1) * rows], NT).astype(LOW) for i in range(objects)]
        )

    def column_terms(value, grads_t):
        return [
            mul(value, grads_t[i : i + cols], (((0,), (1,)), ((), ())))
            for i in range(0, grads_t.shape[0], cols)
        ]

    def one_group(group):
        part = slice(group * objects, (group + 1) * objects)
        inputs = tokens[part].reshape(count, width).astype(WIDE)
        patch_in = patches[part].reshape(objects * patch_rows, patch_width)
        lengths = patch_len[part]
        grad_low = cotangent[part].reshape(count, width)
        onehot = (cam_index[part].reshape(count)[:, None] == jnp.arange(codes)[None, :]).astype(LOW)
        shift_scale = mul(onehot, table_flat)
        gain_one = 1.0 + shift_scale[:, :width]
        unit_one, rate_one = normed(inputs)
        normed_one = (unit_one * gain_one + shift_scale[:, width:]).astype(LOW)
        qkv_t = by_object(qkv_rows, normed_one)
        by_kind = qkv_t.reshape(objects, heads, 3, HEAD_DIM, rows).transpose(2, 1, 3, 0, 4)
        by_kind = by_kind.reshape(3, cols, count)
        self_pair = lax.all_gather(by_kind[1:], "rows", axis=0)
        patch_mid = mul(patch_in, patch_weights).astype(LOW)
        own_pair = mul(pair_rows, patch_mid, NT).astype(LOW).reshape(2, cols, -1)
        pair_t = lax.all_gather(own_pair, "rows", axis=0)
        self_mixed_t, self_wide, self_log = cross_forward(by_kind[0], self_pair, full_lengths)
        after_self = inputs + over_all_columns(self_mixed_t, self_whole)
        unit_two, rate_two = normed(after_self)
        normed_two = (unit_two * cross_gain_f).astype(LOW)
        cross_q_t = mul(query_rows, normed_two, NT).astype(LOW)
        cross_mixed_t, cross_wide, cross_log = cross_forward(cross_q_t, pair_t, lengths)
        after_cross = after_self + over_all_columns(cross_mixed_t, cross_whole)
        unit_three, rate_three = normed(after_cross)
        normed_three = (unit_three * hidden_gain_f).astype(LOW)
        pre_act = mul(normed_three, widen_weights)
        activated, act_back = jax.vjp(gelu_tanh, pre_act)
        activated = activated.astype(LOW)
        grad_pre = act_back(mul(grad_low, narrow_weights, NT))[0].astype(LOW)
        grad_three = sum_heads(mul(grad_pre, widen_weights, NT)).astype(WIDE)
        yield "heads", {"hidden": mul(activated, narrow_weights)}
        yield "rows", {
            "narrow": mul(activated, grad_low, TN),
            "widen": mul(normed_three, grad_pre, TN),
        }
        hidden_gain_term = jnp.sum(own_columns(grad_three * unit_three), axis=0)
        grad_cross = grad_low.astype(WIDE) + normed_back(
            grad_three * hidden_gain_f, unit_three, rate_three
        )
        grad_cross_low = grad_cross.astype(LOW)
        cross_output_term = mul(cross_mixed_t, grad_cross_low)
        grad_mixed_t = mul(cross_output, grad_cross_low, NT).astype(LOW)
        grad_cq_t, grad_pair_t = cross_backward(
            cross_q_t, pair_t, lengths, grad_mixed_t, cross_wide, cross_log
        )
        grad_two = over_all_columns(grad_cq_t, query_whole)
        grad_pair_t = lax.psum_scatter(grad_pair_t, "rows", scatter_dimension=0, tiled=False)
        grad_pair_t = grad_pair_t.reshape(2 * cols, -1)
        query_term = mul(normed_two, grad_cq_t, (((0,), (1,)), ((), ())))
        cross_gain_term = jnp.sum(own_columns(grad_two * unit_two), axis=0)
        grad_self = grad_cross + normed_back(grad_two * cross_gain_f, unit_two, rate_two)
        grad_self_low = grad_self.astype(LOW)
        self_output_term = mul(self_mixed_t, grad_self_low)
        yield "heads", {"patch": mul(grad_pair_t, pair_rows, TN)}
        yield "rows", {
            "query": query_term,
            "pair": column_terms(patch_mid, grad_pair_t),
            "cross_output": cross_output_term,
            "self_output": self_output_term,
        }
        grad_self_mixed_t = mul(self_output, grad_self_low, NT).astype(LOW)
        grad_q_t, grad_kv_t = cross_backward(
            by_kind[0], self_pair, full_lengths, grad_self_mixed_t, self_wide, self_log
        )
        grad_kv_t = lax.psum_scatter(grad_kv_t, "rows", scatter_dimension=0, tiled=False)
        grad_qkv_t = jnp.concatenate([grad_q_t[None], grad_kv_t]).reshape(3 * cols, count)
        grad_qkv_t = yield "after", (grad_qkv_t, ["patch", "narrow", "widen"])
        grad_mid = yield "take", "patch"
        patch_term = mul(patch_in, own_columns(grad_mid), TN)
        patch_grad = mul(grad_mid, patch_weights, NT)
        grad_one = sum_heads(mul(grad_qkv_t, qkv_rows_back, TN))
        grad_one = yield "after", (grad_one, ["query", "pair", "cross_output", "self_output"])
        grad_one = grad_one.astype(WIDE)
        input_grad = grad_self + normed_back(grad_one * gain_one, unit_one, rate_one)
        own_grad = own_columns(grad_one)
        table_term = jnp.stack(
            [
                lax.dot_general(onehot.astype(WIDE), v, TN, precision=lax.Precision.HIGHEST)
                for v in (own_grad * own_columns(unit_one), own_grad)
            ],
            axis=1,
        )
        small = [patch_term, table_term.reshape(2 * codes, cols)]
        small += [hidden_gain_term[None], cross_gain_term[None], jnp.zeros((14, cols), WIDE)]
        yield "rows", {
            "self": column_terms(normed_one, grad_qkv_t),
            "small": jnp.concatenate(small, axis=0),
        }
        hidden_sum = yield "take", "hidden"
        result = (after_cross + hidden_sum.astype(WIDE)).astype(LOW)
        yield (
            "done",
            (
                result.reshape(objects, rows, width),
                input_grad.reshape(objects, rows, width),
                patch_grad.reshape(objects, patch_rows, patch_width),
            ),
        )

    steps = [one_group(group) for group in range(groups)]
    asked = [next(step) for step in steps]
    totals, ahead = {}, []
    while asked[0][0] != "done":
        kind, what = asked[0]
        answers = [None] * groups
        if kind == "take":
            answers = jnp.split(totals[what], groups)
        elif kind == "after":
            early = {name: totals[name] for name in what[1]}
            answers = [value for _, (value, _) in asked]
            answers[-1], early = lax.optimization_barrier((answers[-1], early))
            totals.update(early)
        else:
            terms = [value for _, value in asked]
            if kind == "heads":
                terms = jax.tree.map(lambda *parts: jnp.concatenate(parts, axis=0), *terms)
            else:
                for value in terms[1:]:
                    terms[0] = add_trees(terms[0], value)
                terms = terms[0]
            if kind == "rows":
                terms = jax.tree.map(lambda value: value.astype(LOW), terms)
            if kind == "heads":
                totals.update({name: sum_heads(value) for name, value in terms.items()})
            else:
                before = {name: totals[name] for name in ahead}
                terms, before = lax.optimization_barrier((terms, before))
                totals.update(before)
                totals.update(lax.psum(terms, kind))
                ahead = list(terms)
        asked = [step.send(value) for step, value in zip(steps, answers)]
    outputs, input_grads, patch_grads = (
        jnp.concatenate([value[i] for _, value in asked], axis=0) for i in range(3)
    )
    patch_total, table_total, gains = jnp.split(
        totals["small"], [patch_width, patch_width + 2 * codes]
    )
    gradients = (
        table_total.reshape(codes, 2, cols),
        jnp.stack(totals["self"]),
        totals["self_output"],
        gains[1],
        totals["query"],
        jnp.stack(totals["pair"]),
        totals["cross_output"],
        patch_total,
        gains[0],
        totals["widen"],
        totals["narrow"],
    )
    return (outputs, input_grads, patch_grads) + tuple(value.astype(WIDE) for value in gradients)


def solution(mesh):
    sizes = mesh.shape
    paired = sizes["heads"] == 4 and sizes["rows"] == 8
    heads = ("far", "near") if paired else "heads"
    if paired:
        names = (*heads, "rows")
        mesh = jax.sharding.Mesh(mesh.devices.reshape(2, 2, sizes["rows"]), names)
    in_specs = (
        P(None, "rows", None),
        P(None, "rows"),
        P(None, "rows", None),
        P(),
        P(),
        P(None, None, heads),
        P(heads, None),
        P(),
        P(None, heads),
        P(None, None, heads),
        P(heads, None),
        P(),
        P(),
        P(None, heads),
        P(heads, None),
        P(None, "rows", None),
    )
    out_specs = (
        P(None, "rows", None),
        P(None, "rows", None),
        P(None, "rows", None),
        P(None, None, heads),
        P(None, None, heads),
        P(heads, None),
        P(heads),
        P(None, heads),
        P(None, None, heads),
        P(heads, None),
        P(None, heads),
        P(heads),
        P(None, heads),
        P(heads, None),
    )
    return jax.shard_map(
        paired_device if paired else per_device,
        mesh=mesh,
        in_specs=in_specs,
        out_specs=out_specs,
        check_vma=False,
    )
```

```python
import jax
import jax.numpy as jnp
from jax import lax
from jax.experimental import pallas as pl
from jax.experimental.pallas import tpu as pltpu
from jax.sharding import PartitionSpec as P

HEAD_DIM = 64
EPSILON = 1e-05
SCALE = HEAD_DIM ** (-0.5)
LOW = jnp.bfloat16
WIDE = jnp.float32

NN = (((1,), (0,)), ((), ()))
NT = (((1,), (1,)), ((), ()))
TN = (((0,), (0,)), ((), ()))
T_LAST = (((0,), (1,)), ((), ()))


def mul(left, right, dims=NN):
    return lax.dot_general(left, right, dims, preferred_element_type=WIDE)


def load_values(values, block, values_t):
    rows = values_t.shape[1]
    at = slice(block * rows, (block + 1) * rows)
    values[at, :HEAD_DIM] = values_t.T
    values[at, HEAD_DIM:] = jnp.ones((rows, HEAD_DIM), values.dtype)


def attend_block(queries, keys_t, values):
    scores = mul(queries, keys_t)
    peak = jnp.max(scores, axis=1, keepdims=True)
    both = mul(jnp.exp(scores - peak).astype(LOW), values).T
    total = both[HEAD_DIM : HEAD_DIM + 1]
    return both[:HEAD_DIM] / total, peak.T + jnp.log(total)


def attend_block_back(scaled_q, grad_t, keys, keys_t, values, log_total, spread):
    probs = jnp.exp(mul(keys, scaled_q) - log_total)
    grad_scores = (probs * (mul(values, grad_t) - spread)).astype(LOW)
    return (
        (mul(keys_t, grad_scores) * SCALE).astype(LOW),
        mul(grad_scores, scaled_q.T),
        mul(probs.astype(LOW), grad_t.T),
    )


def estimate(rows, cols, passes):
    return pl.CostEstimate(
        flops=int(rows * cols * 1200 * passes), transcendentals=int(rows * cols), bytes_accessed=int(rows * 2048)
    )


VMEM_LIMIT = 48 << 20


def by_length(length, full, blocks, run):
    @pl.when(length * 4 > full)
    def _():
        run(blocks)

    @pl.when(length * 4 <= full)
    def _():
        run(blocks // 4)


def cross_forward(queries_t, pair_t, lengths):
    blocks, _, cols, all_patches = pair_t.shape
    objects = lengths.shape[0]
    heads = cols // HEAD_DIM
    rows, patch_rows = queries_t.shape[1] // objects, all_patches // objects

    def kernel(len_ref, q_ref, pair_ref, mixed_ref, wide_ref, log_ref, keys_t, values):
        queries = (q_ref[...] * LOW(SCALE)).T

        def run(live):
            for c in range(live):
                keys_t[:, c * patch_rows : (c + 1) * patch_rows] = pair_ref[c, 0]
                load_values(values, c, pair_ref[c, 1])
            size = live * patch_rows
            mixed, log_total = attend_block(queries, keys_t[:, :size], values[:size])
            mixed_ref[...] = mixed.astype(LOW)
            wide_ref[...] = mixed
            log_ref[...] = log_total

        by_length(len_ref[pl.program_id(0)], blocks * patch_rows, blocks, run)

    block = pl.BlockSpec((HEAD_DIM, rows), lambda b, j, lens: (j, b))
    return pl.pallas_call(
        kernel,
        grid_spec=pltpu.PrefetchScalarGridSpec(
            num_scalar_prefetch=1,
            grid=(objects, heads),
            in_specs=[
                block,
                pl.BlockSpec((blocks, 2, HEAD_DIM, patch_rows), lambda b, j, lens: (0, 0, j, b)),
            ],
            out_specs=[block, block, pl.BlockSpec((None, 1, rows), lambda b, j, lens: (j, 0, b))],
            scratch_shapes=[
                pltpu.VMEM((HEAD_DIM, blocks * patch_rows), LOW),
                pltpu.VMEM((blocks * patch_rows, 2 * HEAD_DIM), LOW),
            ],
        ),
        out_shape=[
            jax.ShapeDtypeStruct(queries_t.shape, LOW),
            jax.ShapeDtypeStruct(queries_t.shape, WIDE),
            jax.ShapeDtypeStruct((heads, 1, queries_t.shape[1]), WIDE),
        ],
        name="cross_forward",
        cost_estimate=estimate(objects * rows, blocks * patch_rows * heads, 1.4),
        compiler_params=pltpu.CompilerParams(vmem_limit_bytes=VMEM_LIMIT),
    )(lengths, queries_t, pair_t)


def cross_backward(queries_t, pair_t, lengths, grad_t_all, wide, log_total):
    blocks, _, cols, all_patches = pair_t.shape
    objects = lengths.shape[0]
    heads = cols // HEAD_DIM
    rows, patch_rows = queries_t.shape[1] // objects, all_patches // objects

    def kernel(len_ref, q_ref, pair_ref, g_ref, wide_ref, log_ref, out_q, out_pair, keys, keys_t, values):
        grad_t = g_ref[...]
        spread = jnp.sum(grad_t.astype(WIDE) * wide_ref[...], axis=0, keepdims=True)

        def run(live):
            for c in range(live):
                at = slice(c * patch_rows, (c + 1) * patch_rows)
                keys[at] = pair_ref[c, 0].T
                keys_t[:, at] = pair_ref[c, 0]
                values[at] = pair_ref[c, 1].T
            size = live * patch_rows
            out_q[...], grad_k, grad_v = attend_block_back(
                q_ref[...] * LOW(SCALE),
                grad_t,
                keys[:size],
                keys_t[:, :size],
                values[:size],
                log_ref[...],
                spread,
            )
            for c in range(live):
                at = slice(c * patch_rows, (c + 1) * patch_rows)
                out_pair[c, 0] = grad_k[at].T.astype(LOW)
                out_pair[c, 1] = grad_v[at].T.astype(LOW)
            for c in range(live, blocks):
                out_pair[c] = jnp.zeros_like(out_pair[c])

        by_length(len_ref[pl.program_id(0)], blocks * patch_rows, blocks, run)

    block = pl.BlockSpec((HEAD_DIM, rows), lambda b, j, lens: (j, b))
    pair_block = pl.BlockSpec((blocks, 2, HEAD_DIM, patch_rows), lambda b, j, lens: (0, 0, j, b))
    return pl.pallas_call(
        kernel,
        grid_spec=pltpu.PrefetchScalarGridSpec(
            num_scalar_prefetch=1,
            grid=(objects, heads),
            in_specs=[
                block,
                pair_block,
                block,
                block,
                pl.BlockSpec((None, 1, rows), lambda b, j, lens: (j, 0, b)),
            ],
            out_specs=[block, pair_block],
            scratch_shapes=[
                pltpu.VMEM((blocks * patch_rows, HEAD_DIM), LOW),
                pltpu.VMEM((HEAD_DIM, blocks * patch_rows), LOW),
                pltpu.VMEM((blocks * patch_rows, HEAD_DIM), LOW),
            ],
        ),
        out_shape=[
            jax.ShapeDtypeStruct(queries_t.shape, LOW),
            jax.ShapeDtypeStruct(pair_t.shape, LOW),
        ],
        name="cross_backward",
        cost_estimate=estimate(objects * rows, blocks * patch_rows * heads, 2.5),
        compiler_params=pltpu.CompilerParams(vmem_limit_bytes=VMEM_LIMIT),
    )(lengths, queries_t, pair_t, grad_t_all, wide, log_total)


def shift(value, step):
    size = lax.axis_size("heads")
    return lax.ppermute(value, "heads", [((i + step) % size, i) for i in range(size)])


def gather_heads(value):
    size = lax.axis_size("heads")
    if size != 4:
        return [value] + [shift(value, step) for step in range(1, size)]
    after, before = shift(value, 1), shift(value, -1)
    inner = lax.ppermute(after, "heads", [(1, 0), (2, 1)]) + lax.ppermute(before, "heads", [(1, 2), (2, 3)])
    return [value, after, inner, before]


def scatter_heads(partial):
    size, me = lax.axis_size("heads"), lax.axis_index("heads")

    def part(step):
        return lax.dynamic_index_in_dim(partial, (me + step) % size, 0, keepdims=False)

    if size != 4:
        total = part(0)
        for step in range(1, size):
            total = total + shift(part(step).astype(LOW), -step).astype(WIDE)
        return total
    far = part(2).astype(LOW)
    up = lax.ppermute(far, "heads", [(0, 1), (1, 2)]).astype(WIDE)
    down = lax.ppermute(far, "heads", [(2, 1), (3, 2)]).astype(WIDE)
    from_below = shift((part(1) + up).astype(LOW), -1)
    from_above = shift((part(3) + down).astype(LOW), 1)
    return part(0) + from_below.astype(WIDE) + from_above.astype(WIDE)


def in_order(parts):
    size, me = lax.axis_size("heads"), lax.axis_index("heads")
    out = jnp.zeros((size,) + parts[0].shape, parts[0].dtype)
    for step, value in enumerate(parts):
        out = lax.dynamic_update_index_in_dim(out, value, (me + step) % size, 0)
    return out.reshape((-1,) + parts[0].shape[1:])


def sum_heads(partial):
    size = lax.axis_size("heads")
    split = partial.reshape((size, -1) + partial.shape[1:])
    return in_order(gather_heads(scatter_heads(split).astype(LOW)))


def exchange_rows(value):
    return lax.all_to_all(value, "rows", 0, 0, tiled=True)


def normed(value):
    centred = value - jnp.mean(value, axis=-1, keepdims=True)
    rate = lax.rsqrt(jnp.mean(centred * centred, axis=-1, keepdims=True) + EPSILON)
    return centred * rate, rate


def normed_back(grad, unit, rate):
    return rate * (
        grad
        - jnp.mean(grad, axis=-1, keepdims=True)
        - unit * jnp.mean(grad * unit, axis=-1, keepdims=True)
    )


def gelu_tanh(pre_act):
    return jax.nn.gelu(pre_act, approximate=True)


def add_trees(former, latter):
    return jax.tree.map(jnp.add, former, latter)


def pair_forward(queries, pair, key_at, length=None):
    blocks, objects, _, width, rows = queries.shape
    pair_rows = pair.shape[4]
    lengths = jnp.full((objects,), blocks * pair_rows, jnp.int32) if length is None else length

    def kernel(len_ref, q_ref, k_ref, v_ref, mixed_ref, wide_ref, log_ref, keys_t, values):
        def run(live):
            @pl.when(pl.program_id(1) == 0)
            def _():
                for c in range(live):
                    keys_t[:, c * pair_rows : (c + 1) * pair_rows] = k_ref[c]
                    load_values(values, c, v_ref[c])

            size = live * pair_rows
            mixed, log_total = attend_block(
                (q_ref[...] * LOW(SCALE)).T, keys_t[:, :size], values[:size]
            )
            mixed_ref[...] = mixed.astype(LOW)
            wide_ref[...] = mixed
            log_ref[...] = log_total

        if length is None:
            run(blocks)
        else:
            by_length(len_ref[pl.program_id(0)], blocks * pair_rows, blocks, run)

    block = pl.BlockSpec((None, None, width, rows), lambda o, i, lens: (i, o, 0, 0))
    return pl.pallas_call(
        kernel,
        grid_spec=pltpu.PrefetchScalarGridSpec(
            num_scalar_prefetch=1,
            grid=(objects, blocks),
            in_specs=[
                pl.BlockSpec((None, None, None, width, rows), lambda o, i, lens: (i, o, 0, 0, 0)),
                pl.BlockSpec((blocks, None, None, width, pair_rows), lambda o, i, lens: (0, o, key_at, 0, 0)),
                pl.BlockSpec((blocks, None, None, width, pair_rows), lambda o, i, lens: (0, o, key_at + 1, 0, 0)),
            ],
            out_specs=[block, block, pl.BlockSpec((None, None, 1, rows), lambda o, i, lens: (i, o, 0, 0))],
            scratch_shapes=[
                pltpu.VMEM((width, blocks * pair_rows), LOW),
                pltpu.VMEM((blocks * pair_rows, 2 * width), LOW),
            ],
        ),
        out_shape=[
            jax.ShapeDtypeStruct((blocks, objects, width, rows), LOW),
            jax.ShapeDtypeStruct((blocks, objects, width, rows), WIDE),
            jax.ShapeDtypeStruct((blocks, objects, 1, rows), WIDE),
        ],
        name="pair_forward",
        cost_estimate=estimate(objects * blocks * rows, blocks * pair_rows, 2 if length is None else 1.4),
        compiler_params=pltpu.CompilerParams(vmem_limit_bytes=VMEM_LIMIT),
    )(lengths, queries, pair, pair)


def pair_backward(queries, pair, key_at, length, grad_mixed, wide, log_total):
    blocks, objects, _, width, rows = queries.shape
    lengths = jnp.full((objects,), blocks * rows, jnp.int32) if length is None else length

    def kernel(len_ref, q_ref, k_ref, v_ref, g_ref, wide_ref, log_ref, out_ref, keys, keys_t, values, grad_k, grad_v):
        i = pl.program_id(1)

        def run(live):
            size = live * rows

            @pl.when(i == 0)
            def _():
                for c in range(live):
                    at = slice(c * rows, (c + 1) * rows)
                    keys[at] = k_ref[c].T
                    keys_t[:, at] = k_ref[c]
                    values[at] = v_ref[c].T

            grad_t = g_ref[...]
            spread = jnp.sum(grad_t.astype(WIDE) * wide_ref[...], axis=0, keepdims=True)
            out_ref[i, 0], term_k, term_v = attend_block_back(
                q_ref[...] * LOW(SCALE),
                grad_t,
                keys[:size],
                keys_t[:, :size],
                values[:size],
                log_ref[...],
                spread,
            )

            @pl.when(i == 0)
            def _():
                grad_k[:size] = term_k
                grad_v[:size] = term_v

            @pl.when(i > 0)
            def _():
                grad_k[:size] += term_k
                grad_v[:size] += term_v

            @pl.when(i == blocks - 1)
            def _():
                for c in range(live):
                    at = slice(c * rows, (c + 1) * rows)
                    out_ref[c, 1] = grad_k[at].T.astype(LOW)
                    out_ref[c, 2] = grad_v[at].T.astype(LOW)
                for c in range(live, blocks):
                    out_ref[c, 1:] = jnp.zeros_like(out_ref[c, 1:])

        if length is None:
            run(blocks)
        else:
            by_length(len_ref[pl.program_id(0)], blocks * rows, blocks, run)

    block = pl.BlockSpec((None, None, width, rows), lambda o, i, lens: (i, o, 0, 0))
    return pl.pallas_call(
        kernel,
        grid_spec=pltpu.PrefetchScalarGridSpec(
            num_scalar_prefetch=1,
            grid=(objects, blocks),
            in_specs=[
                pl.BlockSpec((None, None, None, width, rows), lambda o, i, lens: (i, o, 0, 0, 0)),
                pl.BlockSpec((blocks, None, None, width, rows), lambda o, i, lens: (0, o, key_at, 0, 0)),
                pl.BlockSpec((blocks, None, None, width, rows), lambda o, i, lens: (0, o, key_at + 1, 0, 0)),
                block,
                block,
                pl.BlockSpec((None, None, 1, rows), lambda o, i, lens: (i, o, 0, 0)),
            ],
            out_specs=pl.BlockSpec((blocks, None, 3, width, rows), lambda o, i, lens: (0, o, 0, 0, 0)),
            scratch_shapes=[
                pltpu.VMEM((blocks * rows, width), LOW),
                pltpu.VMEM((width, blocks * rows), LOW),
                pltpu.VMEM((blocks * rows, width), LOW),
                pltpu.VMEM((blocks * rows, width), WIDE),
                pltpu.VMEM((blocks * rows, width), WIDE),
            ],
        ),
        out_shape=jax.ShapeDtypeStruct((blocks, objects, 3, width, rows), LOW),
        name="pair_backward",
        cost_estimate=estimate(objects * blocks * rows, blocks * rows, 3 if length is None else 2),
        compiler_params=pltpu.CompilerParams(vmem_limit_bytes=VMEM_LIMIT),
    )(lengths, queries, pair, pair, grad_mixed, wide, log_total)


def swap(value, axis):
    return lax.ppermute(value, axis, [(0, 1), (1, 0)])


def sum_near(partial):
    low = partial.astype(LOW)
    return low.astype(WIDE) + swap(low, "near").astype(WIDE)


def tie(value, *others):
    return lax.optimization_barrier((value, *others))


def paired_device(
    tokens,
    cam_index,
    patches,
    patch_len,
    camera_table,
    self_weights,
    self_output,
    cross_gain,
    cross_query,
    cross_pair,
    cross_output,
    patch_weights,
    hidden_gain,
    widen_weights,
    narrow_weights,
    cotangent,
):
    objects = tokens.shape[0] // 2
    _, rows, width = tokens.shape
    cols = self_weights.shape[2]
    hidden = widen_weights.shape[1]
    heads = cols // HEAD_DIM
    codes = camera_table.shape[0]
    patch_width = patches.shape[2]
    count = objects * rows
    n_rows = lax.axis_size("rows")
    row_rank = lax.axis_index("rows")
    far, near = lax.axis_index("far"), lax.axis_index("near")

    def objects_of(value):
        return lax.dynamic_slice_in_dim(value, objects * far, objects, 0)

    def piece(value):
        size = value.shape[0] // n_rows
        return lax.dynamic_slice_in_dim(value, row_rank * size, size, 0)

    def join_rows(value):
        return lax.all_gather(value, "rows", axis=0, tiled=True)

    def both_columns(value):
        return [
            lax.dynamic_slice_in_dim(value, (2 * index + near) * cols, cols, value.ndim - 1)
            for index in range(2)
        ]

    def in_order(mine, away, axis=0):
        size = mine.shape[axis]
        shape = list(mine.shape)
        shape[axis] *= 2
        out = lax.dynamic_update_slice_in_dim(jnp.zeros(shape, mine.dtype), mine, far * size, axis)
        return lax.dynamic_update_slice_in_dim(out, away, (1 - far) * size, axis)

    def halves(value):
        value = value.reshape(objects, 2, rows // 2, -1)
        return [
            lax.dynamic_index_in_dim(value, index, 1, keepdims=False).reshape(count // 2, -1)
            for index in (near, 1 - near)
        ]

    def half_sum_near(partial):
        mine, away = halves(partial)
        return mine + swap(away.astype(LOW), "near").astype(WIDE)

    def over_heads(value):
        value = value.reshape(2, 2, objects, rows // 2, -1)
        value = jnp.where(far == 0, value, jnp.flip(value, 1))
        value = jnp.where(near == 0, value, jnp.flip(value, 0))
        return value.transpose(1, 2, 0, 3, 4).reshape(2 * objects, rows, -1)

    def to_pairs(weights, value, slots):
        parts = [
            mul(weights, value[i * rows : (i + 1) * rows], NT)
            .astype(LOW)
            .reshape(n_rows, slots, HEAD_DIM, rows)
            for i in range(objects)
        ]
        return jnp.stack(parts, axis=1)

    def from_pairs(value):
        return value.transpose(0, 2, 3, 1, 4).reshape(-1, count)

    def over_all_columns(value_t, weight):
        return mul(jnp.concatenate([value_t, swap(value_t, "near")]), weight, TN)

    qkv_rows = self_weights.reshape(3, width, heads, HEAD_DIM).transpose(2, 0, 3, 1)
    qkv_rows = qkv_rows.reshape(3 * cols, width)
    pair_rows = cross_pair.reshape(2, width, heads, HEAD_DIM).transpose(2, 0, 3, 1)
    pair_rows = pair_rows.reshape(2 * cols, width)
    query_rows = cross_query.T

    qkv_away = join_rows(swap(piece(qkv_rows), "far"))

    table_flat = camera_table.reshape(codes, -1)
    cross_gain_f = cross_gain.astype(WIDE)
    hidden_gain_f = hidden_gain.astype(WIDE)

    inputs = objects_of(tokens).reshape(count, width).astype(WIDE)
    patch_in = objects_of(patches).reshape(count, patch_width)
    length = objects_of(patch_len)
    grad_low = objects_of(cotangent).reshape(count, width)
    codes_of = objects_of(cam_index).reshape(count)
    onehot = (codes_of[:, None] == jnp.arange(codes)[None, :]).astype(LOW)
    shift_scale = mul(onehot, table_flat)
    gain_one = 1.0 + shift_scale[:, :width]
    unit_one, rate_one = normed(inputs)
    normed_one = (unit_one * gain_one + shift_scale[:, width:]).astype(LOW)

    mine = [piece(v) for v in (self_output, query_rows, cross_output, pair_rows)]
    normed_one, *mine = tie(normed_one, *mine)
    mine = jnp.concatenate(mine, axis=0)
    across = swap(mine, "far")
    size = cols // n_rows
    two = in_order(mine[None, : 3 * size], across[None, : 3 * size])
    four = jnp.concatenate([two, swap(two, "near")])
    sent = jnp.concatenate([four.reshape(-1, width), across[3 * size :]])
    sent = lax.all_gather(sent, "rows", axis=0)
    pair_away = sent[:, 12 * size :].reshape(2 * cols, width)
    whole = sent[:, : 12 * size].reshape(n_rows, 4, 3, size, width).transpose(2, 1, 0, 3, 4)
    self_whole, query_whole, cross_whole = whole.reshape(3, 4 * cols, width)

    qkv_both = in_order(qkv_rows, qkv_away)
    qkv = [
        in_order(*(mul(weight, value, NT).astype(LOW) for weight in (qkv_rows, qkv_away)))
        for value in jnp.split(normed_one, objects)
    ]
    qkv = jnp.stack([value.reshape(n_rows, 3, HEAD_DIM, rows) for value in qkv], axis=1)
    qkv = exchange_rows(qkv)
    patch_mid = mul(patch_in, patch_weights).astype(LOW)
    pair_both = in_order(pair_rows, pair_away)
    pair = to_pairs(pair_both, patch_mid, 2)

    mine = [piece(widen_weights), piece(narrow_weights)]
    qkv, *mine = tie(qkv, *mine)
    size = width // n_rows
    sent = lax.all_gather(jnp.concatenate(mine, axis=0), ("far", "rows"), axis=0)
    sent = sent.reshape(2, n_rows, 2, size, width)
    widen = sent[:, :, 0].reshape(2, width, hidden)
    widen = jnp.concatenate([widen[0], widen[1]], axis=1)
    narrow = sent[:, :, 1].reshape(2 * hidden, width)

    mixed, self_wide, self_log = pair_forward(qkv, qkv, 1)
    mixed, pair = tie(exchange_rows(mixed), pair)
    pair = exchange_rows(pair)
    self_mixed_t = from_pairs(mixed[:, :, None])
    after_self = inputs + over_all_columns(self_mixed_t, self_whole)
    unit_two, rate_two = normed(after_self)
    normed_two = (unit_two * cross_gain_f).astype(LOW)
    cross_q, pair = tie(to_pairs(query_whole[: 2 * cols], normed_two, 1), pair)
    cross_q = exchange_rows(cross_q)
    mixed, cross_wide, cross_log = pair_forward(cross_q, pair, 0, length)
    cross_mixed_t = from_pairs(exchange_rows(mixed)[:, :, None])
    after_cross = after_self + over_all_columns(cross_mixed_t, cross_whole)
    unit_three, rate_three = normed(after_cross)
    normed_three = (unit_three * hidden_gain_f).astype(LOW)
    activated, act_back = jax.vjp(gelu_tanh, mul(normed_three, widen))
    activated = activated.astype(LOW)
    grad_pre = act_back(mul(grad_low, narrow, NT))[0].astype(LOW)
    third, activated, grad_pre = tie(mul(grad_pre, widen, NT).astype(LOW), activated, grad_pre)
    grad_three = third.astype(WIDE) + swap(third, "near").astype(WIDE)
    hidden_mine, hidden_away = halves(mul(activated, narrow))
    hidden_away, grad_three = tie(hidden_away.astype(LOW), grad_three)
    hidden_half = hidden_mine + swap(hidden_away, "near").astype(WIDE)
    result = (halves(after_cross)[0] + hidden_half).astype(LOW)

    def part_rows(both):
        return lax.psum_scatter(both, "rows", scatter_dimension=1, tiled=True)

    def own_and_away(value):
        return [lax.dynamic_index_in_dim(value, index, 0, keepdims=False) for index in (far, 1 - far)]

    def add_far(mine, away):
        return (mine.astype(WIDE) + away.astype(WIDE)).astype(LOW)

    def by_shard(left, right):
        return mul(left, right, NN).astype(LOW).reshape(2, -1, right.shape[1])

    hidden_terms = jnp.concatenate(
        [
            mul(activated, grad_low, TN).astype(LOW).reshape(2, hidden, width),
            jnp.stack(
                [mul(normed_three, value, TN).astype(LOW) for value in jnp.split(grad_pre, 2, axis=1)]
            ),
        ],
        axis=1,
    )
    hidden_part = part_rows(hidden_terms)

    hidden_gain_term = jnp.sum(grad_three * unit_three, axis=0)
    grad_cross = grad_low.astype(WIDE) + normed_back(
        grad_three * hidden_gain_f, unit_three, rate_three
    )
    grad_cross_low = grad_cross.astype(LOW)
    grad_mixed = exchange_rows(to_pairs(cross_whole[: 2 * cols], grad_cross_low, 1)[:, :, 0])
    grad_mixed, result = tie(grad_mixed, result)
    result_two = jnp.stack([result, swap(result, "far")])
    grads = pair_backward(cross_q, pair, 0, length, grad_mixed, cross_wide, cross_log)
    grads, result_two, hidden_part = tie(grads, result_two, hidden_part)
    hidden_own, hidden_away = own_and_away(hidden_part)
    grads, hidden_away = tie(exchange_rows(grads), swap(hidden_away, "far"))
    hidden_total = join_rows(add_far(hidden_own, hidden_away))
    grad_cq_t = from_pairs(grads[:, :, :1])
    grad_pair_t = from_pairs(grads[:, :, 1:])
    middle_terms = jnp.concatenate(
        [
            by_shard(cross_mixed_t, grad_cross_low),
            by_shard(grad_cq_t, normed_two),
            by_shard(grad_pair_t, patch_mid),
        ],
        axis=1,
    )
    grad_cq_away, middle_terms = tie(swap(grad_cq_t, "near"), middle_terms)
    middle_part = part_rows(middle_terms)
    grad_two = mul(jnp.concatenate([grad_cq_t, grad_cq_away]), query_whole, TN)
    grad_two, result_two = tie(grad_two, result_two)
    result_four = jnp.stack([result_two, swap(result_two, "near")])
    cross_gain_term = jnp.sum(grad_two * unit_two, axis=0)
    grad_self = grad_cross + normed_back(grad_two * cross_gain_f, unit_two, rate_two)
    grad_self_low = grad_self.astype(LOW)
    grad_mixed, grad_self_low, grad_mid = tie(
        to_pairs(self_whole[: 2 * cols], grad_self_low, 1)[:, :, 0],
        grad_self_low,
        mul(grad_pair_t, pair_both, TN).astype(LOW),
    )
    grad_mid_away = swap(grad_mid, "near")
    output_terms = by_shard(self_mixed_t, grad_self_low)
    grads = pair_backward(qkv, qkv, 1, None, exchange_rows(grad_mixed), self_wide, self_log)
    grads, grad_mid_away, result_four, hidden_total = tie(grads, grad_mid_away, result_four, hidden_total)
    grad_mid = (grad_mid.astype(WIDE) + grad_mid_away.astype(WIDE)).astype(LOW)
    patch_half = mul(halves(grad_mid)[0], patch_weights, NT).astype(LOW)
    patch_two = jnp.stack([patch_half, swap(patch_half, "far")])
    patch_terms = jnp.stack([mul(value, patch_in, TN).astype(LOW) for value in both_columns(grad_mid)])
    patch_terms = jnp.pad(patch_terms, ((0, 0), (0, 0), (0, width - patch_width)))
    last_terms = jnp.pad(
        jnp.concatenate([output_terms, patch_terms], axis=1), ((0, 0), (3 * cols, 0), (0, 0))
    )
    grads, patch_two, last_terms, middle_part = tie(exchange_rows(grads), patch_two, last_terms, middle_part)
    grad_qkv_t = from_pairs(grads)
    last_terms = lax.dynamic_update_slice_in_dim(last_terms, by_shard(grad_qkv_t, normed_one), 0, 1)
    last_part = part_rows(last_terms)
    middle_own, middle_away = own_and_away(middle_part)
    first_mine, first_away = halves(mul(grad_qkv_t, qkv_both, TN))
    first_away, middle_away = tie(first_away.astype(LOW), middle_away)
    middle_total = join_rows(add_far(middle_own, swap(middle_away, "far")))
    grad_one = first_mine + swap(first_away, "near").astype(WIDE)
    gain_half, unit_half, rate_half, self_half = (
        halves(value)[0] for value in (gain_one, unit_one, rate_one, grad_self)
    )
    input_half = self_half + normed_back(grad_one * gain_half, unit_half, rate_half)
    input_half = input_half.astype(LOW)
    input_two = jnp.stack([input_half, swap(input_half, "far")])
    onehot_half = halves(onehot)[0].astype(WIDE)
    table_term = jnp.concatenate(
        [
            lax.dot_general(onehot_half, value, TN, precision=lax.Precision.HIGHEST)
            for value in (grad_one * unit_half, grad_one)
        ],
        axis=0,
    )
    small = [sum_near(table_term), hidden_gain_term[None], cross_gain_term[None], jnp.zeros((14, width), WIDE)]
    small = jnp.stack(both_columns(jnp.concatenate(small, axis=0).astype(LOW)))
    small = jnp.sum(lax.all_gather(small, "rows", axis=0).astype(WIDE), axis=0).astype(LOW)
    last_part, input_two, patch_two, small = tie(last_part, input_two, patch_two, small)
    input_four = jnp.stack([input_two, swap(input_two, "near")])
    patch_four = jnp.stack([patch_two, swap(patch_two, "near")])
    outputs = over_heads(result_four)
    hidden_gradients = [hidden_total[hidden:].astype(WIDE), hidden_total[:hidden].astype(WIDE)]
    last_own, last_away = own_and_away(last_part)
    last_sum, input_four = tie(add_far(last_own, swap(last_away, "far")), input_four)
    last_total = join_rows(last_sum)
    middle_total, outputs, hidden_gradients = tie(middle_total, outputs, hidden_gradients)
    small_own, small_away = own_and_away(small)
    small = small_own.astype(WIDE) + swap(small_away, "far").astype(WIDE)
    input_four, patch_four = tie(input_four, patch_four)
    input_grads, patch_grads = over_heads(input_four), over_heads(patch_four)

    cross_output_total, query_total = middle_total[:cols], middle_total[cols : 2 * cols]
    pair_total = middle_total[2 * cols :].reshape(heads, 2, HEAD_DIM, width)
    self_total = last_total[: 3 * cols].reshape(heads, 3, HEAD_DIM, width)
    self_output_total = last_total[3 * cols : 4 * cols]
    patch_total = last_total[4 * cols :, :patch_width]
    gradients = (
        small[: 2 * codes].reshape(2, codes, cols).transpose(1, 0, 2),
        self_total.transpose(1, 3, 0, 2).reshape(3, width, cols),
        self_output_total,
        small[2 * codes + 1],
        query_total.T,
        pair_total.transpose(1, 3, 0, 2).reshape(2, width, cols),
        cross_output_total,
        patch_total.T,
        small[2 * codes],
        *hidden_gradients,
    )
    return (outputs, input_grads.astype(WIDE), patch_grads.astype(WIDE)) + tuple(
        value.astype(WIDE) for value in gradients
    )


def per_device(
    tokens,
    cam_index,
    patches,
    patch_len,
    camera_table,
    self_weights,
    self_output,
    cross_gain,
    cross_query,
    cross_pair,
    cross_output,
    patch_weights,
    hidden_gain,
    widen_weights,
    narrow_weights,
    cotangent,
):
    batches, rows, width = tokens.shape
    cols = self_weights.shape[2]
    heads = cols // HEAD_DIM
    codes = camera_table.shape[0]
    patch_rows, patch_width = patches.shape[1:]
    n_rows, n_heads = lax.axis_size("rows"), lax.axis_size("heads")
    row_rank, head_rank = lax.axis_index("rows"), lax.axis_index("heads")
    groups = 1
    objects = batches // groups
    full_lengths = jnp.full((objects,), n_rows * rows, jnp.int32)
    count = objects * rows

    def own_columns(value):
        return lax.dynamic_slice_in_dim(value, head_rank * cols, cols, value.ndim - 1)

    table_flat = camera_table.reshape(codes, -1)
    cross_gain_f = cross_gain.astype(WIDE)
    hidden_gain_f = hidden_gain.astype(WIDE)

    qkv_rows = (
        self_weights.reshape(3, width, heads, HEAD_DIM).transpose(2, 0, 3, 1).reshape(3 * cols, width)
    )
    qkv_rows_back = self_weights.transpose(0, 2, 1).reshape(3 * cols, width)
    pair_rows = cross_pair.transpose(0, 2, 1).reshape(2 * cols, width)
    query_rows = cross_query.T

    local = jnp.stack([self_output, cross_output, query_rows])
    piece = cols // n_rows
    local = lax.dynamic_slice_in_dim(local, row_rank * piece, piece, 1)
    whole = lax.all_gather(jnp.stack(gather_heads(local)), "rows", axis=0)
    whole = whole.transpose(2, 1, 0, 3, 4).reshape(3, n_heads * cols, width)
    self_whole, cross_whole, query_whole = whole[0], whole[1], whole[2]

    def over_all_columns(value_t, weight):
        return mul(jnp.concatenate(gather_heads(value_t), axis=0), weight, TN)

    def by_object(weight, value):
        return jnp.stack(
            [mul(weight, value[i * rows : (i + 1) * rows], NT).astype(LOW) for i in range(objects)]
        )

    def column_terms(value, grads_t):
        return [
            mul(value, grads_t[i : i + cols], (((0,), (1,)), ((), ())))
            for i in range(0, grads_t.shape[0], cols)
        ]

    def one_group(group):
        part = slice(group * objects, (group + 1) * objects)
        inputs = tokens[part].reshape(count, width).astype(WIDE)
        patch_in = patches[part].reshape(objects * patch_rows, patch_width)
        lengths = patch_len[part]
        grad_low = cotangent[part].reshape(count, width)
        onehot = (cam_index[part].reshape(count)[:, None] == jnp.arange(codes)[None, :]).astype(LOW)
        shift_scale = mul(onehot, table_flat)
        gain_one = 1.0 + shift_scale[:, :width]
        unit_one, rate_one = normed(inputs)
        normed_one = (unit_one * gain_one + shift_scale[:, width:]).astype(LOW)
        qkv_t = by_object(qkv_rows, normed_one)
        by_kind = qkv_t.reshape(objects, heads, 3, HEAD_DIM, rows).transpose(2, 1, 3, 0, 4)
        by_kind = by_kind.reshape(3, cols, count)
        self_pair = lax.all_gather(by_kind[1:], "rows", axis=0)
        patch_mid = mul(patch_in, patch_weights).astype(LOW)
        own_pair = mul(pair_rows, patch_mid, NT).astype(LOW).reshape(2, cols, -1)
        pair_t = lax.all_gather(own_pair, "rows", axis=0)
        self_mixed_t, self_wide, self_log = cross_forward(by_kind[0], self_pair, full_lengths)
        after_self = inputs + over_all_columns(self_mixed_t, self_whole)
        unit_two, rate_two = normed(after_self)
        normed_two = (unit_two * cross_gain_f).astype(LOW)
        cross_q_t = mul(query_rows, normed_two, NT).astype(LOW)
        cross_mixed_t, cross_wide, cross_log = cross_forward(cross_q_t, pair_t, lengths)
        after_cross = after_self + over_all_columns(cross_mixed_t, cross_whole)
        unit_three, rate_three = normed(after_cross)
        normed_three = (unit_three * hidden_gain_f).astype(LOW)
        pre_act = mul(normed_three, widen_weights)
        activated, act_back = jax.vjp(gelu_tanh, pre_act)
        activated = activated.astype(LOW)
        grad_pre = act_back(mul(grad_low, narrow_weights, NT))[0].astype(LOW)
        grad_three = sum_heads(mul(grad_pre, widen_weights, NT)).astype(WIDE)
        yield "heads", {"hidden": mul(activated, narrow_weights)}
        yield "rows", {
            "narrow": mul(activated, grad_low, TN),
            "widen": mul(normed_three, grad_pre, TN),
        }
        hidden_gain_term = jnp.sum(own_columns(grad_three * unit_three), axis=0)
        grad_cross = grad_low.astype(WIDE) + normed_back(
            grad_three * hidden_gain_f, unit_three, rate_three
        )
        grad_cross_low = grad_cross.astype(LOW)
        cross_output_term = mul(cross_mixed_t, grad_cross_low)
        grad_mixed_t = mul(cross_output, grad_cross_low, NT).astype(LOW)
        grad_cq_t, grad_pair_t = cross_backward(
            cross_q_t, pair_t, lengths, grad_mixed_t, cross_wide, cross_log
        )
        grad_two = over_all_columns(grad_cq_t, query_whole)
        grad_pair_t = lax.psum_scatter(grad_pair_t, "rows", scatter_dimension=0, tiled=False)
        grad_pair_t = grad_pair_t.reshape(2 * cols, -1)
        query_term = mul(normed_two, grad_cq_t, (((0,), (1,)), ((), ())))
        cross_gain_term = jnp.sum(own_columns(grad_two * unit_two), axis=0)
        grad_self = grad_cross + normed_back(grad_two * cross_gain_f, unit_two, rate_two)
        grad_self_low = grad_self.astype(LOW)
        self_output_term = mul(self_mixed_t, grad_self_low)
        yield "heads", {"patch": mul(grad_pair_t, pair_rows, TN)}
        yield "rows", {
            "query": query_term,
            "pair": column_terms(patch_mid, grad_pair_t),
            "cross_output": cross_output_term,
            "self_output": self_output_term,
        }
        grad_self_mixed_t = mul(self_output, grad_self_low, NT).astype(LOW)
        grad_q_t, grad_kv_t = cross_backward(
            by_kind[0], self_pair, full_lengths, grad_self_mixed_t, self_wide, self_log
        )
        grad_kv_t = lax.psum_scatter(grad_kv_t, "rows", scatter_dimension=0, tiled=False)
        grad_qkv_t = jnp.concatenate([grad_q_t[None], grad_kv_t]).reshape(3 * cols, count)
        grad_qkv_t = yield "after", (grad_qkv_t, ["patch", "narrow", "widen"])
        grad_mid = yield "take", "patch"
        patch_term = mul(patch_in, own_columns(grad_mid), TN)
        patch_grad = mul(grad_mid, patch_weights, NT)
        grad_one = sum_heads(mul(grad_qkv_t, qkv_rows_back, TN))
        grad_one = yield "after", (grad_one, ["query", "pair", "cross_output", "self_output"])
        grad_one = grad_one.astype(WIDE)
        input_grad = grad_self + normed_back(grad_one * gain_one, unit_one, rate_one)
        own_grad = own_columns(grad_one)
        table_term = jnp.stack(
            [
                lax.dot_general(onehot.astype(WIDE), v, TN, precision=lax.Precision.HIGHEST)
                for v in (own_grad * own_columns(unit_one), own_grad)
            ],
            axis=1,
        )
        small = [patch_term, table_term.reshape(2 * codes, cols)]
        small += [hidden_gain_term[None], cross_gain_term[None], jnp.zeros((14, cols), WIDE)]
        yield "rows", {
            "self": column_terms(normed_one, grad_qkv_t),
            "small": jnp.concatenate(small, axis=0),
        }
        hidden_sum = yield "take", "hidden"
        result = (after_cross + hidden_sum.astype(WIDE)).astype(LOW)
        yield (
            "done",
            (
                result.reshape(objects, rows, width),
                input_grad.reshape(objects, rows, width),
                patch_grad.reshape(objects, patch_rows, patch_width),
            ),
        )

    steps = [one_group(group) for group in range(groups)]
    asked = [next(step) for step in steps]
    totals, ahead = {}, []
    while asked[0][0] != "done":
        kind, what = asked[0]
        answers = [None] * groups
        if kind == "take":
            answers = jnp.split(totals[what], groups)
        elif kind == "after":
            early = {name: totals[name] for name in what[1]}
            answers = [value for _, (value, _) in asked]
            answers[-1], early = lax.optimization_barrier((answers[-1], early))
            totals.update(early)
        else:
            terms = [value for _, value in asked]
            if kind == "heads":
                terms = jax.tree.map(lambda *parts: jnp.concatenate(parts, axis=0), *terms)
            else:
                for value in terms[1:]:
                    terms[0] = add_trees(terms[0], value)
                terms = terms[0]
            if kind == "rows":
                terms = jax.tree.map(lambda value: value.astype(LOW), terms)
            if kind == "heads":
                totals.update({name: sum_heads(value) for name, value in terms.items()})
            else:
                before = {name: totals[name] for name in ahead}
                terms, before = lax.optimization_barrier((terms, before))
                totals.update(before)
                totals.update(lax.psum(terms, kind))
                ahead = list(terms)
        asked = [step.send(value) for step, value in zip(steps, answers)]
    outputs, input_grads, patch_grads = (
        jnp.concatenate([value[i] for _, value in asked], axis=0) for i in range(3)
    )
    patch_total, table_total, gains = jnp.split(
        totals["small"], [patch_width, patch_width + 2 * codes]
    )
    gradients = (
        table_total.reshape(codes, 2, cols),
        jnp.stack(totals["self"]),
        totals["self_output"],
        gains[1],
        totals["query"],
        jnp.stack(totals["pair"]),
        totals["cross_output"],
        patch_total,
        gains[0],
        totals["widen"],
        totals["narrow"],
    )
    return (outputs, input_grads, patch_grads) + tuple(value.astype(WIDE) for value in gradients)


def solution(mesh):
    sizes = mesh.shape
    paired = sizes["heads"] == 4 and sizes["rows"] == 8
    heads = ("far", "near") if paired else "heads"
    if paired:
        names = (*heads, "rows")
        mesh = jax.sharding.Mesh(mesh.devices.reshape(2, 2, sizes["rows"]), names)
    in_specs = (
        P(None, "rows", None),
        P(None, "rows"),
        P(None, "rows", None),
        P(),
        P(),
        P(None, None, heads),
        P(heads, None),
        P(),
        P(None, heads),
        P(None, None, heads),
        P(heads, None),
        P(),
        P(),
        P(None, heads),
        P(heads, None),
        P(None, "rows", None),
    )
    out_specs = (
        P(None, "rows", None),
        P(None, "rows", None),
        P(None, "rows", None),
        P(None, None, heads),
        P(None, None, heads),
        P(heads, None),
        P(heads),
        P(None, heads),
        P(None, None, heads),
        P(heads, None),
        P(None, heads),
        P(heads),
        P(None, heads),
        P(heads, None),
    )
    return jax.shard_map(
        paired_device if paired else per_device,
        mesh=mesh,
        in_specs=in_specs,
        out_specs=out_specs,
        check_vma=False,
    )
```
